32 devices in a mesh: row: 4 (over z), col: 8 (over y, x, core).
Axes of the slice: x: 2, y: 2, z: 4, core: 2. Of those that a mesh axis runs over, the one named last changes fastest.
Arguments:
- block_input: bfloat16 [8192, 2048], P('row', 'col'), may hold values from -6 to 6
- seq_lengths: int32 [8], replicated, may hold values from 1 to 1024, 6144 in all
- slot_order: int32 [8], replicated, may hold values from 0 to 7, each once
- routes: int32 [8192, 4], P('row'), may hold values from 0 to 7, all different within a row; in each aligned block of 1024 rows (0 to 1023, 1024 to 2047, ...) at most 1024 rows name the same one
- input_gain: bfloat16 [2048], P('col'), may hold values from 0.5 to 1.5
- query_weight: bfloat16 [2048, 2048], P('row', 'col'), may hold values from -0.125 to 0.125
- key_weight: bfloat16 [2048, 2048], P('row', 'col'), may hold values from -0.125 to 0.125
- value_weight: bfloat16 [2048, 2048], P('row', 'col'), may hold values from -0.125 to 0.125
- output_weight: bfloat16 [2048, 2048], P('col', 'row'), may hold values from -2 to 2
- mlp_gain: bfloat16 [2048], P('col'), may hold values from 0.5 to 1.5
- router_weight: bfloat16 [2048, 8], P('row'), may hold values from -0.0625 to 0.0625
- score_shared: bfloat16 [2048], P('row'), may hold values from -0.125 to 0.125
- gate_shared: bfloat16 [2048, 5632], P('row', 'col'), may hold values from -0.125 to 0.125
- up_shared: bfloat16 [2048, 5632], P('row', 'col'), may hold values from -0.125 to 0.125
- down_shared: bfloat16 [5632, 2048], P('col', 'row'), may hold values from -0.21875 to 0.21875
- gate_expert: bfloat16 [8, 2048, 1408], P('col', 'row'), may hold values from -0.125 to 0.125
- up_expert: bfloat16 [8, 2048, 1408], P('col', 'row'), may hold values from -0.125 to 0.125
- down_expert: bfloat16 [8, 1408, 2048], P('col', None, 'row'), may hold values from -1.25 to 1.25
- grad_output: bfloat16 [8192, 2048], P('row', 'col'), may hold values from -6 to 6
Outputs:
- block_output: bfloat16 [8192, 2048], P('row', 'col')
- grad_input: bfloat16 [8192, 2048], P('row', 'col')
- grad_input_gain: float32 [2048], P('col')
- grad_query: float32 [2048, 2048], P('row', 'col')
- grad_key: float32 [2048, 2048], P('row', 'col')
- grad_value: float32 [2048, 2048], P('row', 'col')
- grad_output_weight: float32 [2048, 2048], P('col', 'row')
- grad_mlp_gain: float32 [2048], P('col')
- grad_router: float32 [2048, 8], P('row')
- grad_score_shared: float32 [2048], P('row')
- grad_gate_shared: float32 [2048, 5632], P('row', 'col')
- grad_up_shared: float32 [2048, 5632], P('row', 'col')
- grad_down_shared: float32 [5632, 2048], P('col', 'row')
- grad_gate_expert: float32 [8, 2048, 1408], P('col', 'row')
- grad_up_expert: float32 [8, 2048, 1408], P('col', 'row')
- grad_down_expert: float32 [8, 1408, 2048], P('col', None, 'row')
The draws below stay inside these ranges and needn't reach their ends.
Inputs may be any that keep to these rules, and one draw needn't show every extreme that they name: `seq_lengths`: they add up to 6144; the longest is exactly 1024. `slot_order`: each slot number appears once. `routes`: each row names 4 different experts; in each aligned block of 1024 consecutive rows (one micro-batch of one row-device's tokens) no expert is named by more than 1024 rows, so any expert may be named by every row of a block, and some block has an expert named by all of its rows.
All inputs are finite; a program needn't handle non-finite values.
Results may differ from the reference program's by a relative error of at most 0.022.
Values may be sent and summed in bfloat16 or wider, within the bound.
A program may use at most 272 MiB of HBM per device.

```python
import math
from functools import partial
import jax
import jax.numpy as jnp
import numpy as np
from jax import lax

D = 2048
HEADS = 16
HEAD_DIM = 128
FS = 5632
FE = 1408
TOP = 4
SEQ_LEN = 1024
EXPERTS = 8
MB_TOK = 1024
TOKENS = 8192
NSEQ = 8
LIVE = 6144
CAP = 1024


def steps_of(stream_key, shape, cuts, low, high):
    level = 1.0
    for axis_at, shards_of in cuts:
        steps = jax.random.uniform(jax.random.fold_in(jax.random.fold_in(stream_key, 6), axis_at), (shards_of,), jnp.float32, low / len(cuts), high / len(cuts))
        level = level * jnp.repeat(jnp.exp(steps), shape[axis_at] // shards_of).reshape((-1,) + (1,) * (len(shape) - 1 - axis_at))
    return level


def length_profile(amount, total, bound, slope):
    loads = [(1 << 20) // math.isqrt(grade ** slope) + 1 for grade in range(2, amount + 1)]
    rest, given = total - bound - (amount - 1), [1] * (amount - 1)
    while rest > 0:
        movable = [i for i in range(amount - 1) if given[i] < bound]
        whole, left = sum([loads[i] for i in movable]), rest
        for i in movable:
            extra = min(bound - given[i], max(1, left * loads[i] // whole), rest)
            given[i] = given[i] + extra
            rest = rest - extra
    return np.array([bound] + given)


def ragged_sizes(own_key, number_of, total, limit, skew):
    if number_of == 2:
        one = jax.random.randint(own_key, (), max(1, total - limit), min(limit, total - 1) + 1)
        return jnp.stack([one, total - one])
    tallies = jnp.asarray(length_profile(number_of, total, limit, skew), jnp.int32)
    twos = (number_of - 1) // 2
    giver, sink = tallies[1:1 + 2 * twos:2], tallies[2:2 + 2 * twos:2]
    room = jnp.minimum(giver - 1, limit - sink)
    moved = jax.random.randint(jax.random.fold_in(own_key, 1), (twos,), 0, 1 << 20) % (room + 1)
    tallies = tallies.at[1:1 + 2 * twos:2].set(giver - moved).at[2:2 + 2 * twos:2].set(sink + moved)
    return tallies[jax.random.permutation(jax.random.fold_in(own_key, 2), number_of)]


def routed_block(key, own, number, rows, number_of, top, most, skew):
    order = jax.random.permutation(key, number_of)
    heavy_load, usual = load_shares(number_of, rows * top, most, skew, True), load_shares(number_of, rows * top, most, skew, False)
    places = jnp.arange(number_of)

    def named(tallies, turn):
        used = int((tallies > 0).sum())
        fixed = max(1, used // 4)
        passed = fixed + (places - fixed + turn * (used - fixed)) % max(1, number_of - fixed)
        return jnp.zeros((number_of,), jnp.int32).at[order[jnp.where(places < fixed, places, passed)]].set(jnp.asarray(tallies, jnp.int32))

    tallies = jnp.where(number % 4 == 0, named(heavy_load, number // 4), named(usual, number - number // 4 - 1))
    mixed = jax.random.permutation(jax.random.fold_in(own, 3), number_of)
    giver, sink = mixed[0:number_of // 2 * 2:2], mixed[1:number_of // 2 * 2:2]
    margin = jnp.minimum(tallies[giver] - 1, most - tallies[sink]) // 2
    margin = jnp.where((giver == order[0]) | (sink == order[0]) | (tallies[sink] == 0), 0, jnp.maximum(margin, 0))
    passed = jax.random.randint(jax.random.fold_in(own, 4), (number_of // 2,), 0, 1 << 20) % (margin + 1)
    tallies = tallies.at[giver].add(-passed).at[sink].add(passed)
    items = jnp.searchsorted(jnp.cumsum(tallies), jnp.arange(rows * top), side="right").astype(jnp.int32)
    listing = items.reshape(top, rows).T
    listing = listing[jax.random.permutation(jax.random.fold_in(own, 1), rows)]
    turn = jax.random.randint(jax.random.fold_in(own, 2), (rows, 1), 0, top)
    return jnp.take_along_axis(listing, (jnp.arange(top)[None, :] + turn) % top, axis=1)


def load_shares(amount, total, reach, lean, full):
    portions = [(1 << 20) // math.isqrt(rank ** lean) + 1 for rank in range(1, amount + 1)]
    largest = reach if full else min(reach, max(-(-total // amount), total * portions[0] // sum(portions)))
    least = 1 if total - largest >= amount - 1 else 0
    holding, surplus = [largest] + [least] * (amount - 1), total - largest - least * (amount - 1)
    while surplus > 0:
        candidates = [i for i in range(1, amount) if holding[i] < largest] or [i for i in range(1, amount) if holding[i] < reach]
        pool, budget = sum([portions[i] for i in candidates]), surplus
        for i in candidates:
            more = min(reach - holding[i], max(1, budget * portions[i] // pool), surplus)
            holding[i] = holding[i] + more
            surplus = surplus - more
    return np.array(holding)


def normal_values(stream_key, dims, scale, most, pieces=(), dtype=jnp.bfloat16):
    drawn = scale * jax.random.normal(stream_key, dims, jnp.float32)
    if pieces:
        drawn = drawn * steps_of(stream_key, dims, pieces, -0.22, 0.18)
    return jnp.clip(drawn, -most, most).astype(dtype)


def setup_inputs(seed: int = 0) -> dict:
    key_list = jax.random.split(jax.random.key(seed), 20)
    block_input = normal_values(key_list[0], (TOKENS, D), 1.0, 6.0, ((0, 4), (1, 8)))
    seq_lengths = ragged_sizes(key_list[1], NSEQ, LIVE, SEQ_LEN, 0).astype(jnp.int32)
    slot_order = jax.random.permutation(key_list[2], NSEQ).astype(jnp.int32)
    routes_keys = jax.random.split(jax.random.fold_in(key_list[3], 1), TOKENS // MB_TOK)
    routes_turns = jax.random.permutation(jax.random.fold_in(key_list[3], 3), TOKENS // MB_TOK)
    routes = jax.vmap(lambda own, number: routed_block(jax.random.fold_in(key_list[3], 2), own, number, MB_TOK, EXPERTS, TOP, CAP, 1))(routes_keys, routes_turns).reshape((TOKENS, TOP))
    input_gain = jnp.clip(1.0 + 0.1 * jax.random.normal(key_list[4], (D,), jnp.float32), 0.5, 1.5).astype(jnp.bfloat16)
    query_weight = normal_values(key_list[5], (D, HEADS * HEAD_DIM), D ** -0.5, 0.125, ((0, 4), (1, 8)))
    key_weight = normal_values(key_list[6], (D, HEADS * HEAD_DIM), D ** -0.5, 0.125, ((0, 4), (1, 8)))
    value_weight = normal_values(key_list[7], (D, HEADS * HEAD_DIM), D ** -0.5, 0.125, ((0, 4), (1, 8)))
    output_weight = normal_values(key_list[8], (HEADS * HEAD_DIM, D), (max(D // 256, 1)) ** -0.5, 2.0, ((0, 8), (1, 4)))
    mlp_gain = jnp.clip(1.0 + 0.1 * jax.random.normal(key_list[9], (D,), jnp.float32), 0.5, 1.5).astype(jnp.bfloat16)
    router_weight = normal_values(key_list[10], (D, EXPERTS), (4 * D) ** -0.5, 0.0625, ((0, 4),))
    score_shared = normal_values(key_list[11], (D,), D ** -0.5, 0.125, ((0, 4),))
    gate_shared = normal_values(key_list[12], (D, FS), D ** -0.5, 0.125, ((0, 4), (1, 8)))
    up_shared = normal_values(key_list[13], (D, FS), D ** -0.5, 0.125, ((0, 4), (1, 8)))
    down_shared = normal_values(key_list[14], (FS, D), (max(FS // 8, 1)) ** -0.5, 0.21875, ((0, 8), (1, 4)))
    gate_expert = normal_values(key_list[15], (EXPERTS, D, FE), D ** -0.5, 0.125, ((0, 8), (1, 4)))
    up_expert = normal_values(key_list[16], (EXPERTS, D, FE), D ** -0.5, 0.125, ((0, 8), (1, 4)))
    down_expert = normal_values(key_list[17], (EXPERTS, FE, D), (max(FE // 64, 1)) ** -0.5, 1.25, ((0, 8), (2, 4)))
    grad_output = normal_values(key_list[18], (TOKENS, D), 1.0, 6.0, ((0, 4), (1, 8)))
    return {"block_input": block_input, "seq_lengths": seq_lengths, "slot_order": slot_order, "routes": routes, "input_gain": input_gain, "query_weight": query_weight, "key_weight": key_weight, "value_weight": value_weight, "output_weight": output_weight, "mlp_gain": mlp_gain, "router_weight": router_weight, "score_shared": score_shared, "gate_shared": gate_shared, "up_shared": up_shared, "down_shared": down_shared, "gate_expert": gate_expert, "up_expert": up_expert, "down_expert": down_expert, "grad_output": grad_output}


@jax.custom_vjp
def low(v):
    return lax.optimization_barrier(v.astype(jnp.bfloat16)).astype(jnp.float32)

@jax.custom_vjp
def low_back(v):
    return v

def low_keep(v):
    return (low(v), None)

def low_pass(kept, grad):
    return (grad,)

def back_keep(v):
    return (v, None)

def back_low(kept, grad):
    return (low(grad),)
low.defvjp(low_keep, low_pass)
low_back.defvjp(back_keep, back_low)
norm_eps = 1e-06
rope_base = 1000000.0
highest = lax.Precision.HIGHEST

def matmul(left, right):
    return jnp.dot(left, right, precision=highest, preferred_element_type=jnp.float32)

def rms_norm(values, gain):
    scale = lax.rsqrt(lax.optimization_barrier(jnp.mean(values * values, axis=-1, keepdims=True)) + norm_eps)
    return values * scale * gain

def rope_tables(length, width):
    positions = jnp.arange(length).astype(jnp.float32)
    freqs = jnp.power(jnp.float32(rope_base), -jnp.arange(0, width, 2).astype(jnp.float32) / width)
    angles = positions[:, None] * freqs[None, :]
    angles = jnp.concatenate([angles, angles], axis=-1)
    return (jnp.cos(angles)[:, None, :], jnp.sin(angles)[:, None, :])

def rotate(values, cosine, sine):
    half = values.shape[-1] // 2
    turned = jnp.concatenate([-values[..., half:], values[..., :half]], axis=-1)
    return values * cosine + turned * sine

def attend(items):
    query, keyset, valueset, length = items
    raw = jnp.einsum('qhd,khd->hqk', query, keyset, precision=highest)
    scores = low_back(raw) * (1.0 / math.sqrt(HEAD_DIM))
    query_pos = jnp.arange(SEQ_LEN)[:, None]
    key_pos = jnp.arange(SEQ_LEN)[None, :]
    allowed = (key_pos <= query_pos) & (key_pos < length)
    scores = jnp.where(allowed[None], scores, -1e+30)
    top = lax.optimization_barrier(jnp.max(scores, axis=-1, keepdims=True))
    expo = jnp.exp(scores - top)
    probs = low(expo / lax.optimization_barrier(jnp.sum(expo, axis=-1, keepdims=True)))
    return jnp.einsum('hqk,khd->qhd', probs, valueset, precision=highest)

def forward_apply(slot_length, routes, input_tuple, attention_norm_gain, query_projection_weight, key_projection_weight, value_projection_weight, output_projection_weight, feedforward_norm_gain, router_matrix, shared_score_weight, shared_gate_weight, shared_up_weight, shared_down_weight, expert_gate_weight, expert_up_weight, expert_down_weight):
    tokens = input_tuple.shape[0]
    slots = tokens // SEQ_LEN
    width = HEADS * HEAD_DIM
    cosine, sine = rope_tables(SEQ_LEN, HEAD_DIM)
    normed_a = low(rms_norm(input_tuple, attention_norm_gain))

    def project(weight, turn):
        raw = low_back(matmul(normed_a, weight)).reshape(slots, SEQ_LEN, HEADS, HEAD_DIM)
        if turn:
            raw = rotate(raw, cosine, sine)
        return low(raw)
    query = project(query_projection_weight, True)
    keyset = project(key_projection_weight, True)
    valueset = project(value_projection_weight, False)
    context = lax.map(jax.checkpoint(attend), (query, keyset, valueset, slot_length))
    context = low(low_back(context)).reshape(tokens, width)
    stream = input_tuple + low_back(matmul(context, output_projection_weight))
    normed_b = low(rms_norm(stream, feedforward_norm_gain))
    logits = matmul(normed_b, router_matrix)
    top = lax.optimization_barrier(jnp.max(logits, axis=-1, keepdims=True))
    expo = jnp.exp(logits - top)
    router_probs = expo / lax.optimization_barrier(jnp.sum(expo, axis=-1, keepdims=True))
    shared_gate = jax.nn.sigmoid(matmul(normed_b, shared_score_weight))
    gate_part = low_back(matmul(normed_b, shared_gate_weight))
    up_part = low_back(matmul(normed_b, shared_up_weight))
    shared_hidden = low(jax.nn.silu(gate_part) * up_part)
    shared_out = low_back(matmul(shared_hidden, shared_down_weight))
    expert_membership = jnp.any(routes[:, :, None] == jnp.arange(EXPERTS)[None, None, :], axis=1)
    weight_bundle = jnp.where(expert_membership, router_probs, 0.0)
    capacity_all = CAP * (tokens // MB_TOK)

    def expert_iteration(total, items):
        w_gate, w_up, w_down, column, chosen = items
        index = jnp.nonzero(chosen, size=capacity_all, fill_value=0)[0].astype(jnp.int32)
        valid = jnp.arange(capacity_all) < jnp.sum(chosen.astype(jnp.int32))
        selected_probability = normed_b[index]
        gate_rows = low_back(matmul(selected_probability, w_gate))
        up_rows = low_back(matmul(selected_probability, w_up))
        hidden = low(jax.nn.silu(gate_rows) * up_rows)
        result = low_back(matmul(hidden, w_down))
        scaled = jnp.where(valid[:, None], column[index][:, None] * result, 0.0)
        return (total.at[index].add(scaled), None)
    start_offset = jnp.zeros((tokens, input_tuple.shape[1]), jnp.float32)
    routed_output, unused_item = lax.scan(jax.checkpoint(expert_iteration), start_offset, (expert_gate_weight, expert_up_weight, expert_down_weight, weight_bundle.T, expert_membership.T))
    return stream + shared_gate[:, None] * shared_out + routed_output

def reference(block_input, seq_lengths, slot_order, routes, input_gain, query_weight, key_weight, value_weight, output_weight, mlp_gain, router_weight, score_shared, gate_shared, up_shared, down_shared, gate_expert, up_expert, down_expert, grad_output):
    slot_length = seq_lengths[slot_order]
    floats = [arr.astype(jnp.float32) for arr in (block_input, input_gain, query_weight, key_weight, value_weight, output_weight, mlp_gain, router_weight, score_shared, gate_shared, up_shared, down_shared, gate_expert, up_expert, down_expert)]
    output, pullback = jax.vjp(partial(forward_apply, slot_length, routes), *floats)
    grads = pullback(grad_output.astype(jnp.float32))
    return (output.astype(jnp.bfloat16), grads[0].astype(jnp.bfloat16), grads[1], grads[2], grads[3], grads[4], grads[5], grads[6], grads[7], grads[8], grads[9], grads[10], grads[11], grads[12], grads[13], grads[14])
```

```python
import functools
import math

import jax
import jax.numpy as jnp
from jax import lax
from jax.experimental import pallas as pl
from jax.experimental.pallas import tpu as pltpu
from jax.sharding import PartitionSpec as P

HEAD_DIM = 128
SEQ_LEN = 1024
QBLOCK = 256
CHUNK = 512
norm_eps = 1e-06
rope_base = 1000000.0
bf16 = jnp.bfloat16
f32 = jnp.float32


def mm(left, right):
    return jnp.dot(left, right, preferred_element_type=f32)


def mm_nt(left, right):
    return lax.dot_general(left, right, (((1,), (1,)), ((), ())), preferred_element_type=f32)


def mm_tn(left, right):
    return lax.dot_general(left, right, (((0,), (0,)), ((), ())), preferred_element_type=f32)


def rope_tables():
    positions = jnp.arange(SEQ_LEN).astype(f32)
    freqs = jnp.power(f32(rope_base), -jnp.arange(0, HEAD_DIM, 2).astype(f32) / HEAD_DIM)
    angles = positions[:, None] * freqs[None, :]
    cosine, sine = jnp.cos(angles), jnp.sin(angles)
    return (
        jnp.concatenate([cosine, cosine], axis=-1),
        jnp.concatenate([-sine, sine], axis=-1),
    )


def block_scores(rows, keys, start, length, scale):
    raw = mm_nt(rows, keys) * scale
    query_pos = start + lax.broadcasted_iota(jnp.int32, raw.shape, 0)
    key_pos = lax.broadcasted_iota(jnp.int32, raw.shape, 1)
    return jnp.where((key_pos <= query_pos) & (key_pos < length), raw, -1e30)


def attend_forward_kernel(length_ref, raw_ref, cos_ref, sin_ref, qkv_ref, context_ref, lse_ref):
    length = length_ref[pl.program_id(0)]
    scale = 1.0 / math.sqrt(HEAD_DIM)
    hd = HEAD_DIM
    for part in range(2):
        raw = raw_ref[:, part * hd : (part + 1) * hd]
        turned = raw * cos_ref[...] + pltpu.roll(raw, hd // 2, 1) * sin_ref[...]
        qkv_ref[:, part * hd : (part + 1) * hd] = turned.astype(bf16)
    qkv_ref[:, 2 * hd :] = raw_ref[:, 2 * hd :].astype(bf16)
    for at in range(0, SEQ_LEN, QBLOCK):
        seen = at + QBLOCK
        scores = block_scores(
            qkv_ref[at:seen, :hd], qkv_ref[:seen, hd : 2 * hd], at, length, scale
        )
        top = jnp.max(scores, axis=-1, keepdims=True)
        expo = jnp.exp(scores - top)
        total = jnp.sum(expo, axis=-1, keepdims=True)
        probs = (expo / total).astype(bf16)
        context_ref[at:seen, :] = mm(probs, qkv_ref[:seen, 2 * hd :]).astype(bf16)
        lse_ref[at:seen, :] = jnp.broadcast_to(top + jnp.log(total), (QBLOCK, hd))


def attend_forward(raw, lengths, cosine, sine):
    tokens, width = raw.shape
    heads = width // (3 * HEAD_DIM)
    slots = tokens // SEQ_LEN
    wide = pl.BlockSpec((SEQ_LEN, 3 * HEAD_DIM), lambda s, h, _: (s, h))
    one = pl.BlockSpec((SEQ_LEN, HEAD_DIM), lambda s, h, _: (s, h))
    table = pl.BlockSpec((SEQ_LEN, HEAD_DIM), lambda s, h, _: (0, 0))
    pairs = slots * heads * SEQ_LEN * SEQ_LEN
    return pl.pallas_call(
        attend_forward_kernel,
        grid_spec=pltpu.PrefetchScalarGridSpec(
            num_scalar_prefetch=1,
            grid=(slots, heads),
            in_specs=[wide, table, table],
            out_specs=[wide, one, one],
        ),
        out_shape=[
            jax.ShapeDtypeStruct((tokens, width), bf16),
            jax.ShapeDtypeStruct((tokens, heads * HEAD_DIM), bf16),
            jax.ShapeDtypeStruct((tokens, heads * HEAD_DIM), f32),
        ],
        cost_estimate=pl.CostEstimate(
            flops=3 * HEAD_DIM * pairs, bytes_accessed=8 * tokens * width, transcendentals=pairs
        ),
        name="attend_forward",
    )(lengths, raw, cosine, sine)


def attend_backward_kernel(
    length_ref, qkv_ref, dcontext_ref, lse_ref, cos_ref, sin_ref, dqkv_ref, inner_ref, dk_ref, dv_ref
):
    length = length_ref[pl.program_id(0)]
    scale = 1.0 / math.sqrt(HEAD_DIM)
    hd = HEAD_DIM
    dk_ref[...] = jnp.zeros_like(dk_ref)
    dv_ref[...] = jnp.zeros_like(dv_ref)

    def turn_back(grad, rows):
        back = grad * cos_ref[rows, :] - pltpu.roll(grad, hd // 2, 1) * sin_ref[rows, :]
        return back.astype(bf16)

    for at in range(0, SEQ_LEN, QBLOCK):
        seen = at + QBLOCK
        rows = qkv_ref[at:seen, :hd]
        keys = qkv_ref[:seen, hd : 2 * hd]
        drows = dcontext_ref[at:seen, :]
        scores = block_scores(rows, keys, at, length, scale)
        probs = jnp.exp(scores - lse_ref[at:seen, :1])
        dv_ref[:seen, :] += mm_tn(probs.astype(bf16), drows)
        dprobs = mm_nt(drows, qkv_ref[:seen, 2 * hd :])
        dscore = probs * (dprobs - jnp.sum(dprobs * probs, axis=-1, keepdims=True))
        draw = (dscore * scale).astype(bf16)
        dquery = mm(draw, keys)
        dk_ref[:seen, :] += mm_tn(draw, rows)
        dqkv_ref[at:seen, :hd] = turn_back(dquery, slice(at, seen))
        inner_ref[at:seen, :] = jnp.broadcast_to(
            jnp.sum(dquery * rows.astype(f32), axis=-1, keepdims=True), (QBLOCK, hd)
        )
    dkey, dvalue = dk_ref[...], dv_ref[...]
    dqkv_ref[:, hd : 2 * hd] = turn_back(dkey, slice(None))
    dqkv_ref[:, 2 * hd :] = dvalue.astype(bf16)
    inner_ref[...] += jnp.broadcast_to(
        jnp.sum(
            dkey * qkv_ref[:, hd : 2 * hd].astype(f32) + dvalue * qkv_ref[:, 2 * hd :].astype(f32),
            axis=-1,
            keepdims=True,
        ),
        inner_ref.shape,
    )


def attend_backward(qkv, dcontext, lse, lengths, cosine, sine):
    tokens, width = qkv.shape
    heads = width // (3 * HEAD_DIM)
    slots = tokens // SEQ_LEN
    wide = pl.BlockSpec((SEQ_LEN, 3 * HEAD_DIM), lambda s, h, _: (s, h))
    one = pl.BlockSpec((SEQ_LEN, HEAD_DIM), lambda s, h, _: (s, h))
    table = pl.BlockSpec((SEQ_LEN, HEAD_DIM), lambda s, h, _: (0, 0))
    pairs = slots * heads * SEQ_LEN * SEQ_LEN
    return pl.pallas_call(
        attend_backward_kernel,
        grid_spec=pltpu.PrefetchScalarGridSpec(
            num_scalar_prefetch=1,
            grid=(slots, heads),
            in_specs=[wide, one, one, table, table],
            out_specs=[wide, one],
            scratch_shapes=[pltpu.VMEM((SEQ_LEN, HEAD_DIM), f32)] * 2,
        ),
        out_shape=[
            jax.ShapeDtypeStruct((tokens, width), bf16),
            jax.ShapeDtypeStruct((tokens, heads * HEAD_DIM), f32),
        ],
        cost_estimate=pl.CostEstimate(
            flops=8 * HEAD_DIM * pairs, bytes_accessed=8 * tokens * width, transcendentals=pairs
        ),
        name="attend_backward",
    )(lengths, qkv, dcontext, lse, cosine, sine)


def gather_rows(part):
    n = lax.axis_size("row")
    if n > 4:
        return lax.all_gather(part, "row", axis=0, tiled=True)
    z = lax.axis_index("row")
    up, down = [part], [part]
    for step in range(1, n):
        up.append(lax.ppermute(up[-1], "row", [(a, a + 1) for a in range(step - 1, n - 1)]))
        down.append(lax.ppermute(down[-1], "row", [(a, a - 1) for a in range(1, n - step + 1)]))
    whole = jnp.zeros((n,) + part.shape, part.dtype)
    for back in range(n):
        piece = part if back == 0 else up[back] + down[n - back]
        whole = lax.dynamic_update_slice_in_dim(whole, piece[None], lax.rem(z + n - back, n), 0)
    return whole.reshape((n * part.shape[0],) + part.shape[1:])


def reduce_rows(grads):
    n = lax.axis_size("row")
    if n > 4:
        whole = jnp.concatenate([g.astype(bf16) for g in grads], axis=1)
        return lax.psum_scatter(whole, "row", scatter_dimension=0, tiled=True).astype(f32)
    z = lax.axis_index("row")
    size = grads[0].shape[0] // n

    def block(j):
        at = jnp.clip(j, 0, n - 1) * size
        return jnp.concatenate(
            [lax.dynamic_slice_in_dim(g, at, size, 0) for g in grads], axis=1
        ).astype(f32)

    up, down = block(n - 1 + z).astype(bf16), block(z - n + 1).astype(bf16)
    for step in range(1, n):
        up_in = lax.ppermute(up, "row", [(a, a + 1) for a in range(step)])
        down_in = lax.ppermute(down, "row", [(a, a - 1) for a in range(n - step, n)])
        if step < n - 1:
            up = (block(n - 1 - step + z) + up_in.astype(f32)).astype(bf16)
            down = (block(z - n + 1 + step) + down_in.astype(f32)).astype(bf16)
    return block(z) + up_in.astype(f32) + down_in.astype(f32)


def split_three(values):
    high = values.astype(bf16)
    rest = values - high.astype(f32)
    middle = rest.astype(bf16)
    return high, middle, (rest - middle.astype(f32)).astype(bf16)


def cuts_of(width):
    at, cuts = 0, []
    while at < width:
        cuts.append((at, min(at + CHUNK, width)))
        at += CHUNK
    return cuts


def per_device(
    block_input,
    seq_lengths,
    slot_order,
    routes,
    input_gain,
    query_weight,
    key_weight,
    value_weight,
    output_weight,
    mlp_gain,
    router_weight,
    score_shared,
    gate_shared,
    up_shared,
    down_shared,
    gate_expert,
    up_expert,
    down_expert,
    grad_output,
):
    tokens, share = block_input.shape
    cols = lax.axis_size("col")
    col_id = lax.axis_index("col")
    row_id = lax.axis_index("row")
    width = share * cols
    slots = tokens // SEQ_LEN
    local_experts = gate_expert.shape[0]
    experts = router_weight.shape[1]
    head_width = query_weight.shape[1]
    heads = head_width // HEAD_DIM
    rows_block = query_weight.shape[0]
    lengths = lax.dynamic_slice_in_dim(seq_lengths[slot_order], row_id * slots, slots, 0)
    cosine, sine = rope_tables()

    def by_head(weight):
        return weight.reshape(rows_block, heads, 1, HEAD_DIM)

    qkv_pack = jnp.concatenate(
        [by_head(query_weight), by_head(key_weight), by_head(value_weight)], axis=2
    ).reshape(rows_block, 3 * head_width)
    attn_weights = gather_rows(jnp.concatenate([qkv_pack, output_weight.T], axis=1))
    qkv_full = attn_weights[:, : 3 * head_width]
    out_full = attn_weights[:, 3 * head_width :]
    units = []
    chunks = [(None, 0, gate_shared.shape[1])]
    units.append(jnp.concatenate([gate_shared, up_shared, down_shared.T], axis=1))
    for local in range(local_experts):
        for a, b in cuts_of(gate_expert.shape[2]):
            chunks.append((local, a, b))
            units.append(
                jnp.concatenate(
                    [gate_expert[local, :, a:b], up_expert[local, :, a:b], down_expert[local, a:b].T],
                    axis=1,
                )
            )
    gathered = [gather_rows(unit) for unit in units]
    router_pack = jnp.concatenate([router_weight, score_shared[:, None]], axis=1)
    router_full = lax.all_gather(router_pack, "row", axis=0, tiled=True)

    rows_in = lax.all_gather(block_input, "col", axis=1, tiled=True)
    gain_a = lax.all_gather(input_gain, "col", axis=0, tiled=True).astype(f32)
    cot_rows = lax.all_gather(grad_output, "col", axis=1, tiled=True)
    rows_f = rows_in.astype(f32)
    scale_a = lax.rsqrt(jnp.mean(rows_f * rows_f, axis=-1, keepdims=True) + norm_eps)
    normed_a = (rows_f * scale_a * gain_a).astype(bf16)
    qkv, context, lse = attend_forward(mm(normed_a, qkv_full), lengths, cosine, sine)
    attn_part = mm_nt(context, out_full).astype(bf16)
    x_share = block_input.astype(f32)
    stream = x_share + lax.psum_scatter(
        attn_part, "col", scatter_dimension=1, tiled=True
    ).astype(f32)
    gain_b = mlp_gain.astype(f32)
    scaled = lax.all_gather((stream * gain_b).astype(bf16), "col", axis=1, tiled=True)
    squares = lax.psum(jnp.sum(stream * stream, axis=1), "col")
    scale_b = lax.rsqrt(squares / width + norm_eps)[:, None]

    both_logits = scale_b * mm(scaled, router_full)
    logits, slogit = both_logits[:, :experts], both_logits[:, experts]
    top = jnp.max(logits, axis=-1, keepdims=True)
    expo = jnp.exp(logits - top)
    router_probs = expo / jnp.sum(expo, axis=-1, keepdims=True)
    shared_gate = jax.nn.sigmoid(slogit)

    moe_part = None
    dscaled_part = None
    unit_grads = []
    inner = jnp.zeros((tokens,), f32)
    dots = {}
    members, shares = {None: None}, {None: shared_gate}
    for local in range(local_experts):
        expert = col_id * local_experts + local
        members[local] = jnp.any(routes == expert, axis=1)
        column = lax.dynamic_index_in_dim(router_probs, expert, 1, False)
        shares[local] = jnp.where(members[local], column, 0.0)
    for (kind, a, b), full in zip(chunks, gathered):
        size = b - a
        weight = shares[kind][:, None]
        pair = mm(scaled, full[:, : 2 * size])
        dhidden = mm(cot_rows, full[:, 2 * size :])
        gate, up = scale_b * pair[:, :size], scale_b * pair[:, size:]
        sigma = jax.nn.sigmoid(gate)
        silu = gate * sigma
        hidden = silu * up
        weighted = (weight * hidden).astype(bf16)
        dots[kind] = dots.get(kind, 0.0) + jnp.sum(hidden * dhidden, axis=1)
        dhidden = weight * dhidden
        dgate = dhidden * up * sigma * (1.0 + gate * (1.0 - sigma))
        dup = dhidden * silu
        inner = inner + jnp.sum(dgate * gate + dup * up, axis=1)
        dpair = jnp.concatenate([scale_b * dgate, scale_b * dup], axis=1).astype(bf16)
        moe_new = mm_nt(weighted, full[:, 2 * size :])
        dscaled_new = mm_nt(dpair, full[:, : 2 * size])
        moe_part = moe_new if moe_part is None else moe_part + moe_new
        dscaled_part = dscaled_new if dscaled_part is None else dscaled_part + dscaled_new
        unit_grads.append(
            reduce_rows([mm_tn(scaled, dpair).astype(bf16), mm_tn(cot_rows, weighted).astype(bf16)])
        )
    moe_share = lax.psum_scatter(
        moe_part.astype(bf16), "col", scatter_dimension=1, tiled=True
    ).astype(f32)
    block_output = (stream + moe_share).astype(bf16)

    table = jnp.zeros((experts, tokens), f32)
    for local in range(local_experts):
        row = jnp.where(members[local], dots[local], 0.0)[None]
        table = lax.dynamic_update_slice_in_dim(table, row, col_id * local_experts + local, 0)
    table = lax.psum(jnp.concatenate([table, dots[None][None], inner[None]], axis=0), "col")
    dprob, dshared_gate, inner = table[:experts].T, table[experts], table[experts + 1]
    dlogits = router_probs * (dprob - jnp.sum(dprob * router_probs, axis=1, keepdims=True))
    dslogit = dshared_gate * shared_gate * (1.0 - shared_gate)
    dboth = jnp.concatenate([dlogits, dslogit[:, None]], axis=1)
    inner = inner + jnp.sum(dboth * both_logits, axis=1)
    dboth = scale_b * dboth
    parts = split_three(dboth)
    stacked = mm_tn(jnp.concatenate(parts, axis=1), scaled)
    grad_router_part = stacked.reshape(3, experts + 1, width).sum(axis=0)
    grad_router_both = lax.psum_scatter(grad_router_part, "row", scatter_dimension=1, tiled=True)
    router_rows = lax.dynamic_slice_in_dim(router_full, col_id * share, share, 0)
    back = mm_nt(jnp.concatenate(parts, axis=1), jnp.concatenate([router_rows] * 3, axis=1))
    dscaled = back + lax.psum_scatter(
        dscaled_part.astype(bf16), "col", scatter_dimension=1, tiled=True
    ).astype(f32)
    cot_share = grad_output.astype(f32)
    dstream = cot_share + gain_b * dscaled - stream * (scale_b * scale_b * inner[:, None] / width)
    gain_b_grad = jnp.sum(dscaled * stream, axis=0)

    dattn = lax.all_gather(dstream.astype(bf16), "col", axis=1, tiled=True)
    out_grad = reduce_rows([mm_tn(dattn, context).astype(bf16)])
    dcontext = mm(dattn, out_full).astype(bf16)
    dqkv, inner_a = attend_backward(qkv, dcontext, lse, lengths, cosine, sine)
    inner_a = lax.psum(
        jnp.sum(inner_a.reshape(tokens, heads, HEAD_DIM)[:, :, 0], axis=1), "col"
    )[:, None]
    qkv_grad = reduce_rows([mm_tn(normed_a, dqkv).astype(bf16)])
    dnormed_a = lax.psum_scatter(
        mm_nt(dqkv, qkv_full).astype(bf16), "col", scatter_dimension=1, tiled=True
    ).astype(f32)
    gain_a_share = input_gain.astype(f32)
    dinput = dstream + scale_a * gain_a_share * dnormed_a
    dinput = dinput - x_share * (scale_a * scale_a * inner_a / width)
    gain_a_grad = jnp.sum(dnormed_a * x_share * scale_a, axis=0)
    grad_gain_a, grad_gain_b = lax.psum((gain_a_grad, gain_b_grad), "row")

    qkv_grad = qkv_grad.reshape(rows_block, heads, 3, HEAD_DIM)
    grad_query, grad_key, grad_value = (
        qkv_grad[:, :, part].reshape(rows_block, head_width) for part in range(3)
    )
    gates, ups, downs = [], [], []
    for (kind, a, b), grad in zip(chunks, unit_grads):
        size = b - a
        pieces = (grad[:, :size], grad[:, size : 2 * size], grad[:, 2 * size :].T)
        if kind is None:
            grad_gate_shared, grad_up_shared, grad_down_shared = pieces
        else:
            if a == 0:
                for into in (gates, ups, downs):
                    into.append([])
            for into, piece in zip((gates, ups, downs), pieces):
                into[-1].append(piece)
    grad_gate_expert = jnp.stack([jnp.concatenate(one, axis=1) for one in gates])
    grad_up_expert = jnp.stack([jnp.concatenate(one, axis=1) for one in ups])
    grad_down_expert = jnp.stack([jnp.concatenate(one, axis=0) for one in downs])
    return (
        block_output,
        dinput.astype(bf16),
        grad_gain_a,
        grad_query,
        grad_key,
        grad_value,
        out_grad.T,
        grad_gain_b,
        grad_router_both[:experts].T,
        grad_router_both[experts],
        grad_gate_shared,
        grad_up_shared,
        grad_down_shared,
        grad_gate_expert,
        grad_up_expert,
        grad_down_expert,
    )


def solution(mesh):
    return jax.shard_map(
        per_device,
        mesh=mesh,
        in_specs=(
            P("row", "col"),
            P(),
            P(),
            P("row", None),
            P("col"),
            P("row", "col"),
            P("row", "col"),
            P("row", "col"),
            P("col", "row"),
            P("col"),
            P("row", None),
            P("row"),
            P("row", "col"),
            P("row", "col"),
            P("col", "row"),
            P("col", "row", None),
            P("col", "row", None),
            P("col", None, "row"),
            P("row", "col"),
        ),
        out_specs=(
            P("row", "col"),
            P("row", "col"),
            P("col"),
            P("row", "col"),
            P("row", "col"),
            P("row", "col"),
            P("col", "row"),
            P("col"),
            P("row", None),
            P("row"),
            P("row", "col"),
            P("row", "col"),
            P("col", "row"),
            P("col", "row", None),
            P("col", "row", None),
            P("col", None, "row"),
        ),
        check_vma=False,
    )
```

```python
import functools
import math

import jax
import jax.numpy as jnp
from jax import lax
from jax.experimental import pallas as pl
from jax.experimental.pallas import tpu as pltpu
from jax.sharding import PartitionSpec as P

HEAD_DIM = 128
SEQ_LEN = 1024
QBLOCK = 256
TILE = 256
CHUNK = 512
norm_eps = 1e-06
rope_base = 1000000.0
bf16 = jnp.bfloat16
f32 = jnp.float32


def mm(left, right):
    return jnp.dot(left, right, preferred_element_type=f32)


def mm_nt(left, right):
    return lax.dot_general(left, right, (((1,), (1,)), ((), ())), preferred_element_type=f32)


def mm_tn(left, right):
    return lax.dot_general(left, right, (((0,), (0,)), ((), ())), preferred_element_type=f32)


def rope_tables():
    positions = jnp.arange(SEQ_LEN).astype(f32)
    freqs = jnp.power(f32(rope_base), -jnp.arange(0, HEAD_DIM, 2).astype(f32) / HEAD_DIM)
    angles = positions[:, None] * freqs[None, :]
    cosine, sine = jnp.cos(angles), jnp.sin(angles)
    return (
        jnp.concatenate([cosine, cosine], axis=-1),
        jnp.concatenate([-sine, sine], axis=-1),
    )


def block_scores(rows, keys, start, length, scale):
    raw = mm_nt(rows, keys) * scale
    query_pos = start + lax.broadcasted_iota(jnp.int32, raw.shape, 0)
    key_pos = lax.broadcasted_iota(jnp.int32, raw.shape, 1)
    return jnp.where((key_pos <= query_pos) & (key_pos < length), raw, -1e30)


def attend_forward_kernel(length_ref, raw_ref, cos_ref, sin_ref, qkv_ref, context_ref, lse_ref):
    length = length_ref[pl.program_id(0)]
    scale = 1.0 / math.sqrt(HEAD_DIM)
    hd = HEAD_DIM
    for part in range(2):
        raw = raw_ref[:, part * hd : (part + 1) * hd]
        turned = raw * cos_ref[...] + pltpu.roll(raw, hd // 2, 1) * sin_ref[...]
        qkv_ref[:, part * hd : (part + 1) * hd] = turned.astype(bf16)
    qkv_ref[:, 2 * hd :] = raw_ref[:, 2 * hd :].astype(bf16)
    for at in range(0, SEQ_LEN, QBLOCK):
        seen = at + QBLOCK
        scores = block_scores(
            qkv_ref[at:seen, :hd], qkv_ref[:seen, hd : 2 * hd], at, length, scale
        )
        top = jnp.max(scores, axis=-1, keepdims=True)
        expo = jnp.exp(scores - top)
        total = jnp.sum(expo, axis=-1, keepdims=True)
        probs = (expo / total).astype(bf16)
        context_ref[at:seen, :] = mm(probs, qkv_ref[:seen, 2 * hd :]).astype(bf16)
        lse_ref[at:seen, :] = jnp.broadcast_to(top + jnp.log(total), (QBLOCK, hd))


def attend_forward(raw, lengths, cosine, sine):
    tokens, width = raw.shape
    heads = width // (3 * HEAD_DIM)
    slots = tokens // SEQ_LEN
    wide = pl.BlockSpec((SEQ_LEN, 3 * HEAD_DIM), lambda s, h, _: (s, h))
    one = pl.BlockSpec((SEQ_LEN, HEAD_DIM), lambda s, h, _: (s, h))
    table = pl.BlockSpec((SEQ_LEN, HEAD_DIM), lambda s, h, _: (0, 0))
    pairs = slots * heads * SEQ_LEN * SEQ_LEN
    return pl.pallas_call(
        attend_forward_kernel,
        grid_spec=pltpu.PrefetchScalarGridSpec(
            num_scalar_prefetch=1,
            grid=(slots, heads),
            in_specs=[wide, table, table],
            out_specs=[wide, one, one],
        ),
        out_shape=[
            jax.ShapeDtypeStruct((tokens, width), bf16),
            jax.ShapeDtypeStruct((tokens, heads * HEAD_DIM), bf16),
            jax.ShapeDtypeStruct((tokens, heads * HEAD_DIM), f32),
        ],
        cost_estimate=pl.CostEstimate(
            flops=3 * HEAD_DIM * pairs, bytes_accessed=8 * tokens * width, transcendentals=pairs
        ),
        name="attend_forward",
    )(lengths, raw, cosine, sine)


def attend_backward_kernel(
    length_ref, qkv_ref, dcontext_ref, lse_ref, cos_ref, sin_ref, dqkv_ref, inner_ref, dk_ref, dv_ref
):
    length = length_ref[pl.program_id(0)]
    scale = 1.0 / math.sqrt(HEAD_DIM)
    hd = HEAD_DIM
    dk_ref[...] = jnp.zeros_like(dk_ref)
    dv_ref[...] = jnp.zeros_like(dv_ref)

    def turn_back(grad, rows):
        back = grad * cos_ref[rows, :] - pltpu.roll(grad, hd // 2, 1) * sin_ref[rows, :]
        return back.astype(bf16)

    for at in range(0, SEQ_LEN, QBLOCK):
        seen = at + QBLOCK
        rows = qkv_ref[at:seen, :hd]
        keys = qkv_ref[:seen, hd : 2 * hd]
        drows = dcontext_ref[at:seen, :]
        scores = block_scores(rows, keys, at, length, scale)
        probs = jnp.exp(scores - lse_ref[at:seen, :1])
        dv_ref[:seen, :] += mm_tn(probs.astype(bf16), drows)
        dprobs = mm_nt(drows, qkv_ref[:seen, 2 * hd :])
        dscore = probs * (dprobs - jnp.sum(dprobs * probs, axis=-1, keepdims=True))
        draw = (dscore * scale).astype(bf16)
        dquery = mm(draw, keys)
        dk_ref[:seen, :] += mm_tn(draw, rows)
        dqkv_ref[at:seen, :hd] = turn_back(dquery, slice(at, seen))
        inner_ref[at:seen, :] = jnp.broadcast_to(
            jnp.sum(dquery * rows.astype(f32), axis=-1, keepdims=True), (QBLOCK, hd)
        )
    dkey, dvalue = dk_ref[...], dv_ref[...]
    dqkv_ref[:, hd : 2 * hd] = turn_back(dkey, slice(None))
    dqkv_ref[:, 2 * hd :] = dvalue.astype(bf16)
    inner_ref[...] += jnp.broadcast_to(
        jnp.sum(
            dkey * qkv_ref[:, hd : 2 * hd].astype(f32) + dvalue * qkv_ref[:, 2 * hd :].astype(f32),
            axis=-1,
            keepdims=True,
        ),
        inner_ref.shape,
    )


def attend_backward(qkv, dcontext, lse, lengths, cosine, sine):
    tokens, width = qkv.shape
    heads = width // (3 * HEAD_DIM)
    slots = tokens // SEQ_LEN
    wide = pl.BlockSpec((SEQ_LEN, 3 * HEAD_DIM), lambda s, h, _: (s, h))
    one = pl.BlockSpec((SEQ_LEN, HEAD_DIM), lambda s, h, _: (s, h))
    table = pl.BlockSpec((SEQ_LEN, HEAD_DIM), lambda s, h, _: (0, 0))
    pairs = slots * heads * SEQ_LEN * SEQ_LEN
    return pl.pallas_call(
        attend_backward_kernel,
        grid_spec=pltpu.PrefetchScalarGridSpec(
            num_scalar_prefetch=1,
            grid=(slots, heads),
            in_specs=[wide, one, one, table, table],
            out_specs=[wide, one],
            scratch_shapes=[pltpu.VMEM((SEQ_LEN, HEAD_DIM), f32)] * 2,
        ),
        out_shape=[
            jax.ShapeDtypeStruct((tokens, width), bf16),
            jax.ShapeDtypeStruct((tokens, heads * HEAD_DIM), f32),
        ],
        cost_estimate=pl.CostEstimate(
            flops=8 * HEAD_DIM * pairs, bytes_accessed=8 * tokens * width, transcendentals=pairs
        ),
        name="attend_backward",
    )(lengths, qkv, dcontext, lse, cosine, sine)


def gather_rows(part):
    n = lax.axis_size("row")
    if n != 4:
        return (lax.all_gather(part, "row", axis=0, tiled=True),)
    partner = lax.ppermute(part, "row", [(0, 1), (1, 0), (2, 3), (3, 2)])
    middle, outward = [(1, 2), (2, 1)], [(1, 0), (2, 3)]
    near_mid = lax.ppermute(part, "row", middle)
    far_mid = lax.ppermute(partner, "row", middle)
    near_out = lax.ppermute(near_mid, "row", outward)
    far_out = lax.ppermute(far_mid, "row", outward)
    return part, partner, near_mid, far_mid, near_out, far_out


def places(z):
    pair = z // 2
    return z, z + 1 - 2 * lax.rem(z, 2), 2 - pair, 3 - 3 * pair


def join_rows(pieces):
    if len(pieces) == 1:
        return pieces[0]
    part = pieces[0]
    z = lax.axis_index("row")
    whole = jnp.zeros((4,) + part.shape, part.dtype)
    blocks = (part, pieces[1], pieces[2] + pieces[4], pieces[3] + pieces[5])
    for at, piece in zip(places(z), blocks):
        whole = lax.dynamic_update_slice_in_dim(whole, piece[None], at, 0)
    return whole.reshape((4 * part.shape[0],) + part.shape[1:])


def reduce_rows(grads):
    n = lax.axis_size("row")
    if n != 4:
        total = lax.psum_scatter(grads, "row", scatter_dimension=0, tiled=True)
        return total.astype(f32), total
    own, partner, near, far = places(lax.axis_index("row"))
    size = grads.shape[0] // n
    inward, middle = [(0, 1), (3, 2)], [(1, 2), (2, 1)]

    def block(at, *others):
        piece = lax.dynamic_slice_in_dim(grads, at * size, size, 0)
        if others:
            piece = piece.astype(f32)
            for other in others:
                piece = piece + other.astype(f32)
        return piece

    far_in = lax.ppermute(block(far), "row", inward)
    near_in = lax.ppermute(block(near), "row", inward)
    far_sum = lax.ppermute(block(far, far_in).astype(bf16), "row", middle)
    near_sum = lax.ppermute(block(near, near_in).astype(bf16), "row", middle)
    exchanged = lax.ppermute(
        block(partner, far_sum).astype(bf16), "row", [(0, 1), (1, 0), (2, 3), (3, 2)]
    )
    return block(own, near_sum, exchanged), near_in


def after(value, *others):
    return lax.optimization_barrier((value,) + others)[0]


def expert_kernel(size, steps, count, z_ref, *refs):
    pieces = refs[:count]
    (x_ref, cot_ref, x_cols, cot_cols, coef_ref) = refs[count : count + 5]
    (dpair_ref, hidden_ref, sums_ref, grads_ref, whole_ref) = refs[count + 5 : count + 10]
    weights, dpair, hidden, sems, out_sem = refs[count + 10 :]
    step = pl.program_id(0)
    write = pltpu.make_async_copy(weights, whole_ref, out_sem)

    @pl.when(step == 0)
    def _():
        if count == 1:
            copy = pltpu.make_async_copy(pieces[0], weights, sems.at[0])
            copy.start()
            copy.wait()
        else:
            z = z_ref[0]
            block = pieces[0].shape[0]

            def copy_of(piece, which):
                at = pl.multiple_of(places(z)[which] * block, block)
                return pltpu.make_async_copy(
                    piece, weights.at[pl.ds(at, block)], sems.at[which]
                )

            copy_of(pieces[0], 0).start()
            copy_of(pieces[1], 1).start()
            in_middle = (z == 1) | (z == 2)

            @pl.when(in_middle)
            def _():
                copy_of(pieces[2], 2).start()
                copy_of(pieces[3], 3).start()

            @pl.when(jnp.logical_not(in_middle))
            def _():
                copy_of(pieces[4], 2).start()
                copy_of(pieces[5], 3).start()

            for which in range(4):
                copy_of(pieces[which], which).wait()
        write.start()

    @pl.when(step < steps)
    def _():
        at = pl.multiple_of(step * TILE, TILE)
        rows, cots = x_ref[...], cot_ref[...]
        scale, weight = coef_ref[:, 0:1], coef_ref[:, 1:2]
        dots = jnp.zeros((TILE, 1), f32)
        inner = jnp.zeros((TILE, 1), f32)
        for a in range(0, size, TILE):
            b = min(a + TILE, size)
            gate = scale * mm(rows, weights[:, a:b])
            up = scale * mm(rows, weights[:, size + a : size + b])
            dhid = mm(cots, weights[:, 2 * size + a : 2 * size + b])
            sigma = jax.nn.sigmoid(gate)
            silu = gate * sigma
            hid = silu * up
            dots += jnp.sum(hid * dhid, axis=1, keepdims=True)
            dhid = weight * dhid
            dgate = dhid * up * sigma * (1.0 + gate * (1.0 - sigma))
            dup = dhid * silu
            inner += jnp.sum(dgate * gate + dup * up, axis=1, keepdims=True)
            for into, at_col, value in (
                ((hidden_ref, hidden), a, weight * hid),
                ((dpair_ref, dpair), a, scale * dgate),
                ((dpair_ref, dpair), size + a, scale * dup),
            ):
                value = value.astype(bf16)
                into[0][:, at_col : at_col + b - a] = value
                into[1][pl.ds(at, TILE), at_col : at_col + b - a] = value
        sums_ref[:, 0:1] = dots
        sums_ref[:, 1:2] = inner

    @pl.when(step >= steps)
    def _():
        for a in range(0, 2 * size, TILE):
            b = min(a + TILE, 2 * size)
            grads_ref[:, a:b] = mm_tn(x_cols[...], dpair[:, a:b]).astype(bf16)
        for a in range(0, size, TILE):
            b = min(a + TILE, size)
            grads_ref[:, 2 * size + a : 2 * size + b] = mm_tn(
                cot_cols[...], hidden[:, a:b]
            ).astype(bf16)

    @pl.when(step == pl.num_programs(0) - 1)
    def _():
        write.wait()


def expert_chunk(pieces, scaled, cots, coef):
    tokens, width = scaled.shape
    size = pieces[0].shape[1] // 3
    steps, more = tokens // TILE, width // TILE
    count = len(pieces)
    rows = lambda i, _: (jnp.minimum(i, steps - 1), 0)
    cols = lambda i, _: (0, jnp.maximum(i - steps, 0))
    down = lambda i, _: (jnp.maximum(i - steps, 0), 0)
    z = jnp.reshape(lax.axis_index("row"), (1,)).astype(jnp.int32)
    return pl.pallas_call(
        functools.partial(expert_kernel, size, steps, count),
        grid_spec=pltpu.PrefetchScalarGridSpec(
            num_scalar_prefetch=1,
            grid=(steps + more,),
            in_specs=[pl.BlockSpec(memory_space=pl.ANY)] * count
            + [
                pl.BlockSpec((TILE, width), rows),
                pl.BlockSpec((TILE, width), rows),
                pl.BlockSpec((tokens, TILE), cols),
                pl.BlockSpec((tokens, TILE), cols),
                pl.BlockSpec((TILE, 2), rows),
            ],
            out_specs=[
                pl.BlockSpec((TILE, 2 * size), rows),
                pl.BlockSpec((TILE, size), rows),
                pl.BlockSpec((TILE, 2), rows),
                pl.BlockSpec((TILE, 3 * size), down),
                pl.BlockSpec(memory_space=pl.ANY),
            ],
            scratch_shapes=[
                pltpu.VMEM((width, 3 * size), bf16),
                pltpu.VMEM((tokens, 2 * size), bf16),
                pltpu.VMEM((tokens, size), bf16),
                pltpu.SemaphoreType.DMA((4,)),
                pltpu.SemaphoreType.DMA,
            ],
        ),
        out_shape=[
            jax.ShapeDtypeStruct((tokens, 2 * size), bf16),
            jax.ShapeDtypeStruct((tokens, size), bf16),
            jax.ShapeDtypeStruct((tokens, 2), f32),
            jax.ShapeDtypeStruct((width, 3 * size), bf16),
            jax.ShapeDtypeStruct((width, 3 * size), bf16),
        ],
        cost_estimate=pl.CostEstimate(
            flops=12 * tokens * width * size,
            bytes_accessed=8 * tokens * width + 24 * width * size,
            transcendentals=tokens * size,
        ),
        name="expert_chunk",
    )(z, *pieces, scaled, cots, scaled, cots, coef)


def joint_kernel(count, *refs):
    out_ref = refs[-1]
    for a in range(0, out_ref.shape[1], TILE):
        total = None
        for left, weights in zip(refs[:count], refs[count:-1]):
            part = mm_nt(left[...], weights[a : a + TILE, :])
            total = part if total is None else total + part
        out_ref[:, a : a + TILE] = total.astype(bf16)


def joint_back(lefts, weights, column):
    tokens, width = lefts[0].shape[0], weights[0].shape[0]
    row = lambda i: (i, 0)
    fixed = lambda i: (0, column)
    depth = sum(left.shape[1] for left in lefts)
    return pl.pallas_call(
        functools.partial(joint_kernel, len(lefts)),
        grid=(tokens // TILE,),
        in_specs=[pl.BlockSpec((TILE, left.shape[1]), row) for left in lefts]
        + [
            pl.BlockSpec((width, left.shape[1]), fixed, pipeline_mode=pl.Buffered(1))
            for left in lefts
        ],
        out_specs=pl.BlockSpec((TILE, width), row),
        out_shape=jax.ShapeDtypeStruct((tokens, width), bf16),
        cost_estimate=pl.CostEstimate(
            flops=2 * tokens * width * depth,
            bytes_accessed=2 * (tokens + width) * depth + 2 * tokens * width,
            transcendentals=0,
        ),
        name="joint_back",
    )(*lefts, *weights)


def split_three(values):
    high = values.astype(bf16)
    rest = values - high.astype(f32)
    middle = rest.astype(bf16)
    return high, middle, (rest - middle.astype(f32)).astype(bf16)


def cuts_of(width):
    at, cuts = 0, []
    while at < width:
        cuts.append((at, min(at + CHUNK, width)))
        at += CHUNK
    return cuts


def per_device(
    block_input,
    seq_lengths,
    slot_order,
    routes,
    input_gain,
    query_weight,
    key_weight,
    value_weight,
    output_weight,
    mlp_gain,
    router_weight,
    score_shared,
    gate_shared,
    up_shared,
    down_shared,
    gate_expert,
    up_expert,
    down_expert,
    grad_output,
):
    tokens, share = block_input.shape
    cols = lax.axis_size("col")
    col_id = lax.axis_index("col")
    row_id = lax.axis_index("row")
    width = share * cols
    slots = tokens // SEQ_LEN
    local_experts = gate_expert.shape[0]
    experts = router_weight.shape[1]
    head_width = query_weight.shape[1]
    heads = head_width // HEAD_DIM
    rows_block = query_weight.shape[0]
    lengths = lax.dynamic_slice_in_dim(seq_lengths[slot_order], row_id * slots, slots, 0)
    cosine, sine = rope_tables()

    def by_head(weight):
        return weight.reshape(rows_block, heads, 1, HEAD_DIM)

    qkv_pack = jnp.concatenate(
        [by_head(query_weight), by_head(key_weight), by_head(value_weight)], axis=2
    ).reshape(rows_block, 3 * head_width)
    router_pack = jnp.concatenate([router_weight, score_shared[:, None]], axis=1)
    router_pack = jnp.pad(router_pack, ((0, 0), (0, -router_pack.shape[1] % 128)))
    attn_weights = join_rows(
        gather_rows(jnp.concatenate([qkv_pack, output_weight.T, router_pack], axis=1))
    )
    qkv_full = attn_weights[:, : 3 * head_width]
    out_full = attn_weights[:, 3 * head_width : 4 * head_width]
    router_full = attn_weights[:, 4 * head_width : 4 * head_width + experts + 1]
    shared_cuts = [(None, a, b) for a, b in cuts_of(gate_shared.shape[1])]
    expert_cuts = [
        (local, a, b) for local in range(local_experts) for a, b in cuts_of(gate_expert.shape[2])
    ]
    chunks = shared_cuts[-1:] + expert_cuts[:-1] + shared_cuts[:-1] + expert_cuts[-1:]

    def pack(kind, a, b):
        if kind is None:
            parts = [gate_shared[:, a:b], up_shared[:, a:b], down_shared[a:b].T]
        else:
            parts = [gate_expert[kind, :, a:b], up_expert[kind, :, a:b], down_expert[kind, a:b].T]
        fill = -(b - a) % 128
        return jnp.concatenate([jnp.pad(part, ((0, 0), (0, fill))) for part in parts], axis=1)

    gathered = [gather_rows(pack(*chunk)) for chunk in chunks]

    rows_in = lax.all_gather(block_input, "col", axis=1, tiled=True)
    gains = lax.all_gather(jnp.stack([input_gain, mlp_gain]), "col", axis=1, tiled=True).astype(f32)
    cot_rows = lax.all_gather(grad_output, "col", axis=1, tiled=True)
    rows_f = rows_in.astype(f32)
    scale_a = lax.rsqrt(jnp.mean(rows_f * rows_f, axis=-1, keepdims=True) + norm_eps)
    normed_a = (rows_f * scale_a * gains[0]).astype(bf16)
    qkv, context, lse = attend_forward(mm(normed_a, qkv_full), lengths, cosine, sine)
    attn_part = mm_nt(context, out_full).astype(bf16)
    x_share = block_input.astype(f32)
    stream = x_share + lax.psum_scatter(
        attn_part, "col", scatter_dimension=1, tiled=True
    ).astype(f32)
    gain_b = mlp_gain.astype(f32)
    scaled = lax.all_gather((stream * gain_b).astype(bf16), "col", axis=1, tiled=True)
    stream_f = scaled.astype(f32) / gains[1]
    scale_b = lax.rsqrt(jnp.mean(stream_f * stream_f, axis=1, keepdims=True) + norm_eps)

    both_logits = scale_b * mm(scaled, router_full)
    logits, slogit = both_logits[:, :experts], both_logits[:, experts]
    top = jnp.max(logits, axis=-1, keepdims=True)
    expo = jnp.exp(logits - top)
    router_probs = expo / jnp.sum(expo, axis=-1, keepdims=True)
    shared_gate = jax.nn.sigmoid(slogit)

    inner = jnp.zeros((tokens,), f32)
    dots = {}
    members, shares = {None: None}, {None: shared_gate}
    for local in range(local_experts):
        expert = col_id * local_experts + local
        members[local] = jnp.any(routes == expert, axis=1)
        column = lax.dynamic_index_in_dim(router_probs, expert, 1, False)
        shares[local] = jnp.where(members[local], column, 0.0)
    dpairs, hiddens, wholes, unit_grads, arrived = [], [], [], [], []
    for at, ((kind, a, b), pieces) in enumerate(zip(chunks, gathered)):
        coef = jnp.concatenate([scale_b, shares[kind][:, None]], axis=1)
        if at >= 2:
            coef = after(coef, arrived[at - 2])
        dpair, hidden, sums, grads, whole = expert_chunk(pieces, scaled, cot_rows, coef)
        dots[kind] = dots.get(kind, 0.0) + sums[:, 0]
        inner = inner + sums[:, 1]
        dpairs.append(dpair)
        hiddens.append(hidden)
        wholes.append(whole)
        reduced, first = reduce_rows(grads)
        unit_grads.append(reduced)
        arrived.append(first)
    dscaled_part = joint_back(dpairs, wholes, 0)
    moe_share = lax.psum_scatter(
        joint_back(hiddens, wholes, 2), "col", scatter_dimension=1, tiled=True
    ).astype(f32)
    block_output = (stream + moe_share).astype(bf16)

    table = jnp.zeros((experts, tokens), f32)
    for local in range(local_experts):
        row = jnp.where(members[local], dots[local], 0.0)[None]
        table = lax.dynamic_update_slice_in_dim(table, row, col_id * local_experts + local, 0)
    table = lax.psum(jnp.concatenate([table, dots[None][None], inner[None]], axis=0), "col")
    dprob, dshared_gate, inner = table[:experts].T, table[experts], table[experts + 1]
    dlogits = router_probs * (dprob - jnp.sum(dprob * router_probs, axis=1, keepdims=True))
    dslogit = dshared_gate * shared_gate * (1.0 - shared_gate)
    dboth = jnp.concatenate([dlogits, dslogit[:, None]], axis=1)
    inner = inner + jnp.sum(dboth * both_logits, axis=1)
    dboth = scale_b * dboth
    parts = split_three(dboth)
    stacked = mm_tn(jnp.concatenate(parts, axis=1), scaled)
    grad_router_part = stacked.reshape(3, experts + 1, width).sum(axis=0)
    grad_router_both = lax.psum_scatter(grad_router_part, "row", scatter_dimension=1, tiled=True)
    router_rows = lax.dynamic_slice_in_dim(router_full, col_id * share, share, 0)
    back = mm_nt(jnp.concatenate(parts, axis=1), jnp.concatenate([router_rows] * 3, axis=1))
    dscaled = back + lax.psum_scatter(
        dscaled_part, "col", scatter_dimension=1, tiled=True
    ).astype(f32)
    cot_share = grad_output.astype(f32)
    dstream = cot_share + gain_b * dscaled - stream * (scale_b * scale_b * inner[:, None] / width)
    gain_b_grad = jnp.sum(dscaled * stream, axis=0)

    dattn = lax.all_gather(dstream.astype(bf16), "col", axis=1, tiled=True)
    out_grad, _ = reduce_rows(mm_tn(dattn, context).astype(bf16))
    dcontext = mm(dattn, out_full).astype(bf16)
    dqkv, inner_a = attend_backward(qkv, dcontext, lse, lengths, cosine, sine)
    inner_a = lax.psum(
        jnp.sum(inner_a.reshape(tokens, heads, HEAD_DIM)[:, :, 0], axis=1), "col"
    )[:, None]
    qkv_grad, _ = reduce_rows(mm_tn(normed_a, dqkv).astype(bf16))
    dnormed_a = lax.psum_scatter(
        mm_nt(dqkv, qkv_full).astype(bf16), "col", scatter_dimension=1, tiled=True
    ).astype(f32)
    gain_a_share = input_gain.astype(f32)
    dinput = dstream + scale_a * gain_a_share * dnormed_a
    dinput = dinput - x_share * (scale_a * scale_a * inner_a / width)
    gain_a_grad = jnp.sum(dnormed_a * x_share * scale_a, axis=0)
    grad_gain_a, grad_gain_b = lax.psum((gain_a_grad, gain_b_grad), "row")

    qkv_grad = qkv_grad.reshape(rows_block, heads, 3, HEAD_DIM)
    grad_query, grad_key, grad_value = (
        qkv_grad[:, :, part].reshape(rows_block, head_width) for part in range(3)
    )
    def unpack(kind, which):
        found = []
        for (of, a, b), grad in zip(chunks, unit_grads):
            if of == kind:
                size = grad.shape[1] // 3
                part = grad[:, which * size : which * size + b - a]
                found.append((a, part.T if which == 2 else part))
        found = [part for _, part in sorted(found, key=lambda item: item[0])]
        return jnp.concatenate(found, axis=0 if which == 2 else 1)

    locals_ = range(local_experts)
    return (
        block_output,
        dinput.astype(bf16),
        grad_gain_a,
        grad_query,
        grad_key,
        grad_value,
        out_grad.T,
        grad_gain_b,
        grad_router_both[:experts].T,
        grad_router_both[experts],
        unpack(None, 0),
        unpack(None, 1),
        unpack(None, 2),
        jnp.stack([unpack(local, 0) for local in locals_]),
        jnp.stack([unpack(local, 1) for local in locals_]),
        jnp.stack([unpack(local, 2) for local in locals_]),
    )


def solution(mesh):
    return jax.shard_map(
        per_device,
        mesh=mesh,
        in_specs=(
            P("row", "col"),
            P(),
            P(),
            P("row", None),
            P("col"),
            P("row", "col"),
            P("row", "col"),
            P("row", "col"),
            P("col", "row"),
            P("col"),
            P("row", None),
            P("row"),
            P("row", "col"),
            P("row", "col"),
            P("col", "row"),
            P("col", "row", None),
            P("col", "row", None),
            P("col", None, "row"),
            P("row", "col"),
        ),
        out_specs=(
            P("row", "col"),
            P("row", "col"),
            P("col"),
            P("row", "col"),
            P("row", "col"),
            P("row", "col"),
            P("col", "row"),
            P("col"),
            P("row", None),
            P("row"),
            P("row", "col"),
            P("row", "col"),
            P("col", "row"),
            P("col", "row", None),
            P("col", "row", None),
            P("col", None, "row"),
        ),
        check_vma=False,
    )
```

```python
import functools
import math

import jax
import jax.numpy as jnp
from jax import lax
from jax.experimental import pallas as pl
from jax.experimental.pallas import tpu as pltpu
from jax.sharding import PartitionSpec as P

HEAD_DIM = 128
SEQ_LEN = 1024
QBLOCK = 256
TILE = 256
CHUNK = 512
norm_eps = 1e-06
rope_base = 1000000.0
bf16 = jnp.bfloat16
f32 = jnp.float32


def mm(left, right):
    return jnp.dot(left, right, preferred_element_type=f32)


def mm_nt(left, right):
    return lax.dot_general(left, right, (((1,), (1,)), ((), ())), preferred_element_type=f32)


def mm_tn(left, right):
    return lax.dot_general(left, right, (((0,), (0,)), ((), ())), preferred_element_type=f32)


def rope_tables():
    positions = jnp.arange(SEQ_LEN).astype(f32)
    freqs = jnp.power(f32(rope_base), -jnp.arange(0, HEAD_DIM, 2).astype(f32) / HEAD_DIM)
    angles = positions[:, None] * freqs[None, :]
    cosine, sine = jnp.cos(angles), jnp.sin(angles)
    return (
        jnp.concatenate([cosine, cosine], axis=-1),
        jnp.concatenate([-sine, sine], axis=-1),
    )


def block_scores(rows, keys, start, length, scale):
    raw = mm_nt(rows, keys) * scale
    query_pos = start + lax.broadcasted_iota(jnp.int32, raw.shape, 0)
    key_pos = lax.broadcasted_iota(jnp.int32, raw.shape, 1)
    return jnp.where((key_pos <= query_pos) & (key_pos < length), raw, -1e30)


def attend_forward_kernel(length_ref, raw_ref, cos_ref, sin_ref, qkv_ref, context_ref, lse_ref):
    length = length_ref[pl.program_id(0)]
    scale = 1.0 / math.sqrt(HEAD_DIM)
    hd = HEAD_DIM
    for part in range(2):
        raw = raw_ref[:, part * hd : (part + 1) * hd]
        turned = raw * cos_ref[...] + pltpu.roll(raw, hd // 2, 1) * sin_ref[...]
        qkv_ref[:, part * hd : (part + 1) * hd] = turned.astype(bf16)
    qkv_ref[:, 2 * hd :] = raw_ref[:, 2 * hd :].astype(bf16)
    for at in range(0, SEQ_LEN, QBLOCK):
        seen = at + QBLOCK
        scores = block_scores(
            qkv_ref[at:seen, :hd], qkv_ref[:seen, hd : 2 * hd], at, length, scale
        )
        top = jnp.max(scores, axis=-1, keepdims=True)
        expo = jnp.exp(scores - top)
        total = jnp.sum(expo, axis=-1, keepdims=True)
        probs = (expo / total).astype(bf16)
        context_ref[at:seen, :] = mm(probs, qkv_ref[:seen, 2 * hd :]).astype(bf16)
        lse_ref[at:seen, :] = jnp.broadcast_to(top + jnp.log(total), (QBLOCK, hd))


def attend_forward(raw, lengths, cosine, sine):
    tokens, width = raw.shape
    heads = width // (3 * HEAD_DIM)
    slots = tokens // SEQ_LEN
    wide = pl.BlockSpec((SEQ_LEN, 3 * HEAD_DIM), lambda s, h, _: (s, h))
    one = pl.BlockSpec((SEQ_LEN, HEAD_DIM), lambda s, h, _: (s, h))
    table = pl.BlockSpec((SEQ_LEN, HEAD_DIM), lambda s, h, _: (0, 0))
    pairs = slots * heads * SEQ_LEN * SEQ_LEN
    return pl.pallas_call(
        attend_forward_kernel,
        grid_spec=pltpu.PrefetchScalarGridSpec(
            num_scalar_prefetch=1,
            grid=(slots, heads),
            in_specs=[wide, table, table],
            out_specs=[wide, one, one],
        ),
        out_shape=[
            jax.ShapeDtypeStruct((tokens, width), bf16),
            jax.ShapeDtypeStruct((tokens, heads * HEAD_DIM), bf16),
            jax.ShapeDtypeStruct((tokens, heads * HEAD_DIM), f32),
        ],
        cost_estimate=pl.CostEstimate(
            flops=3 * HEAD_DIM * pairs, bytes_accessed=8 * tokens * width, transcendentals=pairs
        ),
        name="attend_forward",
    )(lengths, raw, cosine, sine)


def attend_backward_kernel(
    length_ref, qkv_ref, dcontext_ref, lse_ref, cos_ref, sin_ref, dqkv_ref, inner_ref, dk_ref, dv_ref
):
    length = length_ref[pl.program_id(0)]
    scale = 1.0 / math.sqrt(HEAD_DIM)
    hd = HEAD_DIM
    @pl.when(pl.program_id(1) == 0)
    def _():
        inner_ref[...] = jnp.zeros_like(inner_ref)

    dk_ref[...] = jnp.zeros_like(dk_ref)
    dv_ref[...] = jnp.zeros_like(dv_ref)

    def turn_back(grad, rows):
        back = grad * cos_ref[rows, :] - pltpu.roll(grad, hd // 2, 1) * sin_ref[rows, :]
        return back.astype(bf16)

    for at in range(0, SEQ_LEN, QBLOCK):
        seen = at + QBLOCK
        rows = qkv_ref[at:seen, :hd]
        keys = qkv_ref[:seen, hd : 2 * hd]
        drows = dcontext_ref[at:seen, :]
        scores = block_scores(rows, keys, at, length, scale)
        probs = jnp.exp(scores - lse_ref[at:seen, :1])
        dv_ref[:seen, :] += mm_tn(probs.astype(bf16), drows)
        dprobs = mm_nt(drows, qkv_ref[:seen, 2 * hd :])
        dscore = probs * (dprobs - jnp.sum(dprobs * probs, axis=-1, keepdims=True))
        draw = (dscore * scale).astype(bf16)
        dquery = mm(draw, keys)
        dk_ref[:seen, :] += mm_tn(draw, rows)
        dqkv_ref[at:seen, :hd] = turn_back(dquery, slice(at, seen))
        inner_ref[at:seen, :] += jnp.sum(dquery * rows.astype(f32), axis=-1, keepdims=True)
    dkey, dvalue = dk_ref[...], dv_ref[...]
    dqkv_ref[:, hd : 2 * hd] = turn_back(dkey, slice(None))
    dqkv_ref[:, 2 * hd :] = dvalue.astype(bf16)
    inner_ref[...] += jnp.sum(
        dkey * qkv_ref[:, hd : 2 * hd].astype(f32) + dvalue * qkv_ref[:, 2 * hd :].astype(f32),
        axis=-1,
        keepdims=True,
    )


def attend_backward(qkv, dcontext, lse, lengths, cosine, sine):
    tokens, width = qkv.shape
    heads = width // (3 * HEAD_DIM)
    slots = tokens // SEQ_LEN
    wide = pl.BlockSpec((SEQ_LEN, 3 * HEAD_DIM), lambda s, h, _: (s, h))
    one = pl.BlockSpec((SEQ_LEN, HEAD_DIM), lambda s, h, _: (s, h))
    table = pl.BlockSpec((SEQ_LEN, HEAD_DIM), lambda s, h, _: (0, 0))
    pairs = slots * heads * SEQ_LEN * SEQ_LEN
    return pl.pallas_call(
        attend_backward_kernel,
        grid_spec=pltpu.PrefetchScalarGridSpec(
            num_scalar_prefetch=1,
            grid=(slots, heads),
            in_specs=[wide, one, one, table, table],
            out_specs=[wide, pl.BlockSpec((SEQ_LEN, 1), lambda s, h, _: (s, 0))],
            scratch_shapes=[pltpu.VMEM((SEQ_LEN, HEAD_DIM), f32)] * 2,
        ),
        out_shape=[
            jax.ShapeDtypeStruct((tokens, width), bf16),
            jax.ShapeDtypeStruct((tokens, 1), f32),
        ],
        cost_estimate=pl.CostEstimate(
            flops=8 * HEAD_DIM * pairs, bytes_accessed=8 * tokens * width, transcendentals=pairs
        ),
        name="attend_backward",
    )(lengths, qkv, dcontext, lse, cosine, sine)


def gather_rows(part):
    n = lax.axis_size("row")
    if n != 4:
        return (lax.all_gather(part, "row", axis=0, tiled=True),), ((), (), ())
    partner = lax.ppermute(part, "row", [(0, 1), (1, 0), (2, 3), (3, 2)])
    middle, outward = [(1, 2), (2, 1)], [(1, 0), (2, 3)]
    near_mid = lax.ppermute(part, "row", middle)
    far_mid = lax.ppermute(partner, "row", middle)
    near_out = lax.ppermute(near_mid, "row", outward)
    far_out = lax.ppermute(far_mid, "row", outward)
    hops = ((partner, near_mid), (far_mid, near_out), (far_out,))
    return (part, partner, near_mid, far_mid, near_out, far_out), hops


def places(z):
    pair = z // 2
    return z, z + 1 - 2 * lax.rem(z, 2), 2 - pair, 3 - 3 * pair


def join_rows(pieces):
    if len(pieces) == 1:
        return pieces[0]
    part = pieces[0]
    z = lax.axis_index("row")
    whole = jnp.zeros((4,) + part.shape, part.dtype)
    blocks = (part, pieces[1], pieces[2] + pieces[4], pieces[3] + pieces[5])
    for at, piece in zip(places(z), blocks):
        whole = lax.dynamic_update_slice_in_dim(whole, piece[None], at, 0)
    return whole.reshape((4 * part.shape[0],) + part.shape[1:])


def reduce_rows(grads):
    n = lax.axis_size("row")
    if n != 4:
        total = lax.psum_scatter(grads, "row", scatter_dimension=0, tiled=True)
        return total.astype(f32), ((), (), ())
    own, partner, near, far = places(lax.axis_index("row"))
    size = grads.shape[0] // n
    inward, middle = [(0, 1), (3, 2)], [(1, 2), (2, 1)]

    def block(at, *others):
        piece = lax.dynamic_slice_in_dim(grads, at * size, size, 0)
        if others:
            piece = piece.astype(f32)
            for other in others:
                piece = piece + other.astype(f32)
        return piece

    far_in = lax.ppermute(block(far), "row", inward)
    near_in = lax.ppermute(block(near), "row", inward)
    far_sum = lax.ppermute(block(far, far_in).astype(bf16), "row", middle)
    near_sum = lax.ppermute(block(near, near_in).astype(bf16), "row", middle)
    exchanged = lax.ppermute(
        block(partner, far_sum).astype(bf16), "row", [(0, 1), (1, 0), (2, 3), (3, 2)]
    )
    hops = ((far_in, near_in), (far_sum, near_sum), (exchanged,))
    return block(own, near_sum, exchanged), hops


def after(value, *groups):
    others = tuple(item for group in groups for item in group)
    return lax.optimization_barrier((value,) + others)[0] if others else value


def expert_kernel(size, steps, count, z_ref, *refs):
    pieces = refs[:count]
    (x_ref, cot_ref, x_cols, cot_cols, coef_ref) = refs[count : count + 5]
    (dpair_ref, hidden_ref, sums_ref, grads_ref, whole_ref) = refs[count + 5 : count + 10]
    weights, dpair, hidden, sems, out_sem = refs[count + 10 :]
    step = pl.program_id(0)
    write = pltpu.make_async_copy(weights, whole_ref, out_sem)

    @pl.when(step == 0)
    def _():
        if count == 1:
            copy = pltpu.make_async_copy(pieces[0], weights, sems.at[0])
            copy.start()
            copy.wait()
        else:
            z = z_ref[0]
            block = pieces[0].shape[0]

            def copy_of(piece, which):
                at = pl.multiple_of(places(z)[which] * block, block)
                return pltpu.make_async_copy(
                    piece, weights.at[pl.ds(at, block)], sems.at[which]
                )

            copy_of(pieces[0], 0).start()
            copy_of(pieces[1], 1).start()
            in_middle = (z == 1) | (z == 2)

            @pl.when(in_middle)
            def _():
                copy_of(pieces[2], 2).start()
                copy_of(pieces[3], 3).start()

            @pl.when(jnp.logical_not(in_middle))
            def _():
                copy_of(pieces[4], 2).start()
                copy_of(pieces[5], 3).start()

            for which in range(4):
                copy_of(pieces[which], which).wait()
        write.start()

    @pl.when(step < steps)
    def _():
        at = pl.multiple_of(step * TILE, TILE)
        rows, cots = x_ref[...], cot_ref[...]
        scale, weight = coef_ref[:, 0:1], coef_ref[:, 1:2]
        dots = jnp.zeros((TILE, 1), f32)
        inner = jnp.zeros((TILE, 1), f32)
        for a in range(0, size, TILE):
            b = min(a + TILE, size)
            gate = scale * mm(rows, weights[:, a:b])
            up = scale * mm(rows, weights[:, size + a : size + b])
            dhid = mm(cots, weights[:, 2 * size + a : 2 * size + b])
            sigma = jax.nn.sigmoid(gate)
            silu = gate * sigma
            hid = silu * up
            dots += jnp.sum(hid * dhid, axis=1, keepdims=True)
            dhid = weight * dhid
            dgate = dhid * up * sigma * (1.0 + gate * (1.0 - sigma))
            dup = dhid * silu
            inner += jnp.sum(dgate * gate + dup * up, axis=1, keepdims=True)
            for into, at_col, value in (
                ((hidden_ref, hidden), a, weight * hid),
                ((dpair_ref, dpair), a, scale * dgate),
                ((dpair_ref, dpair), size + a, scale * dup),
            ):
                value = value.astype(bf16)
                into[0][:, at_col : at_col + b - a] = value
                into[1][pl.ds(at, TILE), at_col : at_col + b - a] = value
        sums_ref[:, 0:1] = dots
        sums_ref[:, 1:2] = inner

    @pl.when(step >= steps)
    def _():
        for a in range(0, 2 * size, TILE):
            b = min(a + TILE, 2 * size)
            grads_ref[:, a:b] = mm_tn(x_cols[...], dpair[:, a:b]).astype(bf16)
        for a in range(0, size, TILE):
            b = min(a + TILE, size)
            grads_ref[:, 2 * size + a : 2 * size + b] = mm_tn(
                cot_cols[...], hidden[:, a:b]
            ).astype(bf16)

    @pl.when(step == pl.num_programs(0) - 1)
    def _():
        write.wait()


def expert_chunk(pieces, scaled, cots, coef):
    tokens, width = scaled.shape
    size = pieces[0].shape[1] // 3
    steps, more = tokens // TILE, width // TILE
    count = len(pieces)
    rows = lambda i, _: (jnp.minimum(i, steps - 1), 0)
    cols = lambda i, _: (0, jnp.maximum(i - steps, 0))
    down = lambda i, _: (jnp.maximum(i - steps, 0), 0)
    z = jnp.reshape(lax.axis_index("row"), (1,)).astype(jnp.int32)
    return pl.pallas_call(
        functools.partial(expert_kernel, size, steps, count),
        grid_spec=pltpu.PrefetchScalarGridSpec(
            num_scalar_prefetch=1,
            grid=(steps + more,),
            in_specs=[pl.BlockSpec(memory_space=pl.ANY)] * count
            + [
                pl.BlockSpec((TILE, width), rows),
                pl.BlockSpec((TILE, width), rows),
                pl.BlockSpec((tokens, TILE), cols),
                pl.BlockSpec((tokens, TILE), cols),
                pl.BlockSpec((TILE, 2), rows),
            ],
            out_specs=[
                pl.BlockSpec((TILE, 2 * size), rows),
                pl.BlockSpec((TILE, size), rows),
                pl.BlockSpec((TILE, 2), rows),
                pl.BlockSpec((TILE, 3 * size), down),
                pl.BlockSpec(memory_space=pl.ANY),
            ],
            scratch_shapes=[
                pltpu.VMEM((width, 3 * size), bf16),
                pltpu.VMEM((tokens, 2 * size), bf16),
                pltpu.VMEM((tokens, size), bf16),
                pltpu.SemaphoreType.DMA((4,)),
                pltpu.SemaphoreType.DMA,
            ],
        ),
        out_shape=[
            jax.ShapeDtypeStruct((tokens, 2 * size), bf16),
            jax.ShapeDtypeStruct((tokens, size), bf16),
            jax.ShapeDtypeStruct((tokens, 2), f32),
            jax.ShapeDtypeStruct((width, 3 * size), bf16),
            jax.ShapeDtypeStruct((width, 3 * size), bf16),
        ],
        cost_estimate=pl.CostEstimate(
            flops=12 * tokens * width * size,
            bytes_accessed=8 * tokens * width + 24 * width * size,
            transcendentals=tokens * size,
        ),
        name="expert_chunk",
    )(z, *pieces, scaled, cots, scaled, cots, coef)


def joint_kernel(count, *refs):
    out_ref = refs[-1]
    for a in range(0, out_ref.shape[1], TILE):
        total = None
        for left, weights in zip(refs[:count], refs[count:-1]):
            part = mm_nt(left[...], weights[a : a + TILE, :])
            total = part if total is None else total + part
        out_ref[:, a : a + TILE] = total.astype(bf16)


def joint_back(lefts, weights, column):
    tokens, width = lefts[0].shape[0], weights[0].shape[0]
    row = lambda i: (i, 0)
    fixed = lambda i: (0, column)
    depth = sum(left.shape[1] for left in lefts)
    return pl.pallas_call(
        functools.partial(joint_kernel, len(lefts)),
        grid=(tokens // TILE,),
        in_specs=[pl.BlockSpec((TILE, left.shape[1]), row) for left in lefts]
        + [
            pl.BlockSpec((width, left.shape[1]), fixed, pipeline_mode=pl.Buffered(1))
            for left in lefts
        ],
        out_specs=pl.BlockSpec((TILE, width), row),
        out_shape=jax.ShapeDtypeStruct((tokens, width), bf16),
        cost_estimate=pl.CostEstimate(
            flops=2 * tokens * width * depth,
            bytes_accessed=2 * (tokens + width) * depth + 2 * tokens * width,
            transcendentals=0,
        ),
        name="joint_back",
    )(*lefts, *weights)


def split_three(values):
    high = values.astype(bf16)
    rest = values - high.astype(f32)
    middle = rest.astype(bf16)
    return high, middle, (rest - middle.astype(f32)).astype(bf16)


def cuts_of(width):
    at, cuts = 0, []
    while at < width:
        cuts.append((at, min(at + CHUNK, width)))
        at += CHUNK
    return cuts


def per_device(
    block_input,
    seq_lengths,
    slot_order,
    routes,
    input_gain,
    query_weight,
    key_weight,
    value_weight,
    output_weight,
    mlp_gain,
    router_weight,
    score_shared,
    gate_shared,
    up_shared,
    down_shared,
    gate_expert,
    up_expert,
    down_expert,
    grad_output,
):
    tokens, share = block_input.shape
    cols = lax.axis_size("col")
    col_id = lax.axis_index("col")
    row_id = lax.axis_index("row")
    width = share * cols
    slots = tokens // SEQ_LEN
    local_experts = gate_expert.shape[0]
    experts = router_weight.shape[1]
    head_width = query_weight.shape[1]
    heads = head_width // HEAD_DIM
    rows_block = query_weight.shape[0]
    lengths = lax.dynamic_slice_in_dim(seq_lengths[slot_order], row_id * slots, slots, 0)
    cosine, sine = rope_tables()

    def by_head(weight):
        return weight.reshape(rows_block, heads, 1, HEAD_DIM)

    qkv_pack = jnp.concatenate(
        [by_head(query_weight), by_head(key_weight), by_head(value_weight)], axis=2
    ).reshape(rows_block, 3 * head_width)
    router_pack = jnp.concatenate([router_weight, score_shared[:, None]], axis=1)
    router_pack = jnp.pad(router_pack, ((0, 0), (0, -router_pack.shape[1] % 128)))
    attn_weights = join_rows(
        gather_rows(jnp.concatenate([qkv_pack, output_weight.T, router_pack], axis=1))[0]
    )
    qkv_full = attn_weights[:, : 3 * head_width]
    out_full = attn_weights[:, 3 * head_width : 4 * head_width]
    router_full = attn_weights[:, 4 * head_width : 4 * head_width + experts + 1]
    shared_cuts = [(None, a, b) for a, b in cuts_of(gate_shared.shape[1])]
    expert_cuts = [
        (local, a, b) for local in range(local_experts) for a, b in cuts_of(gate_expert.shape[2])
    ]
    chunks = shared_cuts[-1:] + expert_cuts[:-1] + shared_cuts[:-1] + expert_cuts[-1:]

    def pack(kind, a, b):
        if kind is None:
            parts = [gate_shared[:, a:b], up_shared[:, a:b], down_shared[a:b].T]
        else:
            parts = [gate_expert[kind, :, a:b], up_expert[kind, :, a:b], down_expert[kind, a:b].T]
        fill = -(b - a) % 128
        return jnp.concatenate([jnp.pad(part, ((0, 0), (0, fill))) for part in parts], axis=1)

    gathered, came = zip(*[gather_rows(pack(*chunk)) for chunk in chunks])

    def hop(arrivals, at, which):
        return arrivals[at][which] if 0 <= at < len(arrivals) else ()

    rows_in = lax.all_gather(block_input, "col", axis=1, tiled=True)
    gains = lax.all_gather(jnp.stack([input_gain, mlp_gain]), "col", axis=1, tiled=True).astype(f32)
    cot_rows = lax.all_gather(grad_output, "col", axis=1, tiled=True)
    rows_f = rows_in.astype(f32)
    scale_a = lax.rsqrt(jnp.mean(rows_f * rows_f, axis=-1, keepdims=True) + norm_eps)
    normed_a = after((rows_f * scale_a * gains[0]).astype(bf16), hop(came, 0, 0))
    qkv, context, lse = attend_forward(mm(normed_a, qkv_full), lengths, cosine, sine)
    attn_part = after(mm_nt(context, out_full).astype(bf16), (cot_rows,))
    x_share = block_input.astype(f32)
    attn_sum = lax.psum_scatter(attn_part, "col", scatter_dimension=1, tiled=True)
    attn_sum = after(
        attn_sum, hop(came, 0, 1), hop(came, 0, 2), hop(came, 1, 0), hop(came, 1, 1)
    )
    stream = x_share + attn_sum.astype(f32)
    gain_b = mlp_gain.astype(f32)
    scaled = lax.all_gather((stream * gain_b).astype(bf16), "col", axis=1, tiled=True)
    stream_f = scaled.astype(f32) / gains[1]
    scale_b = lax.rsqrt(jnp.mean(stream_f * stream_f, axis=1, keepdims=True) + norm_eps)

    both_logits = scale_b * mm(scaled, router_full)
    logits, slogit = both_logits[:, :experts], both_logits[:, experts]
    top = jnp.max(logits, axis=-1, keepdims=True)
    expo = jnp.exp(logits - top)
    router_probs = expo / jnp.sum(expo, axis=-1, keepdims=True)
    shared_gate = jax.nn.sigmoid(slogit)

    inner = jnp.zeros((tokens,), f32)
    dots = {}
    members, shares = {None: None}, {None: shared_gate}
    for local in range(local_experts):
        expert = col_id * local_experts + local
        members[local] = jnp.any(routes == expert, axis=1)
        column = lax.dynamic_index_in_dim(router_probs, expert, 1, False)
        shares[local] = jnp.where(members[local], column, 0.0)
    dpairs, hiddens, wholes, unit_grads, went = [], [], [], [], []
    for at, ((kind, a, b), pieces) in enumerate(zip(chunks, gathered)):
        coef = jnp.concatenate([scale_b, shares[kind][:, None]], axis=1)
        if at == 0:
            coef = after(coef, hop(came, 1, 2), hop(came, 2, 0))
        elif at == 1:
            coef = after(coef, hop(came, 2, 1))
        else:
            coef = after(
                coef,
                hop(came, at + 1, 0),
                hop(went, at - 2, 0),
                hop(went, at - 3, 1),
                hop(went, at - 4, 2),
            )
        dpair, hidden, sums, grads, whole = expert_chunk(pieces, scaled, cot_rows, coef)
        dots[kind] = dots.get(kind, 0.0) + sums[:, 0]
        inner = inner + sums[:, 1]
        dpairs.append(dpair)
        hiddens.append(hidden)
        wholes.append(whole)
        reduced, arrivals = reduce_rows(grads)
        unit_grads.append(reduced)
        went.append(arrivals)
    last = len(chunks) - 1
    dpairs[-1] = after(dpairs[-1], hop(went, last - 1, 0), hop(went, last - 2, 1))
    dscaled_part = joint_back(dpairs, wholes, 0)
    moe_share = lax.psum_scatter(
        joint_back(hiddens, wholes, 2), "col", scatter_dimension=1, tiled=True
    ).astype(f32)
    block_output = (stream + moe_share).astype(bf16)

    table = jnp.zeros((experts, tokens), f32)
    for local in range(local_experts):
        row = jnp.where(members[local], dots[local], 0.0)[None]
        table = lax.dynamic_update_slice_in_dim(table, row, col_id * local_experts + local, 0)
    table = lax.psum(jnp.concatenate([table, dots[None][None], inner[None]], axis=0), "col")
    dprob, dshared_gate, inner = table[:experts].T, table[experts], table[experts + 1]
    dlogits = router_probs * (dprob - jnp.sum(dprob * router_probs, axis=1, keepdims=True))
    dslogit = dshared_gate * shared_gate * (1.0 - shared_gate)
    dboth = jnp.concatenate([dlogits, dslogit[:, None]], axis=1)
    inner = inner + jnp.sum(dboth * both_logits, axis=1)
    dboth = scale_b * dboth
    parts = split_three(dboth)
    stacked = mm_tn(jnp.concatenate(parts, axis=1), scaled)
    grad_router_part = stacked.reshape(3, experts + 1, width).sum(axis=0)
    grad_router_both = lax.psum_scatter(grad_router_part, "row", scatter_dimension=1, tiled=True)
    router_rows = lax.dynamic_slice_in_dim(router_full, col_id * share, share, 0)
    back = mm_nt(jnp.concatenate(parts, axis=1), jnp.concatenate([router_rows] * 3, axis=1))
    dscaled_sum = after(
        lax.psum_scatter(dscaled_part, "col", scatter_dimension=1, tiled=True),
        hop(went, last - 3, 2),
        hop(went, last - 2, 2),
        hop(went, last - 1, 1),
        hop(went, last, 0),
    )
    dscaled = back + dscaled_sum.astype(f32)
    cot_share = grad_output.astype(f32)
    dstream = cot_share + gain_b * dscaled - stream * (scale_b * scale_b * inner[:, None] / width)
    gain_b_grad = jnp.sum(dscaled * stream, axis=0)

    dattn = lax.all_gather(dstream.astype(bf16), "col", axis=1, tiled=True)
    dattn = after(dattn, hop(went, last - 1, 2), hop(went, last, 1))
    out_grad, _ = reduce_rows(mm_tn(dattn, context).astype(bf16))
    dcontext = mm(dattn, out_full).astype(bf16)
    dqkv, inner_a = attend_backward(qkv, dcontext, lse, lengths, cosine, sine)
    inner_a = lax.psum(inner_a[:, 0], "col")[:, None]
    qkv_grad, _ = reduce_rows(mm_tn(normed_a, dqkv).astype(bf16))
    dnormed_sum = lax.psum_scatter(
        mm_nt(dqkv, qkv_full).astype(bf16), "col", scatter_dimension=1, tiled=True
    )
    dnormed_a = after(dnormed_sum, (inner_a,), hop(went, last, 2)).astype(f32)
    gain_a_share = input_gain.astype(f32)
    dinput = dstream + scale_a * gain_a_share * dnormed_a
    dinput = dinput - x_share * (scale_a * scale_a * inner_a / width)
    gain_a_grad = jnp.sum(dnormed_a * x_share * scale_a, axis=0)
    grad_gain_a, grad_gain_b = lax.psum((gain_a_grad, gain_b_grad), "row")

    qkv_grad = qkv_grad.reshape(rows_block, heads, 3, HEAD_DIM)
    grad_query, grad_key, grad_value = (
        qkv_grad[:, :, part].reshape(rows_block, head_width) for part in range(3)
    )
    def unpack(kind, which):
        found = []
        for (of, a, b), grad in zip(chunks, unit_grads):
            if of == kind:
                size = grad.shape[1] // 3
                part = grad[:, which * size : which * size + b - a]
                found.append((a, part.T if which == 2 else part))
        found = [part for _, part in sorted(found, key=lambda item: item[0])]
        return jnp.concatenate(found, axis=0 if which == 2 else 1)

    locals_ = range(local_experts)
    return (
        block_output,
        dinput.astype(bf16),
        grad_gain_a,
        grad_query,
        grad_key,
        grad_value,
        out_grad.T,
        grad_gain_b,
        grad_router_both[:experts].T,
        grad_router_both[experts],
        unpack(None, 0),
        unpack(None, 1),
        unpack(None, 2),
        jnp.stack([unpack(local, 0) for local in locals_]),
        jnp.stack([unpack(local, 1) for local in locals_]),
        jnp.stack([unpack(local, 2) for local in locals_]),
    )


def solution(mesh):
    return jax.shard_map(
        per_device,
        mesh=mesh,
        in_specs=(
            P("row", "col"),
            P(),
            P(),
            P("row", None),
            P("col"),
            P("row", "col"),
            P("row", "col"),
            P("row", "col"),
            P("col", "row"),
            P("col"),
            P("row", None),
            P("row"),
            P("row", "col"),
            P("row", "col"),
            P("col", "row"),
            P("col", "row", None),
            P("col", "row", None),
            P("col", None, "row"),
            P("row", "col"),
        ),
        out_specs=(
            P("row", "col"),
            P("row", "col"),
            P("col"),
            P("row", "col"),
            P("row", "col"),
            P("row", "col"),
            P("col", "row"),
            P("col"),
            P("row", None),
            P("row"),
            P("row", "col"),
            P("row", "col"),
            P("col", "row"),
            P("col", "row", None),
            P("col", "row", None),
            P("col", None, "row"),
        ),
        check_vma=False,
    )
```

```python
import functools
import math

import jax
import jax.numpy as jnp
from jax import lax
from jax.experimental import pallas as pl
from jax.experimental.pallas import tpu as pltpu
from jax.sharding import PartitionSpec as P

HEAD_DIM = 128
SEQ_LEN = 1024
QBLOCK = 256
TILE = 256
CHUNK = 512
norm_eps = 1e-06
rope_base = 1000000.0
bf16 = jnp.bfloat16
f32 = jnp.float32


def mm(left, right):
    return jnp.dot(left, right, preferred_element_type=f32)


def mm_nt(left, right):
    return lax.dot_general(left, right, (((1,), (1,)), ((), ())), preferred_element_type=f32)


def mm_tn(left, right):
    return lax.dot_general(left, right, (((0,), (0,)), ((), ())), preferred_element_type=f32)


def rope_tables():
    positions = jnp.arange(SEQ_LEN).astype(f32)
    freqs = jnp.power(f32(rope_base), -jnp.arange(0, HEAD_DIM, 2).astype(f32) / HEAD_DIM)
    angles = positions[:, None] * freqs[None, :]
    cosine, sine = jnp.cos(angles), jnp.sin(angles)
    return (
        jnp.concatenate([cosine, cosine], axis=-1),
        jnp.concatenate([-sine, sine], axis=-1),
    )


def block_scores(rows, keys, start, length, scale):
    raw = mm_nt(rows, keys) * scale
    query_pos = start + lax.broadcasted_iota(jnp.int32, raw.shape, 0)
    key_pos = lax.broadcasted_iota(jnp.int32, raw.shape, 1)
    return jnp.where((key_pos <= query_pos) & (key_pos < length), raw, -1e30)


def attend_forward_kernel(length_ref, raw_ref, cos_ref, sin_ref, qkv_ref, context_ref, lse_ref):
    length = length_ref[pl.program_id(0)]
    scale = 1.0 / math.sqrt(HEAD_DIM)
    hd = HEAD_DIM
    for part in range(2):
        raw = raw_ref[:, part * hd : (part + 1) * hd]
        turned = raw * cos_ref[...] + pltpu.roll(raw, hd // 2, 1) * sin_ref[...]
        qkv_ref[:, part * hd : (part + 1) * hd] = turned.astype(bf16)
    qkv_ref[:, 2 * hd :] = raw_ref[:, 2 * hd :].astype(bf16)
    for at in range(0, SEQ_LEN, QBLOCK):
        seen = at + QBLOCK
        scores = block_scores(
            qkv_ref[at:seen, :hd], qkv_ref[:seen, hd : 2 * hd], at, length, scale
        )
        top = jnp.max(scores, axis=-1, keepdims=True)
        expo = jnp.exp(scores - top)
        total = jnp.sum(expo, axis=-1, keepdims=True)
        probs = (expo / total).astype(bf16)
        context_ref[at:seen, :] = mm(probs, qkv_ref[:seen, 2 * hd :]).astype(bf16)
        lse_ref[at:seen, :] = jnp.broadcast_to(top + jnp.log(total), (QBLOCK, hd))


def attend_forward(raw, lengths, cosine, sine):
    tokens, width = raw.shape
    heads = width // (3 * HEAD_DIM)
    slots = tokens // SEQ_LEN
    wide = pl.BlockSpec((SEQ_LEN, 3 * HEAD_DIM), lambda s, h, _: (s, h))
    one = pl.BlockSpec((SEQ_LEN, HEAD_DIM), lambda s, h, _: (s, h))
    table = pl.BlockSpec((SEQ_LEN, HEAD_DIM), lambda s, h, _: (0, 0))
    pairs = slots * heads * SEQ_LEN * SEQ_LEN
    return pl.pallas_call(
        attend_forward_kernel,
        grid_spec=pltpu.PrefetchScalarGridSpec(
            num_scalar_prefetch=1,
            grid=(slots, heads),
            in_specs=[wide, table, table],
            out_specs=[wide, one, one],
        ),
        out_shape=[
            jax.ShapeDtypeStruct((tokens, width), bf16),
            jax.ShapeDtypeStruct((tokens, heads * HEAD_DIM), bf16),
            jax.ShapeDtypeStruct((tokens, heads * HEAD_DIM), f32),
        ],
        cost_estimate=pl.CostEstimate(
            flops=3 * HEAD_DIM * pairs, bytes_accessed=8 * tokens * width, transcendentals=pairs
        ),
        name="attend_forward",
    )(lengths, raw, cosine, sine)


def attend_backward_kernel(
    length_ref, qkv_ref, dcontext_ref, lse_ref, cos_ref, sin_ref, dqkv_ref, inner_ref, dk_ref, dv_ref
):
    length = length_ref[pl.program_id(0)]
    scale = 1.0 / math.sqrt(HEAD_DIM)
    hd = HEAD_DIM
    @pl.when(pl.program_id(1) == 0)
    def _():
        inner_ref[...] = jnp.zeros_like(inner_ref)

    dk_ref[...] = jnp.zeros_like(dk_ref)
    dv_ref[...] = jnp.zeros_like(dv_ref)

    def turn_back(grad, rows):
        back = grad * cos_ref[rows, :] - pltpu.roll(grad, hd // 2, 1) * sin_ref[rows, :]
        return back.astype(bf16)

    for at in range(0, SEQ_LEN, QBLOCK):
        seen = at + QBLOCK
        rows = qkv_ref[at:seen, :hd]
        keys = qkv_ref[:seen, hd : 2 * hd]
        drows = dcontext_ref[at:seen, :]
        scores = block_scores(rows, keys, at, length, scale)
        probs = jnp.exp(scores - lse_ref[at:seen, :1])
        dv_ref[:seen, :] += mm_tn(probs.astype(bf16), drows)
        dprobs = mm_nt(drows, qkv_ref[:seen, 2 * hd :])
        dscore = probs * (dprobs - jnp.sum(dprobs * probs, axis=-1, keepdims=True))
        draw = (dscore * scale).astype(bf16)
        dquery = mm(draw, keys)
        dk_ref[:seen, :] += mm_tn(draw, rows)
        dqkv_ref[at:seen, :hd] = turn_back(dquery, slice(at, seen))
        inner_ref[at:seen, :] += jnp.sum(dquery * rows.astype(f32), axis=-1, keepdims=True)
    dkey, dvalue = dk_ref[...], dv_ref[...]
    dqkv_ref[:, hd : 2 * hd] = turn_back(dkey, slice(None))
    dqkv_ref[:, 2 * hd :] = dvalue.astype(bf16)
    inner_ref[...] += jnp.sum(
        dkey * qkv_ref[:, hd : 2 * hd].astype(f32) + dvalue * qkv_ref[:, 2 * hd :].astype(f32),
        axis=-1,
        keepdims=True,
    )


def attend_backward(qkv, dcontext, lse, lengths, cosine, sine):
    tokens, width = qkv.shape
    heads = width // (3 * HEAD_DIM)
    slots = tokens // SEQ_LEN
    wide = pl.BlockSpec((SEQ_LEN, 3 * HEAD_DIM), lambda s, h, _: (s, h))
    one = pl.BlockSpec((SEQ_LEN, HEAD_DIM), lambda s, h, _: (s, h))
    table = pl.BlockSpec((SEQ_LEN, HEAD_DIM), lambda s, h, _: (0, 0))
    pairs = slots * heads * SEQ_LEN * SEQ_LEN
    return pl.pallas_call(
        attend_backward_kernel,
        grid_spec=pltpu.PrefetchScalarGridSpec(
            num_scalar_prefetch=1,
            grid=(slots, heads),
            in_specs=[wide, one, one, table, table],
            out_specs=[wide, pl.BlockSpec((SEQ_LEN, 1), lambda s, h, _: (s, 0))],
            scratch_shapes=[pltpu.VMEM((SEQ_LEN, HEAD_DIM), f32)] * 2,
        ),
        out_shape=[
            jax.ShapeDtypeStruct((tokens, width), bf16),
            jax.ShapeDtypeStruct((tokens, 1), f32),
        ],
        cost_estimate=pl.CostEstimate(
            flops=8 * HEAD_DIM * pairs, bytes_accessed=8 * tokens * width, transcendentals=pairs
        ),
        name="attend_backward",
    )(lengths, qkv, dcontext, lse, cosine, sine)


def gather_rows(part):
    n = lax.axis_size("row")
    if n != 4:
        return (lax.all_gather(part, "row", axis=0, tiled=True),), ((), (), ())
    partner = lax.ppermute(part, "row", [(0, 1), (1, 0), (2, 3), (3, 2)])
    middle, outward = [(1, 2), (2, 1)], [(1, 0), (2, 3)]
    near_mid = lax.ppermute(part, "row", middle)
    far_mid = lax.ppermute(partner, "row", middle)
    near_out = lax.ppermute(near_mid, "row", outward)
    far_out = lax.ppermute(far_mid, "row", outward)
    hops = ((partner, near_mid), (far_mid, near_out), (far_out,))
    return (part, partner, near_mid, far_mid, near_out, far_out), hops


def places(z):
    pair = z // 2
    return z, z + 1 - 2 * lax.rem(z, 2), 2 - pair, 3 - 3 * pair


def join_rows(pieces):
    if len(pieces) == 1:
        return pieces[0]
    part = pieces[0]
    z = lax.axis_index("row")
    whole = jnp.zeros((4,) + part.shape, part.dtype)
    blocks = (part, pieces[1], pieces[2] + pieces[4], pieces[3] + pieces[5])
    for at, piece in zip(places(z), blocks):
        whole = lax.dynamic_update_slice_in_dim(whole, piece[None], at, 0)
    return whole.reshape((4 * part.shape[0],) + part.shape[1:])


def reduce_rows(grads):
    n = lax.axis_size("row")
    if n != 4:
        total = lax.psum_scatter(grads, "row", scatter_dimension=0, tiled=True)
        return total.astype(f32), ((), (), ())
    own, partner, near, far = places(lax.axis_index("row"))
    size = grads.shape[0] // n
    inward, middle = [(0, 1), (3, 2)], [(1, 2), (2, 1)]

    def block(at, *others):
        piece = lax.dynamic_slice_in_dim(grads, at * size, size, 0)
        if others:
            piece = piece.astype(f32)
            for other in others:
                piece = piece + other.astype(f32)
        return piece

    far_in = lax.ppermute(block(far), "row", inward)
    near_in = lax.ppermute(block(near), "row", inward)
    far_sum = lax.ppermute(block(far, far_in).astype(bf16), "row", middle)
    near_sum = lax.ppermute(block(near, near_in).astype(bf16), "row", middle)
    exchanged = lax.ppermute(
        block(partner, far_sum).astype(bf16), "row", [(0, 1), (1, 0), (2, 3), (3, 2)]
    )
    hops = ((far_in, near_in), (far_sum, near_sum), (exchanged,))
    return block(own, near_sum, exchanged), hops


def after(value, *groups):
    others = tuple(item for group in groups for item in group)
    return lax.optimization_barrier((value,) + others)[0] if others else value


def expert_kernel(size, steps, count, z_ref, *refs):
    pieces = refs[:count]
    (x_ref, cot_ref, x_cols, cot_cols, coef_ref) = refs[count : count + 5]
    (dpair_ref, hidden_ref, sums_ref, grads_ref, whole_ref) = refs[count + 5 : count + 10]
    weights, dpair, hidden, sems, out_sem = refs[count + 10 :]
    step = pl.program_id(0)
    write = pltpu.make_async_copy(weights, whole_ref, out_sem)

    @pl.when(step == 0)
    def _():
        if count == 1:
            copy = pltpu.make_async_copy(pieces[0], weights, sems.at[0])
            copy.start()
            copy.wait()
        else:
            z = z_ref[0]
            block = pieces[0].shape[0]

            def copy_of(piece, which):
                at = pl.multiple_of(places(z)[which] * block, block)
                return pltpu.make_async_copy(
                    piece, weights.at[pl.ds(at, block)], sems.at[which]
                )

            copy_of(pieces[0], 0).start()
            copy_of(pieces[1], 1).start()
            in_middle = (z == 1) | (z == 2)

            @pl.when(in_middle)
            def _():
                copy_of(pieces[2], 2).start()
                copy_of(pieces[3], 3).start()

            @pl.when(jnp.logical_not(in_middle))
            def _():
                copy_of(pieces[4], 2).start()
                copy_of(pieces[5], 3).start()

            for which in range(4):
                copy_of(pieces[which], which).wait()
        write.start()

    @pl.when(step < steps)
    def _():
        at = pl.multiple_of(step * TILE, TILE)
        rows, cots = x_ref[...], cot_ref[...]
        scale, weight = coef_ref[:, 0:1], coef_ref[:, 1:2]
        dots = jnp.zeros((TILE, 1), f32)
        inner = jnp.zeros((TILE, 1), f32)
        for a in range(0, size, TILE):
            b = min(a + TILE, size)
            gate = scale * mm(rows, weights[:, a:b])
            up = scale * mm(rows, weights[:, size + a : size + b])
            dhid = mm(cots, weights[:, 2 * size + a : 2 * size + b])
            sigma = jax.nn.sigmoid(gate)
            silu = gate * sigma
            hid = silu * up
            dots += jnp.sum(hid * dhid, axis=1, keepdims=True)
            dhid = weight * dhid
            dgate = dhid * up * sigma * (1.0 + gate * (1.0 - sigma))
            dup = dhid * silu
            inner += jnp.sum(dgate * gate + dup * up, axis=1, keepdims=True)
            for into, at_col, value in (
                ((hidden_ref, hidden), a, weight * hid),
                ((dpair_ref, dpair), a, scale * dgate),
                ((dpair_ref, dpair), size + a, scale * dup),
            ):
                value = value.astype(bf16)
                into[0][:, at_col : at_col + b - a] = value
                into[1][pl.ds(at, TILE), at_col : at_col + b - a] = value
        sums_ref[:, 0:1] = dots
        sums_ref[:, 1:2] = inner

    @pl.when(step >= steps)
    def _():
        for a in range(0, 2 * size, TILE):
            b = min(a + TILE, 2 * size)
            grads_ref[:, a:b] = mm_tn(x_cols[...], dpair[:, a:b]).astype(bf16)
        for a in range(0, size, TILE):
            b = min(a + TILE, size)
            grads_ref[:, 2 * size + a : 2 * size + b] = mm_tn(
                cot_cols[...], hidden[:, a:b]
            ).astype(bf16)

    @pl.when(step == pl.num_programs(0) - 1)
    def _():
        write.wait()


def expert_chunk(pieces, scaled, cots, coef):
    tokens, width = scaled.shape
    size = pieces[0].shape[1] // 3
    steps, more = tokens // TILE, width // TILE
    count = len(pieces)
    rows = lambda i, _: (jnp.minimum(i, steps - 1), 0)
    cols = lambda i, _: (0, jnp.maximum(i - steps, 0))
    down = lambda i, _: (jnp.maximum(i - steps, 0), 0)
    z = jnp.reshape(lax.axis_index("row"), (1,)).astype(jnp.int32)
    return pl.pallas_call(
        functools.partial(expert_kernel, size, steps, count),
        grid_spec=pltpu.PrefetchScalarGridSpec(
            num_scalar_prefetch=1,
            grid=(steps + more,),
            in_specs=[pl.BlockSpec(memory_space=pl.ANY)] * count
            + [
                pl.BlockSpec((TILE, width), rows),
                pl.BlockSpec((TILE, width), rows),
                pl.BlockSpec((tokens, TILE), cols),
                pl.BlockSpec((tokens, TILE), cols),
                pl.BlockSpec((TILE, 2), rows),
            ],
            out_specs=[
                pl.BlockSpec((TILE, 2 * size), rows),
                pl.BlockSpec((TILE, size), rows),
                pl.BlockSpec((TILE, 2), rows),
                pl.BlockSpec((TILE, 3 * size), down),
                pl.BlockSpec(memory_space=pl.ANY),
            ],
            scratch_shapes=[
                pltpu.VMEM((width, 3 * size), bf16),
                pltpu.VMEM((tokens, 2 * size), bf16),
                pltpu.VMEM((tokens, size), bf16),
                pltpu.SemaphoreType.DMA((4,)),
                pltpu.SemaphoreType.DMA,
            ],
        ),
        out_shape=[
            jax.ShapeDtypeStruct((tokens, 2 * size), bf16),
            jax.ShapeDtypeStruct((tokens, size), bf16),
            jax.ShapeDtypeStruct((tokens, 2), f32),
            jax.ShapeDtypeStruct((width, 3 * size), bf16),
            jax.ShapeDtypeStruct((width, 3 * size), bf16),
        ],
        cost_estimate=pl.CostEstimate(
            flops=12 * tokens * width * size,
            bytes_accessed=8 * tokens * width + 24 * width * size,
            transcendentals=tokens * size,
        ),
        name="expert_chunk",
    )(z, *pieces, scaled, cots, scaled, cots, coef)


def joint_kernel(count, based, *refs):
    out_ref = refs[-1]
    for a in range(0, out_ref.shape[1], TILE):
        total = refs[2 * count][:, a : a + TILE] if based else None
        for left, weights in zip(refs[:count], refs[count : 2 * count]):
            part = mm_nt(left[...], weights[a : a + TILE, :])
            total = part if total is None else total + part
        out_ref[:, a : a + TILE] = total.astype(out_ref.dtype)


def joint_back(lefts, weights, column, kind, *base):
    tokens, width = lefts[0].shape[0], weights[0].shape[0]
    row = lambda i: (i, 0)
    fixed = lambda i: (0, column)
    depth = sum(left.shape[1] for left in lefts)
    return pl.pallas_call(
        functools.partial(joint_kernel, len(lefts), len(base) > 0),
        grid=(tokens // TILE,),
        in_specs=[pl.BlockSpec((TILE, left.shape[1]), row) for left in lefts]
        + [
            pl.BlockSpec((width, left.shape[1]), fixed, pipeline_mode=pl.Buffered(1))
            for left in lefts
        ]
        + [pl.BlockSpec((TILE, width), row)] * len(base),
        out_specs=pl.BlockSpec((TILE, width), row),
        out_shape=jax.ShapeDtypeStruct((tokens, width), kind),
        cost_estimate=pl.CostEstimate(
            flops=2 * tokens * width * depth,
            bytes_accessed=2 * (tokens + width) * depth + 4 * tokens * width,
            transcendentals=0,
        ),
        name="joint_back",
    )(*lefts, *weights, *base)


def split_three(values):
    high = values.astype(bf16)
    rest = values - high.astype(f32)
    middle = rest.astype(bf16)
    return high, middle, (rest - middle.astype(f32)).astype(bf16)


def cuts_of(width):
    at, cuts = 0, []
    while at < width:
        cuts.append((at, min(at + CHUNK, width)))
        at += CHUNK
    return cuts


def per_device(
    block_input,
    seq_lengths,
    slot_order,
    routes,
    input_gain,
    query_weight,
    key_weight,
    value_weight,
    output_weight,
    mlp_gain,
    router_weight,
    score_shared,
    gate_shared,
    up_shared,
    down_shared,
    gate_expert,
    up_expert,
    down_expert,
    grad_output,
):
    tokens, share = block_input.shape
    cols = lax.axis_size("col")
    col_id = lax.axis_index("col")
    row_id = lax.axis_index("row")
    width = share * cols
    slots = tokens // SEQ_LEN
    local_experts = gate_expert.shape[0]
    experts = router_weight.shape[1]
    head_width = query_weight.shape[1]
    heads = head_width // HEAD_DIM
    rows_block = query_weight.shape[0]
    lengths = lax.dynamic_slice_in_dim(seq_lengths[slot_order], row_id * slots, slots, 0)
    cosine, sine = rope_tables()

    def by_head(weight):
        return weight.reshape(rows_block, heads, 1, HEAD_DIM)

    qkv_pack = jnp.concatenate(
        [by_head(query_weight), by_head(key_weight), by_head(value_weight)], axis=2
    ).reshape(rows_block, 3 * head_width)
    router_pack = jnp.concatenate([router_weight, score_shared[:, None]], axis=1)
    router_pack = jnp.pad(router_pack, ((0, 0), (0, -router_pack.shape[1] % 128)))
    qkv_full = join_rows(gather_rows(qkv_pack)[0])
    out_pack = jnp.concatenate([output_weight.T, router_pack], axis=1)
    out_weights = join_rows(gather_rows(out_pack)[0])
    out_full = out_weights[:, :head_width]
    router_full = out_weights[:, head_width : head_width + experts + 1]
    shared_cuts = [(None, a, b) for a, b in cuts_of(gate_shared.shape[1])]
    expert_cuts = [
        (local, a, b) for local in range(local_experts) for a, b in cuts_of(gate_expert.shape[2])
    ]
    chunks = shared_cuts[-1:] + expert_cuts[:-1] + shared_cuts[:-1] + expert_cuts[-1:]

    def pack(kind, a, b):
        if kind is None:
            parts = [gate_shared[:, a:b], up_shared[:, a:b], down_shared[a:b].T]
        else:
            parts = [gate_expert[kind, :, a:b], up_expert[kind, :, a:b], down_expert[kind, a:b].T]
        fill = -(b - a) % 128
        return jnp.concatenate([jnp.pad(part, ((0, 0), (0, fill))) for part in parts], axis=1)

    gathered, came = zip(*[gather_rows(pack(*chunk)) for chunk in chunks])

    def hop(arrivals, at, which):
        return arrivals[at][which] if 0 <= at < len(arrivals) else ()

    rows_in = lax.all_gather(block_input, "col", axis=1, tiled=True)
    gains = lax.all_gather(jnp.stack([input_gain, mlp_gain]), "col", axis=1, tiled=True).astype(f32)
    cot_rows = lax.all_gather(grad_output, "col", axis=1, tiled=True)
    rows_f = rows_in.astype(f32)
    scale_a = lax.rsqrt(jnp.mean(rows_f * rows_f, axis=-1, keepdims=True) + norm_eps)
    normed_a = (rows_f * scale_a * gains[0]).astype(bf16)
    qkv, context, lse = attend_forward(mm(normed_a, qkv_full), lengths, cosine, sine)
    attn_part = after(mm_nt(context, out_full).astype(bf16), (cot_rows,), hop(came, 0, 0))
    x_share = block_input.astype(f32)
    attn_sum = lax.psum_scatter(attn_part, "col", scatter_dimension=1, tiled=True)
    attn_sum = after(attn_sum, hop(came, 0, 1), hop(came, 0, 2), hop(came, 1, 0))
    stream = x_share + attn_sum.astype(f32)
    gain_b = mlp_gain.astype(f32)
    scaled = lax.all_gather((stream * gain_b).astype(bf16), "col", axis=1, tiled=True)
    stream_f = scaled.astype(f32) / gains[1]
    scale_b = lax.rsqrt(jnp.mean(stream_f * stream_f, axis=1, keepdims=True) + norm_eps)

    both_logits = scale_b * mm(scaled, router_full)
    logits, slogit = both_logits[:, :experts], both_logits[:, experts]
    top = jnp.max(logits, axis=-1, keepdims=True)
    expo = jnp.exp(logits - top)
    router_probs = expo / jnp.sum(expo, axis=-1, keepdims=True)
    shared_gate = jax.nn.sigmoid(slogit)

    inner = jnp.zeros((tokens,), f32)
    dots = {}
    members, shares = {None: None}, {None: shared_gate}
    for local in range(local_experts):
        expert = col_id * local_experts + local
        members[local] = jnp.any(routes == expert, axis=1)
        column = lax.dynamic_index_in_dim(router_probs, expert, 1, False)
        shares[local] = jnp.where(members[local], column, 0.0)
    dpairs, hiddens, wholes, unit_grads, went = [], [], [], [], []
    last = len(chunks) - 1
    for at, ((kind, a, b), pieces) in enumerate(zip(chunks, gathered)):
        coef = jnp.concatenate([scale_b, shares[kind][:, None]], axis=1)
        if at == 0:
            coef = after(coef, hop(came, 1, 1), hop(came, 1, 2))
        elif at == 1:
            coef = after(coef, hop(came, 2, 0))
        else:
            coef = after(
                coef,
                hop(came, at + 1, 0),
                hop(went, at - 2, 0),
                hop(went, at - 3, 1),
                hop(went, at - 4, 2),
            )
        if at == last:
            dscaled_early = joint_back(dpairs, wholes, 0, f32)
            moe_early = joint_back(hiddens, wholes, 2, f32)
            coef = after(coef, (dscaled_early, moe_early))
        dpair, hidden, sums, grads, whole = expert_chunk(pieces, scaled, cot_rows, coef)
        dots[kind] = dots.get(kind, 0.0) + sums[:, 0]
        inner = inner + sums[:, 1]
        dpairs.append(dpair)
        hiddens.append(hidden)
        wholes.append(whole)
        reduced, arrivals = reduce_rows(grads)
        unit_grads.append(reduced)
        went.append(arrivals)
    dscaled_part = joint_back([dpair], [whole], 0, bf16, dscaled_early)
    moe_part = joint_back([hidden], [whole], 2, bf16, moe_early)

    named = [jnp.where(members[local], dots[local], 0.0) for local in range(local_experts)]
    table = lax.all_gather(jnp.stack(named + [dots[None], inner]), "col", axis=0)
    dprob = table[:, :local_experts].reshape(experts, tokens).T
    dshared_gate, inner = jnp.sum(table[:, local_experts], axis=0), jnp.sum(table[:, local_experts + 1], axis=0)
    dlogits = router_probs * (dprob - jnp.sum(dprob * router_probs, axis=1, keepdims=True))
    dslogit = dshared_gate * shared_gate * (1.0 - shared_gate)
    dboth = jnp.concatenate([dlogits, dslogit[:, None]], axis=1)
    inner = inner + jnp.sum(dboth * both_logits, axis=1)
    dboth = scale_b * dboth
    parts = split_three(dboth)
    stacked = mm_tn(jnp.concatenate(parts, axis=1), scaled)
    grad_router_part = stacked.reshape(3, experts + 1, width).sum(axis=0)
    grad_router_both = lax.psum_scatter(grad_router_part, "row", scatter_dimension=1, tiled=True)
    router_rows = lax.dynamic_slice_in_dim(router_full, col_id * share, share, 0)
    back = mm_nt(jnp.concatenate(parts, axis=1), jnp.concatenate([router_rows] * 3, axis=1))
    dscaled_sum = after(
        lax.psum_scatter(dscaled_part, "col", scatter_dimension=1, tiled=True),
        (moe_part,),
        hop(went, last - 1, 0),
        hop(went, last - 2, 1),
        hop(went, last - 3, 2),
        hop(went, last - 1, 1),
        hop(went, last, 0),
    )
    dscaled = back + dscaled_sum.astype(f32)
    cot_share = grad_output.astype(f32)
    dstream = cot_share + gain_b * dscaled - stream * (scale_b * scale_b * inner[:, None] / width)
    gain_b_grad = jnp.sum(dscaled * stream, axis=0)

    dattn = lax.all_gather(dstream.astype(bf16), "col", axis=1, tiled=True)
    dattn = after(dattn, hop(went, last - 2, 2), hop(went, last - 1, 2), hop(went, last, 1))
    moe_share = lax.psum_scatter(
        after(moe_part, (dattn,)), "col", scatter_dimension=1, tiled=True
    ).astype(f32)
    block_output = (stream + moe_share).astype(bf16)
    out_grad, _ = reduce_rows(mm_tn(dattn, context).astype(bf16))
    dcontext = mm(dattn, out_full).astype(bf16)
    dqkv, inner_a = attend_backward(qkv, dcontext, lse, lengths, cosine, sine)
    inner_a = lax.psum(inner_a[:, 0], "col")[:, None]
    qkv_grad, _ = reduce_rows(mm_tn(normed_a, dqkv).astype(bf16))
    dnormed_sum = lax.psum_scatter(
        mm_nt(dqkv, qkv_full).astype(bf16), "col", scatter_dimension=1, tiled=True
    )
    dnormed_a = after(dnormed_sum, (inner_a,), hop(went, last, 2)).astype(f32)
    gain_a_share = input_gain.astype(f32)
    dinput = dstream + scale_a * gain_a_share * dnormed_a
    dinput = dinput - x_share * (scale_a * scale_a * inner_a / width)
    gain_a_grad = jnp.sum(dnormed_a * x_share * scale_a, axis=0)
    grad_gain_a, grad_gain_b = lax.psum((gain_a_grad, gain_b_grad), "row")

    qkv_grad = qkv_grad.reshape(rows_block, heads, 3, HEAD_DIM)
    grad_query, grad_key, grad_value = (
        qkv_grad[:, :, part].reshape(rows_block, head_width) for part in range(3)
    )
    def unpack(kind, which):
        found = []
        for (of, a, b), grad in zip(chunks, unit_grads):
            if of == kind:
                size = grad.shape[1] // 3
                part = grad[:, which * size : which * size + b - a]
                found.append((a, part.T if which == 2 else part))
        found = [part for _, part in sorted(found, key=lambda item: item[0])]
        return jnp.concatenate(found, axis=0 if which == 2 else 1)

    locals_ = range(local_experts)
    return (
        block_output,
        dinput.astype(bf16),
        grad_gain_a,
        grad_query,
        grad_key,
        grad_value,
        out_grad.T,
        grad_gain_b,
        grad_router_both[:experts].T,
        grad_router_both[experts],
        unpack(None, 0),
        unpack(None, 1),
        unpack(None, 2),
        jnp.stack([unpack(local, 0) for local in locals_]),
        jnp.stack([unpack(local, 1) for local in locals_]),
        jnp.stack([unpack(local, 2) for local in locals_]),
    )


def solution(mesh):
    return jax.shard_map(
        per_device,
        mesh=mesh,
        in_specs=(
            P("row", "col"),
            P(),
            P(),
            P("row", None),
            P("col"),
            P("row", "col"),
            P("row", "col"),
            P("row", "col"),
            P("col", "row"),
            P("col"),
            P("row", None),
            P("row"),
            P("row", "col"),
            P("row", "col"),
            P("col", "row"),
            P("col", "row", None),
            P("col", "row", None),
            P("col", None, "row"),
            P("row", "col"),
        ),
        out_specs=(
            P("row", "col"),
            P("row", "col"),
            P("col"),
            P("row", "col"),
            P("row", "col"),
            P("row", "col"),
            P("col", "row"),
            P("col"),
            P("row", None),
            P("row"),
            P("row", "col"),
            P("row", "col"),
            P("col", "row"),
            P("col", "row", None),
            P("col", "row", None),
            P("col", None, "row"),
        ),
        check_vma=False,
    )
```

```python
import functools
import math

import jax
import jax.numpy as jnp
from jax import lax
from jax.experimental import pallas as pl
from jax.experimental.pallas import tpu as pltpu
from jax.sharding import PartitionSpec as P

HEAD_DIM = 128
SEQ_LEN = 1024
QBLOCK = 256
TILE = 256
norm_eps = 1e-06
rope_base = 1000000.0
bf16 = jnp.bfloat16
f32 = jnp.float32


def mm(left, right):
    return jnp.dot(left, right, preferred_element_type=f32)


def mm_nt(left, right):
    return lax.dot_general(left, right, (((1,), (1,)), ((), ())), preferred_element_type=f32)


def mm_tn(left, right):
    return lax.dot_general(left, right, (((0,), (0,)), ((), ())), preferred_element_type=f32)


def rope_tables():
    positions = jnp.arange(SEQ_LEN).astype(f32)
    freqs = jnp.power(f32(rope_base), -jnp.arange(0, HEAD_DIM, 2).astype(f32) / HEAD_DIM)
    angles = positions[:, None] * freqs[None, :]
    cosine, sine = jnp.cos(angles), jnp.sin(angles)
    return (
        jnp.concatenate([cosine, cosine], axis=-1),
        jnp.concatenate([-sine, sine], axis=-1),
    )


def block_scores(rows, keys, start, length, scale):
    raw = mm_nt(rows, keys) * scale
    query_pos = start + lax.broadcasted_iota(jnp.int32, raw.shape, 0)
    key_pos = lax.broadcasted_iota(jnp.int32, raw.shape, 1)
    return jnp.where((key_pos <= query_pos) & (key_pos < length), raw, -1e30)


def attend_forward_kernel(length_ref, raw_ref, cos_ref, sin_ref, qkv_ref, context_ref, lse_ref):
    length = length_ref[pl.program_id(0)]
    scale = 1.0 / math.sqrt(HEAD_DIM)
    hd = HEAD_DIM
    for part in range(2):
        raw = raw_ref[:, part * hd : (part + 1) * hd]
        turned = raw * cos_ref[...] + pltpu.roll(raw, hd // 2, 1) * sin_ref[...]
        qkv_ref[:, part * hd : (part + 1) * hd] = turned.astype(bf16)
    qkv_ref[:, 2 * hd :] = raw_ref[:, 2 * hd :].astype(bf16)
    for at in range(0, SEQ_LEN, QBLOCK):
        seen = at + QBLOCK
        scores = block_scores(
            qkv_ref[at:seen, :hd], qkv_ref[:seen, hd : 2 * hd], at, length, scale
        )
        top = jnp.max(scores, axis=-1, keepdims=True)
        expo = jnp.exp(scores - top)
        total = jnp.sum(expo, axis=-1, keepdims=True)
        probs = (expo / total).astype(bf16)
        context_ref[at:seen, :] = mm(probs, qkv_ref[:seen, 2 * hd :]).astype(bf16)
        lse_ref[at:seen, :] = jnp.broadcast_to(top + jnp.log(total), (QBLOCK, hd))


def attend_forward(raw, lengths, cosine, sine):
    tokens, width = raw.shape
    heads = width // (3 * HEAD_DIM)
    slots = tokens // SEQ_LEN
    wide = pl.BlockSpec((SEQ_LEN, 3 * HEAD_DIM), lambda s, h, _: (s, h))
    one = pl.BlockSpec((SEQ_LEN, HEAD_DIM), lambda s, h, _: (s, h))
    table = pl.BlockSpec((SEQ_LEN, HEAD_DIM), lambda s, h, _: (0, 0))
    pairs = slots * heads * SEQ_LEN * SEQ_LEN
    return pl.pallas_call(
        attend_forward_kernel,
        grid_spec=pltpu.PrefetchScalarGridSpec(
            num_scalar_prefetch=1,
            grid=(slots, heads),
            in_specs=[wide, table, table],
            out_specs=[wide, one, one],
        ),
        out_shape=[
            jax.ShapeDtypeStruct((tokens, width), bf16),
            jax.ShapeDtypeStruct((tokens, heads * HEAD_DIM), bf16),
            jax.ShapeDtypeStruct((tokens, heads * HEAD_DIM), f32),
        ],
        cost_estimate=pl.CostEstimate(
            flops=3 * HEAD_DIM * pairs, bytes_accessed=8 * tokens * width, transcendentals=pairs
        ),
        name="attend_forward",
    )(lengths, raw, cosine, sine)


def attend_backward_kernel(
    length_ref, qkv_ref, dcontext_ref, lse_ref, cos_ref, sin_ref, dqkv_ref, inner_ref, dk_ref, dv_ref
):
    length = length_ref[pl.program_id(0)]
    scale = 1.0 / math.sqrt(HEAD_DIM)
    hd = HEAD_DIM
    @pl.when(pl.program_id(1) == 0)
    def _():
        inner_ref[...] = jnp.zeros_like(inner_ref)

    dk_ref[...] = jnp.zeros_like(dk_ref)
    dv_ref[...] = jnp.zeros_like(dv_ref)

    def turn_back(grad, rows):
        back = grad * cos_ref[rows, :] - pltpu.roll(grad, hd // 2, 1) * sin_ref[rows, :]
        return back.astype(bf16)

    for at in range(0, SEQ_LEN, QBLOCK):
        seen = at + QBLOCK
        rows = qkv_ref[at:seen, :hd]
        keys = qkv_ref[:seen, hd : 2 * hd]
        drows = dcontext_ref[at:seen, :]
        scores = block_scores(rows, keys, at, length, scale)
        probs = jnp.exp(scores - lse_ref[at:seen, :1])
        dv_ref[:seen, :] += mm_tn(probs.astype(bf16), drows)
        dprobs = mm_nt(drows, qkv_ref[:seen, 2 * hd :])
        dscore = probs * (dprobs - jnp.sum(dprobs * probs, axis=-1, keepdims=True))
        draw = (dscore * scale).astype(bf16)
        dquery = mm(draw, keys)
        dk_ref[:seen, :] += mm_tn(draw, rows)
        dqkv_ref[at:seen, :hd] = turn_back(dquery, slice(at, seen))
        inner_ref[at:seen, :] += jnp.sum(dquery * rows.astype(f32), axis=-1, keepdims=True)
    dkey, dvalue = dk_ref[...], dv_ref[...]
    dqkv_ref[:, hd : 2 * hd] = turn_back(dkey, slice(None))
    dqkv_ref[:, 2 * hd :] = dvalue.astype(bf16)
    inner_ref[...] += jnp.sum(
        dkey * qkv_ref[:, hd : 2 * hd].astype(f32) + dvalue * qkv_ref[:, 2 * hd :].astype(f32),
        axis=-1,
        keepdims=True,
    )


def attend_backward(qkv, dcontext, lse, lengths, cosine, sine):
    tokens, width = qkv.shape
    heads = width // (3 * HEAD_DIM)
    slots = tokens // SEQ_LEN
    wide = pl.BlockSpec((SEQ_LEN, 3 * HEAD_DIM), lambda s, h, _: (s, h))
    one = pl.BlockSpec((SEQ_LEN, HEAD_DIM), lambda s, h, _: (s, h))
    table = pl.BlockSpec((SEQ_LEN, HEAD_DIM), lambda s, h, _: (0, 0))
    pairs = slots * heads * SEQ_LEN * SEQ_LEN
    return pl.pallas_call(
        attend_backward_kernel,
        grid_spec=pltpu.PrefetchScalarGridSpec(
            num_scalar_prefetch=1,
            grid=(slots, heads),
            in_specs=[wide, one, one, table, table],
            out_specs=[wide, pl.BlockSpec((SEQ_LEN, 1), lambda s, h, _: (s, 0))],
            scratch_shapes=[pltpu.VMEM((SEQ_LEN, HEAD_DIM), f32)] * 2,
        ),
        out_shape=[
            jax.ShapeDtypeStruct((tokens, width), bf16),
            jax.ShapeDtypeStruct((tokens, 1), f32),
        ],
        cost_estimate=pl.CostEstimate(
            flops=8 * HEAD_DIM * pairs, bytes_accessed=8 * tokens * width, transcendentals=pairs
        ),
        name="attend_backward",
    )(lengths, qkv, dcontext, lse, cosine, sine)


def gather_rows(part):
    n = lax.axis_size("row")
    if n != 4:
        return (lax.all_gather(part, "row", axis=0, tiled=True),), ((), (), ())
    partner = lax.ppermute(part, "row", [(0, 1), (1, 0), (2, 3), (3, 2)])
    middle, outward = [(1, 2), (2, 1)], [(1, 0), (2, 3)]
    near_mid = lax.ppermute(part, "row", middle)
    far_mid = lax.ppermute(partner, "row", middle)
    near_out = lax.ppermute(near_mid, "row", outward)
    far_out = lax.ppermute(far_mid, "row", outward)
    hops = ((partner, near_mid), (far_mid, near_out), (far_out,))
    return (part, partner, near_mid, far_mid, near_out, far_out), hops


def places(z):
    pair = z // 2
    return z, z + 1 - 2 * lax.rem(z, 2), 2 - pair, 3 - 3 * pair


def gather_kernel(count, *refs):
    packs, wholes, (send_sems, recv_sems) = refs[:count], refs[count : 2 * count], refs[2 * count :]
    z = lax.axis_index("row")
    own, partner, near, far = places(z)
    across = 3 - z
    in_middle = (z == 1) | (z == 2)
    barrier = pltpu.get_barrier_semaphore()

    def copy_of(kind, at, source, block, target):
        return pltpu.make_async_remote_copy(
            src_ref=source,
            dst_ref=wholes[at].at[block],
            send_sem=send_sems.at[kind, at],
            recv_sem=recv_sems.at[kind, at],
            device_id={"row": target},
            device_id_type=pl.DeviceIdType.MESH,
        )

    def swap(at):
        return copy_of(0, at, packs[at], own, partner)

    def swap_middle(at):
        return copy_of(1, at, packs[at], own, across)

    def second_middle(at):
        return copy_of(2, at, wholes[at].at[partner], partner, across)

    def hand_near(at):
        return copy_of(3, at, wholes[at].at[near], near, partner)

    def hand_far(at):
        return copy_of(4, at, wholes[at].at[far], far, partner)

    pl.semaphore_signal(barrier, inc=1, device_id={"row": partner}, device_id_type=pl.DeviceIdType.MESH)

    @pl.when(in_middle)
    def _():
        pl.semaphore_signal(
            barrier, inc=1, device_id={"row": across}, device_id_type=pl.DeviceIdType.MESH
        )
        pl.semaphore_wait(barrier, 2)
        for at in range(count):
            swap_middle(at).start()
            swap(at).start()
        for at in range(count):
            swap_middle(at).wait_recv()
            hand_near(at).start()
            swap(at).wait_recv()
            second_middle(at).start()
        for at in range(count):
            second_middle(at).wait_recv()
            hand_far(at).start()
        for at in range(count):
            for copy in (swap, swap_middle, second_middle, hand_near, hand_far):
                copy(at).wait_send()

    @pl.when(jnp.logical_not(in_middle))
    def _():
        pl.semaphore_wait(barrier, 1)
        for at in range(count):
            swap(at).start()
        for at in range(count):
            swap(at).wait()
            hand_near(at).wait_recv()
            hand_far(at).wait_recv()


def gather_now(packs, number):
    if lax.axis_size("row") != 4:
        return [lax.all_gather(pack, "row", axis=0, tiled=True) for pack in packs]
    count = len(packs)
    sent = sum(pack.size for pack in packs) * 2
    anywhere = pl.BlockSpec(memory_space=pl.ANY)
    wholes = pl.pallas_call(
        functools.partial(gather_kernel, count),
        in_specs=[anywhere] * count,
        out_specs=[anywhere] * count,
        out_shape=[jax.ShapeDtypeStruct((4,) + pack.shape, pack.dtype) for pack in packs],
        scratch_shapes=[pltpu.SemaphoreType.DMA((5, count)), pltpu.SemaphoreType.DMA((5, count))],
        compiler_params=pltpu.CompilerParams(collective_id=number, has_side_effects=True),
        cost_estimate=pl.CostEstimate(
            flops=6 * 9000 * sent, bytes_accessed=6 * sent, transcendentals=0
        ),
        name="gather_rows",
    )(*packs)
    return [whole.reshape((4 * whole.shape[1],) + whole.shape[2:]) for whole in wholes]


def put_own(whole, part):
    if lax.axis_size("row") != 4:
        return whole
    return lax.dynamic_update_slice_in_dim(
        whole, part, lax.axis_index("row") * part.shape[0], 0
    )


def join_rows(pieces):
    if len(pieces) == 1:
        return pieces[0]
    part = pieces[0]
    z = lax.axis_index("row")
    whole = jnp.zeros((4,) + part.shape, part.dtype)
    blocks = (part, pieces[1], pieces[2] + pieces[4], pieces[3] + pieces[5])
    for at, piece in zip(places(z), blocks):
        whole = lax.dynamic_update_slice_in_dim(whole, piece[None], at, 0)
    return whole.reshape((4 * part.shape[0],) + part.shape[1:])


def reduce_rows(grads):
    n = lax.axis_size("row")
    if n != 4:
        total = lax.psum_scatter(grads, "row", scatter_dimension=0, tiled=True)
        return total.astype(f32), ((), (), ())
    own, partner, near, far = places(lax.axis_index("row"))
    size = grads.shape[0] // n
    inward, middle = [(0, 1), (3, 2)], [(1, 2), (2, 1)]

    def block(at, *others):
        piece = lax.dynamic_slice_in_dim(grads, at * size, size, 0)
        if others:
            piece = piece.astype(f32)
            for other in others:
                piece = piece + other.astype(f32)
        return piece

    far_in = lax.ppermute(block(far), "row", inward)
    near_in = lax.ppermute(block(near), "row", inward)
    far_sum = lax.ppermute(block(far, far_in).astype(bf16), "row", middle)
    near_sum = lax.ppermute(block(near, near_in).astype(bf16), "row", middle)
    exchanged = lax.ppermute(
        block(partner, far_sum).astype(bf16), "row", [(0, 1), (1, 0), (2, 3), (3, 2)]
    )
    hops = ((far_in, near_in), (far_sum, near_sum), (exchanged,))
    return block(own, near_sum, exchanged), hops


def after(value, *groups):
    others = tuple(item for group in groups for item in group)
    return lax.optimization_barrier((value,) + others)[0] if others else value


def expert_kernel(size, steps, count, z_ref, *refs):
    pieces = refs[:count]
    (x_ref, cot_ref, x_cols, cot_cols, coef_ref) = refs[count : count + 5]
    (dpair_ref, hidden_ref, sums_ref, grads_ref, whole_ref) = refs[count + 5 : count + 10]
    weights, dpair, hidden, sems, out_sem = refs[count + 10 :]
    step = pl.program_id(0)
    write = pltpu.make_async_copy(weights, whole_ref, out_sem)

    @pl.when(step == 0)
    def _():
        if count == 1:
            copy = pltpu.make_async_copy(pieces[0], weights, sems.at[0])
            copy.start()
            copy.wait()
        elif count == 2:
            block = pieces[0].shape[0]

            def block_copy(back):
                at = pl.multiple_of(lax.rem(z_ref[0] + back, 4) * block, block)
                source = pieces[1].at[pl.ds(at, block)] if back else pieces[0]
                return pltpu.make_async_copy(source, weights.at[pl.ds(at, block)], sems.at[back])

            for back in range(4):
                block_copy(back).start()
            for back in range(4):
                block_copy(back).wait()
        else:
            z = z_ref[0]
            block = pieces[0].shape[0]

            def copy_of(piece, which):
                at = pl.multiple_of(places(z)[which] * block, block)
                return pltpu.make_async_copy(
                    piece, weights.at[pl.ds(at, block)], sems.at[which]
                )

            copy_of(pieces[0], 0).start()
            copy_of(pieces[1], 1).start()
            in_middle = (z == 1) | (z == 2)

            @pl.when(in_middle)
            def _():
                copy_of(pieces[2], 2).start()
                copy_of(pieces[3], 3).start()

            @pl.when(jnp.logical_not(in_middle))
            def _():
                copy_of(pieces[4], 2).start()
                copy_of(pieces[5], 3).start()

            for which in range(4):
                copy_of(pieces[which], which).wait()
        write.start()

    @pl.when(step < steps)
    def _():
        at = pl.multiple_of(step * TILE, TILE)
        rows, cots = x_ref[...], cot_ref[...]
        scale, weight = coef_ref[:, 0:1], coef_ref[:, 1:2]
        dots = jnp.zeros((TILE, 1), f32)
        inner = jnp.zeros((TILE, 1), f32)
        for a in range(0, size, TILE):
            b = min(a + TILE, size)
            gate = scale * mm(rows, weights[:, a:b])
            up = scale * mm(rows, weights[:, size + a : size + b])
            dhid = mm(cots, weights[:, 2 * size + a : 2 * size + b])
            sigma = jax.nn.sigmoid(gate)
            silu = gate * sigma
            hid = silu * up
            dots += jnp.sum(hid * dhid, axis=1, keepdims=True)
            dhid = weight * dhid
            dgate = dhid * up * sigma * (1.0 + gate * (1.0 - sigma))
            dup = dhid * silu
            inner += jnp.sum(dgate * gate + dup * up, axis=1, keepdims=True)
            for into, at_col, value in (
                ((hidden_ref, hidden), a, weight * hid),
                ((dpair_ref, dpair), a, scale * dgate),
                ((dpair_ref, dpair), size + a, scale * dup),
            ):
                value = value.astype(bf16)
                into[0][:, at_col : at_col + b - a] = value
                into[1][pl.ds(at, TILE), at_col : at_col + b - a] = value
        sums_ref[:, 0:1] = dots
        sums_ref[:, 1:2] = inner

    @pl.when(step >= steps)
    def _():
        for a in range(0, 2 * size, TILE):
            b = min(a + TILE, 2 * size)
            grads_ref[:, a:b] = mm_tn(x_cols[...], dpair[:, a:b]).astype(bf16)
        for a in range(0, size, TILE):
            b = min(a + TILE, size)
            grads_ref[:, 2 * size + a : 2 * size + b] = mm_tn(
                cot_cols[...], hidden[:, a:b]
            ).astype(bf16)

    @pl.when(step == pl.num_programs(0) - 1)
    def _():
        write.wait()


def expert_chunk(pieces, scaled, cots, coef):
    tokens, width = scaled.shape
    size = pieces[0].shape[1] // 3
    steps, more = tokens // TILE, width // TILE
    count = len(pieces)
    rows = lambda i, _: (jnp.minimum(i, steps - 1), 0)
    cols = lambda i, _: (0, jnp.maximum(i - steps, 0))
    down = lambda i, _: (jnp.maximum(i - steps, 0), 0)
    z = jnp.reshape(lax.axis_index("row"), (1,)).astype(jnp.int32)
    return pl.pallas_call(
        functools.partial(expert_kernel, size, steps, count),
        grid_spec=pltpu.PrefetchScalarGridSpec(
            num_scalar_prefetch=1,
            grid=(steps + more,),
            in_specs=[pl.BlockSpec(memory_space=pl.ANY)] * count
            + [
                pl.BlockSpec((TILE, width), rows),
                pl.BlockSpec((TILE, width), rows),
                pl.BlockSpec((tokens, TILE), cols),
                pl.BlockSpec((tokens, TILE), cols),
                pl.BlockSpec((TILE, 2), rows),
            ],
            out_specs=[
                pl.BlockSpec((TILE, 2 * size), rows),
                pl.BlockSpec((TILE, size), rows),
                pl.BlockSpec((TILE, 2), rows),
                pl.BlockSpec((TILE, 3 * size), down),
                pl.BlockSpec(memory_space=pl.ANY),
            ],
            scratch_shapes=[
                pltpu.VMEM((width, 3 * size), bf16),
                pltpu.VMEM((tokens, 2 * size), bf16),
                pltpu.VMEM((tokens, size), bf16),
                pltpu.SemaphoreType.DMA((4,)),
                pltpu.SemaphoreType.DMA,
            ],
        ),
        out_shape=[
            jax.ShapeDtypeStruct((tokens, 2 * size), bf16),
            jax.ShapeDtypeStruct((tokens, size), bf16),
            jax.ShapeDtypeStruct((tokens, 2), f32),
            jax.ShapeDtypeStruct((width, 3 * size), bf16),
            jax.ShapeDtypeStruct((width, 3 * size), bf16),
        ],
        cost_estimate=pl.CostEstimate(
            flops=12 * tokens * width * size,
            bytes_accessed=8 * tokens * width + 24 * width * size,
            transcendentals=tokens * size,
        ),
        name="expert_chunk",
    )(z, *pieces, scaled, cots, scaled, cots, coef)


def joint_kernel(count, based, *refs):
    out_ref = refs[-1]
    for a in range(0, out_ref.shape[1], TILE):
        total = refs[2 * count][:, a : a + TILE] if based else None
        for left, weights in zip(refs[:count], refs[count : 2 * count]):
            part = mm_nt(left[...], weights[a : a + TILE, :])
            total = part if total is None else total + part
        out_ref[:, a : a + TILE] = total.astype(out_ref.dtype)


def joint_back(lefts, weights, column, kind, *base):
    tokens, width = lefts[0].shape[0], weights[0].shape[0]
    row = lambda i: (i, 0)
    fixed = lambda i: (0, column)
    depth = sum(left.shape[1] for left in lefts)
    return pl.pallas_call(
        functools.partial(joint_kernel, len(lefts), len(base) > 0),
        grid=(tokens // TILE,),
        in_specs=[pl.BlockSpec((TILE, left.shape[1]), row) for left in lefts]
        + [
            pl.BlockSpec((width, left.shape[1]), fixed, pipeline_mode=pl.Buffered(1))
            for left in lefts
        ]
        + [pl.BlockSpec((TILE, width), row)] * len(base),
        out_specs=pl.BlockSpec((TILE, width), row),
        out_shape=jax.ShapeDtypeStruct((tokens, width), kind),
        cost_estimate=pl.CostEstimate(
            flops=2 * tokens * width * depth,
            bytes_accessed=2 * (tokens + width) * depth + 4 * tokens * width,
            transcendentals=0,
        ),
        name="joint_back",
    )(*lefts, *weights, *base)


def split_three(values):
    high = values.astype(bf16)
    rest = values - high.astype(f32)
    middle = rest.astype(bf16)
    return high, middle, (rest - middle.astype(f32)).astype(bf16)


def cuts_of(width, sizes):
    cuts, at = [], 0
    for size in sizes:
        if at + size < width:
            cuts.append((at, at + size))
            at += size
    return cuts + [(at, width)]


def per_device(
    block_input,
    seq_lengths,
    slot_order,
    routes,
    input_gain,
    query_weight,
    key_weight,
    value_weight,
    output_weight,
    mlp_gain,
    router_weight,
    score_shared,
    gate_shared,
    up_shared,
    down_shared,
    gate_expert,
    up_expert,
    down_expert,
    grad_output,
):
    tokens, share = block_input.shape
    cols = lax.axis_size("col")
    col_id = lax.axis_index("col")
    row_id = lax.axis_index("row")
    width = share * cols
    slots = tokens // SEQ_LEN
    local_experts = gate_expert.shape[0]
    experts = router_weight.shape[1]
    head_width = query_weight.shape[1]
    heads = head_width // HEAD_DIM
    rows_block = query_weight.shape[0]
    lengths = lax.dynamic_slice_in_dim(seq_lengths[slot_order], row_id * slots, slots, 0)
    cosine, sine = rope_tables()

    def by_head(weight):
        return weight.reshape(rows_block, heads, 1, HEAD_DIM)

    qkv_pack = jnp.concatenate(
        [by_head(query_weight), by_head(key_weight), by_head(value_weight)], axis=2
    ).reshape(rows_block, 3 * head_width)
    router_pack = jnp.concatenate([router_weight, score_shared[:, None]], axis=1)
    router_pack = jnp.pad(router_pack, ((0, 0), (0, -router_pack.shape[1] % 128)))
    out_pack = jnp.concatenate([output_weight.T, router_pack], axis=1)
    qkv_whole, out_whole = gather_now([qkv_pack, out_pack], 0)
    qkv_full, out_weights = put_own(qkv_whole, qkv_pack), put_own(out_whole, out_pack)
    out_full = out_weights[:, :head_width]
    router_full = out_weights[:, head_width : head_width + experts + 1]
    shared_cuts = [(None, a, b) for a, b in cuts_of(gate_shared.shape[1], (512,))]
    expert_cuts = [
        (local, a, b)
        for local in range(local_experts)
        for a, b in cuts_of(gate_expert.shape[2], (384, 256, 384))
    ]
    chunks = shared_cuts[-1:] + expert_cuts[:2] + shared_cuts[:-1] + expert_cuts[2:]

    def pack(kind, a, b):
        if kind is None:
            parts = [gate_shared[:, a:b], up_shared[:, a:b], down_shared[a:b].T]
        else:
            parts = [gate_expert[kind, :, a:b], up_expert[kind, :, a:b], down_expert[kind, a:b].T]
        fill = -(b - a) % 128
        return jnp.concatenate([jnp.pad(part, ((0, 0), (0, fill))) for part in parts], axis=1)

    packs = [pack(*chunk) for chunk in chunks]
    chained = lax.axis_size("row") == 4
    gathered, came = {}, {}
    early = 3 if chained else len(chunks)
    for at in range(early):
        if not (chained and at in (1, 2)):
            gathered[at], came[at] = gather_rows(packs[at])

    def hop(arrivals, at, which):
        return arrivals[at][which] if 0 <= at < len(chunks) and at in arrivals else ()

    rows_in = lax.all_gather(block_input, "col", axis=1, tiled=True)
    gains = lax.all_gather(jnp.stack([input_gain, mlp_gain]), "col", axis=1, tiled=True).astype(f32)
    cot_rows = lax.all_gather(grad_output, "col", axis=1, tiled=True)
    rows_f = rows_in.astype(f32)
    scale_a = lax.rsqrt(jnp.mean(rows_f * rows_f, axis=-1, keepdims=True) + norm_eps)
    normed_a = (rows_f * scale_a * gains[0]).astype(bf16)
    raw = after(mm(normed_a, qkv_full), hop(came, 0, 0))
    qkv, context, lse = attend_forward(raw, lengths, cosine, sine)
    attn_part = after(mm_nt(context, out_full).astype(bf16), (cot_rows,), hop(came, 0, 1))
    x_share = block_input.astype(f32)
    attn_sum = lax.psum_scatter(attn_part, "col", scatter_dimension=1, tiled=True)
    wait_for = ()
    if chained:
        wait_for = gather_now([after(packs[1], (attn_part,))], 1)
        gathered[1] = (packs[1], wait_for[0])
    attn_sum = after(attn_sum, wait_for, hop(came, 0, 2))
    stream = x_share + attn_sum.astype(f32)
    gain_b = mlp_gain.astype(f32)
    scaled_share = (stream * gain_b).astype(bf16)
    scaled = lax.all_gather(scaled_share, "col", axis=1, tiled=True)
    wait_for = ()
    if chained:
        wait_for = gather_now([after(packs[2], (scaled_share,))], 2)
        gathered[2] = (packs[2], wait_for[0])
    for at in range(early, len(chunks)):
        gathered[at], came[at] = gather_rows(after(packs[at], wait_for))
    scaled = after(scaled, wait_for)
    stream_f = scaled.astype(f32) / gains[1]
    scale_b = lax.rsqrt(jnp.mean(stream_f * stream_f, axis=1, keepdims=True) + norm_eps)

    both_logits = scale_b * mm(scaled, router_full)
    logits, slogit = both_logits[:, :experts], both_logits[:, experts]
    top = jnp.max(logits, axis=-1, keepdims=True)
    expo = jnp.exp(logits - top)
    router_probs = expo / jnp.sum(expo, axis=-1, keepdims=True)
    shared_gate = jax.nn.sigmoid(slogit)

    inner = jnp.zeros((tokens,), f32)
    dots = {}
    members, shares = {None: None}, {None: shared_gate}
    for local in range(local_experts):
        expert = col_id * local_experts + local
        members[local] = jnp.any(routes == expert, axis=1)
        column = lax.dynamic_index_in_dim(router_probs, expert, 1, False)
        shares[local] = jnp.where(members[local], column, 0.0)
    dpairs, hiddens, wholes, unit_grads, went = [], [], [], [], {}
    last = len(chunks) - 1
    for at, (kind, a, b) in enumerate(chunks):
        pieces = gathered[at]
        coef = jnp.concatenate([scale_b, shares[kind][:, None]], axis=1)
        if at == 1:
            coef = after(coef, hop(came, 3, 0))
        elif at == 2:
            coef = after(coef, hop(came, 3, 1), hop(came, 4, 0), hop(went, 0, 0))
        elif at > 2:
            coef = after(
                coef,
                hop(came, at + 1, 0),
                hop(came, at + 1, 1),
                hop(went, at - 2, 0),
                hop(went, at - 3, 1),
                hop(went, at - 4, 2),
            )
        if at == last:
            dscaled_early = joint_back(dpairs, wholes, 0, f32)
            coef = after(coef, (dscaled_early,))
        dpair, hidden, sums, grads, whole = expert_chunk(pieces, scaled, cot_rows, coef)
        dots[kind] = dots.get(kind, 0.0) + sums[:, 0]
        inner = inner + sums[:, 1]
        dpairs.append(dpair)
        hiddens.append(hidden)
        wholes.append(whole)
        reduced, arrivals = reduce_rows(grads)
        unit_grads.append(reduced)
        went[at] = arrivals
    dscaled_part = joint_back([dpair], [whole], 0, bf16, dscaled_early)
    moe_part = joint_back(hiddens, wholes, 2, bf16)

    named = [jnp.where(members[local], dots[local], 0.0) for local in range(local_experts)]
    table = lax.all_gather(jnp.stack(named + [dots[None], inner]), "col", axis=0)
    dprob = table[:, :local_experts].reshape(experts, tokens).T
    dshared_gate, inner = jnp.sum(table[:, local_experts], axis=0), jnp.sum(table[:, local_experts + 1], axis=0)
    dlogits = router_probs * (dprob - jnp.sum(dprob * router_probs, axis=1, keepdims=True))
    dslogit = dshared_gate * shared_gate * (1.0 - shared_gate)
    dboth = jnp.concatenate([dlogits, dslogit[:, None]], axis=1)
    inner = inner + jnp.sum(dboth * both_logits, axis=1)
    dboth = scale_b * dboth
    parts = split_three(dboth)
    stacked = mm_tn(jnp.concatenate(parts, axis=1), scaled)
    grad_router_part = stacked.reshape(3, experts + 1, width).sum(axis=0)
    grad_router_both = lax.psum_scatter(grad_router_part, "row", scatter_dimension=1, tiled=True)
    router_rows = lax.dynamic_slice_in_dim(router_full, col_id * share, share, 0)
    back = mm_nt(jnp.concatenate(parts, axis=1), jnp.concatenate([router_rows] * 3, axis=1))
    dscaled_sum = after(
        lax.psum_scatter(dscaled_part, "col", scatter_dimension=1, tiled=True),
        (moe_part,),
        hop(went, last - 1, 0),
        hop(went, last - 2, 1),
        hop(went, last - 3, 2),
        hop(went, last - 1, 1),
        hop(went, last, 0),
    )
    dscaled = back + dscaled_sum.astype(f32)
    cot_share = grad_output.astype(f32)
    dstream = cot_share + gain_b * dscaled - stream * (scale_b * scale_b * inner[:, None] / width)
    gain_b_grad = jnp.sum(dscaled * stream, axis=0)

    dstream_low = dstream.astype(bf16)
    dattn = lax.all_gather(dstream_low, "col", axis=1, tiled=True)
    dattn = after(dattn, hop(went, last - 2, 2), hop(went, last - 1, 2), hop(went, last, 1))
    moe_share = lax.psum_scatter(
        after(moe_part, (dstream_low,)), "col", scatter_dimension=1, tiled=True
    ).astype(f32)
    block_output = (stream + moe_share).astype(bf16)
    out_grad, _ = reduce_rows(mm_tn(dattn, context).astype(bf16))
    dcontext = mm(dattn, out_full).astype(bf16)
    dqkv, inner_a = attend_backward(qkv, dcontext, lse, lengths, cosine, sine)
    inner_a = lax.psum(inner_a[:, 0], "col")[:, None]
    qkv_grad, _ = reduce_rows(mm_tn(normed_a, dqkv).astype(bf16))
    dnormed_part = after(mm_nt(dqkv, qkv_full).astype(bf16), (moe_share,))
    dnormed_sum = lax.psum_scatter(dnormed_part, "col", scatter_dimension=1, tiled=True)
    dnormed_a = after(dnormed_sum, (inner_a,), hop(went, last, 2)).astype(f32)
    gain_a_share = input_gain.astype(f32)
    dinput = dstream + scale_a * gain_a_share * dnormed_a
    dinput = dinput - x_share * (scale_a * scale_a * inner_a / width)
    gain_a_grad = jnp.sum(dnormed_a * x_share * scale_a, axis=0)
    grad_gain_a, grad_gain_b = lax.psum((gain_a_grad, gain_b_grad), "row")

    qkv_grad = qkv_grad.reshape(rows_block, heads, 3, HEAD_DIM)
    grad_query, grad_key, grad_value = (
        qkv_grad[:, :, part].reshape(rows_block, head_width) for part in range(3)
    )
    def unpack(kind, which):
        found = []
        for (of, a, b), grad in zip(chunks, unit_grads):
            if of == kind:
                size = grad.shape[1] // 3
                part = grad[:, which * size : which * size + b - a]
                found.append((a, part.T if which == 2 else part))
        found = [part for _, part in sorted(found, key=lambda item: item[0])]
        return jnp.concatenate(found, axis=0 if which == 2 else 1)

    locals_ = range(local_experts)
    return (
        block_output,
        dinput.astype(bf16),
        grad_gain_a,
        grad_query,
        grad_key,
        grad_value,
        out_grad.T,
        grad_gain_b,
        grad_router_both[:experts].T,
        grad_router_both[experts],
        unpack(None, 0),
        unpack(None, 1),
        unpack(None, 2),
        jnp.stack([unpack(local, 0) for local in locals_]),
        jnp.stack([unpack(local, 1) for local in locals_]),
        jnp.stack([unpack(local, 2) for local in locals_]),
    )


def solution(mesh):
    return jax.shard_map(
        per_device,
        mesh=mesh,
        in_specs=(
            P("row", "col"),
            P(),
            P(),
            P("row", None),
            P("col"),
            P("row", "col"),
            P("row", "col"),
            P("row", "col"),
            P("col", "row"),
            P("col"),
            P("row", None),
            P("row"),
            P("row", "col"),
            P("row", "col"),
            P("col", "row"),
            P("col", "row", None),
            P("col", "row", None),
            P("col", None, "row"),
            P("row", "col"),
        ),
        out_specs=(
            P("row", "col"),
            P("row", "col"),
            P("col"),
            P("row", "col"),
            P("row", "col"),
            P("row", "col"),
            P("col", "row"),
            P("col"),
            P("row", None),
            P("row"),
            P("row", "col"),
            P("row", "col"),
            P("col", "row"),
            P("col", "row", None),
            P("col", "row", None),
            P("col", None, "row"),
        ),
        check_vma=False,
    )
```

```python
import functools
import math

import jax
import jax.numpy as jnp
from jax import lax
from jax.experimental import pallas as pl
from jax.experimental.pallas import tpu as pltpu
from jax.sharding import PartitionSpec as P

HEAD_DIM = 128
SEQ_LEN = 1024
QBLOCK = 256
TILE = 256
norm_eps = 1e-06
rope_base = 1000000.0
bf16 = jnp.bfloat16
f32 = jnp.float32


def mm(left, right):
    return jnp.dot(left, right, preferred_element_type=f32)


def mm_nt(left, right):
    return lax.dot_general(left, right, (((1,), (1,)), ((), ())), preferred_element_type=f32)


def mm_tn(left, right):
    return lax.dot_general(left, right, (((0,), (0,)), ((), ())), preferred_element_type=f32)


def rope_tables():
    positions = jnp.arange(SEQ_LEN).astype(f32)
    freqs = jnp.power(f32(rope_base), -jnp.arange(0, HEAD_DIM, 2).astype(f32) / HEAD_DIM)
    angles = positions[:, None] * freqs[None, :]
    cosine, sine = jnp.cos(angles), jnp.sin(angles)
    return (
        jnp.concatenate([cosine, cosine], axis=-1),
        jnp.concatenate([-sine, sine], axis=-1),
    )


def block_scores(rows, keys, start, length, scale):
    raw = mm_nt(rows, keys) * scale
    query_pos = start + lax.broadcasted_iota(jnp.int32, raw.shape, 0)
    key_pos = lax.broadcasted_iota(jnp.int32, raw.shape, 1)
    return jnp.where((key_pos <= query_pos) & (key_pos < length), raw, -1e30)


def attend_forward_kernel(length_ref, raw_ref, cos_ref, sin_ref, qkv_ref, context_ref, lse_ref):
    length = length_ref[pl.program_id(0)]
    scale = 1.0 / math.sqrt(HEAD_DIM)
    hd = HEAD_DIM
    for part in range(2):
        raw = raw_ref[:, part * hd : (part + 1) * hd]
        turned = raw * cos_ref[...] + pltpu.roll(raw, hd // 2, 1) * sin_ref[...]
        qkv_ref[:, part * hd : (part + 1) * hd] = turned.astype(bf16)
    qkv_ref[:, 2 * hd :] = raw_ref[:, 2 * hd :].astype(bf16)
    for at in range(0, SEQ_LEN, QBLOCK):
        seen = at + QBLOCK
        scores = block_scores(
            qkv_ref[at:seen, :hd], qkv_ref[:seen, hd : 2 * hd], at, length, scale
        )
        top = jnp.max(scores, axis=-1, keepdims=True)
        expo = jnp.exp(scores - top)
        total = jnp.sum(expo, axis=-1, keepdims=True)
        probs = (expo / total).astype(bf16)
        context_ref[at:seen, :] = mm(probs, qkv_ref[:seen, 2 * hd :]).astype(bf16)
        lse_ref[at:seen, :] = jnp.broadcast_to(top + jnp.log(total), (QBLOCK, hd))


def attend_forward(raw, lengths, cosine, sine):
    tokens, width = raw.shape
    heads = width // (3 * HEAD_DIM)
    slots = tokens // SEQ_LEN
    wide = pl.BlockSpec((SEQ_LEN, 3 * HEAD_DIM), lambda s, h, _: (s, h))
    one = pl.BlockSpec((SEQ_LEN, HEAD_DIM), lambda s, h, _: (s, h))
    table = pl.BlockSpec((SEQ_LEN, HEAD_DIM), lambda s, h, _: (0, 0))
    pairs = slots * heads * SEQ_LEN * SEQ_LEN
    return pl.pallas_call(
        attend_forward_kernel,
        grid_spec=pltpu.PrefetchScalarGridSpec(
            num_scalar_prefetch=1,
            grid=(slots, heads),
            in_specs=[wide, table, table],
            out_specs=[wide, one, one],
        ),
        out_shape=[
            jax.ShapeDtypeStruct((tokens, width), bf16),
            jax.ShapeDtypeStruct((tokens, heads * HEAD_DIM), bf16),
            jax.ShapeDtypeStruct((tokens, heads * HEAD_DIM), f32),
        ],
        cost_estimate=pl.CostEstimate(
            flops=3 * HEAD_DIM * pairs, bytes_accessed=8 * tokens * width, transcendentals=pairs
        ),
        name="attend_forward",
    )(lengths, raw, cosine, sine)


def attend_backward_kernel(
    length_ref, qkv_ref, dcontext_ref, lse_ref, cos_ref, sin_ref, dqkv_ref, inner_ref, dk_ref, dv_ref
):
    length = length_ref[pl.program_id(0)]
    scale = 1.0 / math.sqrt(HEAD_DIM)
    hd = HEAD_DIM
    @pl.when(pl.program_id(1) == 0)
    def _():
        inner_ref[...] = jnp.zeros_like(inner_ref)

    dk_ref[...] = jnp.zeros_like(dk_ref)
    dv_ref[...] = jnp.zeros_like(dv_ref)

    def turn_back(grad, rows):
        back = grad * cos_ref[rows, :] - pltpu.roll(grad, hd // 2, 1) * sin_ref[rows, :]
        return back.astype(bf16)

    for at in range(0, SEQ_LEN, QBLOCK):
        seen = at + QBLOCK
        rows = qkv_ref[at:seen, :hd]
        keys = qkv_ref[:seen, hd : 2 * hd]
        drows = dcontext_ref[at:seen, :]
        scores = block_scores(rows, keys, at, length, scale)
        probs = jnp.exp(scores - lse_ref[at:seen, :1])
        dv_ref[:seen, :] += mm_tn(probs.astype(bf16), drows)
        dprobs = mm_nt(drows, qkv_ref[:seen, 2 * hd :])
        dscore = probs * (dprobs - jnp.sum(dprobs * probs, axis=-1, keepdims=True))
        draw = (dscore * scale).astype(bf16)
        dquery = mm(draw, keys)
        dk_ref[:seen, :] += mm_tn(draw, rows)
        dqkv_ref[at:seen, :hd] = turn_back(dquery, slice(at, seen))
        inner_ref[at:seen, :] += jnp.sum(dquery * rows.astype(f32), axis=-1, keepdims=True)
    dkey, dvalue = dk_ref[...], dv_ref[...]
    dqkv_ref[:, hd : 2 * hd] = turn_back(dkey, slice(None))
    dqkv_ref[:, 2 * hd :] = dvalue.astype(bf16)
    inner_ref[...] += jnp.sum(
        dkey * qkv_ref[:, hd : 2 * hd].astype(f32) + dvalue * qkv_ref[:, 2 * hd :].astype(f32),
        axis=-1,
        keepdims=True,
    )


def attend_backward(qkv, dcontext, lse, lengths, cosine, sine):
    tokens, width = qkv.shape
    heads = width // (3 * HEAD_DIM)
    slots = tokens // SEQ_LEN
    wide = pl.BlockSpec((SEQ_LEN, 3 * HEAD_DIM), lambda s, h, _: (s, h))
    one = pl.BlockSpec((SEQ_LEN, HEAD_DIM), lambda s, h, _: (s, h))
    table = pl.BlockSpec((SEQ_LEN, HEAD_DIM), lambda s, h, _: (0, 0))
    pairs = slots * heads * SEQ_LEN * SEQ_LEN
    return pl.pallas_call(
        attend_backward_kernel,
        grid_spec=pltpu.PrefetchScalarGridSpec(
            num_scalar_prefetch=1,
            grid=(slots, heads),
            in_specs=[wide, one, one, table, table],
            out_specs=[wide, pl.BlockSpec((SEQ_LEN, 1), lambda s, h, _: (s, 0))],
            scratch_shapes=[pltpu.VMEM((SEQ_LEN, HEAD_DIM), f32)] * 2,
        ),
        out_shape=[
            jax.ShapeDtypeStruct((tokens, width), bf16),
            jax.ShapeDtypeStruct((tokens, 1), f32),
        ],
        cost_estimate=pl.CostEstimate(
            flops=8 * HEAD_DIM * pairs, bytes_accessed=8 * tokens * width, transcendentals=pairs
        ),
        name="attend_backward",
    )(lengths, qkv, dcontext, lse, cosine, sine)


PAIRS = [(0, 1), (1, 0), (2, 3), (3, 2)]
MIDDLE = [(1, 2), (2, 1)]
OUTWARD = [(1, 0), (2, 3)]
INWARD = [(0, 1), (3, 2)]


class Gathered:
    def __init__(self, part, *groups):
        self.part = part
        if lax.axis_size("row") != 4:
            self.pieces = (lax.all_gather(part, "row", axis=0, tiled=True),)
            return
        part = after(part, *groups)
        self.partner = lax.ppermute(part, "row", PAIRS)
        self.near_mid = lax.ppermute(part, "row", MIDDLE)
        self.pieces = None

    def second(self, *groups):
        if self.pieces is None:
            self.near_out = lax.ppermute(after(self.near_mid, *groups), "row", OUTWARD)
            self.far_mid = lax.ppermute(after(self.partner, *groups), "row", MIDDLE)
            return (self.partner, self.near_mid)
        return ()

    def third(self, *groups):
        if self.pieces is None:
            self.far_out = lax.ppermute(after(self.far_mid, *groups), "row", OUTWARD)
            self.pieces = (
                self.part, self.partner, self.near_mid, self.far_mid, self.near_out, self.far_out
            )
            return (self.far_mid, self.near_out)
        return ()


def places(z):
    pair = z // 2
    return z, z + 1 - 2 * lax.rem(z, 2), 2 - pair, 3 - 3 * pair


class RowGather:
    def __init__(self, packs, wholes, sems):
        self.packs, self.wholes, (self.send_sems, self.recv_sems) = packs, wholes, sems
        self.z = lax.axis_index("row")
        self.own, self.partner, self.near, self.far = places(self.z)
        self.across = 3 - self.z
        self.in_middle = (self.z == 1) | (self.z == 2)
        self.outside = jnp.logical_not(self.in_middle)

    def copy_of(self, kind, at, source, block, target):
        return pltpu.make_async_remote_copy(
            src_ref=source,
            dst_ref=self.wholes[at].at[block],
            send_sem=self.send_sems.at[kind, at],
            recv_sem=self.recv_sems.at[kind, at],
            device_id={"row": target},
            device_id_type=pl.DeviceIdType.MESH,
        )

    def swap(self, at):
        return self.copy_of(0, at, self.packs[at], self.own, self.partner)

    def swap_middle(self, at):
        return self.copy_of(1, at, self.packs[at], self.own, self.across)

    def second_middle(self, at):
        return self.copy_of(2, at, self.wholes[at].at[self.partner], self.partner, self.across)

    def hand_near(self, at):
        return self.copy_of(3, at, self.wholes[at].at[self.near], self.near, self.partner)

    def hand_far(self, at):
        return self.copy_of(4, at, self.wholes[at].at[self.far], self.far, self.partner)

    def greet(self, barrier):
        signal_to(barrier, {"row": self.partner})

        @pl.when(self.in_middle)
        def _():
            signal_to(barrier, {"row": self.across})
            pl.semaphore_wait(barrier, 2)

        @pl.when(self.outside)
        def _():
            pl.semaphore_wait(barrier, 1)

    def begin(self):
        for at in range(len(self.packs)):
            @pl.when(self.in_middle)
            def _():
                self.swap_middle(at).start()

            self.swap(at).start()

    def hand_on(self, at):
        @pl.when(self.in_middle)
        def _():
            self.swap_middle(at).wait_recv()
            self.hand_near(at).start()
            self.swap(at).wait_recv()
            self.second_middle(at).start()

    def hand_last(self, at):
        @pl.when(self.in_middle)
        def _():
            self.second_middle(at).wait_recv()
            self.hand_far(at).start()

    def finish(self):
        for at in range(len(self.packs)):
            @pl.when(self.in_middle)
            def _():
                for copy in (
                    self.swap,
                    self.swap_middle,
                    self.second_middle,
                    self.hand_near,
                    self.hand_far,
                ):
                    copy(at).wait_send()

            @pl.when(self.outside)
            def _():
                self.swap(at).wait()
                self.hand_near(at).wait_recv()
                self.hand_far(at).wait_recv()


def signal_to(barrier, device):
    pl.semaphore_signal(barrier, inc=1, device_id=device, device_id_type=pl.DeviceIdType.MESH)


def gather_kernel(count, *refs):
    rows = RowGather(refs[:count], refs[count : 2 * count], refs[2 * count :])
    rows.greet(pltpu.get_barrier_semaphore())
    rows.begin()
    for at in range(count):
        rows.hand_on(at)
    for at in range(count):
        rows.hand_last(at)
    rows.finish()


PIECES = 4


def plane_kernel(pointwise, given, made, gather, count, *refs):
    p_ref, inputs = refs[0], refs[1 : 1 + given]
    at = 1 + given
    packs = refs[at : at + count]
    at += count
    results = refs[at : at + made]
    at += made
    whole_refs = refs[at : at + gather + count]
    at += gather + count
    mine, from_core, from_first, summed, from_second, shared, send_sems, recv_sems, local_sems = refs[
        at : at + 9
    ]
    out_ref = whole_refs[0] if gather else None
    me = lax.axis_index("col")
    core, x, y = lax.rem(me, 2), lax.rem(me // 2, 2), me // 4
    core_mate, x_mate, y_mate = me + 1 - 2 * core, me + 2 - 4 * x, me + 4 - 8 * y
    diagonal = x_mate + 4 - 8 * y
    size = mine.shape[3]
    share = mine.shape[4]
    barrier = pltpu.get_barrier_semaphore()
    for mate in (core_mate, x_mate, y_mate):
        signal_to(barrier, {"col": mate})
    rows = None
    if count:
        rows = RowGather(packs, whole_refs[gather:], refs[at + 9 : at + 11])
        signal_to(barrier, {"row": rows.partner})

        @pl.when(rows.in_middle)
        def _():
            signal_to(barrier, {"row": rows.across})
            pl.semaphore_wait(barrier, 5)

        @pl.when(rows.outside)
        def _():
            pl.semaphore_wait(barrier, 4)

        rows.begin()
    else:
        pl.semaphore_wait(barrier, 3)

    def remote(kind, i, source, target, mate):
        return pltpu.make_async_remote_copy(
            src_ref=source,
            dst_ref=target,
            send_sem=send_sems.at[kind, i],
            recv_sem=recv_sems.at[kind, i],
            device_id={"col": mate},
            device_id_type=pl.DeviceIdType.MESH,
        )

    def x_first(i):
        return i < PIECES // 2

    def span(i):
        return pl.ds(i * size, size)

    def core_copy(i):
        return remote(0, i, p_ref.at[:, :, 1 - core, span(i), :], from_core.at[i], core_mate)

    def load(i):
        return pltpu.make_async_copy(
            p_ref.at[:, :, core, span(i), :], mine.at[i], local_sems.at[0, i]
        )

    def first_copy(i):
        if x_first(i):
            return remote(1, i, mine.at[i, :, 1 - x], from_first.at[i], x_mate)
        return remote(1, i, mine.at[i, 1 - y], from_first.at[i], y_mate)

    def second_copy(i):
        if x_first(i):
            return remote(2, i, summed.at[i, 1 - y], from_second.at[i], y_mate)
        return remote(2, i, summed.at[i, 1 - x], from_second.at[i], x_mate)

    def columns(i, device):
        return out_ref.at[span(i), pl.ds(pl.multiple_of(device * share, share), share)]

    def spread(kind, i, mate):
        return remote(kind, i, shared.at[i], columns(i, me), mate)

    def keep(i):
        return pltpu.make_async_copy(shared.at[i], columns(i, me), local_sems.at[1, i])

    def pass_on(kind, i, device, mate):
        return remote(kind, i, columns(i, device), columns(i, device), mate)

    def forward(i):
        if x_first(i):
            return pass_on(6, i, y_mate, x_mate)
        return pass_on(6, i, x_mate, y_mate)

    order = [0, 2, 1, 3]
    for i in order:
        core_copy(i).start()
        load(i).start()
    for i in order:
        load(i).wait()
        core_copy(i).wait_recv()
        for a in range(2):
            for b in range(2):
                mine[i, a, b] = (mine[i, a, b].astype(f32) + from_core[i, a, b].astype(f32)).astype(bf16)
        first_copy(i).start()
    for i in order:
        first_copy(i).wait_recv()
        for a in range(2):
            kept = mine[i, a, x] if x_first(i) else mine[i, y, a]
            summed[i, a] = (kept.astype(f32) + from_first[i, a].astype(f32)).astype(bf16)
        second_copy(i).start()
    if count:
        for at in range(count):
            rows.hand_on(at)
    for i in order:
        second_copy(i).wait_recv()
        total = summed[i, y if x_first(i) else x].astype(f32) + from_second[i].astype(f32)
        span_rows = slice(i * size, (i + 1) * size)
        values = pointwise(
            total, *[ref[span_rows, :] if ref.shape[0] > 8 else ref[...] for ref in inputs]
        )
        if gather:
            shared[i] = values[0].astype(bf16)
            values = values[1:]
        for ref, value in zip(results, values):
            ref[span_rows, :] = value
        if gather:
            spread(4, i, x_mate).start()
            spread(5, i, y_mate).start()
            spread(3, i, core_mate).start()
            keep(i).start()
    if count:
        rows.hand_last(0)
    if gather:
        for i in order:
            spread(5 if x_first(i) else 4, i, y_mate).wait_recv()
            forward(i).start()
            pass_on(7, i, y_mate if x_first(i) else x_mate, core_mate).start()
        for i in order:
            spread(4 if x_first(i) else 5, i, x_mate).wait_recv()
            pass_on(8, i, x_mate if x_first(i) else y_mate, core_mate).start()
    if count:
        for at in range(1, count):
            rows.hand_last(at)
    if gather:
        for i in order:
            forward(i).wait_recv()
            pass_on(9, i, diagonal, core_mate).start()
    for i in order:
        core_copy(i).wait_send()
        first_copy(i).wait_send()
        second_copy(i).wait_send()
        if gather:
            keep(i).wait()
            spread(3, i, core_mate).wait()
            spread(4, i, x_mate).wait_send()
            spread(5, i, y_mate).wait_send()
            forward(i).wait_send()
            for kind, device in (
                (7, y_mate if x_first(i) else x_mate),
                (8, x_mate if x_first(i) else y_mate),
                (9, diagonal),
            ):
                pass_on(kind, i, device, core_mate).wait()
    if count:
        rows.finish()


def plane_step(partial, pointwise, inputs, made, gather, number, packs=()):
    tokens, share = partial.shape[3:]
    size = tokens // PIECES
    count = len(packs)
    anywhere = pl.BlockSpec(memory_space=pl.ANY)
    vmem = pl.BlockSpec(memory_space=pltpu.VMEM)
    whole_shapes = [jax.ShapeDtypeStruct((tokens, 8 * share), bf16)] * gather + [
        jax.ShapeDtypeStruct((4,) + pack.shape, bf16) for pack in packs
    ]
    outs = pl.pallas_call(
        functools.partial(plane_kernel, pointwise, len(inputs), made, gather, count),
        in_specs=[anywhere] + [vmem] * len(inputs) + [anywhere] * count,
        out_specs=[vmem] * made + [anywhere] * (gather + count),
        out_shape=[jax.ShapeDtypeStruct((tokens, share), f32)] * made + whole_shapes,
        scratch_shapes=[
            pltpu.VMEM((PIECES, 2, 2, size, share), bf16),
            pltpu.VMEM((PIECES, 2, 2, size, share), bf16),
            pltpu.VMEM((PIECES, 2, size, share), bf16),
            pltpu.VMEM((PIECES, 2, size, share), bf16),
            pltpu.VMEM((PIECES, size, share), bf16),
            pltpu.VMEM((PIECES, size, share), bf16),
            pltpu.SemaphoreType.DMA((10, PIECES)),
            pltpu.SemaphoreType.DMA((10, PIECES)),
            pltpu.SemaphoreType.DMA((2, PIECES)),
        ]
        + [pltpu.SemaphoreType.DMA((5, count))] * (2 if count else 0),
        compiler_params=pltpu.CompilerParams(collective_id=number, has_side_effects=True),
        cost_estimate=pl.CostEstimate(
            flops=60 * 10**9, bytes_accessed=32 * tokens * share, transcendentals=0
        ),
        name="plane_step",
    )(partial, *inputs, *packs)
    wholes = [whole.reshape((4 * whole.shape[1],) + whole.shape[2:]) for whole in outs[made + gather :]]
    return outs[:made], outs[made : made + gather], wholes


def gather_now(packs, number):
    if lax.axis_size("row") != 4:
        return [lax.all_gather(pack, "row", axis=0, tiled=True) for pack in packs]
    count = len(packs)
    sent = sum(pack.size for pack in packs) * 2
    anywhere = pl.BlockSpec(memory_space=pl.ANY)
    wholes = pl.pallas_call(
        functools.partial(gather_kernel, count),
        in_specs=[anywhere] * count,
        out_specs=[anywhere] * count,
        out_shape=[jax.ShapeDtypeStruct((4,) + pack.shape, pack.dtype) for pack in packs],
        scratch_shapes=[pltpu.SemaphoreType.DMA((5, count)), pltpu.SemaphoreType.DMA((5, count))],
        compiler_params=pltpu.CompilerParams(collective_id=number, has_side_effects=True),
        cost_estimate=pl.CostEstimate(
            flops=6 * 9000 * sent, bytes_accessed=6 * sent, transcendentals=0
        ),
        name="gather_rows",
    )(*packs)
    return [whole.reshape((4 * whole.shape[1],) + whole.shape[2:]) for whole in wholes]


def put_own(whole, part):
    if lax.axis_size("row") != 4:
        return whole
    return lax.dynamic_update_slice_in_dim(
        whole, part, lax.axis_index("row") * part.shape[0], 0
    )


class Reduced:
    def __init__(self, grads):
        n = lax.axis_size("row")
        self.chained = n == 4
        self.total = None
        if not self.chained:
            self.total = lax.psum_scatter(grads, "row", scatter_dimension=0, tiled=True).astype(f32)
            return
        self.grads, self.size = grads, grads.shape[0] // n
        self.own, self.partner, self.near, self.far = places(lax.axis_index("row"))
        self.far_in = lax.ppermute(self.block(self.far), "row", INWARD)
        self.near_in = lax.ppermute(self.block(self.near), "row", INWARD)

    def block(self, at, *others):
        piece = lax.dynamic_slice_in_dim(self.grads, at * self.size, self.size, 0)
        if others:
            piece = piece.astype(f32)
            for other in others:
                piece = piece + other.astype(f32)
        return piece

    def second(self, *groups):
        if not self.chained:
            return ()
        far = self.block(self.far, after(self.far_in, *groups)).astype(bf16)
        near = self.block(self.near, after(self.near_in, *groups)).astype(bf16)
        self.far_sum = lax.ppermute(far, "row", MIDDLE)
        self.near_sum = lax.ppermute(near, "row", MIDDLE)
        return (far, near)

    def third(self, *groups):
        if not self.chained:
            return ()
        piece = self.block(self.partner, after(self.far_sum, *groups)).astype(bf16)
        self.exchanged = lax.ppermute(piece, "row", PAIRS)
        return (piece,)

    def result(self, *groups):
        if self.total is None:
            self.total = self.block(self.own, after(self.near_sum, *groups), self.exchanged)
        return self.total


def after(value, *groups):
    others = tuple(item for group in groups for item in group)
    return lax.optimization_barrier((value,) + others)[0] if others else value


def expert_kernel(size, steps, count, z_ref, *refs):
    pieces = refs[:count]
    (x_ref, cot_ref, x_cols, cot_cols, coef_ref) = refs[count : count + 5]
    (dpair_ref, hidden_ref, sums_ref, grads_ref, whole_ref) = refs[count + 5 : count + 10]
    weights, dpair, hidden, sems, out_sem = refs[count + 10 :]
    step = pl.program_id(0)
    write = pltpu.make_async_copy(weights, whole_ref, out_sem)

    @pl.when(step == 0)
    def _():
        if count == 1:
            copy = pltpu.make_async_copy(pieces[0], weights, sems.at[0])
            copy.start()
            copy.wait()
        elif count == 2:
            block = pieces[0].shape[0]

            def block_copy(back):
                at = pl.multiple_of(lax.rem(z_ref[0] + back, 4) * block, block)
                source = pieces[1].at[pl.ds(at, block)] if back else pieces[0]
                return pltpu.make_async_copy(source, weights.at[pl.ds(at, block)], sems.at[back])

            for back in range(4):
                block_copy(back).start()
            for back in range(4):
                block_copy(back).wait()
        else:
            z = z_ref[0]
            block = pieces[0].shape[0]

            def copy_of(piece, which):
                at = pl.multiple_of(places(z)[which] * block, block)
                return pltpu.make_async_copy(
                    piece, weights.at[pl.ds(at, block)], sems.at[which]
                )

            copy_of(pieces[0], 0).start()
            copy_of(pieces[1], 1).start()
            in_middle = (z == 1) | (z == 2)

            @pl.when(in_middle)
            def _():
                copy_of(pieces[2], 2).start()
                copy_of(pieces[3], 3).start()

            @pl.when(jnp.logical_not(in_middle))
            def _():
                copy_of(pieces[4], 2).start()
                copy_of(pieces[5], 3).start()

            for which in range(4):
                copy_of(pieces[which], which).wait()
        write.start()

    @pl.when(step < steps)
    def _():
        at = pl.multiple_of(step * TILE, TILE)
        rows, cots = x_ref[...], cot_ref[...]
        scale, weight = coef_ref[:, 0:1], coef_ref[:, 1:2]
        dots = jnp.zeros((TILE, 1), f32)
        inner = jnp.zeros((TILE, 1), f32)
        for a in range(0, size, TILE):
            b = min(a + TILE, size)
            gate = scale * mm(rows, weights[:, a:b])
            up = scale * mm(rows, weights[:, size + a : size + b])
            dhid = mm(cots, weights[:, 2 * size + a : 2 * size + b])
            sigma = jax.nn.sigmoid(gate)
            silu = gate * sigma
            hid = silu * up
            dots += jnp.sum(hid * dhid, axis=1, keepdims=True)
            dhid = weight * dhid
            dgate = dhid * up * sigma * (1.0 + gate * (1.0 - sigma))
            dup = dhid * silu
            inner += jnp.sum(dgate * gate + dup * up, axis=1, keepdims=True)
            for into, at_col, value in (
                ((hidden_ref, hidden), a, weight * hid),
                ((dpair_ref, dpair), a, scale * dgate),
                ((dpair_ref, dpair), size + a, scale * dup),
            ):
                value = value.astype(bf16)
                into[0][:, at_col : at_col + b - a] = value
                into[1][pl.ds(at, TILE), at_col : at_col + b - a] = value
        sums_ref[:, 0:1] = dots
        sums_ref[:, 1:2] = inner

    @pl.when(step >= steps)
    def _():
        for a in range(0, 2 * size, TILE):
            b = min(a + TILE, 2 * size)
            grads_ref[:, a:b] = mm_tn(x_cols[...], dpair[:, a:b]).astype(bf16)
        for a in range(0, size, TILE):
            b = min(a + TILE, size)
            grads_ref[:, 2 * size + a : 2 * size + b] = mm_tn(
                cot_cols[...], hidden[:, a:b]
            ).astype(bf16)

    @pl.when(step == pl.num_programs(0) - 1)
    def _():
        write.wait()


def expert_chunk(pieces, scaled, cots, coef):
    tokens, width = scaled.shape
    size = pieces[0].shape[1] // 3
    steps, more = tokens // TILE, width // TILE
    count = len(pieces)
    rows = lambda i, _: (jnp.minimum(i, steps - 1), 0)
    cols = lambda i, _: (0, jnp.maximum(i - steps, 0))
    down = lambda i, _: (jnp.maximum(i - steps, 0), 0)
    z = jnp.reshape(lax.axis_index("row"), (1,)).astype(jnp.int32)
    return pl.pallas_call(
        functools.partial(expert_kernel, size, steps, count),
        grid_spec=pltpu.PrefetchScalarGridSpec(
            num_scalar_prefetch=1,
            grid=(steps + more,),
            in_specs=[pl.BlockSpec(memory_space=pl.ANY)] * count
            + [
                pl.BlockSpec((TILE, width), rows),
                pl.BlockSpec((TILE, width), rows),
                pl.BlockSpec((tokens, TILE), cols),
                pl.BlockSpec((tokens, TILE), cols),
                pl.BlockSpec((TILE, 2), rows),
            ],
            out_specs=[
                pl.BlockSpec((TILE, 2 * size), rows),
                pl.BlockSpec((TILE, size), rows),
                pl.BlockSpec((TILE, 2), rows),
                pl.BlockSpec((TILE, 3 * size), down),
                pl.BlockSpec(memory_space=pl.ANY),
            ],
            scratch_shapes=[
                pltpu.VMEM((width, 3 * size), bf16),
                pltpu.VMEM((tokens, 2 * size), bf16),
                pltpu.VMEM((tokens, size), bf16),
                pltpu.SemaphoreType.DMA((4,)),
                pltpu.SemaphoreType.DMA,
            ],
        ),
        out_shape=[
            jax.ShapeDtypeStruct((tokens, 2 * size), bf16),
            jax.ShapeDtypeStruct((tokens, size), bf16),
            jax.ShapeDtypeStruct((tokens, 2), f32),
            jax.ShapeDtypeStruct((width, 3 * size), bf16),
            jax.ShapeDtypeStruct((width, 3 * size), bf16),
        ],
        cost_estimate=pl.CostEstimate(
            flops=12 * tokens * width * size,
            bytes_accessed=8 * tokens * width + 24 * width * size,
            transcendentals=tokens * size,
        ),
        name="expert_chunk",
    )(z, *pieces, scaled, cots, scaled, cots, coef)


def joint_kernel(count, based, planar, *refs):
    out_ref = refs[-1]
    for a in range(0, refs[count].shape[0], TILE):
        total = refs[2 * count][:, a : a + TILE] if based else None
        for left, weights in zip(refs[:count], refs[count : 2 * count]):
            part = mm_nt(left[...], weights[a : a + TILE, :])
            total = part if total is None else total + part
        if planar:
            at = a // TILE
            out_ref[at // 4, at // 2 % 2, at % 2] = total.astype(out_ref.dtype)
        else:
            out_ref[:, a : a + TILE] = total.astype(out_ref.dtype)


def joint_back(lefts, weights, column, kind, *base, planar=False):
    tokens, width = lefts[0].shape[0], weights[0].shape[0]
    row = lambda i: (i, 0)
    fixed = lambda i: (0, column)
    depth = sum(left.shape[1] for left in lefts)
    return pl.pallas_call(
        functools.partial(joint_kernel, len(lefts), len(base) > 0, planar),
        grid=(tokens // TILE,),
        in_specs=[pl.BlockSpec((TILE, left.shape[1]), row) for left in lefts]
        + [
            pl.BlockSpec((width, left.shape[1]), fixed, pipeline_mode=pl.Buffered(1))
            for left in lefts
        ]
        + [pl.BlockSpec((TILE, width), row)] * len(base),
        out_specs=pl.BlockSpec((2, 2, 2, TILE, TILE), lambda i: (0, 0, 0, i, 0))
        if planar
        else pl.BlockSpec((TILE, width), row),
        out_shape=jax.ShapeDtypeStruct((2, 2, 2, tokens, TILE) if planar else (tokens, width), kind),
        cost_estimate=pl.CostEstimate(
            flops=2 * tokens * width * depth,
            bytes_accessed=2 * (tokens + width) * depth + 4 * tokens * width,
            transcendentals=0,
        ),
        name="joint_back",
    )(*lefts, *weights, *base)


def split_three(values):
    high = values.astype(bf16)
    rest = values - high.astype(f32)
    middle = rest.astype(bf16)
    return high, middle, (rest - middle.astype(f32)).astype(bf16)


def cuts_of(width, sizes):
    cuts, at = [], 0
    for size in sizes:
        if at + size < width:
            cuts.append((at, at + size))
            at += size
    return cuts + [(at, width)]


def stream_step(total, rows, gain):
    stream = rows.astype(f32) + total
    return stream * gain, stream


def dstream_step(total, back, cots, stream, damp, gain):
    dscaled = back + total
    dstream = cots.astype(f32) + gain * dscaled - stream * damp
    return dstream, dstream, dscaled


def per_device(
    block_input,
    seq_lengths,
    slot_order,
    routes,
    input_gain,
    query_weight,
    key_weight,
    value_weight,
    output_weight,
    mlp_gain,
    router_weight,
    score_shared,
    gate_shared,
    up_shared,
    down_shared,
    gate_expert,
    up_expert,
    down_expert,
    grad_output,
):
    tokens, share = block_input.shape
    cols = lax.axis_size("col")
    col_id = lax.axis_index("col")
    row_id = lax.axis_index("row")
    width = share * cols
    slots = tokens // SEQ_LEN
    local_experts = gate_expert.shape[0]
    experts = router_weight.shape[1]
    head_width = query_weight.shape[1]
    heads = head_width // HEAD_DIM
    rows_block = query_weight.shape[0]
    lengths = lax.dynamic_slice_in_dim(seq_lengths[slot_order], row_id * slots, slots, 0)
    cosine, sine = rope_tables()

    def by_head(weight):
        return weight.reshape(rows_block, heads, 1, HEAD_DIM)

    qkv_pack = jnp.concatenate(
        [by_head(query_weight), by_head(key_weight), by_head(value_weight)], axis=2
    ).reshape(rows_block, 3 * head_width)
    router_pack = jnp.concatenate([router_weight, score_shared[:, None]], axis=1)
    router_pack = jnp.pad(router_pack, ((0, 0), (0, -router_pack.shape[1] % 128)))
    out_pack = jnp.concatenate([output_weight.T, router_pack], axis=1)
    qkv_whole, out_whole = gather_now([qkv_pack, out_pack], 0)
    qkv_full, out_weights = put_own(qkv_whole, qkv_pack), put_own(out_whole, out_pack)
    out_full = out_weights[:, :head_width]
    router_full = out_weights[:, head_width : head_width + experts + 1]
    shared_cuts = [(None, a, b) for a, b in cuts_of(gate_shared.shape[1], (512,))]
    expert_cuts = [
        (local, a, b)
        for local in range(local_experts)
        for a, b in cuts_of(gate_expert.shape[2], (256, 256, 512))
    ]
    chunks = shared_cuts[-1:] + expert_cuts[:2] + shared_cuts[:-1] + expert_cuts[2:]

    def pack(kind, a, b):
        if kind is None:
            parts = [gate_shared[:, a:b], up_shared[:, a:b], down_shared[a:b].T]
        else:
            parts = [gate_expert[kind, :, a:b], up_expert[kind, :, a:b], down_expert[kind, a:b].T]
        fill = -(b - a) % 128
        return jnp.concatenate([jnp.pad(part, ((0, 0), (0, fill))) for part in parts], axis=1)

    packs = [pack(*chunk) for chunk in chunks]
    chained = lax.axis_size("row") == 4
    planar = chained and cols == 8 and share == TILE
    gathered = {}
    gathered[0] = Gathered(packs[0])

    rows_in = lax.all_gather(block_input, "col", axis=1, tiled=True)
    gains = lax.all_gather(jnp.stack([input_gain, mlp_gain]), "col", axis=1, tiled=True).astype(f32)
    cot_rows = lax.all_gather(grad_output, "col", axis=1, tiled=True)
    rows_f = rows_in.astype(f32)
    scale_a = lax.rsqrt(jnp.mean(rows_f * rows_f, axis=-1, keepdims=True) + norm_eps)
    normed_a = (rows_f * scale_a * gains[0]).astype(bf16)
    raw = mm(normed_a, qkv_full)
    raw = after(raw, gathered[0].second())
    qkv, context, lse = attend_forward(raw, lengths, cosine, sine)
    context = after(context, gathered[0].third())
    x_share = block_input.astype(f32)
    gain_b = mlp_gain.astype(f32)
    if planar:
        attn_part = joint_back([context], [out_weights], 0, bf16, planar=True)
        attn_part = after(attn_part, (cot_rows,))
        (stream,), (scaled,), wholes_now = plane_step(
            attn_part, stream_step, [block_input, gain_b[None]], 1, 1, 1, packs[1:3]
        )
        for at in (1, 2):
            gathered[at] = (packs[at], wholes_now[at - 1])
    else:
        attn_part = mm_nt(context, out_full).astype(bf16)
        attn_sum = lax.psum_scatter(attn_part, "col", scatter_dimension=1, tiled=True)
        scaled_share, stream = stream_step(attn_sum.astype(f32), block_input, gain_b[None])
        scaled = lax.all_gather(scaled_share.astype(bf16), "col", axis=1, tiled=True)
    for at in range(1, len(chunks)):
        if at not in gathered and (at <= 3 or not chained):
            gathered[at] = Gathered(packs[at], (scaled,))

    def pieces_of(at):
        return gathered[at] if isinstance(gathered[at], tuple) else gathered[at].pieces

    stream_f = scaled.astype(f32) / gains[1]
    scale_b = lax.rsqrt(jnp.mean(stream_f * stream_f, axis=1, keepdims=True) + norm_eps)

    both_logits = scale_b * mm(scaled, router_full)
    logits, slogit = both_logits[:, :experts], both_logits[:, experts]
    top = jnp.max(logits, axis=-1, keepdims=True)
    expo = jnp.exp(logits - top)
    router_probs = expo / jnp.sum(expo, axis=-1, keepdims=True)
    shared_gate = jax.nn.sigmoid(slogit)

    inner = jnp.zeros((tokens,), f32)
    dots = {}
    members, shares = {None: None}, {None: shared_gate}
    for local in range(local_experts):
        expert = col_id * local_experts + local
        members[local] = jnp.any(routes == expert, axis=1)
        column = lax.dynamic_index_in_dim(router_probs, expert, 1, False)
        shares[local] = jnp.where(members[local], column, 0.0)
    dpairs, hiddens, wholes, reduced = [], [], [], []
    last = len(chunks) - 1
    waits = ()
    for at, (kind, a, b) in enumerate(chunks):
        coef = after(jnp.concatenate([scale_b, shares[kind][:, None]], axis=1), waits)
        dpair, hidden, sums, grads, whole = expert_chunk(pieces_of(at), scaled, cot_rows, coef)
        dots[kind] = dots.get(kind, 0.0) + sums[:, 0]
        inner = inner + sums[:, 1]
        dpairs.append(dpair)
        hiddens.append(hidden)
        wholes.append(whole)
        now = (sums,)
        waits = ()
        if planar:
            if at == 0:
                waits += gathered[3].second(now)
            elif at == 1:
                waits += gathered[3].third(now)
                gathered[4] = Gathered(packs[4], now)
            elif at == 3:
                waits += gathered[4].second(now)
                gathered[5] = Gathered(packs[5], now)
                dscaled_early = joint_back(dpairs, wholes, 0, f32)
                early = (dscaled_early,)
                waits += early
                waits += gathered[4].third(early)
                waits += gathered[5].second(early)
            elif at == 4:
                waits += gathered[5].third(now)
        elif at == last - 1:
            dscaled_early = joint_back(dpairs, wholes, 0, f32)
        if at >= 1:
            waits += reduced[at - 1].second(now)
        if at >= 2:
            waits += reduced[at - 2].third(now)
        reduced.append(Reduced(grads))
        if at >= 3:
            waits += (reduced[at - 3].result(now),) if chained else ()
    if planar:
        late_pairs, late_wholes = dpairs[4:], wholes[4:]
    else:
        late_pairs, late_wholes = dpairs[last:], wholes[last:]
    late_pairs[-1] = after(late_pairs[-1], waits)
    dscaled_part = joint_back(late_pairs, late_wholes, 0, bf16, dscaled_early, planar=planar)
    moe_part = joint_back(hiddens, wholes, 2, bf16)

    named = [jnp.where(members[local], dots[local], 0.0) for local in range(local_experts)]
    table = lax.all_gather(jnp.stack(named + [dots[None], inner]), "col", axis=0)
    dprob = table[:, :local_experts].reshape(experts, tokens).T
    dshared_gate, inner = jnp.sum(table[:, local_experts], axis=0), jnp.sum(table[:, local_experts + 1], axis=0)
    dlogits = router_probs * (dprob - jnp.sum(dprob * router_probs, axis=1, keepdims=True))
    dslogit = dshared_gate * shared_gate * (1.0 - shared_gate)
    dboth = jnp.concatenate([dlogits, dslogit[:, None]], axis=1)
    inner = inner + jnp.sum(dboth * both_logits, axis=1)
    dboth = scale_b * dboth
    parts = split_three(dboth)
    stacked = mm_tn(jnp.concatenate(parts, axis=1), scaled)
    grad_router_part = stacked.reshape(3, experts + 1, width).sum(axis=0)
    grad_router_both = lax.psum_scatter(grad_router_part, "row", scatter_dimension=1, tiled=True)
    router_rows = lax.dynamic_slice_in_dim(router_full, col_id * share, share, 0)
    back_term = mm_nt(jnp.concatenate(parts, axis=1), jnp.concatenate([router_rows] * 3, axis=1))
    damp = scale_b * scale_b * inner[:, None] / width
    step_inputs = [back_term, grad_output, stream, damp, gain_b[None]]
    if planar:
        (dstream, dscaled), (dattn,), _ = plane_step(dscaled_part, dstream_step, step_inputs, 2, 1, 2)
    else:
        dscaled_sum = lax.psum_scatter(dscaled_part, "col", scatter_dimension=1, tiled=True)
        dstream_low, dstream, dscaled = dstream_step(dscaled_sum.astype(f32), *step_inputs)
        dattn = lax.all_gather(dstream_low.astype(bf16), "col", axis=1, tiled=True)
    gain_b_grad = jnp.sum(dscaled * stream, axis=0)

    moe_share = lax.psum_scatter(
        after(moe_part, (dattn,)), "col", scatter_dimension=1, tiled=True
    ).astype(f32)
    block_output = (stream + moe_share).astype(bf16)
    now = (dattn,)
    waits = reduced[last].second(now) + reduced[last - 1].third(now)
    out_reduced = Reduced(mm_tn(dattn, context).astype(bf16))
    dcontext = after(mm(dattn, out_full).astype(bf16), waits)
    dqkv, inner_a = attend_backward(qkv, dcontext, lse, lengths, cosine, sine)
    now = (inner_a,)
    waits = reduced[last].third(now) + out_reduced.second(now)
    dnormed_part = after(mm_nt(dqkv, qkv_full).astype(bf16), waits)
    dnormed_sum = lax.psum_scatter(dnormed_part, "col", scatter_dimension=1, tiled=True)
    qkv_reduced = Reduced(mm_tn(normed_a, dqkv).astype(bf16))
    out_reduced.third()
    qkv_reduced.second()
    qkv_reduced.third()
    inner_a = lax.psum(inner_a[:, 0], "col")[:, None]
    qkv_grad, out_grad = qkv_reduced.result(), out_reduced.result()
    unit_grads = [one.result() for one in reduced]
    dnormed_a = after(dnormed_sum, (inner_a,)).astype(f32)
    gain_a_share = input_gain.astype(f32)
    dinput = dstream + scale_a * gain_a_share * dnormed_a
    dinput = dinput - x_share * (scale_a * scale_a * inner_a / width)
    gain_a_grad = jnp.sum(dnormed_a * x_share * scale_a, axis=0)
    grad_gain_a, grad_gain_b = lax.psum((gain_a_grad, gain_b_grad), "row")

    qkv_grad = qkv_grad.reshape(rows_block, heads, 3, HEAD_DIM)
    grad_query, grad_key, grad_value = (
        qkv_grad[:, :, part].reshape(rows_block, head_width) for part in range(3)
    )
    def unpack(kind, which):
        found = []
        for (of, a, b), grad in zip(chunks, unit_grads):
            if of == kind:
                size = grad.shape[1] // 3
                part = grad[:, which * size : which * size + b - a]
                found.append((a, part.T if which == 2 else part))
        found = [part for _, part in sorted(found, key=lambda item: item[0])]
        return jnp.concatenate(found, axis=0 if which == 2 else 1)

    locals_ = range(local_experts)
    return (
        block_output,
        dinput.astype(bf16),
        grad_gain_a,
        grad_query,
        grad_key,
        grad_value,
        out_grad.T,
        grad_gain_b,
        grad_router_both[:experts].T,
        grad_router_both[experts],
        unpack(None, 0),
        unpack(None, 1),
        unpack(None, 2),
        jnp.stack([unpack(local, 0) for local in locals_]),
        jnp.stack([unpack(local, 1) for local in locals_]),
        jnp.stack([unpack(local, 2) for local in locals_]),
    )


def solution(mesh):
    return jax.shard_map(
        per_device,
        mesh=mesh,
        in_specs=(
            P("row", "col"),
            P(),
            P(),
            P("row", None),
            P("col"),
            P("row", "col"),
            P("row", "col"),
            P("row", "col"),
            P("col", "row"),
            P("col"),
            P("row", None),
            P("row"),
            P("row", "col"),
            P("row", "col"),
            P("col", "row"),
            P("col", "row", None),
            P("col", "row", None),
            P("col", None, "row"),
            P("row", "col"),
        ),
        out_specs=(
            P("row", "col"),
            P("row", "col"),
            P("col"),
            P("row", "col"),
            P("row", "col"),
            P("row", "col"),
            P("col", "row"),
            P("col"),
            P("row", None),
            P("row"),
            P("row", "col"),
            P("row", "col"),
            P("col", "row"),
            P("col", "row", None),
            P("col", "row", None),
            P("col", None, "row"),
        ),
        check_vma=False,
    )
```

```python
import functools
import math

import jax
import jax.numpy as jnp
from jax import lax
from jax.experimental import pallas as pl
from jax.experimental.pallas import tpu as pltpu
from jax.sharding import PartitionSpec as P

HEAD_DIM = 128
SEQ_LEN = 1024
QBLOCK = 256
TILE = 256
norm_eps = 1e-06
rope_base = 1000000.0
bf16 = jnp.bfloat16
f32 = jnp.float32


def mm(left, right):
    return jnp.dot(left, right, preferred_element_type=f32)


def mm_nt(left, right):
    return lax.dot_general(left, right, (((1,), (1,)), ((), ())), preferred_element_type=f32)


def mm_tn(left, right):
    return lax.dot_general(left, right, (((0,), (0,)), ((), ())), preferred_element_type=f32)


def rope_tables():
    positions = jnp.arange(SEQ_LEN).astype(f32)
    freqs = jnp.power(f32(rope_base), -jnp.arange(0, HEAD_DIM, 2).astype(f32) / HEAD_DIM)
    angles = positions[:, None] * freqs[None, :]
    cosine, sine = jnp.cos(angles), jnp.sin(angles)
    return (
        jnp.concatenate([cosine, cosine], axis=-1),
        jnp.concatenate([-sine, sine], axis=-1),
    )


def block_scores(rows, keys, start, length, scale):
    raw = mm_nt(rows, keys) * scale
    query_pos = start + lax.broadcasted_iota(jnp.int32, raw.shape, 0)
    key_pos = lax.broadcasted_iota(jnp.int32, raw.shape, 1)
    return jnp.where((key_pos <= query_pos) & (key_pos < length), raw, -1e30)


def attend_forward_kernel(length_ref, raw_ref, cos_ref, sin_ref, qkv_ref, context_ref, lse_ref):
    length = length_ref[pl.program_id(0)]
    scale = 1.0 / math.sqrt(HEAD_DIM)
    hd = HEAD_DIM
    for part in range(2):
        raw = raw_ref[:, part * hd : (part + 1) * hd]
        turned = raw * cos_ref[...] + pltpu.roll(raw, hd // 2, 1) * sin_ref[...]
        qkv_ref[:, part * hd : (part + 1) * hd] = turned.astype(bf16)
    qkv_ref[:, 2 * hd :] = raw_ref[:, 2 * hd :].astype(bf16)
    for at in range(0, SEQ_LEN, QBLOCK):
        seen = at + QBLOCK
        scores = block_scores(
            qkv_ref[at:seen, :hd], qkv_ref[:seen, hd : 2 * hd], at, length, scale
        )
        top = jnp.max(scores, axis=-1, keepdims=True)
        expo = jnp.exp(scores - top)
        total = jnp.sum(expo, axis=-1, keepdims=True)
        probs = (expo / total).astype(bf16)
        context_ref[at:seen, :] = mm(probs, qkv_ref[:seen, 2 * hd :]).astype(bf16)
        lse_ref[at:seen, :] = jnp.broadcast_to(top + jnp.log(total), (QBLOCK, hd))


def attend_forward(raw, lengths, cosine, sine):
    tokens, width = raw.shape
    heads = width // (3 * HEAD_DIM)
    slots = tokens // SEQ_LEN
    wide = pl.BlockSpec((SEQ_LEN, 3 * HEAD_DIM), lambda s, h, _: (s, h))
    one = pl.BlockSpec((SEQ_LEN, HEAD_DIM), lambda s, h, _: (s, h))
    table = pl.BlockSpec((SEQ_LEN, HEAD_DIM), lambda s, h, _: (0, 0))
    pairs = slots * heads * SEQ_LEN * SEQ_LEN
    return pl.pallas_call(
        attend_forward_kernel,
        grid_spec=pltpu.PrefetchScalarGridSpec(
            num_scalar_prefetch=1,
            grid=(slots, heads),
            in_specs=[wide, table, table],
            out_specs=[wide, one, one],
        ),
        out_shape=[
            jax.ShapeDtypeStruct((tokens, width), bf16),
            jax.ShapeDtypeStruct((tokens, heads * HEAD_DIM), bf16),
            jax.ShapeDtypeStruct((tokens, heads * HEAD_DIM), f32),
        ],
        cost_estimate=pl.CostEstimate(
            flops=3 * HEAD_DIM * pairs, bytes_accessed=8 * tokens * width, transcendentals=pairs
        ),
        name="attend_forward",
    )(lengths, raw, cosine, sine)


def attend_backward_kernel(
    length_ref, qkv_ref, dcontext_ref, lse_ref, cos_ref, sin_ref, dqkv_ref, inner_ref, dk_ref, dv_ref
):
    length = length_ref[pl.program_id(0)]
    scale = 1.0 / math.sqrt(HEAD_DIM)
    hd = HEAD_DIM
    @pl.when(pl.program_id(1) == 0)
    def _():
        inner_ref[...] = jnp.zeros_like(inner_ref)

    dk_ref[...] = jnp.zeros_like(dk_ref)
    dv_ref[...] = jnp.zeros_like(dv_ref)

    def turn_back(grad, rows):
        back = grad * cos_ref[rows, :] - pltpu.roll(grad, hd // 2, 1) * sin_ref[rows, :]
        return back.astype(bf16)

    for at in range(0, SEQ_LEN, QBLOCK):
        seen = at + QBLOCK
        rows = qkv_ref[at:seen, :hd]
        keys = qkv_ref[:seen, hd : 2 * hd]
        drows = dcontext_ref[at:seen, :]
        scores = block_scores(rows, keys, at, length, scale)
        probs = jnp.exp(scores - lse_ref[at:seen, :1])
        dv_ref[:seen, :] += mm_tn(probs.astype(bf16), drows)
        dprobs = mm_nt(drows, qkv_ref[:seen, 2 * hd :])
        dscore = probs * (dprobs - jnp.sum(dprobs * probs, axis=-1, keepdims=True))
        draw = (dscore * scale).astype(bf16)
        dquery = mm(draw, keys)
        dk_ref[:seen, :] += mm_tn(draw, rows)
        dqkv_ref[at:seen, :hd] = turn_back(dquery, slice(at, seen))
        inner_ref[at:seen, :] += jnp.sum(dquery * rows.astype(f32), axis=-1, keepdims=True)
    dkey, dvalue = dk_ref[...], dv_ref[...]
    dqkv_ref[:, hd : 2 * hd] = turn_back(dkey, slice(None))
    dqkv_ref[:, 2 * hd :] = dvalue.astype(bf16)
    inner_ref[...] += jnp.sum(
        dkey * qkv_ref[:, hd : 2 * hd].astype(f32) + dvalue * qkv_ref[:, 2 * hd :].astype(f32),
        axis=-1,
        keepdims=True,
    )


def attend_backward(qkv, dcontext, lse, lengths, cosine, sine):
    tokens, width = qkv.shape
    heads = width // (3 * HEAD_DIM)
    slots = tokens // SEQ_LEN
    wide = pl.BlockSpec((SEQ_LEN, 3 * HEAD_DIM), lambda s, h, _: (s, h))
    one = pl.BlockSpec((SEQ_LEN, HEAD_DIM), lambda s, h, _: (s, h))
    table = pl.BlockSpec((SEQ_LEN, HEAD_DIM), lambda s, h, _: (0, 0))
    pairs = slots * heads * SEQ_LEN * SEQ_LEN
    return pl.pallas_call(
        attend_backward_kernel,
        grid_spec=pltpu.PrefetchScalarGridSpec(
            num_scalar_prefetch=1,
            grid=(slots, heads),
            in_specs=[wide, one, one, table, table],
            out_specs=[wide, pl.BlockSpec((SEQ_LEN, 1), lambda s, h, _: (s, 0))],
            scratch_shapes=[pltpu.VMEM((SEQ_LEN, HEAD_DIM), f32)] * 2,
        ),
        out_shape=[
            jax.ShapeDtypeStruct((tokens, width), bf16),
            jax.ShapeDtypeStruct((tokens, 1), f32),
        ],
        cost_estimate=pl.CostEstimate(
            flops=8 * HEAD_DIM * pairs, bytes_accessed=8 * tokens * width, transcendentals=pairs
        ),
        name="attend_backward",
    )(lengths, qkv, dcontext, lse, cosine, sine)


PAIRS = [(0, 1), (1, 0), (2, 3), (3, 2)]
MIDDLE = [(1, 2), (2, 1)]
OUTWARD = [(1, 0), (2, 3)]
INWARD = [(0, 1), (3, 2)]


class Gathered:
    def __init__(self, part, *groups):
        self.part = part
        if lax.axis_size("row") != 4:
            self.pieces = (lax.all_gather(part, "row", axis=0, tiled=True),)
            return
        part = after(part, *groups)
        self.partner = lax.ppermute(part, "row", PAIRS)
        self.near_mid = lax.ppermute(part, "row", MIDDLE)
        self.pieces = None

    def second(self, *groups):
        if self.pieces is None:
            self.near_out = lax.ppermute(after(self.near_mid, *groups), "row", OUTWARD)
            self.far_mid = lax.ppermute(after(self.partner, *groups), "row", MIDDLE)
            return (self.partner, self.near_mid)
        return ()

    def third(self, *groups):
        if self.pieces is None:
            self.far_out = lax.ppermute(after(self.far_mid, *groups), "row", OUTWARD)
            self.pieces = (
                self.part, self.partner, self.near_mid, self.far_mid, self.near_out, self.far_out
            )
            return (self.far_mid, self.near_out)
        return ()


def places(z):
    pair = z // 2
    return z, z + 1 - 2 * lax.rem(z, 2), 2 - pair, 3 - 3 * pair


class RowGather:
    def __init__(self, packs, wholes, sems):
        self.packs, self.wholes, (self.send_sems, self.recv_sems) = packs, wholes, sems
        self.z = lax.axis_index("row")
        self.own, self.partner, self.near, self.far = places(self.z)
        self.across = 3 - self.z
        self.in_middle = (self.z == 1) | (self.z == 2)
        self.outside = jnp.logical_not(self.in_middle)

    def copy_of(self, kind, at, source, block, target):
        return pltpu.make_async_remote_copy(
            src_ref=source,
            dst_ref=self.wholes[at].at[block],
            send_sem=self.send_sems.at[kind, at],
            recv_sem=self.recv_sems.at[kind, at],
            device_id={"row": target},
            device_id_type=pl.DeviceIdType.MESH,
        )

    def swap(self, at):
        return self.copy_of(0, at, self.packs[at], self.own, self.partner)

    def swap_middle(self, at):
        return self.copy_of(1, at, self.packs[at], self.own, self.across)

    def second_middle(self, at):
        return self.copy_of(2, at, self.wholes[at].at[self.partner], self.partner, self.across)

    def hand_near(self, at):
        return self.copy_of(3, at, self.wholes[at].at[self.near], self.near, self.partner)

    def hand_far(self, at):
        return self.copy_of(4, at, self.wholes[at].at[self.far], self.far, self.partner)

    def greet(self, barrier):
        signal_to(barrier, {"row": self.partner})

        @pl.when(self.in_middle)
        def _():
            signal_to(barrier, {"row": self.across})
            pl.semaphore_wait(barrier, 2)

        @pl.when(self.outside)
        def _():
            pl.semaphore_wait(barrier, 1)

    def begin(self):
        for at in range(len(self.packs)):
            @pl.when(self.in_middle)
            def _():
                self.swap_middle(at).start()

            self.swap(at).start()

    def hand_on(self, at):
        @pl.when(self.in_middle)
        def _():
            self.swap_middle(at).wait_recv()
            self.hand_near(at).start()
            self.swap(at).wait_recv()
            self.second_middle(at).start()

    def hand_last(self, at):
        @pl.when(self.in_middle)
        def _():
            self.second_middle(at).wait_recv()
            self.hand_far(at).start()

    def finish(self):
        for at in range(len(self.packs)):
            @pl.when(self.in_middle)
            def _():
                for copy in (
                    self.swap,
                    self.swap_middle,
                    self.second_middle,
                    self.hand_near,
                    self.hand_far,
                ):
                    copy(at).wait_send()

            @pl.when(self.outside)
            def _():
                self.swap(at).wait()
                self.hand_near(at).wait_recv()
                self.hand_far(at).wait_recv()


def signal_to(barrier, device):
    pl.semaphore_signal(barrier, inc=1, device_id=device, device_id_type=pl.DeviceIdType.MESH)


def gather_kernel(count, *refs):
    rows = RowGather(refs[:count], refs[count : 2 * count], refs[2 * count :])
    rows.greet(pltpu.get_barrier_semaphore())
    rows.begin()
    for at in range(count):
        rows.hand_on(at)
    for at in range(count):
        rows.hand_last(at)
    rows.finish()


PIECES = 4


def plane_kernel(pointwise, given, made, gather, count, *refs):
    p_ref, inputs = refs[0], refs[1 : 1 + given]
    at = 1 + given
    packs = refs[at : at + count]
    at += count
    results = refs[at : at + made]
    at += made
    whole_refs = refs[at : at + gather + count]
    at += gather + count
    mine, from_core, from_first, summed, from_second, shared, send_sems, recv_sems, local_sems = refs[
        at : at + 9
    ]
    out_ref = whole_refs[0] if gather else None
    me = lax.axis_index("col")
    core, x, y = lax.rem(me, 2), lax.rem(me // 2, 2), me // 4
    core_mate, x_mate, y_mate = me + 1 - 2 * core, me + 2 - 4 * x, me + 4 - 8 * y
    diagonal = x_mate + 4 - 8 * y
    size = mine.shape[3]
    share = mine.shape[4]
    barrier = pltpu.get_barrier_semaphore()
    for mate in (core_mate, x_mate, y_mate):
        signal_to(barrier, {"col": mate})
    rows = None
    if count:
        rows = RowGather(packs, whole_refs[gather:], refs[at + 9 : at + 11])
        signal_to(barrier, {"row": rows.partner})

        @pl.when(rows.in_middle)
        def _():
            signal_to(barrier, {"row": rows.across})
            pl.semaphore_wait(barrier, 5)

        @pl.when(rows.outside)
        def _():
            pl.semaphore_wait(barrier, 4)

        rows.begin()
    else:
        pl.semaphore_wait(barrier, 3)

    def remote(kind, i, source, target, mate):
        return pltpu.make_async_remote_copy(
            src_ref=source,
            dst_ref=target,
            send_sem=send_sems.at[kind, i],
            recv_sem=recv_sems.at[kind, i],
            device_id={"col": mate},
            device_id_type=pl.DeviceIdType.MESH,
        )

    def x_first(i):
        return i < PIECES // 2

    def span(i):
        return pl.ds(i * size, size)

    def core_copy(i):
        return remote(0, i, p_ref.at[:, :, 1 - core, span(i), :], from_core.at[i], core_mate)

    def load(i):
        return pltpu.make_async_copy(
            p_ref.at[:, :, core, span(i), :], mine.at[i], local_sems.at[0, i]
        )

    def first_copy(i):
        if x_first(i):
            return remote(1, i, mine.at[i, :, 1 - x], from_first.at[i], x_mate)
        return remote(1, i, mine.at[i, 1 - y], from_first.at[i], y_mate)

    def second_copy(i):
        if x_first(i):
            return remote(2, i, summed.at[i, 1 - y], from_second.at[i], y_mate)
        return remote(2, i, summed.at[i, 1 - x], from_second.at[i], x_mate)

    def columns(i, device):
        return out_ref.at[span(i), pl.ds(pl.multiple_of(device * share, share), share)]

    def spread(kind, i, mate):
        return remote(kind, i, shared.at[i], columns(i, me), mate)

    def keep(i):
        return pltpu.make_async_copy(shared.at[i], columns(i, me), local_sems.at[1, i])

    def pass_on(kind, i, device, mate):
        return remote(kind, i, columns(i, device), columns(i, device), mate)

    def forward(i):
        if x_first(i):
            return pass_on(6, i, y_mate, x_mate)
        return pass_on(6, i, x_mate, y_mate)

    order = [0, 2, 1, 3]
    for i in order:
        core_copy(i).start()
        load(i).start()
    for i in order:
        load(i).wait()
        core_copy(i).wait_recv()
        for a in range(2):
            for b in range(2):
                mine[i, a, b] = (mine[i, a, b].astype(f32) + from_core[i, a, b].astype(f32)).astype(bf16)
        first_copy(i).start()
    for i in order:
        first_copy(i).wait_recv()
        for a in range(2):
            kept = mine[i, a, x] if x_first(i) else mine[i, y, a]
            summed[i, a] = (kept.astype(f32) + from_first[i, a].astype(f32)).astype(bf16)
        second_copy(i).start()
    if count:
        for at in range(count):
            rows.hand_on(at)
    for i in order:
        second_copy(i).wait_recv()
        total = summed[i, y if x_first(i) else x].astype(f32) + from_second[i].astype(f32)
        span_rows = slice(i * size, (i + 1) * size)
        values = pointwise(
            total, *[ref[span_rows, :] if ref.shape[0] > 8 else ref[...] for ref in inputs]
        )
        if gather:
            shared[i] = values[0].astype(bf16)
            values = values[1:]
        for ref, value in zip(results, values):
            ref[span_rows, :] = value
        if gather:
            spread(4, i, x_mate).start()
            spread(5, i, y_mate).start()
            spread(3, i, core_mate).start()
            keep(i).start()
    if count:
        rows.hand_last(0)
    if gather:
        for i in order:
            spread(5 if x_first(i) else 4, i, y_mate).wait_recv()
            forward(i).start()
            pass_on(7, i, y_mate if x_first(i) else x_mate, core_mate).start()
        for i in order:
            spread(4 if x_first(i) else 5, i, x_mate).wait_recv()
            pass_on(8, i, x_mate if x_first(i) else y_mate, core_mate).start()
    if count:
        for at in range(1, count):
            rows.hand_last(at)
    if gather:
        for i in order:
            forward(i).wait_recv()
            pass_on(9, i, diagonal, core_mate).start()
    for i in order:
        core_copy(i).wait_send()
        first_copy(i).wait_send()
        second_copy(i).wait_send()
        if gather:
            keep(i).wait()
            spread(3, i, core_mate).wait()
            spread(4, i, x_mate).wait_send()
            spread(5, i, y_mate).wait_send()
            forward(i).wait_send()
            for kind, device in (
                (7, y_mate if x_first(i) else x_mate),
                (8, x_mate if x_first(i) else y_mate),
                (9, diagonal),
            ):
                pass_on(kind, i, device, core_mate).wait()
    if count:
        rows.finish()


def plane_step(partial, pointwise, inputs, made, gather, number, packs=()):
    tokens, share = partial.shape[3:]
    size = tokens // PIECES
    count = len(packs)
    anywhere = pl.BlockSpec(memory_space=pl.ANY)
    vmem = pl.BlockSpec(memory_space=pltpu.VMEM)
    whole_shapes = [jax.ShapeDtypeStruct((tokens, 8 * share), bf16)] * gather + [
        jax.ShapeDtypeStruct((4,) + pack.shape, bf16) for pack in packs
    ]
    outs = pl.pallas_call(
        functools.partial(plane_kernel, pointwise, len(inputs), made, gather, count),
        in_specs=[anywhere] + [vmem] * len(inputs) + [anywhere] * count,
        out_specs=[vmem] * made + [anywhere] * (gather + count),
        out_shape=[jax.ShapeDtypeStruct((tokens, share), f32)] * made + whole_shapes,
        scratch_shapes=[
            pltpu.VMEM((PIECES, 2, 2, size, share), bf16),
            pltpu.VMEM((PIECES, 2, 2, size, share), bf16),
            pltpu.VMEM((PIECES, 2, size, share), bf16),
            pltpu.VMEM((PIECES, 2, size, share), bf16),
            pltpu.VMEM((PIECES, size, share), bf16),
            pltpu.VMEM((PIECES, size, share), bf16),
            pltpu.SemaphoreType.DMA((10, PIECES)),
            pltpu.SemaphoreType.DMA((10, PIECES)),
            pltpu.SemaphoreType.DMA((2, PIECES)),
        ]
        + [pltpu.SemaphoreType.DMA((5, count))] * (2 if count else 0),
        compiler_params=pltpu.CompilerParams(collective_id=number, has_side_effects=True),
        cost_estimate=pl.CostEstimate(
            flops=60 * 10**9, bytes_accessed=32 * tokens * share, transcendentals=0
        ),
        name="plane_step",
    )(partial, *inputs, *packs)
    wholes = [whole.reshape((4 * whole.shape[1],) + whole.shape[2:]) for whole in outs[made + gather :]]
    return outs[:made], outs[made : made + gather], wholes


def gather_now(packs, number):
    if lax.axis_size("row") != 4:
        return [lax.all_gather(pack, "row", axis=0, tiled=True) for pack in packs]
    count = len(packs)
    sent = sum(pack.size for pack in packs) * 2
    anywhere = pl.BlockSpec(memory_space=pl.ANY)
    wholes = pl.pallas_call(
        functools.partial(gather_kernel, count),
        in_specs=[anywhere] * count,
        out_specs=[anywhere] * count,
        out_shape=[jax.ShapeDtypeStruct((4,) + pack.shape, pack.dtype) for pack in packs],
        scratch_shapes=[pltpu.SemaphoreType.DMA((5, count)), pltpu.SemaphoreType.DMA((5, count))],
        compiler_params=pltpu.CompilerParams(collective_id=number, has_side_effects=True),
        cost_estimate=pl.CostEstimate(
            flops=6 * 9000 * sent, bytes_accessed=6 * sent, transcendentals=0
        ),
        name="gather_rows",
    )(*packs)
    return [whole.reshape((4 * whole.shape[1],) + whole.shape[2:]) for whole in wholes]


def put_own(whole, part):
    if lax.axis_size("row") != 4:
        return whole
    return lax.dynamic_update_slice_in_dim(
        whole, part, lax.axis_index("row") * part.shape[0], 0
    )


class Reduced:
    def __init__(self, grads):
        n = lax.axis_size("row")
        self.chained = n == 4
        self.total = None
        if not self.chained:
            self.total = lax.psum_scatter(grads, "row", scatter_dimension=0, tiled=True).astype(f32)
            return
        self.grads, self.size = grads, grads.shape[0] // n
        self.own, self.partner, self.near, self.far = places(lax.axis_index("row"))
        self.far_in = lax.ppermute(self.block(self.far), "row", INWARD)
        self.near_in = lax.ppermute(self.block(self.near), "row", INWARD)

    def block(self, at, *others):
        piece = lax.dynamic_slice_in_dim(self.grads, at * self.size, self.size, 0)
        if others:
            piece = piece.astype(f32)
            for other in others:
                piece = piece + other.astype(f32)
        return piece

    def second(self, *groups):
        if not self.chained:
            return ()
        far = self.block(self.far, after(self.far_in, *groups)).astype(bf16)
        near = self.block(self.near, after(self.near_in, *groups)).astype(bf16)
        self.far_sum = lax.ppermute(far, "row", MIDDLE)
        self.near_sum = lax.ppermute(near, "row", MIDDLE)
        return (far, near)

    def third(self, *groups):
        if not self.chained:
            return ()
        piece = self.block(self.partner, after(self.far_sum, *groups)).astype(bf16)
        self.exchanged = lax.ppermute(piece, "row", PAIRS)
        return (piece,)

    def result(self, *groups):
        if self.total is None:
            self.total = self.block(self.own, after(self.near_sum, *groups), self.exchanged)
        return self.total


def after(value, *groups):
    others = tuple(item for group in groups for item in group)
    return lax.optimization_barrier((value,) + others)[0] if others else value


def expert_kernel(size, steps, count, z_ref, *refs):
    pieces = refs[:count]
    (x_ref, cot_ref, x_cols, cot_cols, coef_ref) = refs[count : count + 5]
    (dpair_ref, hidden_ref, sums_ref, grads_ref, whole_ref) = refs[count + 5 : count + 10]
    weights, dpair, hidden, sems, out_sem = refs[count + 10 :]
    step = pl.program_id(0)
    write = pltpu.make_async_copy(weights, whole_ref, out_sem)

    @pl.when(step == 0)
    def _():
        if count == 1:
            copy = pltpu.make_async_copy(pieces[0], weights, sems.at[0])
            copy.start()
            copy.wait()
        elif count == 2:
            block = pieces[0].shape[0]

            def block_copy(back):
                at = pl.multiple_of(lax.rem(z_ref[0] + back, 4) * block, block)
                source = pieces[1].at[pl.ds(at, block)] if back else pieces[0]
                return pltpu.make_async_copy(source, weights.at[pl.ds(at, block)], sems.at[back])

            for back in range(4):
                block_copy(back).start()
            for back in range(4):
                block_copy(back).wait()
        else:
            z = z_ref[0]
            block = pieces[0].shape[0]

            def copy_of(piece, which):
                at = pl.multiple_of(places(z)[which] * block, block)
                return pltpu.make_async_copy(
                    piece, weights.at[pl.ds(at, block)], sems.at[which]
                )

            copy_of(pieces[0], 0).start()
            copy_of(pieces[1], 1).start()
            in_middle = (z == 1) | (z == 2)

            @pl.when(in_middle)
            def _():
                copy_of(pieces[2], 2).start()
                copy_of(pieces[3], 3).start()

            @pl.when(jnp.logical_not(in_middle))
            def _():
                copy_of(pieces[4], 2).start()
                copy_of(pieces[5], 3).start()

            for which in range(4):
                copy_of(pieces[which], which).wait()
        write.start()

    @pl.when(step < steps)
    def _():
        at = pl.multiple_of(step * TILE, TILE)
        rows, cots = x_ref[...], cot_ref[...]
        scale, weight = coef_ref[:, 0:1], coef_ref[:, 1:2]
        dots = jnp.zeros((TILE, 1), f32)
        inner = jnp.zeros((TILE, 1), f32)
        for a in range(0, size, TILE):
            b = min(a + TILE, size)
            gate = scale * mm(rows, weights[:, a:b])
            up = scale * mm(rows, weights[:, size + a : size + b])
            dhid = mm(cots, weights[:, 2 * size + a : 2 * size + b])
            sigma = jax.nn.sigmoid(gate)
            silu = gate * sigma
            hid = silu * up
            dots += jnp.sum(hid * dhid, axis=1, keepdims=True)
            dhid = weight * dhid
            dgate = dhid * up * sigma * (1.0 + gate * (1.0 - sigma))
            dup = dhid * silu
            inner += jnp.sum(dgate * gate + dup * up, axis=1, keepdims=True)
            for into, at_col, value in (
                ((hidden_ref, hidden), a, weight * hid),
                ((dpair_ref, dpair), a, scale * dgate),
                ((dpair_ref, dpair), size + a, scale * dup),
            ):
                value = value.astype(bf16)
                into[0][:, at_col : at_col + b - a] = value
                into[1][pl.ds(at, TILE), at_col : at_col + b - a] = value
        sums_ref[:, 0:1] = dots
        sums_ref[:, 1:2] = inner

    @pl.when(step >= steps)
    def _():
        for a in range(0, 2 * size, TILE):
            b = min(a + TILE, 2 * size)
            grads_ref[:, a:b] = mm_tn(x_cols[...], dpair[:, a:b]).astype(bf16)
        for a in range(0, size, TILE):
            b = min(a + TILE, size)
            grads_ref[:, 2 * size + a : 2 * size + b] = mm_tn(
                cot_cols[...], hidden[:, a:b]
            ).astype(bf16)

    @pl.when(step == pl.num_programs(0) - 1)
    def _():
        write.wait()


def expert_chunk(pieces, scaled, cots, coef):
    tokens, width = scaled.shape
    size = pieces[0].shape[1] // 3
    steps, more = tokens // TILE, width // TILE
    count = len(pieces)
    rows = lambda i, _: (jnp.minimum(i, steps - 1), 0)
    cols = lambda i, _: (0, jnp.maximum(i - steps, 0))
    down = lambda i, _: (jnp.maximum(i - steps, 0), 0)
    z = jnp.reshape(lax.axis_index("row"), (1,)).astype(jnp.int32)
    return pl.pallas_call(
        functools.partial(expert_kernel, size, steps, count),
        grid_spec=pltpu.PrefetchScalarGridSpec(
            num_scalar_prefetch=1,
            grid=(steps + more,),
            in_specs=[pl.BlockSpec(memory_space=pl.ANY)] * count
            + [
                pl.BlockSpec((TILE, width), rows),
                pl.BlockSpec((TILE, width), rows),
                pl.BlockSpec((tokens, TILE), cols),
                pl.BlockSpec((tokens, TILE), cols),
                pl.BlockSpec((TILE, 2), rows),
            ],
            out_specs=[
                pl.BlockSpec((TILE, 2 * size), rows),
                pl.BlockSpec((TILE, size), rows),
                pl.BlockSpec((TILE, 2), rows),
                pl.BlockSpec((TILE, 3 * size), down),
                pl.BlockSpec(memory_space=pl.ANY),
            ],
            scratch_shapes=[
                pltpu.VMEM((width, 3 * size), bf16),
                pltpu.VMEM((tokens, 2 * size), bf16),
                pltpu.VMEM((tokens, size), bf16),
                pltpu.SemaphoreType.DMA((4,)),
                pltpu.SemaphoreType.DMA,
            ],
        ),
        out_shape=[
            jax.ShapeDtypeStruct((tokens, 2 * size), bf16),
            jax.ShapeDtypeStruct((tokens, size), bf16),
            jax.ShapeDtypeStruct((tokens, 2), f32),
            jax.ShapeDtypeStruct((width, 3 * size), bf16),
            jax.ShapeDtypeStruct((width, 3 * size), bf16),
        ],
        cost_estimate=pl.CostEstimate(
            flops=12 * tokens * width * size,
            bytes_accessed=8 * tokens * width + 24 * width * size,
            transcendentals=tokens * size,
        ),
        name="expert_chunk",
    )(z, *pieces, scaled, cots, scaled, cots, coef)


def joint_kernel(count, based, planar, *refs):
    out_ref = refs[-1]
    for a in range(0, refs[count].shape[0], TILE):
        total = refs[2 * count][:, a : a + TILE] if based else None
        for left, weights in zip(refs[:count], refs[count : 2 * count]):
            part = mm_nt(left[...], weights[a : a + TILE, :])
            total = part if total is None else total + part
        if planar:
            at = a // TILE
            out_ref[at // 4, at // 2 % 2, at % 2] = total.astype(out_ref.dtype)
        else:
            out_ref[:, a : a + TILE] = total.astype(out_ref.dtype)


def joint_back(lefts, weights, column, kind, *base, planar=False):
    tokens, width = lefts[0].shape[0], weights[0].shape[0]
    row = lambda i: (i, 0)
    fixed = lambda i: (0, column)
    depth = sum(left.shape[1] for left in lefts)
    return pl.pallas_call(
        functools.partial(joint_kernel, len(lefts), len(base) > 0, planar),
        grid=(tokens // TILE,),
        in_specs=[pl.BlockSpec((TILE, left.shape[1]), row) for left in lefts]
        + [
            pl.BlockSpec((width, left.shape[1]), fixed, pipeline_mode=pl.Buffered(1))
            for left in lefts
        ]
        + [pl.BlockSpec((TILE, width), row)] * len(base),
        out_specs=pl.BlockSpec((2, 2, 2, TILE, TILE), lambda i: (0, 0, 0, i, 0))
        if planar
        else pl.BlockSpec((TILE, width), row),
        out_shape=jax.ShapeDtypeStruct((2, 2, 2, tokens, TILE) if planar else (tokens, width), kind),
        cost_estimate=pl.CostEstimate(
            flops=2 * tokens * width * depth,
            bytes_accessed=2 * (tokens + width) * depth + 4 * tokens * width,
            transcendentals=0,
        ),
        name="joint_back",
    )(*lefts, *weights, *base)


def split_three(values):
    high = values.astype(bf16)
    rest = values - high.astype(f32)
    middle = rest.astype(bf16)
    return high, middle, (rest - middle.astype(f32)).astype(bf16)


def cuts_of(width, sizes):
    cuts, at = [], 0
    for size in sizes:
        if at + size < width:
            cuts.append((at, at + size))
            at += size
    return cuts + [(at, width)]


def stream_step(total, rows, gain):
    stream = rows.astype(f32) + total
    return stream * gain, stream


def dstream_step(total, back, cots, stream, damp, gain):
    dscaled = back + total
    dstream = cots.astype(f32) + gain * dscaled - stream * damp
    return dstream, dstream, dscaled


def per_device(
    block_input,
    seq_lengths,
    slot_order,
    routes,
    input_gain,
    query_weight,
    key_weight,
    value_weight,
    output_weight,
    mlp_gain,
    router_weight,
    score_shared,
    gate_shared,
    up_shared,
    down_shared,
    gate_expert,
    up_expert,
    down_expert,
    grad_output,
):
    tokens, share = block_input.shape
    cols = lax.axis_size("col")
    col_id = lax.axis_index("col")
    row_id = lax.axis_index("row")
    width = share * cols
    slots = tokens // SEQ_LEN
    local_experts = gate_expert.shape[0]
    experts = router_weight.shape[1]
    head_width = query_weight.shape[1]
    heads = head_width // HEAD_DIM
    rows_block = query_weight.shape[0]
    lengths = lax.dynamic_slice_in_dim(seq_lengths[slot_order], row_id * slots, slots, 0)
    cosine, sine = rope_tables()

    def by_head(weight):
        return weight.reshape(rows_block, heads, 1, HEAD_DIM)

    qkv_pack = jnp.concatenate(
        [by_head(query_weight), by_head(key_weight), by_head(value_weight)], axis=2
    ).reshape(rows_block, 3 * head_width)
    router_pack = jnp.concatenate([router_weight, score_shared[:, None]], axis=1)
    router_pack = jnp.pad(router_pack, ((0, 0), (0, -router_pack.shape[1] % 128)))
    out_pack = jnp.concatenate([output_weight.T, router_pack], axis=1)
    qkv_whole, out_whole = gather_now([qkv_pack, out_pack], 0)
    qkv_full, out_weights = put_own(qkv_whole, qkv_pack), put_own(out_whole, out_pack)
    out_full = out_weights[:, :head_width]
    router_full = out_weights[:, head_width : head_width + experts + 1]
    shared_cuts = [(None, a, b) for a, b in cuts_of(gate_shared.shape[1], (512,))]
    expert_cuts = [
        (local, a, b)
        for local in range(local_experts)
        for a, b in cuts_of(gate_expert.shape[2], (256, 256, 512))
    ]
    chunks = shared_cuts[-1:] + expert_cuts[:2] + shared_cuts[:-1] + expert_cuts[2:]

    def pack(kind, a, b):
        if kind is None:
            parts = [gate_shared[:, a:b], up_shared[:, a:b], down_shared[a:b].T]
        else:
            parts = [gate_expert[kind, :, a:b], up_expert[kind, :, a:b], down_expert[kind, a:b].T]
        fill = -(b - a) % 128
        return jnp.concatenate([jnp.pad(part, ((0, 0), (0, fill))) for part in parts], axis=1)

    packs = [pack(*chunk) for chunk in chunks]
    chained = lax.axis_size("row") == 4
    planar = chained and cols == 8 and share == TILE
    gathered = {}
    gathered[0] = Gathered(packs[0])

    rows_in = lax.all_gather(block_input, "col", axis=1, tiled=True)
    gains = lax.all_gather(jnp.stack([input_gain, mlp_gain]), "col", axis=1, tiled=True).astype(f32)
    cot_rows = lax.all_gather(grad_output, "col", axis=1, tiled=True)
    rows_f = rows_in.astype(f32)
    scale_a = lax.rsqrt(jnp.mean(rows_f * rows_f, axis=-1, keepdims=True) + norm_eps)
    normed_a = (rows_f * scale_a * gains[0]).astype(bf16)
    raw = mm(normed_a, qkv_full)
    raw = after(raw, gathered[0].second())
    qkv, context, lse = attend_forward(raw, lengths, cosine, sine)
    context = after(context, gathered[0].third())
    x_share = block_input.astype(f32)
    gain_b = mlp_gain.astype(f32)
    if planar:
        attn_part = joint_back([context], [out_weights], 0, bf16, planar=True)
        attn_part = after(attn_part, (cot_rows,))
        (stream,), (scaled,), wholes_now = plane_step(
            attn_part, stream_step, [block_input, gain_b[None]], 1, 1, 1, packs[1:3]
        )
        for at in (1, 2):
            gathered[at] = (packs[at], wholes_now[at - 1])
    else:
        attn_part = mm_nt(context, out_full).astype(bf16)
        attn_sum = lax.psum_scatter(attn_part, "col", scatter_dimension=1, tiled=True)
        scaled_share, stream = stream_step(attn_sum.astype(f32), block_input, gain_b[None])
        scaled = lax.all_gather(scaled_share.astype(bf16), "col", axis=1, tiled=True)
    for at in range(1, len(chunks)):
        if at not in gathered and (at <= 3 or not chained):
            gathered[at] = Gathered(packs[at], (scaled,))

    def pieces_of(at):
        return gathered[at] if isinstance(gathered[at], tuple) else gathered[at].pieces

    stream_f = scaled.astype(f32) / gains[1]
    scale_b = lax.rsqrt(jnp.mean(stream_f * stream_f, axis=1, keepdims=True) + norm_eps)

    both_logits = scale_b * mm(scaled, router_full)
    logits, slogit = both_logits[:, :experts], both_logits[:, experts]
    top = jnp.max(logits, axis=-1, keepdims=True)
    expo = jnp.exp(logits - top)
    router_probs = expo / jnp.sum(expo, axis=-1, keepdims=True)
    shared_gate = jax.nn.sigmoid(slogit)

    inner = jnp.zeros((tokens,), f32)
    dots = {}
    members, shares = {None: None}, {None: shared_gate}
    for local in range(local_experts):
        expert = col_id * local_experts + local
        members[local] = jnp.any(routes == expert, axis=1)
        column = lax.dynamic_index_in_dim(router_probs, expert, 1, False)
        shares[local] = jnp.where(members[local], column, 0.0)
    dpairs, hiddens, wholes, reduced = [], [], [], []
    last = len(chunks) - 1
    came, went = {}, {}

    def gather_all(at, *groups):
        gathered[at] = Gathered(packs[at], *groups)
        came[at] = (gathered[at].second(), gathered[at].third())

    def hop(arrivals, at, which):
        return arrivals[at][which] if at in arrivals else ()

    if planar:
        came[3] = (gathered[3].second(), gathered[3].third())
    for at, (kind, a, b) in enumerate(chunks):
        coef = jnp.concatenate([scale_b, shares[kind][:, None]], axis=1)
        if planar:
            if at == 1:
                coef = after(coef, hop(came, 3, 0))
                gather_all(4, (sums,))
            if at == 2:
                coef = after(coef, hop(came, 3, 1), hop(went, 0, 0))
                gather_all(5, (sums,))
            if at == 3:
                coef = after(coef, hop(came, 4, 0), hop(went, 1, 0), hop(went, 0, 1))
            if at == 4:
                dscaled_early = joint_back(dpairs, wholes, 0, f32)
                coef = after(
                    coef, (dscaled_early,), hop(came, 5, 0), hop(went, 2, 0), hop(went, 1, 1), hop(went, 0, 2)
                )
            if at == 5:
                moe_early = joint_back(hiddens, wholes, 2, f32)
                coef = after(coef, (moe_early,), hop(went, 3, 0), hop(went, 2, 1), hop(went, 1, 2))
        elif at == last:
            dscaled_early = joint_back(dpairs, wholes, 0, f32)
            moe_early = joint_back(hiddens, wholes, 2, f32)
        dpair, hidden, sums, grads, whole = expert_chunk(pieces_of(at), scaled, cot_rows, coef)
        dots[kind] = dots.get(kind, 0.0) + sums[:, 0]
        inner = inner + sums[:, 1]
        dpairs.append(dpair)
        hiddens.append(hidden)
        wholes.append(whole)
        one = Reduced(grads)
        reduced.append(one)
        if chained:
            went[at] = ((one.far_in, one.near_in), one.second(), one.third())
            went[at] = (went[at][0], (one.far_sum, one.near_sum), (one.exchanged,))
    first_late = 4 if planar else last
    late_pairs, late_wholes = dpairs[first_late:], wholes[first_late:]
    if planar:
        late_pairs[-1] = after(late_pairs[-1], hop(went, 4, 0), hop(went, 3, 1), hop(went, 2, 2))
    dscaled_part = joint_back(late_pairs, late_wholes, 0, bf16, dscaled_early, planar=planar)
    moe_part = joint_back(hiddens[last:], wholes[last:], 2, bf16, moe_early)

    named = [jnp.where(members[local], dots[local], 0.0) for local in range(local_experts)]
    table = lax.all_gather(jnp.stack(named + [dots[None], inner]), "col", axis=0)
    dprob = table[:, :local_experts].reshape(experts, tokens).T
    dshared_gate, inner = jnp.sum(table[:, local_experts], axis=0), jnp.sum(table[:, local_experts + 1], axis=0)
    dlogits = router_probs * (dprob - jnp.sum(dprob * router_probs, axis=1, keepdims=True))
    dslogit = dshared_gate * shared_gate * (1.0 - shared_gate)
    dboth = jnp.concatenate([dlogits, dslogit[:, None]], axis=1)
    inner = inner + jnp.sum(dboth * both_logits, axis=1)
    dboth = scale_b * dboth
    parts = split_three(dboth)
    stacked = mm_tn(jnp.concatenate(parts, axis=1), scaled)
    grad_router_part = stacked.reshape(3, experts + 1, width).sum(axis=0)
    grad_router_both = lax.psum_scatter(grad_router_part, "row", scatter_dimension=1, tiled=True)
    router_rows = lax.dynamic_slice_in_dim(router_full, col_id * share, share, 0)
    back_term = mm_nt(jnp.concatenate(parts, axis=1), jnp.concatenate([router_rows] * 3, axis=1))
    damp = scale_b * scale_b * inner[:, None] / width
    step_inputs = [back_term, grad_output, stream, damp, gain_b[None]]
    if planar:
        (dstream, dscaled), (dattn,), _ = plane_step(dscaled_part, dstream_step, step_inputs, 2, 1, 2)
    else:
        dscaled_sum = lax.psum_scatter(dscaled_part, "col", scatter_dimension=1, tiled=True)
        dstream_low, dstream, dscaled = dstream_step(dscaled_sum.astype(f32), *step_inputs)
        dattn = lax.all_gather(dstream_low.astype(bf16), "col", axis=1, tiled=True)
    gain_b_grad = jnp.sum(dscaled * stream, axis=0)

    moe_share = lax.psum_scatter(
        after(moe_part, (dattn,)), "col", scatter_dimension=1, tiled=True
    ).astype(f32)
    block_output = (stream + moe_share).astype(bf16)
    waits = hop(went, 4, 1) + hop(went, 3, 2) + hop(went, 5, 0)
    out_reduced = Reduced(mm_tn(dattn, context).astype(bf16))
    dcontext = after(mm(dattn, out_full).astype(bf16), waits)
    dqkv, inner_a = attend_backward(qkv, dcontext, lse, lengths, cosine, sine)
    waits = hop(went, 5, 1) + hop(went, 4, 2)
    out_reduced.second()
    dnormed_part = after(mm_nt(dqkv, qkv_full).astype(bf16), waits)
    dnormed_sum = lax.psum_scatter(dnormed_part, "col", scatter_dimension=1, tiled=True)
    qkv_reduced = Reduced(mm_tn(normed_a, dqkv).astype(bf16))
    out_reduced.third()
    qkv_reduced.second()
    qkv_reduced.third()
    inner_a = lax.psum(inner_a[:, 0], "col")[:, None]
    qkv_grad, out_grad = qkv_reduced.result(), out_reduced.result()
    unit_grads = [one.result() for one in reduced]
    dnormed_a = after(dnormed_sum, (inner_a,)).astype(f32)
    gain_a_share = input_gain.astype(f32)
    dinput = dstream + scale_a * gain_a_share * dnormed_a
    dinput = dinput - x_share * (scale_a * scale_a * inner_a / width)
    gain_a_grad = jnp.sum(dnormed_a * x_share * scale_a, axis=0)
    grad_gain_a, grad_gain_b = lax.psum((gain_a_grad, gain_b_grad), "row")

    qkv_grad = qkv_grad.reshape(rows_block, heads, 3, HEAD_DIM)
    grad_query, grad_key, grad_value = (
        qkv_grad[:, :, part].reshape(rows_block, head_width) for part in range(3)
    )
    def unpack(kind, which):
        found = []
        for (of, a, b), grad in zip(chunks, unit_grads):
            if of == kind:
                size = grad.shape[1] // 3
                part = grad[:, which * size : which * size + b - a]
                found.append((a, part.T if which == 2 else part))
        found = [part for _, part in sorted(found, key=lambda item: item[0])]
        return jnp.concatenate(found, axis=0 if which == 2 else 1)

    locals_ = range(local_experts)
    return (
        block_output,
        dinput.astype(bf16),
        grad_gain_a,
        grad_query,
        grad_key,
        grad_value,
        out_grad.T,
        grad_gain_b,
        grad_router_both[:experts].T,
        grad_router_both[experts],
        unpack(None, 0),
        unpack(None, 1),
        unpack(None, 2),
        jnp.stack([unpack(local, 0) for local in locals_]),
        jnp.stack([unpack(local, 1) for local in locals_]),
        jnp.stack([unpack(local, 2) for local in locals_]),
    )


def solution(mesh):
    return jax.shard_map(
        per_device,
        mesh=mesh,
        in_specs=(
            P("row", "col"),
            P(),
            P(),
            P("row", None),
            P("col"),
            P("row", "col"),
            P("row", "col"),
            P("row", "col"),
            P("col", "row"),
            P("col"),
            P("row", None),
            P("row"),
            P("row", "col"),
            P("row", "col"),
            P("col", "row"),
            P("col", "row", None),
            P("col", "row", None),
            P("col", None, "row"),
            P("row", "col"),
        ),
        out_specs=(
            P("row", "col"),
            P("row", "col"),
            P("col"),
            P("row", "col"),
            P("row", "col"),
            P("row", "col"),
            P("col", "row"),
            P("col"),
            P("row", None),
            P("row"),
            P("row", "col"),
            P("row", "col"),
            P("col", "row"),
            P("col", "row", None),
            P("col", "row", None),
            P("col", None, "row"),
        ),
        check_vma=False,
    )
```

```python
import functools
import math

import jax
import jax.numpy as jnp
from jax import lax
from jax.experimental import pallas as pl
from jax.experimental.pallas import tpu as pltpu
from jax.sharding import PartitionSpec as P

HEAD_DIM = 128
SEQ_LEN = 1024
QBLOCK = 256
TILE = 256
norm_eps = 1e-06
rope_base = 1000000.0
bf16 = jnp.bfloat16
f32 = jnp.float32


def mm(left, right):
    return jnp.dot(left, right, preferred_element_type=f32)


def mm_nt(left, right):
    return lax.dot_general(left, right, (((1,), (1,)), ((), ())), preferred_element_type=f32)


def mm_tn(left, right):
    return lax.dot_general(left, right, (((0,), (0,)), ((), ())), preferred_element_type=f32)


def rope_tables():
    positions = jnp.arange(SEQ_LEN).astype(f32)
    freqs = jnp.power(f32(rope_base), -jnp.arange(0, HEAD_DIM, 2).astype(f32) / HEAD_DIM)
    angles = positions[:, None] * freqs[None, :]
    cosine, sine = jnp.cos(angles), jnp.sin(angles)
    return (
        jnp.concatenate([cosine, cosine], axis=-1),
        jnp.concatenate([-sine, sine], axis=-1),
    )


def block_scores(rows, keys, start, length, scale):
    raw = mm_nt(rows, keys) * scale
    query_pos = start + lax.broadcasted_iota(jnp.int32, raw.shape, 0)
    key_pos = lax.broadcasted_iota(jnp.int32, raw.shape, 1)
    return jnp.where((key_pos <= query_pos) & (key_pos < length), raw, -1e30)


def attend_forward_kernel(length_ref, raw_ref, cos_ref, sin_ref, qkv_ref, context_ref, lse_ref):
    length = length_ref[pl.program_id(0)]
    scale = 1.0 / math.sqrt(HEAD_DIM)
    hd = HEAD_DIM
    for part in range(2):
        raw = raw_ref[:, part * hd : (part + 1) * hd]
        turned = raw * cos_ref[...] + pltpu.roll(raw, hd // 2, 1) * sin_ref[...]
        qkv_ref[:, part * hd : (part + 1) * hd] = turned.astype(bf16)
    qkv_ref[:, 2 * hd :] = raw_ref[:, 2 * hd :].astype(bf16)
    for at in range(0, SEQ_LEN, QBLOCK):
        seen = at + QBLOCK
        scores = block_scores(
            qkv_ref[at:seen, :hd], qkv_ref[:seen, hd : 2 * hd], at, length, scale
        )
        top = jnp.max(scores, axis=-1, keepdims=True)
        expo = jnp.exp(scores - top)
        total = jnp.sum(expo, axis=-1, keepdims=True)
        probs = (expo / total).astype(bf16)
        context_ref[at:seen, :] = mm(probs, qkv_ref[:seen, 2 * hd :]).astype(bf16)
        lse_ref[at:seen, :] = jnp.broadcast_to(top + jnp.log(total), (QBLOCK, hd))


def attend_forward(raw, lengths, cosine, sine):
    tokens, width = raw.shape
    heads = width // (3 * HEAD_DIM)
    slots = tokens // SEQ_LEN
    wide = pl.BlockSpec((SEQ_LEN, 3 * HEAD_DIM), lambda s, h, _: (s, h))
    one = pl.BlockSpec((SEQ_LEN, HEAD_DIM), lambda s, h, _: (s, h))
    table = pl.BlockSpec((SEQ_LEN, HEAD_DIM), lambda s, h, _: (0, 0))
    pairs = slots * heads * SEQ_LEN * SEQ_LEN
    return pl.pallas_call(
        attend_forward_kernel,
        grid_spec=pltpu.PrefetchScalarGridSpec(
            num_scalar_prefetch=1,
            grid=(slots, heads),
            in_specs=[wide, table, table],
            out_specs=[wide, one, one],
        ),
        out_shape=[
            jax.ShapeDtypeStruct((tokens, width), bf16),
            jax.ShapeDtypeStruct((tokens, heads * HEAD_DIM), bf16),
            jax.ShapeDtypeStruct((tokens, heads * HEAD_DIM), f32),
        ],
        cost_estimate=pl.CostEstimate(
            flops=3 * HEAD_DIM * pairs, bytes_accessed=8 * tokens * width, transcendentals=pairs
        ),
        name="attend_forward",
    )(lengths, raw, cosine, sine)


def attend_backward_kernel(
    length_ref, qkv_ref, dcontext_ref, lse_ref, cos_ref, sin_ref, dqkv_ref, inner_ref, dk_ref, dv_ref
):
    length = length_ref[pl.program_id(0)]
    scale = 1.0 / math.sqrt(HEAD_DIM)
    hd = HEAD_DIM
    @pl.when(pl.program_id(1) == 0)
    def _():
        inner_ref[...] = jnp.zeros_like(inner_ref)

    dk_ref[...] = jnp.zeros_like(dk_ref)
    dv_ref[...] = jnp.zeros_like(dv_ref)

    def turn_back(grad, rows):
        back = grad * cos_ref[rows, :] - pltpu.roll(grad, hd // 2, 1) * sin_ref[rows, :]
        return back.astype(bf16)

    for at in range(0, SEQ_LEN, QBLOCK):
        seen = at + QBLOCK
        rows = qkv_ref[at:seen, :hd]
        keys = qkv_ref[:seen, hd : 2 * hd]
        drows = dcontext_ref[at:seen, :]
        scores = block_scores(rows, keys, at, length, scale)
        probs = jnp.exp(scores - lse_ref[at:seen, :1])
        dv_ref[:seen, :] += mm_tn(probs.astype(bf16), drows)
        dprobs = mm_nt(drows, qkv_ref[:seen, 2 * hd :])
        dscore = probs * (dprobs - jnp.sum(dprobs * probs, axis=-1, keepdims=True))
        draw = (dscore * scale).astype(bf16)
        dquery = mm(draw, keys)
        dk_ref[:seen, :] += mm_tn(draw, rows)
        dqkv_ref[at:seen, :hd] = turn_back(dquery, slice(at, seen))
        inner_ref[at:seen, :] += jnp.sum(dquery * rows.astype(f32), axis=-1, keepdims=True)
    dkey, dvalue = dk_ref[...], dv_ref[...]
    dqkv_ref[:, hd : 2 * hd] = turn_back(dkey, slice(None))
    dqkv_ref[:, 2 * hd :] = dvalue.astype(bf16)
    inner_ref[...] += jnp.sum(
        dkey * qkv_ref[:, hd : 2 * hd].astype(f32) + dvalue * qkv_ref[:, 2 * hd :].astype(f32),
        axis=-1,
        keepdims=True,
    )


def attend_backward(qkv, dcontext, lse, lengths, cosine, sine):
    tokens, width = qkv.shape
    heads = width // (3 * HEAD_DIM)
    slots = tokens // SEQ_LEN
    wide = pl.BlockSpec((SEQ_LEN, 3 * HEAD_DIM), lambda s, h, _: (s, h))
    one = pl.BlockSpec((SEQ_LEN, HEAD_DIM), lambda s, h, _: (s, h))
    table = pl.BlockSpec((SEQ_LEN, HEAD_DIM), lambda s, h, _: (0, 0))
    pairs = slots * heads * SEQ_LEN * SEQ_LEN
    return pl.pallas_call(
        attend_backward_kernel,
        grid_spec=pltpu.PrefetchScalarGridSpec(
            num_scalar_prefetch=1,
            grid=(slots, heads),
            in_specs=[wide, one, one, table, table],
            out_specs=[wide, pl.BlockSpec((SEQ_LEN, 1), lambda s, h, _: (s, 0))],
            scratch_shapes=[pltpu.VMEM((SEQ_LEN, HEAD_DIM), f32)] * 2,
        ),
        out_shape=[
            jax.ShapeDtypeStruct((tokens, width), bf16),
            jax.ShapeDtypeStruct((tokens, 1), f32),
        ],
        cost_estimate=pl.CostEstimate(
            flops=8 * HEAD_DIM * pairs, bytes_accessed=8 * tokens * width, transcendentals=pairs
        ),
        name="attend_backward",
    )(lengths, qkv, dcontext, lse, cosine, sine)


PAIRS = [(0, 1), (1, 0), (2, 3), (3, 2)]
MIDDLE = [(1, 2), (2, 1)]
OUTWARD = [(1, 0), (2, 3)]
INWARD = [(0, 1), (3, 2)]


class Gathered:
    def __init__(self, part, *groups):
        self.part = part
        if lax.axis_size("row") != 4:
            self.pieces = (lax.all_gather(part, "row", axis=0, tiled=True),)
            return
        part = after(part, *groups)
        self.partner = lax.ppermute(part, "row", PAIRS)
        self.near_mid = lax.ppermute(part, "row", MIDDLE)
        self.pieces = None

    def second(self, *groups):
        if self.pieces is None:
            self.near_out = lax.ppermute(after(self.near_mid, *groups), "row", OUTWARD)
            self.far_mid = lax.ppermute(after(self.partner, *groups), "row", MIDDLE)
            return (self.partner, self.near_mid)
        return ()

    def third(self, *groups):
        if self.pieces is None:
            self.far_out = lax.ppermute(after(self.far_mid, *groups), "row", OUTWARD)
            self.pieces = (
                self.part, self.partner, self.near_mid, self.far_mid, self.near_out, self.far_out
            )
            return (self.far_mid, self.near_out)
        return ()


def places(z):
    pair = z // 2
    return z, z + 1 - 2 * lax.rem(z, 2), 2 - pair, 3 - 3 * pair


class RowGather:
    def __init__(self, packs, wholes, sems):
        self.packs, self.wholes, (self.send_sems, self.recv_sems) = packs, wholes, sems
        self.z = lax.axis_index("row")
        self.own, self.partner, self.near, self.far = places(self.z)
        self.across = 3 - self.z
        self.in_middle = (self.z == 1) | (self.z == 2)
        self.outside = jnp.logical_not(self.in_middle)

    def copy_of(self, kind, at, source, block, target):
        return pltpu.make_async_remote_copy(
            src_ref=source,
            dst_ref=self.wholes[at].at[block],
            send_sem=self.send_sems.at[kind, at],
            recv_sem=self.recv_sems.at[kind, at],
            device_id={"row": target},
            device_id_type=pl.DeviceIdType.MESH,
        )

    def swap(self, at):
        return self.copy_of(0, at, self.packs[at], self.own, self.partner)

    def swap_middle(self, at):
        return self.copy_of(1, at, self.packs[at], self.own, self.across)

    def second_middle(self, at):
        return self.copy_of(2, at, self.wholes[at].at[self.partner], self.partner, self.across)

    def hand_near(self, at):
        return self.copy_of(3, at, self.wholes[at].at[self.near], self.near, self.partner)

    def hand_far(self, at):
        return self.copy_of(4, at, self.wholes[at].at[self.far], self.far, self.partner)

    def greet(self, barrier):
        signal_to(barrier, {"row": self.partner})

        @pl.when(self.in_middle)
        def _():
            signal_to(barrier, {"row": self.across})
            pl.semaphore_wait(barrier, 2)

        @pl.when(self.outside)
        def _():
            pl.semaphore_wait(barrier, 1)

    def begin(self):
        for at in range(len(self.packs)):
            @pl.when(self.in_middle)
            def _():
                self.swap_middle(at).start()

            self.swap(at).start()

    def hand_on(self, at):
        @pl.when(self.in_middle)
        def _():
            self.swap_middle(at).wait_recv()
            self.hand_near(at).start()
            self.swap(at).wait_recv()
            self.second_middle(at).start()

    def hand_last(self, at):
        @pl.when(self.in_middle)
        def _():
            self.second_middle(at).wait_recv()
            self.hand_far(at).start()

    def finish(self):
        for at in range(len(self.packs)):
            @pl.when(self.in_middle)
            def _():
                for copy in (
                    self.swap,
                    self.swap_middle,
                    self.second_middle,
                    self.hand_near,
                    self.hand_far,
                ):
                    copy(at).wait_send()

            @pl.when(self.outside)
            def _():
                self.swap(at).wait()
                self.hand_near(at).wait_recv()
                self.hand_far(at).wait_recv()


class RowReduce:
    def __init__(self, grads, total, refs):
        self.grads, self.total = grads, total
        self.far_in, self.near_in, self.far_sum, self.near_sum, self.last = refs[:5]
        self.held, self.more, self.send_sems, self.recv_sems, self.local_sems = refs[5:]
        self.z = lax.axis_index("row")
        self.own, self.partner, self.near, self.far = places(self.z)
        self.across = 3 - self.z
        self.in_middle = (self.z == 1) | (self.z == 2)
        self.outside = jnp.logical_not(self.in_middle)

    def copy_of(self, kind, source, target, device):
        return pltpu.make_async_remote_copy(
            src_ref=source,
            dst_ref=target,
            send_sem=self.send_sems.at[kind],
            recv_sem=self.recv_sems.at[kind],
            device_id={"row": device},
            device_id_type=pl.DeviceIdType.MESH,
        )

    def send_far(self):
        return self.copy_of(0, self.grads.at[self.far], self.far_in, self.partner)

    def send_near(self):
        return self.copy_of(1, self.grads.at[self.near], self.near_in, self.partner)

    def cross_far(self):
        return self.copy_of(2, self.far_in, self.far_sum, self.across)

    def cross_near(self):
        return self.copy_of(3, self.near_in, self.near_sum, self.across)

    def swap_middle(self):
        return self.copy_of(4, self.far_sum, self.last, self.partner)

    def swap_outer(self):
        return self.copy_of(4, self.grads.at[self.partner], self.last, self.partner)

    def load(self, kind, block):
        target = self.more if kind % 2 else self.held
        return pltpu.make_async_copy(self.grads.at[block], target, self.local_sems.at[kind])

    def add(self, target, source):
        @pl.loop(0, target.shape[0], step=64)
        def _(at):
            tile = pl.ds(pl.multiple_of(at, 64), 64)
            target[tile, :] = (target[tile, :].astype(f32) + source[tile, :].astype(f32)).astype(bf16)

    def begin(self):
        @pl.when(self.outside)
        def _():
            self.send_far().start()
            self.send_near().start()
            self.swap_outer().start()
            self.load(3, self.own).start()

        @pl.when(self.in_middle)
        def _():
            self.load(0, self.far).start()
            self.load(1, self.near).start()

    def second_far(self):
        @pl.when(self.in_middle)
        def _():
            self.load(0, self.far).wait()
            self.send_far().wait_recv()
            self.add(self.far_in, self.held)
            self.cross_far().start()
            self.load(2, self.partner).start()

    def second_near(self):
        @pl.when(self.in_middle)
        def _():
            self.load(1, self.near).wait()
            self.send_near().wait_recv()
            self.add(self.near_in, self.more)
            self.cross_near().start()
            self.load(3, self.own).start()

    def third(self):
        @pl.when(self.in_middle)
        def _():
            self.load(2, self.partner).wait()
            self.cross_far().wait_recv()
            self.add(self.far_sum, self.held)
            self.swap_middle().start()

    def finish(self):
        self.load(3, self.own).wait()
        self.swap_outer().wait_recv()

        @pl.when(self.in_middle)
        def _():
            self.cross_near().wait_recv()

        @pl.loop(0, self.total.shape[0], step=64)
        def _(at):
            tile = pl.ds(pl.multiple_of(at, 64), 64)
            self.total[tile, :] = self.more[tile, :].astype(f32) + self.last[tile, :].astype(f32)

        @pl.when(self.in_middle)
        def _():
            @pl.loop(0, self.total.shape[0], step=64)
            def _(at):
                tile = pl.ds(pl.multiple_of(at, 64), 64)
                self.total[tile, :] += self.near_sum[tile, :].astype(f32)

            self.cross_far().wait_send()
            self.cross_near().wait_send()
            self.swap_middle().wait_send()

        @pl.when(self.outside)
        def _():
            self.send_far().wait_send()
            self.send_near().wait_send()
            self.swap_outer().wait_send()


def signal_to(barrier, device):
    pl.semaphore_signal(barrier, inc=1, device_id=device, device_id_type=pl.DeviceIdType.MESH)


def gather_kernel(count, *refs):
    rows = RowGather(refs[:count], refs[count : 2 * count], refs[2 * count :])
    rows.greet(pltpu.get_barrier_semaphore())
    rows.begin()
    for at in range(count):
        rows.hand_on(at)
    for at in range(count):
        rows.hand_last(at)
    rows.finish()


PIECES = 4


def plane_kernel(pointwise, given, made, gather, count, reducing, *refs):
    p_ref, inputs = refs[0], refs[1 : 1 + given]
    at = 1 + given
    packs = refs[at : at + count]
    at += count
    grads = refs[at] if reducing else None
    at += reducing
    results = refs[at : at + made]
    at += made
    total_ref = refs[at] if reducing else None
    at += reducing
    whole_refs = refs[at : at + gather + count]
    at += gather + count
    mine, from_core, from_first, summed, from_second, shared, send_sems, recv_sems, local_sems = refs[
        at : at + 9
    ]
    out_ref = whole_refs[0] if gather else None
    me = lax.axis_index("col")
    core, x, y = lax.rem(me, 2), lax.rem(me // 2, 2), me // 4
    core_mate, x_mate, y_mate = me + 1 - 2 * core, me + 2 - 4 * x, me + 4 - 8 * y
    diagonal = x_mate + 4 - 8 * y
    size = mine.shape[3]
    share = mine.shape[4]
    barrier = pltpu.get_barrier_semaphore()
    for mate in (core_mate, x_mate, y_mate):
        signal_to(barrier, {"col": mate})
    rows, reduction = None, None
    if count or reducing:
        if count:
            rows = RowGather(packs, whole_refs[gather:], refs[at + 9 : at + 11])
            at += 2
        if reducing:
            reduction = RowReduce(grads, total_ref, refs[at + 9 : at + 19])
        chain = rows or reduction
        signal_to(barrier, {"row": chain.partner})

        @pl.when(chain.in_middle)
        def _():
            signal_to(barrier, {"row": chain.across})
            pl.semaphore_wait(barrier, 5)

        @pl.when(chain.outside)
        def _():
            pl.semaphore_wait(barrier, 4)

        if count:
            rows.begin()
        if reducing:
            reduction.begin()
    else:
        pl.semaphore_wait(barrier, 3)

    def remote(kind, i, source, target, mate):
        return pltpu.make_async_remote_copy(
            src_ref=source,
            dst_ref=target,
            send_sem=send_sems.at[kind, i],
            recv_sem=recv_sems.at[kind, i],
            device_id={"col": mate},
            device_id_type=pl.DeviceIdType.MESH,
        )

    def x_first(i):
        return i < PIECES // 2

    def span(i):
        return pl.ds(i * size, size)

    def core_copy(i):
        return remote(0, i, p_ref.at[:, :, 1 - core, span(i), :], from_core.at[i], core_mate)

    def load(i):
        return pltpu.make_async_copy(
            p_ref.at[:, :, core, span(i), :], mine.at[i], local_sems.at[0, i]
        )

    def first_copy(i):
        if x_first(i):
            return remote(1, i, mine.at[i, :, 1 - x], from_first.at[i], x_mate)
        return remote(1, i, mine.at[i, 1 - y], from_first.at[i], y_mate)

    def second_copy(i):
        if x_first(i):
            return remote(2, i, summed.at[i, 1 - y], from_second.at[i], y_mate)
        return remote(2, i, summed.at[i, 1 - x], from_second.at[i], x_mate)

    def columns(i, device):
        return out_ref.at[span(i), pl.ds(pl.multiple_of(device * share, share), share)]

    def spread(kind, i, mate):
        return remote(kind, i, shared.at[i], columns(i, me), mate)

    def keep(i):
        return pltpu.make_async_copy(shared.at[i], columns(i, me), local_sems.at[1, i])

    def pass_on(kind, i, device, mate):
        return remote(kind, i, columns(i, device), columns(i, device), mate)

    def forward(i):
        if x_first(i):
            return pass_on(6, i, y_mate, x_mate)
        return pass_on(6, i, x_mate, y_mate)

    order = [0, 2, 1, 3]
    for i in order:
        core_copy(i).start()
        load(i).start()
    for i in order:
        load(i).wait()
        core_copy(i).wait_recv()
        for a in range(2):
            for b in range(2):
                mine[i, a, b] = (mine[i, a, b].astype(f32) + from_core[i, a, b].astype(f32)).astype(bf16)
        first_copy(i).start()
    for i in order:
        first_copy(i).wait_recv()
        for a in range(2):
            kept = mine[i, a, x] if x_first(i) else mine[i, y, a]
            summed[i, a] = (kept.astype(f32) + from_first[i, a].astype(f32)).astype(bf16)
        second_copy(i).start()
    if count:
        for at in range(count):
            rows.hand_on(at)
    if reducing:
        reduction.second_far()
    for i in order:
        second_copy(i).wait_recv()
        total = summed[i, y if x_first(i) else x].astype(f32) + from_second[i].astype(f32)
        span_rows = slice(i * size, (i + 1) * size)
        values = pointwise(
            total, *[ref[span_rows, :] if ref.shape[0] > 8 else ref[...] for ref in inputs]
        )
        if gather:
            shared[i] = values[0].astype(bf16)
            values = values[1:]
        for ref, value in zip(results, values):
            ref[span_rows, :] = value
        if gather:
            spread(4, i, x_mate).start()
            spread(5, i, y_mate).start()
            spread(3, i, core_mate).start()
            keep(i).start()
    if count:
        rows.hand_last(0)
    if reducing and not gather:
        reduction.second_near()
    if gather:
        for i in order:
            spread(5 if x_first(i) else 4, i, y_mate).wait_recv()
            forward(i).start()
            pass_on(7, i, y_mate if x_first(i) else x_mate, core_mate).start()
        for i in order:
            spread(4 if x_first(i) else 5, i, x_mate).wait_recv()
            pass_on(8, i, x_mate if x_first(i) else y_mate, core_mate).start()
    if count:
        for at in range(1, count):
            rows.hand_last(at)
    if reducing and gather:
        reduction.second_near()
    if reducing:
        reduction.third()
    if gather:
        for i in order:
            forward(i).wait_recv()
            pass_on(9, i, diagonal, core_mate).start()
    for i in order:
        core_copy(i).wait_send()
        first_copy(i).wait_send()
        second_copy(i).wait_send()
        if gather:
            keep(i).wait()
            spread(3, i, core_mate).wait()
            spread(4, i, x_mate).wait_send()
            spread(5, i, y_mate).wait_send()
            forward(i).wait_send()
            for kind, device in (
                (7, y_mate if x_first(i) else x_mate),
                (8, x_mate if x_first(i) else y_mate),
                (9, diagonal),
            ):
                pass_on(kind, i, device, core_mate).wait()
    if count:
        rows.finish()
    if reducing:
        reduction.finish()


def plane_step(partial, pointwise, inputs, made, gather, number, packs=(), grads=None):
    tokens, share = partial.shape[3:]
    size = tokens // PIECES
    count = len(packs)
    reducing = 0 if grads is None else 1
    totals, more_scratch, given_grads = [], [], []
    if reducing:
        block, columns = grads.shape[0] // 4, grads.shape[1]
        given_grads = [grads.reshape(4, block, columns)]
        totals = [jax.ShapeDtypeStruct((block, columns), f32)]
        more_scratch = [pltpu.VMEM((block, columns), bf16)] * 7 + [
            pltpu.SemaphoreType.DMA((5,)),
            pltpu.SemaphoreType.DMA((5,)),
            pltpu.SemaphoreType.DMA((4,)),
        ]
    anywhere = pl.BlockSpec(memory_space=pl.ANY)
    vmem = pl.BlockSpec(memory_space=pltpu.VMEM)
    whole_shapes = [jax.ShapeDtypeStruct((tokens, 8 * share), bf16)] * gather + [
        jax.ShapeDtypeStruct((4,) + pack.shape, bf16) for pack in packs
    ]
    outs = pl.pallas_call(
        functools.partial(plane_kernel, pointwise, len(inputs), made, gather, count, reducing),
        in_specs=[anywhere] + [vmem] * len(inputs) + [anywhere] * (count + reducing),
        out_specs=[vmem] * (made + reducing) + [anywhere] * (gather + count),
        out_shape=[jax.ShapeDtypeStruct((tokens, share), f32)] * made + totals + whole_shapes,
        scratch_shapes=[
            pltpu.VMEM((PIECES, 2, 2, size, share), bf16),
            pltpu.VMEM((PIECES, 2, 2, size, share), bf16),
            pltpu.VMEM((PIECES, 2, size, share), bf16),
            pltpu.VMEM((PIECES, 2, size, share), bf16),
            pltpu.VMEM((PIECES, size, share), bf16),
            pltpu.VMEM((PIECES, size, share), bf16),
            pltpu.SemaphoreType.DMA((10, PIECES)),
            pltpu.SemaphoreType.DMA((10, PIECES)),
            pltpu.SemaphoreType.DMA((2, PIECES)),
        ]
        + [pltpu.SemaphoreType.DMA((5, count))] * (2 if count else 0)
        + more_scratch,
        compiler_params=pltpu.CompilerParams(collective_id=number, has_side_effects=True),
        cost_estimate=pl.CostEstimate(
            flops=60 * 10**9, bytes_accessed=32 * tokens * share, transcendentals=0
        ),
        name="plane_step",
    )(partial, *inputs, *packs, *given_grads)
    at = made + reducing
    wholes = [whole.reshape((4 * whole.shape[1],) + whole.shape[2:]) for whole in outs[at + gather :]]
    return outs[:at], outs[at : at + gather], wholes


def gather_now(packs, number):
    if lax.axis_size("row") != 4:
        return [lax.all_gather(pack, "row", axis=0, tiled=True) for pack in packs]
    count = len(packs)
    sent = sum(pack.size for pack in packs) * 2
    anywhere = pl.BlockSpec(memory_space=pl.ANY)
    wholes = pl.pallas_call(
        functools.partial(gather_kernel, count),
        in_specs=[anywhere] * count,
        out_specs=[anywhere] * count,
        out_shape=[jax.ShapeDtypeStruct((4,) + pack.shape, pack.dtype) for pack in packs],
        scratch_shapes=[pltpu.SemaphoreType.DMA((5, count)), pltpu.SemaphoreType.DMA((5, count))],
        compiler_params=pltpu.CompilerParams(collective_id=number, has_side_effects=True),
        cost_estimate=pl.CostEstimate(
            flops=6 * 9000 * sent, bytes_accessed=6 * sent, transcendentals=0
        ),
        name="gather_rows",
    )(*packs)
    return [whole.reshape((4 * whole.shape[1],) + whole.shape[2:]) for whole in wholes]


def put_own(whole, part):
    if lax.axis_size("row") != 4:
        return whole
    return lax.dynamic_update_slice_in_dim(
        whole, part, lax.axis_index("row") * part.shape[0], 0
    )


class Reduced:
    def __init__(self, grads):
        self.chained = lax.axis_size("row") == 4
        if not self.chained:
            self.total = lax.psum_scatter(grads, "row", scatter_dimension=0, tiled=True).astype(f32)
            self.hops = ((), (), ())
            return
        z = lax.axis_index("row")
        own, partner, _, _ = places(z)
        size = grads.shape[0] // 4
        other = (1 - z // 2) * 2 * size

        def rows_of(value, at, count):
            return lax.dynamic_slice_in_dim(value, at, count, 0)

        pair = rows_of(grads, other, 2 * size)
        first = lax.ppermute(pair, "row", INWARD)
        second = lax.ppermute(
            (pair.astype(f32) + first.astype(f32)).astype(bf16), "row", MIDDLE
        )
        swapped = rows_of(grads, partner * size, size).astype(f32) + rows_of(
            second, lax.rem(partner, 2) * size, size
        ).astype(f32)
        third = lax.ppermute(swapped.astype(bf16), "row", PAIRS)
        self.total = (
            rows_of(grads, own * size, size).astype(f32)
            + rows_of(second, lax.rem(own, 2) * size, size).astype(f32)
            + third.astype(f32)
        )
        self.hops = ((first,), (second,), (third,))


def after(value, *groups):
    others = tuple(item for group in groups for item in group)
    return lax.optimization_barrier((value,) + others)[0] if others else value


def expert_kernel(size, steps, count, z_ref, *refs):
    pieces = refs[:count]
    (x_ref, cot_ref, x_cols, cot_cols, coef_ref) = refs[count : count + 5]
    (dpair_ref, hidden_ref, sums_ref, grads_ref, whole_ref) = refs[count + 5 : count + 10]
    weights, dpair, hidden, sems, out_sem = refs[count + 10 :]
    step = pl.program_id(0)
    write = pltpu.make_async_copy(weights, whole_ref, out_sem)

    @pl.when(step == 0)
    def _():
        if count == 1:
            copy = pltpu.make_async_copy(pieces[0], weights, sems.at[0])
            copy.start()
            copy.wait()
        elif count == 2:
            block = pieces[0].shape[0]

            def block_copy(back):
                at = pl.multiple_of(lax.rem(z_ref[0] + back, 4) * block, block)
                source = pieces[1].at[pl.ds(at, block)] if back else pieces[0]
                return pltpu.make_async_copy(source, weights.at[pl.ds(at, block)], sems.at[back])

            for back in range(4):
                block_copy(back).start()
            for back in range(4):
                block_copy(back).wait()
        else:
            z = z_ref[0]
            block = pieces[0].shape[0]

            def copy_of(piece, which):
                at = pl.multiple_of(places(z)[which] * block, block)
                return pltpu.make_async_copy(
                    piece, weights.at[pl.ds(at, block)], sems.at[which]
                )

            copy_of(pieces[0], 0).start()
            copy_of(pieces[1], 1).start()
            in_middle = (z == 1) | (z == 2)

            @pl.when(in_middle)
            def _():
                copy_of(pieces[2], 2).start()
                copy_of(pieces[3], 3).start()

            @pl.when(jnp.logical_not(in_middle))
            def _():
                copy_of(pieces[4], 2).start()
                copy_of(pieces[5], 3).start()

            for which in range(4):
                copy_of(pieces[which], which).wait()
        write.start()

    @pl.when(step < steps)
    def _():
        at = pl.multiple_of(step * TILE, TILE)
        rows, cots = x_ref[...], cot_ref[...]
        scale, weight = coef_ref[:, 0:1], coef_ref[:, 1:2]
        dots = jnp.zeros((TILE, 1), f32)
        inner = jnp.zeros((TILE, 1), f32)
        for a in range(0, size, TILE):
            b = min(a + TILE, size)
            gate = scale * mm(rows, weights[:, a:b])
            up = scale * mm(rows, weights[:, size + a : size + b])
            dhid = mm(cots, weights[:, 2 * size + a : 2 * size + b])
            sigma = jax.nn.sigmoid(gate)
            silu = gate * sigma
            hid = silu * up
            dots += jnp.sum(hid * dhid, axis=1, keepdims=True)
            dhid = weight * dhid
            dgate = dhid * up * sigma * (1.0 + gate * (1.0 - sigma))
            dup = dhid * silu
            inner += jnp.sum(dgate * gate + dup * up, axis=1, keepdims=True)
            for into, at_col, value in (
                ((hidden_ref, hidden), a, weight * hid),
                ((dpair_ref, dpair), a, scale * dgate),
                ((dpair_ref, dpair), size + a, scale * dup),
            ):
                value = value.astype(bf16)
                into[0][:, at_col : at_col + b - a] = value
                into[1][pl.ds(at, TILE), at_col : at_col + b - a] = value
        sums_ref[:, 0:1] = dots
        sums_ref[:, 1:2] = inner

    @pl.when(step >= steps)
    def _():
        for a in range(0, 2 * size, TILE):
            b = min(a + TILE, 2 * size)
            grads_ref[:, a:b] = mm_tn(x_cols[...], dpair[:, a:b]).astype(bf16)
        for a in range(0, size, TILE):
            b = min(a + TILE, size)
            grads_ref[:, 2 * size + a : 2 * size + b] = mm_tn(
                cot_cols[...], hidden[:, a:b]
            ).astype(bf16)

    @pl.when(step == pl.num_programs(0) - 1)
    def _():
        write.wait()


def expert_chunk(pieces, scaled, cots, coef):
    tokens, width = scaled.shape
    size = pieces[0].shape[1] // 3
    steps, more = tokens // TILE, width // TILE
    count = len(pieces)
    rows = lambda i, _: (jnp.minimum(i, steps - 1), 0)
    cols = lambda i, _: (0, jnp.maximum(i - steps, 0))
    down = lambda i, _: (jnp.maximum(i - steps, 0), 0)
    z = jnp.reshape(lax.axis_index("row"), (1,)).astype(jnp.int32)
    return pl.pallas_call(
        functools.partial(expert_kernel, size, steps, count),
        grid_spec=pltpu.PrefetchScalarGridSpec(
            num_scalar_prefetch=1,
            grid=(steps + more,),
            in_specs=[pl.BlockSpec(memory_space=pl.ANY)] * count
            + [
                pl.BlockSpec((TILE, width), rows),
                pl.BlockSpec((TILE, width), rows),
                pl.BlockSpec((tokens, TILE), cols),
                pl.BlockSpec((tokens, TILE), cols),
                pl.BlockSpec((TILE, 2), rows),
            ],
            out_specs=[
                pl.BlockSpec((TILE, 2 * size), rows),
                pl.BlockSpec((TILE, size), rows),
                pl.BlockSpec((TILE, 2), rows),
                pl.BlockSpec((TILE, 3 * size), down),
                pl.BlockSpec(memory_space=pl.ANY),
            ],
            scratch_shapes=[
                pltpu.VMEM((width, 3 * size), bf16),
                pltpu.VMEM((tokens, 2 * size), bf16),
                pltpu.VMEM((tokens, size), bf16),
                pltpu.SemaphoreType.DMA((4,)),
                pltpu.SemaphoreType.DMA,
            ],
        ),
        out_shape=[
            jax.ShapeDtypeStruct((tokens, 2 * size), bf16),
            jax.ShapeDtypeStruct((tokens, size), bf16),
            jax.ShapeDtypeStruct((tokens, 2), f32),
            jax.ShapeDtypeStruct((width, 3 * size), bf16),
            jax.ShapeDtypeStruct((width, 3 * size), bf16),
        ],
        cost_estimate=pl.CostEstimate(
            flops=12 * tokens * width * size,
            bytes_accessed=8 * tokens * width + 24 * width * size,
            transcendentals=tokens * size,
        ),
        name="expert_chunk",
    )(z, *pieces, scaled, cots, scaled, cots, coef)


def joint_kernel(count, based, planar, *refs):
    out_ref = refs[-1]
    for a in range(0, refs[count].shape[0], TILE):
        total = refs[2 * count][:, a : a + TILE] if based else None
        for left, weights in zip(refs[:count], refs[count : 2 * count]):
            part = mm_nt(left[...], weights[a : a + TILE, :])
            total = part if total is None else total + part
        if planar:
            at = a // TILE
            out_ref[at // 4, at // 2 % 2, at % 2] = total.astype(out_ref.dtype)
        else:
            out_ref[:, a : a + TILE] = total.astype(out_ref.dtype)


def joint_back(lefts, weights, column, kind, *base, planar=False):
    tokens, width = lefts[0].shape[0], weights[0].shape[0]
    row = lambda i: (i, 0)
    fixed = lambda i: (0, column)
    depth = sum(left.shape[1] for left in lefts)
    return pl.pallas_call(
        functools.partial(joint_kernel, len(lefts), len(base) > 0, planar),
        grid=(tokens // TILE,),
        in_specs=[pl.BlockSpec((TILE, left.shape[1]), row) for left in lefts]
        + [
            pl.BlockSpec((width, left.shape[1]), fixed, pipeline_mode=pl.Buffered(1))
            for left in lefts
        ]
        + [pl.BlockSpec((TILE, width), row)] * len(base),
        out_specs=pl.BlockSpec((2, 2, 2, TILE, TILE), lambda i: (0, 0, 0, i, 0))
        if planar
        else pl.BlockSpec((TILE, width), row),
        out_shape=jax.ShapeDtypeStruct((2, 2, 2, tokens, TILE) if planar else (tokens, width), kind),
        cost_estimate=pl.CostEstimate(
            flops=2 * tokens * width * depth,
            bytes_accessed=2 * (tokens + width) * depth + 4 * tokens * width,
            transcendentals=0,
        ),
        name="joint_back",
    )(*lefts, *weights, *base)


def split_three(values):
    high = values.astype(bf16)
    rest = values - high.astype(f32)
    middle = rest.astype(bf16)
    return high, middle, (rest - middle.astype(f32)).astype(bf16)


def cuts_of(width, sizes):
    cuts, at = [], 0
    for size in sizes:
        if at + size < width:
            cuts.append((at, at + size))
            at += size
    return cuts + [(at, width)]


def stream_step(total, rows, gain):
    stream = rows.astype(f32) + total
    return stream * gain, stream


def dstream_step(total, back, cots, stream, damp, gain):
    dscaled = back + total
    dstream = cots.astype(f32) + gain * dscaled - stream * damp
    return dstream, dstream, dscaled


def per_device(
    block_input,
    seq_lengths,
    slot_order,
    routes,
    input_gain,
    query_weight,
    key_weight,
    value_weight,
    output_weight,
    mlp_gain,
    router_weight,
    score_shared,
    gate_shared,
    up_shared,
    down_shared,
    gate_expert,
    up_expert,
    down_expert,
    grad_output,
):
    tokens, share = block_input.shape
    cols = lax.axis_size("col")
    col_id = lax.axis_index("col")
    row_id = lax.axis_index("row")
    width = share * cols
    slots = tokens // SEQ_LEN
    local_experts = gate_expert.shape[0]
    experts = router_weight.shape[1]
    head_width = query_weight.shape[1]
    heads = head_width // HEAD_DIM
    rows_block = query_weight.shape[0]
    lengths = lax.dynamic_slice_in_dim(seq_lengths[slot_order], row_id * slots, slots, 0)
    cosine, sine = rope_tables()

    def by_head(weight):
        return weight.reshape(rows_block, heads, 1, HEAD_DIM)

    qkv_pack = jnp.concatenate(
        [by_head(query_weight), by_head(key_weight), by_head(value_weight)], axis=2
    ).reshape(rows_block, 3 * head_width)
    router_pack = jnp.concatenate([router_weight, score_shared[:, None]], axis=1)
    router_pack = jnp.pad(router_pack, ((0, 0), (0, -router_pack.shape[1] % 128)))
    out_pack = jnp.concatenate([output_weight.T, router_pack], axis=1)
    qkv_whole, out_whole = gather_now([qkv_pack, out_pack], 0)
    qkv_full, out_weights = put_own(qkv_whole, qkv_pack), put_own(out_whole, out_pack)
    out_full = out_weights[:, :head_width]
    router_full = out_weights[:, head_width : head_width + experts + 1]
    shared_cuts = [(None, a, b) for a, b in cuts_of(gate_shared.shape[1], (512,))]
    expert_cuts = [
        (local, a, b)
        for local in range(local_experts)
        for a, b in cuts_of(gate_expert.shape[2], (512, 512))
    ]
    chunks = shared_cuts[-1:] + expert_cuts[:-1] + shared_cuts[:-1] + expert_cuts[-1:]

    def pack(kind, a, b):
        if kind is None:
            parts = [gate_shared[:, a:b], up_shared[:, a:b], down_shared[a:b].T]
        else:
            parts = [gate_expert[kind, :, a:b], up_expert[kind, :, a:b], down_expert[kind, a:b].T]
        fill = -(b - a) % 128
        return jnp.concatenate([jnp.pad(part, ((0, 0), (0, fill))) for part in parts], axis=1)

    packs = [pack(*chunk) for chunk in chunks]
    chained = lax.axis_size("row") == 4
    planar = chained and cols == 8 and share == TILE
    gathered = {}
    gathered[0] = Gathered(packs[0])

    rows_in = lax.all_gather(block_input, "col", axis=1, tiled=True)
    gains = lax.all_gather(jnp.stack([input_gain, mlp_gain]), "col", axis=1, tiled=True).astype(f32)
    cot_rows = lax.all_gather(grad_output, "col", axis=1, tiled=True)
    rows_f = rows_in.astype(f32)
    scale_a = lax.rsqrt(jnp.mean(rows_f * rows_f, axis=-1, keepdims=True) + norm_eps)
    normed_a = (rows_f * scale_a * gains[0]).astype(bf16)
    raw = mm(normed_a, qkv_full)
    raw = after(raw, gathered[0].second())
    qkv, context, lse = attend_forward(raw, lengths, cosine, sine)
    context = after(context, gathered[0].third())
    x_share = block_input.astype(f32)
    gain_b = mlp_gain.astype(f32)
    if planar:
        attn_part = joint_back([context], [out_weights], 0, bf16, planar=True)
        attn_part = after(attn_part, (cot_rows,))
        (stream,), (scaled,), wholes_now = plane_step(
            attn_part, stream_step, [block_input, gain_b[None]], 1, 1, 1, packs[1:2]
        )
        gathered[1] = (packs[1], wholes_now[0])
    else:
        attn_part = mm_nt(context, out_full).astype(bf16)
        attn_sum = lax.psum_scatter(attn_part, "col", scatter_dimension=1, tiled=True)
        scaled_share, stream = stream_step(attn_sum.astype(f32), block_input, gain_b[None])
        scaled = lax.all_gather(scaled_share.astype(bf16), "col", axis=1, tiled=True)
    for at in range(1, len(chunks)):
        if at not in gathered:
            gathered[at] = Gathered(packs[at], (scaled,))

    def pieces_of(at):
        return gathered[at] if isinstance(gathered[at], tuple) else gathered[at].pieces

    stream_f = scaled.astype(f32) / gains[1]
    scale_b = lax.rsqrt(jnp.mean(stream_f * stream_f, axis=1, keepdims=True) + norm_eps)

    both_logits = scale_b * mm(scaled, router_full)
    logits, slogit = both_logits[:, :experts], both_logits[:, experts]
    top = jnp.max(logits, axis=-1, keepdims=True)
    expo = jnp.exp(logits - top)
    router_probs = expo / jnp.sum(expo, axis=-1, keepdims=True)
    shared_gate = jax.nn.sigmoid(slogit)

    inner = jnp.zeros((tokens,), f32)
    dots = {}
    members, shares = {None: None}, {None: shared_gate}
    for local in range(local_experts):
        expert = col_id * local_experts + local
        members[local] = jnp.any(routes == expert, axis=1)
        column = lax.dynamic_index_in_dim(router_probs, expert, 1, False)
        shares[local] = jnp.where(members[local], column, 0.0)
    dpairs, hiddens, wholes, reduced = [], [], [], []
    last = len(chunks) - 1
    came, went = {}, {}

    def hop(arrivals, at, which):
        return arrivals[at][which] if at in arrivals else ()

    for at in range(1, len(chunks)):
        if not isinstance(gathered[at], tuple):
            came[at] = (gathered[at].second(), gathered[at].third())
    for at, (kind, a, b) in enumerate(chunks):
        coef = jnp.concatenate([scale_b, shares[kind][:, None]], axis=1)
        if at == last:
            dscaled_early = joint_back(dpairs, wholes, 0, f32)
            moe_early = joint_back(hiddens, wholes, 2, f32)
            coef = after(coef, (dscaled_early, moe_early))
        if planar and at > 0:
            coef = after(
                coef,
                hop(came, at + 1, 0),
                hop(came, at, 1) if at < last else (),
                hop(went, at - 2, 0),
                hop(went, at - 3, 1),
                hop(went, at - 4, 2),
            )
        dpair, hidden, sums, grads, whole = expert_chunk(pieces_of(at), scaled, cot_rows, coef)
        dots[kind] = dots.get(kind, 0.0) + sums[:, 0]
        inner = inner + sums[:, 1]
        dpairs.append(dpair)
        hiddens.append(hidden)
        wholes.append(whole)
        if at < last or not planar:
            reduced.append(Reduced(grads))
            went[at] = reduced[at].hops
    late_pairs, late_wholes = dpairs[last:], wholes[last:]
    late_pairs[-1] = after(
        late_pairs[-1], hop(went, last - 1, 0), hop(went, last - 2, 1), hop(went, last - 3, 2)
    )
    dscaled_part = joint_back(late_pairs, late_wholes, 0, bf16, dscaled_early, planar=planar)
    moe_part = joint_back(hiddens[last:], wholes[last:], 2, bf16, moe_early)

    named = [jnp.where(members[local], dots[local], 0.0) for local in range(local_experts)]
    table = lax.all_gather(jnp.stack(named + [dots[None], inner]), "col", axis=0)
    dprob = table[:, :local_experts].reshape(experts, tokens).T
    dshared_gate, inner = jnp.sum(table[:, local_experts], axis=0), jnp.sum(table[:, local_experts + 1], axis=0)
    dlogits = router_probs * (dprob - jnp.sum(dprob * router_probs, axis=1, keepdims=True))
    dslogit = dshared_gate * shared_gate * (1.0 - shared_gate)
    dboth = jnp.concatenate([dlogits, dslogit[:, None]], axis=1)
    inner = inner + jnp.sum(dboth * both_logits, axis=1)
    dboth = scale_b * dboth
    parts = split_three(dboth)
    stacked = mm_tn(jnp.concatenate(parts, axis=1), scaled)
    grad_router_part = stacked.reshape(3, experts + 1, width).sum(axis=0)
    grad_router_both = lax.psum_scatter(grad_router_part, "row", scatter_dimension=1, tiled=True)
    router_rows = lax.dynamic_slice_in_dim(router_full, col_id * share, share, 0)
    back_term = mm_nt(jnp.concatenate(parts, axis=1), jnp.concatenate([router_rows] * 3, axis=1))
    damp = scale_b * scale_b * inner[:, None] / width
    step_inputs = [back_term, grad_output, stream, damp, gain_b[None]]
    if planar:
        (dstream, dscaled, last_grad), (dattn,), _ = plane_step(
            dscaled_part, dstream_step, step_inputs, 2, 1, 2, (), grads
        )
    else:
        dscaled_sum = lax.psum_scatter(dscaled_part, "col", scatter_dimension=1, tiled=True)
        dstream_low, dstream, dscaled = dstream_step(dscaled_sum.astype(f32), *step_inputs)
        dattn = lax.all_gather(dstream_low.astype(bf16), "col", axis=1, tiled=True)
    gain_b_grad = jnp.sum(dscaled * stream, axis=0)

    moe_share = lax.psum_scatter(
        after(moe_part, (dattn,)), "col", scatter_dimension=1, tiled=True
    ).astype(f32)
    block_output = (stream + moe_share).astype(bf16)
    out_part = mm_tn(dattn, context).astype(bf16)
    dcontext = mm(dattn, out_full).astype(bf16)
    dcontext = after(dcontext, hop(went, last - 1, 1), hop(went, last - 2, 2))
    dqkv, inner_a = attend_backward(qkv, dcontext, lse, lengths, cosine, sine)
    inner_a = lax.psum(inner_a[:, 0], "col")[:, None]
    attn_grads = jnp.concatenate([mm_tn(normed_a, dqkv).astype(bf16), out_part], axis=1)
    if planar:
        dnormed_part = joint_back([dqkv], [qkv_full], 0, bf16, planar=True)
        dnormed_part = after(dnormed_part, hop(went, last - 1, 2))
        (dnormed_a, attn_grad), _, _ = plane_step(
            dnormed_part, lambda total: (total,), [], 1, 0, 3, (), attn_grads
        )
    else:
        dnormed_a = lax.psum_scatter(
            mm_nt(dqkv, qkv_full).astype(bf16), "col", scatter_dimension=1, tiled=True
        ).astype(f32)
        attn_grad = Reduced(attn_grads).total
    qkv_grad, out_grad = attn_grad[:, : 3 * head_width], attn_grad[:, 3 * head_width :]
    unit_grads = [one.total for one in reduced]
    if planar:
        unit_grads.append(last_grad)
    gain_a_share = input_gain.astype(f32)
    dinput = dstream + scale_a * gain_a_share * dnormed_a
    dinput = dinput - x_share * (scale_a * scale_a * inner_a / width)
    gain_a_grad = jnp.sum(dnormed_a * x_share * scale_a, axis=0)
    grad_gain_a, grad_gain_b = lax.psum((gain_a_grad, gain_b_grad), "row")

    qkv_grad = qkv_grad.reshape(rows_block, heads, 3, HEAD_DIM)
    grad_query, grad_key, grad_value = (
        qkv_grad[:, :, part].reshape(rows_block, head_width) for part in range(3)
    )
    def unpack(kind, which):
        found = []
        for (of, a, b), grad in zip(chunks, unit_grads):
            if of == kind:
                size = grad.shape[1] // 3
                part = grad[:, which * size : which * size + b - a]
                found.append((a, part.T if which == 2 else part))
        found = [part for _, part in sorted(found, key=lambda item: item[0])]
        return jnp.concatenate(found, axis=0 if which == 2 else 1)

    locals_ = range(local_experts)
    return (
        block_output,
        dinput.astype(bf16),
        grad_gain_a,
        grad_query,
        grad_key,
        grad_value,
        out_grad.T,
        grad_gain_b,
        grad_router_both[:experts].T,
        grad_router_both[experts],
        unpack(None, 0),
        unpack(None, 1),
        unpack(None, 2),
        jnp.stack([unpack(local, 0) for local in locals_]),
        jnp.stack([unpack(local, 1) for local in locals_]),
        jnp.stack([unpack(local, 2) for local in locals_]),
    )


def solution(mesh):
    return jax.shard_map(
        per_device,
        mesh=mesh,
        in_specs=(
            P("row", "col"),
            P(),
            P(),
            P("row", None),
            P("col"),
            P("row", "col"),
            P("row", "col"),
            P("row", "col"),
            P("col", "row"),
            P("col"),
            P("row", None),
            P("row"),
            P("row", "col"),
            P("row", "col"),
            P("col", "row"),
            P("col", "row", None),
            P("col", "row", None),
            P("col", None, "row"),
            P("row", "col"),
        ),
        out_specs=(
            P("row", "col"),
            P("row", "col"),
            P("col"),
            P("row", "col"),
            P("row", "col"),
            P("row", "col"),
            P("col", "row"),
            P("col"),
            P("row", None),
            P("row"),
            P("row", "col"),
            P("row", "col"),
            P("col", "row"),
            P("col", "row", None),
            P("col", "row", None),
            P("col", None, "row"),
        ),
        check_vma=False,
    )
```

```python
import functools
import math

import jax
import jax.numpy as jnp
from jax import lax
from jax.experimental import pallas as pl
from jax.experimental.pallas import tpu as pltpu
from jax.sharding import PartitionSpec as P

HEAD_DIM = 128
SEQ_LEN = 1024
QBLOCK = 256
TILE = 256
norm_eps = 1e-06
rope_base = 1000000.0
bf16 = jnp.bfloat16
f32 = jnp.float32


def mm(left, right):
    return jnp.dot(left, right, preferred_element_type=f32)


def mm_nt(left, right):
    return lax.dot_general(left, right, (((1,), (1,)), ((), ())), preferred_element_type=f32)


def mm_tn(left, right):
    return lax.dot_general(left, right, (((0,), (0,)), ((), ())), preferred_element_type=f32)


def rope_tables():
    positions = jnp.arange(SEQ_LEN).astype(f32)
    freqs = jnp.power(f32(rope_base), -jnp.arange(0, HEAD_DIM, 2).astype(f32) / HEAD_DIM)
    angles = positions[:, None] * freqs[None, :]
    cosine, sine = jnp.cos(angles), jnp.sin(angles)
    return (
        jnp.concatenate([cosine, cosine], axis=-1),
        jnp.concatenate([-sine, sine], axis=-1),
    )


def block_scores(rows, keys, start, length, scale):
    raw = mm_nt(rows, keys) * scale
    query_pos = start + lax.broadcasted_iota(jnp.int32, raw.shape, 0)
    key_pos = lax.broadcasted_iota(jnp.int32, raw.shape, 1)
    return jnp.where((key_pos <= query_pos) & (key_pos < length), raw, -1e30)


def attend_forward_kernel(length_ref, raw_ref, cos_ref, sin_ref, qkv_ref, context_ref, lse_ref):
    length = length_ref[pl.program_id(0)]
    scale = 1.0 / math.sqrt(HEAD_DIM)
    hd = HEAD_DIM
    for part in range(2):
        raw = raw_ref[:, part * hd : (part + 1) * hd]
        turned = raw * cos_ref[...] + pltpu.roll(raw, hd // 2, 1) * sin_ref[...]
        qkv_ref[:, part * hd : (part + 1) * hd] = turned.astype(bf16)
    qkv_ref[:, 2 * hd :] = raw_ref[:, 2 * hd :].astype(bf16)
    for at in range(0, SEQ_LEN, QBLOCK):
        seen = at + QBLOCK
        scores = block_scores(
            qkv_ref[at:seen, :hd], qkv_ref[:seen, hd : 2 * hd], at, length, scale
        )
        top = jnp.max(scores, axis=-1, keepdims=True)
        expo = jnp.exp(scores - top)
        total = jnp.sum(expo, axis=-1, keepdims=True)
        probs = (expo / total).astype(bf16)
        context_ref[at:seen, :] = mm(probs, qkv_ref[:seen, 2 * hd :]).astype(bf16)
        lse_ref[at:seen, :] = jnp.broadcast_to(top + jnp.log(total), (QBLOCK, hd))


def attend_forward(raw, lengths, cosine, sine):
    tokens, width = raw.shape
    heads = width // (3 * HEAD_DIM)
    slots = tokens // SEQ_LEN
    wide = pl.BlockSpec((SEQ_LEN, 3 * HEAD_DIM), lambda s, h, _: (s, h))
    one = pl.BlockSpec((SEQ_LEN, HEAD_DIM), lambda s, h, _: (s, h))
    table = pl.BlockSpec((SEQ_LEN, HEAD_DIM), lambda s, h, _: (0, 0))
    pairs = slots * heads * SEQ_LEN * SEQ_LEN
    return pl.pallas_call(
        attend_forward_kernel,
        grid_spec=pltpu.PrefetchScalarGridSpec(
            num_scalar_prefetch=1,
            grid=(slots, heads),
            in_specs=[wide, table, table],
            out_specs=[wide, one, one],
        ),
        out_shape=[
            jax.ShapeDtypeStruct((tokens, width), bf16),
            jax.ShapeDtypeStruct((tokens, heads * HEAD_DIM), bf16),
            jax.ShapeDtypeStruct((tokens, heads * HEAD_DIM), f32),
        ],
        cost_estimate=pl.CostEstimate(
            flops=3 * HEAD_DIM * pairs, bytes_accessed=8 * tokens * width, transcendentals=pairs
        ),
        name="attend_forward",
    )(lengths, raw, cosine, sine)


def attend_backward_kernel(
    length_ref, qkv_ref, dcontext_ref, lse_ref, cos_ref, sin_ref, dqkv_ref, inner_ref, dk_ref, dv_ref
):
    length = length_ref[pl.program_id(0)]
    scale = 1.0 / math.sqrt(HEAD_DIM)
    hd = HEAD_DIM
    @pl.when(pl.program_id(1) == 0)
    def _():
        inner_ref[...] = jnp.zeros_like(inner_ref)

    dk_ref[...] = jnp.zeros_like(dk_ref)
    dv_ref[...] = jnp.zeros_like(dv_ref)

    def turn_back(grad, rows):
        back = grad * cos_ref[rows, :] - pltpu.roll(grad, hd // 2, 1) * sin_ref[rows, :]
        return back.astype(bf16)

    for at in range(0, SEQ_LEN, QBLOCK):
        seen = at + QBLOCK
        rows = qkv_ref[at:seen, :hd]
        keys = qkv_ref[:seen, hd : 2 * hd]
        drows = dcontext_ref[at:seen, :]
        scores = block_scores(rows, keys, at, length, scale)
        probs = jnp.exp(scores - lse_ref[at:seen, :1])
        dv_ref[:seen, :] += mm_tn(probs.astype(bf16), drows)
        dprobs = mm_nt(drows, qkv_ref[:seen, 2 * hd :])
        dscore = probs * (dprobs - jnp.sum(dprobs * probs, axis=-1, keepdims=True))
        draw = (dscore * scale).astype(bf16)
        dquery = mm(draw, keys)
        dk_ref[:seen, :] += mm_tn(draw, rows)
        dqkv_ref[at:seen, :hd] = turn_back(dquery, slice(at, seen))
        inner_ref[at:seen, :] += jnp.sum(dquery * rows.astype(f32), axis=-1, keepdims=True)
    dkey, dvalue = dk_ref[...], dv_ref[...]
    dqkv_ref[:, hd : 2 * hd] = turn_back(dkey, slice(None))
    dqkv_ref[:, 2 * hd :] = dvalue.astype(bf16)
    inner_ref[...] += jnp.sum(
        dkey * qkv_ref[:, hd : 2 * hd].astype(f32) + dvalue * qkv_ref[:, 2 * hd :].astype(f32),
        axis=-1,
        keepdims=True,
    )


def attend_backward(qkv, dcontext, lse, lengths, cosine, sine):
    tokens, width = qkv.shape
    heads = width // (3 * HEAD_DIM)
    slots = tokens // SEQ_LEN
    wide = pl.BlockSpec((SEQ_LEN, 3 * HEAD_DIM), lambda s, h, _: (s, h))
    one = pl.BlockSpec((SEQ_LEN, HEAD_DIM), lambda s, h, _: (s, h))
    table = pl.BlockSpec((SEQ_LEN, HEAD_DIM), lambda s, h, _: (0, 0))
    pairs = slots * heads * SEQ_LEN * SEQ_LEN
    return pl.pallas_call(
        attend_backward_kernel,
        grid_spec=pltpu.PrefetchScalarGridSpec(
            num_scalar_prefetch=1,
            grid=(slots, heads),
            in_specs=[wide, one, one, table, table],
            out_specs=[wide, pl.BlockSpec((SEQ_LEN, 1), lambda s, h, _: (s, 0))],
            scratch_shapes=[pltpu.VMEM((SEQ_LEN, HEAD_DIM), f32)] * 2,
        ),
        out_shape=[
            jax.ShapeDtypeStruct((tokens, width), bf16),
            jax.ShapeDtypeStruct((tokens, 1), f32),
        ],
        cost_estimate=pl.CostEstimate(
            flops=8 * HEAD_DIM * pairs, bytes_accessed=8 * tokens * width, transcendentals=pairs
        ),
        name="attend_backward",
    )(lengths, qkv, dcontext, lse, cosine, sine)


PAIRS = [(0, 1), (1, 0), (2, 3), (3, 2)]
MIDDLE = [(1, 2), (2, 1)]
OUTWARD = [(1, 0), (2, 3)]
INWARD = [(0, 1), (3, 2)]


class Gathered:
    def __init__(self, part, *groups):
        self.part = part
        if lax.axis_size("row") != 4:
            self.pieces = (lax.all_gather(part, "row", axis=0, tiled=True),)
            return
        part = after(part, *groups)
        self.partner = lax.ppermute(part, "row", PAIRS)
        self.near_mid = lax.ppermute(part, "row", MIDDLE)
        self.pieces = None

    def second(self, *groups):
        if self.pieces is None:
            self.near_out = lax.ppermute(after(self.near_mid, *groups), "row", OUTWARD)
            self.far_mid = lax.ppermute(after(self.partner, *groups), "row", MIDDLE)
            return (self.partner, self.near_mid)
        return ()

    def third(self, *groups):
        if self.pieces is None:
            self.far_out = lax.ppermute(after(self.far_mid, *groups), "row", OUTWARD)
            self.pieces = (
                self.part, self.partner, self.near_mid, self.far_mid, self.near_out, self.far_out
            )
            return (self.far_mid, self.near_out)
        return ()


def places(z):
    pair = z // 2
    return z, z + 1 - 2 * lax.rem(z, 2), 2 - pair, 3 - 3 * pair


class RowGather:
    def __init__(self, packs, wholes, sems):
        self.packs, self.wholes, (self.send_sems, self.recv_sems) = packs, wholes, sems
        self.z = lax.axis_index("row")
        self.own, self.partner, self.near, self.far = places(self.z)
        self.across = 3 - self.z
        self.in_middle = (self.z == 1) | (self.z == 2)
        self.outside = jnp.logical_not(self.in_middle)

    def copy_of(self, kind, at, source, block, target):
        return pltpu.make_async_remote_copy(
            src_ref=source,
            dst_ref=self.wholes[at].at[block],
            send_sem=self.send_sems.at[kind, at],
            recv_sem=self.recv_sems.at[kind, at],
            device_id={"row": target},
            device_id_type=pl.DeviceIdType.MESH,
        )

    def swap(self, at):
        return self.copy_of(0, at, self.packs[at], self.own, self.partner)

    def swap_middle(self, at):
        return self.copy_of(1, at, self.packs[at], self.own, self.across)

    def second_middle(self, at):
        return self.copy_of(2, at, self.wholes[at].at[self.partner], self.partner, self.across)

    def hand_near(self, at):
        return self.copy_of(3, at, self.wholes[at].at[self.near], self.near, self.partner)

    def hand_far(self, at):
        return self.copy_of(4, at, self.wholes[at].at[self.far], self.far, self.partner)

    def greet(self, barrier):
        signal_to(barrier, {"row": self.partner})

        @pl.when(self.in_middle)
        def _():
            signal_to(barrier, {"row": self.across})
            pl.semaphore_wait(barrier, 2)

        @pl.when(self.outside)
        def _():
            pl.semaphore_wait(barrier, 1)

    def begin(self):
        for at in range(len(self.packs)):
            @pl.when(self.in_middle)
            def _():
                self.swap_middle(at).start()

            self.swap(at).start()

    def hand_on(self, at):
        @pl.when(self.in_middle)
        def _():
            self.swap_middle(at).wait_recv()
            self.hand_near(at).start()
            self.swap(at).wait_recv()
            self.second_middle(at).start()

    def hand_last(self, at):
        @pl.when(self.in_middle)
        def _():
            self.second_middle(at).wait_recv()
            self.hand_far(at).start()

    def finish(self):
        for at in range(len(self.packs)):
            @pl.when(self.in_middle)
            def _():
                for copy in (
                    self.swap,
                    self.swap_middle,
                    self.second_middle,
                    self.hand_near,
                    self.hand_far,
                ):
                    copy(at).wait_send()

            @pl.when(self.outside)
            def _():
                self.swap(at).wait()
                self.hand_near(at).wait_recv()
                self.hand_far(at).wait_recv()


class RowReduce:
    def __init__(self, grads, total, refs):
        self.grads, self.total = grads, total
        self.far_in, self.near_in, self.far_sum, self.near_sum, self.last = refs[:5]
        self.held, self.more, self.send_sems, self.recv_sems, self.local_sems = refs[5:]
        self.z = lax.axis_index("row")
        self.own, self.partner, self.near, self.far = places(self.z)
        self.across = 3 - self.z
        self.in_middle = (self.z == 1) | (self.z == 2)
        self.outside = jnp.logical_not(self.in_middle)

    def copy_of(self, kind, source, target, device):
        return pltpu.make_async_remote_copy(
            src_ref=source,
            dst_ref=target,
            send_sem=self.send_sems.at[kind],
            recv_sem=self.recv_sems.at[kind],
            device_id={"row": device},
            device_id_type=pl.DeviceIdType.MESH,
        )

    def send_far(self):
        return self.copy_of(0, self.grads.at[self.far], self.far_in, self.partner)

    def send_near(self):
        return self.copy_of(1, self.grads.at[self.near], self.near_in, self.partner)

    def cross_far(self):
        return self.copy_of(2, self.far_in, self.far_sum, self.across)

    def cross_near(self):
        return self.copy_of(3, self.near_in, self.near_sum, self.across)

    def swap_middle(self):
        return self.copy_of(4, self.far_sum, self.last, self.partner)

    def swap_outer(self):
        return self.copy_of(4, self.grads.at[self.partner], self.last, self.partner)

    def load(self, kind, block):
        target = self.more if kind % 2 else self.held
        return pltpu.make_async_copy(self.grads.at[block], target, self.local_sems.at[kind])

    def add(self, target, source):
        @pl.loop(0, target.shape[0], step=64)
        def _(at):
            tile = pl.ds(pl.multiple_of(at, 64), 64)
            target[tile, :] = (target[tile, :].astype(f32) + source[tile, :].astype(f32)).astype(bf16)

    def begin(self):
        @pl.when(self.outside)
        def _():
            self.send_far().start()
            self.send_near().start()
            self.swap_outer().start()
            self.load(3, self.own).start()

        @pl.when(self.in_middle)
        def _():
            self.load(0, self.far).start()
            self.load(1, self.near).start()

    def second_far(self):
        @pl.when(self.in_middle)
        def _():
            self.load(0, self.far).wait()
            self.send_far().wait_recv()
            self.add(self.far_in, self.held)
            self.cross_far().start()
            self.load(2, self.partner).start()

    def second_near(self):
        @pl.when(self.in_middle)
        def _():
            self.load(1, self.near).wait()
            self.send_near().wait_recv()
            self.add(self.near_in, self.more)
            self.cross_near().start()
            self.load(3, self.own).start()

    def third(self):
        @pl.when(self.in_middle)
        def _():
            self.load(2, self.partner).wait()
            self.cross_far().wait_recv()
            self.add(self.far_sum, self.held)
            self.swap_middle().start()

    def finish(self):
        self.load(3, self.own).wait()
        self.swap_outer().wait_recv()

        @pl.when(self.in_middle)
        def _():
            self.cross_near().wait_recv()

        @pl.loop(0, self.total.shape[0], step=64)
        def _(at):
            tile = pl.ds(pl.multiple_of(at, 64), 64)
            self.total[tile, :] = self.more[tile, :].astype(f32) + self.last[tile, :].astype(f32)

        @pl.when(self.in_middle)
        def _():
            @pl.loop(0, self.total.shape[0], step=64)
            def _(at):
                tile = pl.ds(pl.multiple_of(at, 64), 64)
                self.total[tile, :] += self.near_sum[tile, :].astype(f32)

            self.cross_far().wait_send()
            self.cross_near().wait_send()
            self.swap_middle().wait_send()

        @pl.when(self.outside)
        def _():
            self.send_far().wait_send()
            self.send_near().wait_send()
            self.swap_outer().wait_send()


def signal_to(barrier, device):
    pl.semaphore_signal(barrier, inc=1, device_id=device, device_id_type=pl.DeviceIdType.MESH)


def gather_kernel(count, *refs):
    rows = RowGather(refs[:count], refs[count : 2 * count], refs[2 * count :])
    rows.greet(pltpu.get_barrier_semaphore())
    rows.begin()
    for at in range(count):
        rows.hand_on(at)
    for at in range(count):
        rows.hand_last(at)
    rows.finish()


PIECES = 4


def plane_kernel(pointwise, given, made, gather, count, reducing, *refs):
    p_ref, inputs = refs[0], refs[1 : 1 + given]
    at = 1 + given
    packs = refs[at : at + count]
    at += count
    grads = refs[at] if reducing else None
    at += reducing
    results = refs[at : at + made]
    at += made
    total_ref = refs[at] if reducing else None
    at += reducing
    whole_refs = refs[at : at + gather + count]
    at += gather + count
    mine, from_core, from_first, summed, from_second, shared, send_sems, recv_sems, local_sems = refs[
        at : at + 9
    ]
    out_ref = whole_refs[0] if gather else None
    me = lax.axis_index("col")
    core, x, y = lax.rem(me, 2), lax.rem(me // 2, 2), me // 4
    core_mate, x_mate, y_mate = me + 1 - 2 * core, me + 2 - 4 * x, me + 4 - 8 * y
    diagonal = x_mate + 4 - 8 * y
    size = mine.shape[3]
    share = mine.shape[4]
    barrier = pltpu.get_barrier_semaphore()
    for mate in (core_mate, x_mate, y_mate):
        signal_to(barrier, {"col": mate})
    rows, reduction = None, None
    if count or reducing:
        if count:
            rows = RowGather(packs, whole_refs[gather:], refs[at + 9 : at + 11])
            at += 2
        if reducing:
            reduction = RowReduce(grads, total_ref, refs[at + 9 : at + 19])
        chain = rows or reduction
        signal_to(barrier, {"row": chain.partner})

        @pl.when(chain.in_middle)
        def _():
            signal_to(barrier, {"row": chain.across})
            pl.semaphore_wait(barrier, 5)

        @pl.when(chain.outside)
        def _():
            pl.semaphore_wait(barrier, 4)

        if count:
            rows.begin()
        if reducing:
            reduction.begin()
    else:
        pl.semaphore_wait(barrier, 3)

    def remote(kind, i, source, target, mate):
        return pltpu.make_async_remote_copy(
            src_ref=source,
            dst_ref=target,
            send_sem=send_sems.at[kind, i],
            recv_sem=recv_sems.at[kind, i],
            device_id={"col": mate},
            device_id_type=pl.DeviceIdType.MESH,
        )

    def x_first(i):
        return i < PIECES // 2

    def span(i):
        return pl.ds(i * size, size)

    def core_copy(i):
        return remote(0, i, p_ref.at[:, :, 1 - core, span(i), :], from_core.at[i], core_mate)

    def load(i):
        return pltpu.make_async_copy(
            p_ref.at[:, :, core, span(i), :], mine.at[i], local_sems.at[0, i]
        )

    def first_copy(i):
        if x_first(i):
            return remote(1, i, mine.at[i, :, 1 - x], from_first.at[i], x_mate)
        return remote(1, i, mine.at[i, 1 - y], from_first.at[i], y_mate)

    def second_copy(i):
        if x_first(i):
            return remote(2, i, summed.at[i, 1 - y], from_second.at[i], y_mate)
        return remote(2, i, summed.at[i, 1 - x], from_second.at[i], x_mate)

    def columns(i, device):
        return out_ref.at[span(i), pl.ds(pl.multiple_of(device * share, share), share)]

    def spread(kind, i, mate):
        return remote(kind, i, shared.at[i], columns(i, me), mate)

    def keep(i):
        return pltpu.make_async_copy(shared.at[i], columns(i, me), local_sems.at[1, i])

    def pass_on(kind, i, device, mate):
        return remote(kind, i, columns(i, device), columns(i, device), mate)

    def forward(i):
        if x_first(i):
            return pass_on(6, i, y_mate, x_mate)
        return pass_on(6, i, x_mate, y_mate)

    order = [0, 2, 1, 3]
    for i in order:
        core_copy(i).start()
        load(i).start()
    for i in order:
        load(i).wait()
        core_copy(i).wait_recv()
        for a in range(2):
            for b in range(2):
                mine[i, a, b] = (mine[i, a, b].astype(f32) + from_core[i, a, b].astype(f32)).astype(bf16)
        first_copy(i).start()
    for i in order:
        first_copy(i).wait_recv()
        for a in range(2):
            kept = mine[i, a, x] if x_first(i) else mine[i, y, a]
            summed[i, a] = (kept.astype(f32) + from_first[i, a].astype(f32)).astype(bf16)
        second_copy(i).start()
    if count:
        for at in range(count):
            rows.hand_on(at)
    if reducing:
        reduction.second_far()
    for i in order:
        second_copy(i).wait_recv()
        total = summed[i, y if x_first(i) else x].astype(f32) + from_second[i].astype(f32)
        span_rows = slice(i * size, (i + 1) * size)
        values = pointwise(
            total, *[ref[span_rows, :] if ref.shape[0] > 8 else ref[...] for ref in inputs]
        )
        if gather:
            shared[i] = values[0].astype(bf16)
            values = values[1:]
        for ref, value in zip(results, values):
            ref[span_rows, :] = value
        if gather:
            spread(4, i, x_mate).start()
            spread(5, i, y_mate).start()
            spread(3, i, core_mate).start()
            keep(i).start()
    if count:
        rows.hand_last(0)
    if reducing and not gather:
        reduction.second_near()
    if gather:
        for i in order:
            spread(5 if x_first(i) else 4, i, y_mate).wait_recv()
            forward(i).start()
            pass_on(7, i, y_mate if x_first(i) else x_mate, core_mate).start()
        for i in order:
            spread(4 if x_first(i) else 5, i, x_mate).wait_recv()
            pass_on(8, i, x_mate if x_first(i) else y_mate, core_mate).start()
    if count:
        for at in range(1, count):
            rows.hand_last(at)
    if reducing and gather:
        reduction.second_near()
    if reducing:
        reduction.third()
    if gather:
        for i in order:
            forward(i).wait_recv()
            pass_on(9, i, diagonal, core_mate).start()
    for i in order:
        core_copy(i).wait_send()
        first_copy(i).wait_send()
        second_copy(i).wait_send()
        if gather:
            keep(i).wait()
            spread(3, i, core_mate).wait()
            spread(4, i, x_mate).wait_send()
            spread(5, i, y_mate).wait_send()
            forward(i).wait_send()
            for kind, device in (
                (7, y_mate if x_first(i) else x_mate),
                (8, x_mate if x_first(i) else y_mate),
                (9, diagonal),
            ):
                pass_on(kind, i, device, core_mate).wait()
    if count:
        rows.finish()
    if reducing:
        reduction.finish()


def plane_step(partial, pointwise, inputs, made, gather, number, packs=(), grads=None):
    tokens, share = partial.shape[3:]
    size = tokens // PIECES
    count = len(packs)
    reducing = 0 if grads is None else 1
    totals, more_scratch, given_grads = [], [], []
    if reducing:
        block, columns = grads.shape[0] // 4, grads.shape[1]
        given_grads = [grads.reshape(4, block, columns)]
        totals = [jax.ShapeDtypeStruct((block, columns), f32)]
        more_scratch = [pltpu.VMEM((block, columns), bf16)] * 7 + [
            pltpu.SemaphoreType.DMA((5,)),
            pltpu.SemaphoreType.DMA((5,)),
            pltpu.SemaphoreType.DMA((4,)),
        ]
    anywhere = pl.BlockSpec(memory_space=pl.ANY)
    vmem = pl.BlockSpec(memory_space=pltpu.VMEM)
    whole_shapes = [jax.ShapeDtypeStruct((tokens, 8 * share), bf16)] * gather + [
        jax.ShapeDtypeStruct((4,) + pack.shape, bf16) for pack in packs
    ]
    outs = pl.pallas_call(
        functools.partial(plane_kernel, pointwise, len(inputs), made, gather, count, reducing),
        in_specs=[anywhere] + [vmem] * len(inputs) + [anywhere] * (count + reducing),
        out_specs=[vmem] * (made + reducing) + [anywhere] * (gather + count),
        out_shape=[jax.ShapeDtypeStruct((tokens, share), f32)] * made + totals + whole_shapes,
        scratch_shapes=[
            pltpu.VMEM((PIECES, 2, 2, size, share), bf16),
            pltpu.VMEM((PIECES, 2, 2, size, share), bf16),
            pltpu.VMEM((PIECES, 2, size, share), bf16),
            pltpu.VMEM((PIECES, 2, size, share), bf16),
            pltpu.VMEM((PIECES, size, share), bf16),
            pltpu.VMEM((PIECES, size, share), bf16),
            pltpu.SemaphoreType.DMA((10, PIECES)),
            pltpu.SemaphoreType.DMA((10, PIECES)),
            pltpu.SemaphoreType.DMA((2, PIECES)),
        ]
        + [pltpu.SemaphoreType.DMA((5, count))] * (2 if count else 0)
        + more_scratch,
        compiler_params=pltpu.CompilerParams(collective_id=number, has_side_effects=True),
        cost_estimate=pl.CostEstimate(
            flops=60 * 10**9, bytes_accessed=32 * tokens * share, transcendentals=0
        ),
        name="plane_step",
    )(partial, *inputs, *packs, *given_grads)
    at = made + reducing
    wholes = [whole.reshape((4 * whole.shape[1],) + whole.shape[2:]) for whole in outs[at + gather :]]
    return outs[:at], outs[at : at + gather], wholes


def gather_now(packs, number):
    if lax.axis_size("row") != 4:
        return [lax.all_gather(pack, "row", axis=0, tiled=True) for pack in packs]
    count = len(packs)
    sent = sum(pack.size for pack in packs) * 2
    anywhere = pl.BlockSpec(memory_space=pl.ANY)
    wholes = pl.pallas_call(
        functools.partial(gather_kernel, count),
        in_specs=[anywhere] * count,
        out_specs=[anywhere] * count,
        out_shape=[jax.ShapeDtypeStruct((4,) + pack.shape, pack.dtype) for pack in packs],
        scratch_shapes=[pltpu.SemaphoreType.DMA((5, count)), pltpu.SemaphoreType.DMA((5, count))],
        compiler_params=pltpu.CompilerParams(collective_id=number, has_side_effects=True),
        cost_estimate=pl.CostEstimate(
            flops=6 * 9000 * sent, bytes_accessed=6 * sent, transcendentals=0
        ),
        name="gather_rows",
    )(*packs)
    return [whole.reshape((4 * whole.shape[1],) + whole.shape[2:]) for whole in wholes]


def put_own(whole, part):
    if lax.axis_size("row") != 4:
        return whole
    return lax.dynamic_update_slice_in_dim(
        whole, part, lax.axis_index("row") * part.shape[0], 0
    )


class Reduced:
    def __init__(self, grads):
        self.chained = lax.axis_size("row") == 4
        if not self.chained:
            self.total = lax.psum_scatter(grads, "row", scatter_dimension=0, tiled=True).astype(f32)
            return
        z = lax.axis_index("row")
        self.own, self.partner, _, _ = places(z)
        self.grads, self.size = grads, grads.shape[0] // 4
        self.pair = self.rows_of(grads, (1 - z // 2) * 2, 2)
        self.first = lax.ppermute(self.pair, "row", INWARD)

    def rows_of(self, value, at, count):
        return lax.dynamic_slice_in_dim(value, at * self.size, count * self.size, 0)

    def two(self, at):
        mine = self.rows_of(self.grads, at, 1).astype(f32)
        return mine + self.rows_of(self.crossed, lax.rem(at, 2), 1).astype(f32)

    def second(self, *groups):
        if not self.chained:
            return ()
        first = after(self.first, *groups)
        value = (self.pair.astype(f32) + first.astype(f32)).astype(bf16)
        self.crossed = lax.ppermute(value, "row", MIDDLE)
        return (value,)

    def third(self, *groups):
        if not self.chained:
            return ()
        self.crossed = after(self.crossed, *groups)
        value = self.two(self.partner).astype(bf16)
        self.swapped = lax.ppermute(value, "row", PAIRS)
        return (value,)

    def result(self):
        if self.chained:
            return self.two(self.own) + self.swapped.astype(f32)
        return self.total


def one_reduction(grads):
    one = Reduced(grads)
    one.second()
    one.third()
    return one.result()


def after(value, *groups):
    others = tuple(item for group in groups for item in group)
    return lax.optimization_barrier((value,) + others)[0] if others else value


def expert_kernel(size, steps, count, z_ref, *refs):
    pieces = refs[:count]
    (x_ref, cot_ref, x_cols, cot_cols, coef_ref) = refs[count : count + 5]
    (dpair_ref, hidden_ref, sums_ref, grads_ref, whole_ref) = refs[count + 5 : count + 10]
    weights, dpair, hidden, sems, out_sem = refs[count + 10 :]
    step = pl.program_id(0)
    write = pltpu.make_async_copy(weights, whole_ref, out_sem)

    @pl.when(step == 0)
    def _():
        if count == 1:
            copy = pltpu.make_async_copy(pieces[0], weights, sems.at[0])
            copy.start()
            copy.wait()
        elif count == 2:
            block = pieces[0].shape[0]

            def block_copy(back):
                at = pl.multiple_of(lax.rem(z_ref[0] + back, 4) * block, block)
                source = pieces[1].at[pl.ds(at, block)] if back else pieces[0]
                return pltpu.make_async_copy(source, weights.at[pl.ds(at, block)], sems.at[back])

            for back in range(4):
                block_copy(back).start()
            for back in range(4):
                block_copy(back).wait()
        else:
            z = z_ref[0]
            block = pieces[0].shape[0]

            def copy_of(piece, which):
                at = pl.multiple_of(places(z)[which] * block, block)
                return pltpu.make_async_copy(
                    piece, weights.at[pl.ds(at, block)], sems.at[which]
                )

            copy_of(pieces[0], 0).start()
            copy_of(pieces[1], 1).start()
            in_middle = (z == 1) | (z == 2)

            @pl.when(in_middle)
            def _():
                copy_of(pieces[2], 2).start()
                copy_of(pieces[3], 3).start()

            @pl.when(jnp.logical_not(in_middle))
            def _():
                copy_of(pieces[4], 2).start()
                copy_of(pieces[5], 3).start()

            for which in range(4):
                copy_of(pieces[which], which).wait()
        write.start()

    @pl.when(step < steps)
    def _():
        at = pl.multiple_of(step * TILE, TILE)
        rows, cots = x_ref[...], cot_ref[...]
        scale, weight = coef_ref[:, 0:1], coef_ref[:, 1:2]
        dots = jnp.zeros((TILE, 1), f32)
        inner = jnp.zeros((TILE, 1), f32)
        for a in range(0, size, TILE):
            b = min(a + TILE, size)
            gate = scale * mm(rows, weights[:, a:b])
            up = scale * mm(rows, weights[:, size + a : size + b])
            dhid = mm(cots, weights[:, 2 * size + a : 2 * size + b])
            sigma = jax.nn.sigmoid(gate)
            silu = gate * sigma
            hid = silu * up
            dots += jnp.sum(hid * dhid, axis=1, keepdims=True)
            dhid = weight * dhid
            dgate = dhid * up * sigma * (1.0 + gate * (1.0 - sigma))
            dup = dhid * silu
            inner += jnp.sum(dgate * gate + dup * up, axis=1, keepdims=True)
            for into, at_col, value in (
                ((hidden_ref, hidden), a, weight * hid),
                ((dpair_ref, dpair), a, scale * dgate),
                ((dpair_ref, dpair), size + a, scale * dup),
            ):
                value = value.astype(bf16)
                into[0][:, at_col : at_col + b - a] = value
                into[1][pl.ds(at, TILE), at_col : at_col + b - a] = value
        sums_ref[:, 0:1] = dots
        sums_ref[:, 1:2] = inner

    @pl.when(step >= steps)
    def _():
        for a in range(0, 2 * size, TILE):
            b = min(a + TILE, 2 * size)
            grads_ref[:, a:b] = mm_tn(x_cols[...], dpair[:, a:b]).astype(bf16)
        for a in range(0, size, TILE):
            b = min(a + TILE, size)
            grads_ref[:, 2 * size + a : 2 * size + b] = mm_tn(
                cot_cols[...], hidden[:, a:b]
            ).astype(bf16)

    @pl.when(step == pl.num_programs(0) - 1)
    def _():
        write.wait()


def expert_chunk(pieces, scaled, cots, coef):
    tokens, width = scaled.shape
    size = pieces[0].shape[1] // 3
    steps, more = tokens // TILE, width // TILE
    count = len(pieces)
    rows = lambda i, _: (jnp.minimum(i, steps - 1), 0)
    cols = lambda i, _: (0, jnp.maximum(i - steps, 0))
    down = lambda i, _: (jnp.maximum(i - steps, 0), 0)
    z = jnp.reshape(lax.axis_index("row"), (1,)).astype(jnp.int32)
    return pl.pallas_call(
        functools.partial(expert_kernel, size, steps, count),
        grid_spec=pltpu.PrefetchScalarGridSpec(
            num_scalar_prefetch=1,
            grid=(steps + more,),
            in_specs=[pl.BlockSpec(memory_space=pl.ANY)] * count
            + [
                pl.BlockSpec((TILE, width), rows),
                pl.BlockSpec((TILE, width), rows),
                pl.BlockSpec((tokens, TILE), cols),
                pl.BlockSpec((tokens, TILE), cols),
                pl.BlockSpec((TILE, 2), rows),
            ],
            out_specs=[
                pl.BlockSpec((TILE, 2 * size), rows),
                pl.BlockSpec((TILE, size), rows),
                pl.BlockSpec((TILE, 2), rows),
                pl.BlockSpec((TILE, 3 * size), down),
                pl.BlockSpec(memory_space=pl.ANY),
            ],
            scratch_shapes=[
                pltpu.VMEM((width, 3 * size), bf16),
                pltpu.VMEM((tokens, 2 * size), bf16),
                pltpu.VMEM((tokens, size), bf16),
                pltpu.SemaphoreType.DMA((4,)),
                pltpu.SemaphoreType.DMA,
            ],
        ),
        out_shape=[
            jax.ShapeDtypeStruct((tokens, 2 * size), bf16),
            jax.ShapeDtypeStruct((tokens, size), bf16),
            jax.ShapeDtypeStruct((tokens, 2), f32),
            jax.ShapeDtypeStruct((width, 3 * size), bf16),
            jax.ShapeDtypeStruct((width, 3 * size), bf16),
        ],
        cost_estimate=pl.CostEstimate(
            flops=12 * tokens * width * size,
            bytes_accessed=8 * tokens * width + 24 * width * size,
            transcendentals=tokens * size,
        ),
        name="expert_chunk",
    )(z, *pieces, scaled, cots, scaled, cots, coef)


def joint_kernel(count, based, planar, *refs):
    out_ref = refs[-1]
    for a in range(0, refs[count].shape[0], TILE):
        total = refs[2 * count][:, a : a + TILE] if based else None
        for left, weights in zip(refs[:count], refs[count : 2 * count]):
            part = mm_nt(left[...], weights[a : a + TILE, :])
            total = part if total is None else total + part
        if planar:
            at = a // TILE
            out_ref[at // 4, at // 2 % 2, at % 2] = total.astype(out_ref.dtype)
        else:
            out_ref[:, a : a + TILE] = total.astype(out_ref.dtype)


def joint_back(lefts, weights, column, kind, *base, planar=False):
    tokens, width = lefts[0].shape[0], weights[0].shape[0]
    row = lambda i: (i, 0)
    fixed = lambda i: (0, column)
    depth = sum(left.shape[1] for left in lefts)
    return pl.pallas_call(
        functools.partial(joint_kernel, len(lefts), len(base) > 0, planar),
        grid=(tokens // TILE,),
        in_specs=[pl.BlockSpec((TILE, left.shape[1]), row) for left in lefts]
        + [
            pl.BlockSpec((width, left.shape[1]), fixed, pipeline_mode=pl.Buffered(1))
            for left in lefts
        ]
        + [pl.BlockSpec((TILE, width), row)] * len(base),
        out_specs=pl.BlockSpec((2, 2, 2, TILE, TILE), lambda i: (0, 0, 0, i, 0))
        if planar
        else pl.BlockSpec((TILE, width), row),
        out_shape=jax.ShapeDtypeStruct((2, 2, 2, tokens, TILE) if planar else (tokens, width), kind),
        cost_estimate=pl.CostEstimate(
            flops=2 * tokens * width * depth,
            bytes_accessed=2 * (tokens + width) * depth + 4 * tokens * width,
            transcendentals=0,
        ),
        name="joint_back",
    )(*lefts, *weights, *base)


def split_three(values):
    high = values.astype(bf16)
    rest = values - high.astype(f32)
    middle = rest.astype(bf16)
    return high, middle, (rest - middle.astype(f32)).astype(bf16)


def cuts_of(width, sizes):
    cuts, at = [], 0
    for size in sizes:
        if at + size < width:
            cuts.append((at, at + size))
            at += size
    return cuts + [(at, width)]


def stream_step(total, rows, gain):
    stream = rows.astype(f32) + total
    return stream * gain, stream


def dstream_step(total, back, cots, stream, damp, gain):
    dscaled = back + total
    dstream = cots.astype(f32) + gain * dscaled - stream * damp
    return dstream, dstream, dscaled


def per_device(
    block_input,
    seq_lengths,
    slot_order,
    routes,
    input_gain,
    query_weight,
    key_weight,
    value_weight,
    output_weight,
    mlp_gain,
    router_weight,
    score_shared,
    gate_shared,
    up_shared,
    down_shared,
    gate_expert,
    up_expert,
    down_expert,
    grad_output,
):
    tokens, share = block_input.shape
    cols = lax.axis_size("col")
    col_id = lax.axis_index("col")
    row_id = lax.axis_index("row")
    width = share * cols
    slots = tokens // SEQ_LEN
    local_experts = gate_expert.shape[0]
    experts = router_weight.shape[1]
    head_width = query_weight.shape[1]
    heads = head_width // HEAD_DIM
    rows_block = query_weight.shape[0]
    lengths = lax.dynamic_slice_in_dim(seq_lengths[slot_order], row_id * slots, slots, 0)
    cosine, sine = rope_tables()

    def by_head(weight):
        return weight.reshape(rows_block, heads, 1, HEAD_DIM)

    qkv_pack = jnp.concatenate(
        [by_head(query_weight), by_head(key_weight), by_head(value_weight)], axis=2
    ).reshape(rows_block, 3 * head_width)
    router_pack = jnp.concatenate([router_weight, score_shared[:, None]], axis=1)
    router_pack = jnp.pad(router_pack, ((0, 0), (0, -router_pack.shape[1] % 128)))
    out_pack = jnp.concatenate([output_weight.T, router_pack], axis=1)
    qkv_whole, out_whole = gather_now([qkv_pack, out_pack], 0)
    qkv_full, out_weights = put_own(qkv_whole, qkv_pack), put_own(out_whole, out_pack)
    out_full = out_weights[:, :head_width]
    router_full = out_weights[:, head_width : head_width + experts + 1]
    shared_cuts = [(None, a, b) for a, b in cuts_of(gate_shared.shape[1], (512,))]
    expert_cuts = [
        (local, a, b)
        for local in range(local_experts)
        for a, b in cuts_of(gate_expert.shape[2], (512, 512))
    ]
    chunks = shared_cuts[-1:] + expert_cuts[:-1] + shared_cuts[:-1] + expert_cuts[-1:]

    def pack(kind, a, b):
        if kind is None:
            parts = [gate_shared[:, a:b], up_shared[:, a:b], down_shared[a:b].T]
        else:
            parts = [gate_expert[kind, :, a:b], up_expert[kind, :, a:b], down_expert[kind, a:b].T]
        fill = -(b - a) % 128
        return jnp.concatenate([jnp.pad(part, ((0, 0), (0, fill))) for part in parts], axis=1)

    packs = [pack(*chunk) for chunk in chunks]
    chained = lax.axis_size("row") == 4
    planar = chained and cols == 8 and share == TILE
    gathered = {}
    gathered[0] = Gathered(packs[0])

    rows_in = lax.all_gather(block_input, "col", axis=1, tiled=True)
    gains = lax.all_gather(jnp.stack([input_gain, mlp_gain]), "col", axis=1, tiled=True).astype(f32)
    cot_rows = lax.all_gather(grad_output, "col", axis=1, tiled=True)
    rows_f = rows_in.astype(f32)
    scale_a = lax.rsqrt(jnp.mean(rows_f * rows_f, axis=-1, keepdims=True) + norm_eps)
    normed_a = (rows_f * scale_a * gains[0]).astype(bf16)
    raw = mm(normed_a, qkv_full)
    raw = after(raw, gathered[0].second())
    qkv, context, lse = attend_forward(raw, lengths, cosine, sine)
    context = after(context, gathered[0].third())
    x_share = block_input.astype(f32)
    gain_b = mlp_gain.astype(f32)
    if planar:
        attn_part = joint_back([context], [out_weights], 0, bf16, planar=True)
        attn_part = after(attn_part, (cot_rows,))
        (stream,), (scaled,), wholes_now = plane_step(
            attn_part, stream_step, [block_input, gain_b[None]], 1, 1, 1, packs[1:2]
        )
        gathered[1] = (packs[1], wholes_now[0])
    else:
        attn_part = mm_nt(context, out_full).astype(bf16)
        attn_sum = lax.psum_scatter(attn_part, "col", scatter_dimension=1, tiled=True)
        scaled_share, stream = stream_step(attn_sum.astype(f32), block_input, gain_b[None])
        scaled = lax.all_gather(scaled_share.astype(bf16), "col", axis=1, tiled=True)
    for at in range(1, 3 if planar else len(chunks)):
        if at not in gathered:
            gathered[at] = Gathered(packs[at], (scaled,))

    def pieces_of(at):
        return gathered[at] if isinstance(gathered[at], tuple) else gathered[at].pieces

    stream_f = scaled.astype(f32) / gains[1]
    scale_b = lax.rsqrt(jnp.mean(stream_f * stream_f, axis=1, keepdims=True) + norm_eps)

    both_logits = scale_b * mm(scaled, router_full)
    logits, slogit = both_logits[:, :experts], both_logits[:, experts]
    top = jnp.max(logits, axis=-1, keepdims=True)
    expo = jnp.exp(logits - top)
    router_probs = expo / jnp.sum(expo, axis=-1, keepdims=True)
    shared_gate = jax.nn.sigmoid(slogit)

    inner = jnp.zeros((tokens,), f32)
    dots = {}
    members, shares = {None: None}, {None: shared_gate}
    for local in range(local_experts):
        expert = col_id * local_experts + local
        members[local] = jnp.any(routes == expert, axis=1)
        column = lax.dynamic_index_in_dim(router_probs, expert, 1, False)
        shares[local] = jnp.where(members[local], column, 0.0)
    dpairs, hiddens, wholes, reduced = [], [], [], []
    last = len(chunks) - 1
    waits = ()
    if not planar:
        for at in range(1, len(chunks)):
            gathered[at].second()
            gathered[at].third()

    def joints(*base):
        return (
            joint_back(dpairs[-2:], wholes[-2:], 0, f32, *base[:1]),
            joint_back(hiddens[-2:], wholes[-2:], 2, f32, *base[1:]),
        )

    for at, (kind, a, b) in enumerate(chunks):
        coef = jnp.concatenate([scale_b, shares[kind][:, None]], axis=1)
        coef = after(coef, waits)
        dpair, hidden, sums, grads, whole = expert_chunk(pieces_of(at), scaled, cot_rows, coef)
        dots[kind] = dots.get(kind, 0.0) + sums[:, 0]
        inner = inner + sums[:, 1]
        dpairs.append(dpair)
        hiddens.append(hidden)
        wholes.append(whole)
        now = (sums,)
        waits = ()
        if at == 1:
            early, joined = joints(), 2
            waits += early
        elif at == 3 and at < last:
            early, joined = joints(*early), 4
            waits += early
        if planar and at + 2 <= last:
            if at == 0:
                waits += gathered[2].second(now)
            elif at == 1:
                gathered[2].third(now)
                gathered[3] = Gathered(packs[3], (gathered[2].far_mid,))
            elif at == 2:
                gathered[3].second(now)
                gathered[3].third()
                gathered[4] = Gathered(packs[4], (gathered[3].far_mid,))
        if planar and at == 3:
            gathered[4].second(now)
            gathered[4].third()
        if not planar:
            reduced.append(Reduced(grads))
        elif at < last:
            if at >= 1:
                waits += reduced[at - 1].second(now)
            if at >= 2:
                waits += reduced[at - 2].third(now)
            reduced.append(Reduced(grads))
    now = (sums,)
    if planar:
        waits = reduced[3].second(now)
        waits += reduced[2].third(now)
    else:
        waits = ()
        for one in reduced:
            one.second()
            one.third()
    late_pairs, late_wholes, late_hiddens = dpairs[joined:], wholes[joined:], hiddens[joined:]
    late_pairs[-1] = after(late_pairs[-1], waits)
    dscaled_part = joint_back(late_pairs, late_wholes, 0, bf16, early[0], planar=planar)

    named = [jnp.where(members[local], dots[local], 0.0) for local in range(local_experts)]
    table = lax.all_gather(jnp.stack(named + [dots[None], inner]), "col", axis=0)
    dprob = table[:, :local_experts].reshape(experts, tokens).T
    dshared_gate, inner = jnp.sum(table[:, local_experts], axis=0), jnp.sum(table[:, local_experts + 1], axis=0)
    dlogits = router_probs * (dprob - jnp.sum(dprob * router_probs, axis=1, keepdims=True))
    dslogit = dshared_gate * shared_gate * (1.0 - shared_gate)
    dboth = jnp.concatenate([dlogits, dslogit[:, None]], axis=1)
    inner = inner + jnp.sum(dboth * both_logits, axis=1)
    dboth = scale_b * dboth
    parts = split_three(dboth)
    router_rows = lax.dynamic_slice_in_dim(router_full, col_id * share, share, 0)
    back_term = mm_nt(jnp.concatenate(parts, axis=1), jnp.concatenate([router_rows] * 3, axis=1))
    damp = scale_b * scale_b * inner[:, None] / width
    step_inputs = [back_term, grad_output, stream, damp, gain_b[None]]
    if planar:
        (dstream, dscaled, last_grad), (dattn,), _ = plane_step(
            dscaled_part, dstream_step, step_inputs, 2, 1, 2, (), grads
        )
    else:
        dscaled_sum = lax.psum_scatter(dscaled_part, "col", scatter_dimension=1, tiled=True)
        dstream_low, dstream, dscaled = dstream_step(dscaled_sum.astype(f32), *step_inputs)
        dattn = lax.all_gather(dstream_low.astype(bf16), "col", axis=1, tiled=True)
    gain_b_grad = jnp.sum(dscaled * stream, axis=0)

    late_hiddens[-1] = after(late_hiddens[-1], (dattn,))
    moe_part = joint_back(late_hiddens, late_wholes, 2, bf16, early[1])
    moe_share = lax.psum_scatter(moe_part, "col", scatter_dimension=1, tiled=True).astype(f32)
    block_output = (stream + moe_share).astype(bf16)
    out_part = mm_tn(dattn, context).astype(bf16)
    dcontext = mm(dattn, out_full).astype(bf16)
    if planar:
        dcontext = after(dcontext, reduced[3].third((dattn,)))
    router_left = after(jnp.concatenate(parts, axis=1), (dattn,))
    grad_router_part = mm_tn(router_left, scaled).reshape(3, experts + 1, width).sum(axis=0)
    grad_router_both = lax.psum_scatter(grad_router_part, "row", scatter_dimension=1, tiled=True)
    dqkv, inner_a = attend_backward(qkv, dcontext, lse, lengths, cosine, sine)
    inner_a = lax.psum(inner_a[:, 0], "col")[:, None]
    attn_grads = jnp.concatenate([mm_tn(normed_a, dqkv).astype(bf16), out_part], axis=1)
    if planar:
        dnormed_part = joint_back([dqkv], [qkv_full], 0, bf16, planar=True)
        dnormed_part = after(dnormed_part, (inner_a,))
        (dnormed_a, attn_grad), _, _ = plane_step(
            dnormed_part, lambda total: (total,), [], 1, 0, 3, (), attn_grads
        )
    else:
        dnormed_a = lax.psum_scatter(
            mm_nt(dqkv, qkv_full).astype(bf16), "col", scatter_dimension=1, tiled=True
        ).astype(f32)
        attn_grad = one_reduction(attn_grads)
    qkv_grad, out_grad = attn_grad[:, : 3 * head_width], attn_grad[:, 3 * head_width :]
    unit_grads = [one.result() for one in reduced]
    if planar:
        unit_grads.append(last_grad)
    gain_a_share = input_gain.astype(f32)
    dinput = dstream + scale_a * gain_a_share * dnormed_a
    dinput = dinput - x_share * (scale_a * scale_a * inner_a / width)
    gain_a_grad = jnp.sum(dnormed_a * x_share * scale_a, axis=0)
    grad_gain_a, grad_gain_b = lax.psum((gain_a_grad, gain_b_grad), "row")

    qkv_grad = qkv_grad.reshape(rows_block, heads, 3, HEAD_DIM)
    grad_query, grad_key, grad_value = (
        qkv_grad[:, :, part].reshape(rows_block, head_width) for part in range(3)
    )
    def unpack(kind, which):
        found = []
        for (of, a, b), grad in zip(chunks, unit_grads):
            if of == kind:
                size = grad.shape[1] // 3
                part = grad[:, which * size : which * size + b - a]
                found.append((a, part.T if which == 2 else part))
        found = [part for _, part in sorted(found, key=lambda item: item[0])]
        return jnp.concatenate(found, axis=0 if which == 2 else 1)

    locals_ = range(local_experts)
    return (
        block_output,
        dinput.astype(bf16),
        grad_gain_a,
        grad_query,
        grad_key,
        grad_value,
        out_grad.T,
        grad_gain_b,
        grad_router_both[:experts].T,
        grad_router_both[experts],
        unpack(None, 0),
        unpack(None, 1),
        unpack(None, 2),
        jnp.stack([unpack(local, 0) for local in locals_]),
        jnp.stack([unpack(local, 1) for local in locals_]),
        jnp.stack([unpack(local, 2) for local in locals_]),
    )


def solution(mesh):
    return jax.shard_map(
        per_device,
        mesh=mesh,
        in_specs=(
            P("row", "col"),
            P(),
            P(),
            P("row", None),
            P("col"),
            P("row", "col"),
            P("row", "col"),
            P("row", "col"),
            P("col", "row"),
            P("col"),
            P("row", None),
            P("row"),
            P("row", "col"),
            P("row", "col"),
            P("col", "row"),
            P("col", "row", None),
            P("col", "row", None),
            P("col", None, "row"),
            P("row", "col"),
        ),
        out_specs=(
            P("row", "col"),
            P("row", "col"),
            P("col"),
            P("row", "col"),
            P("row", "col"),
            P("row", "col"),
            P("col", "row"),
            P("col"),
            P("row", None),
            P("row"),
            P("row", "col"),
            P("row", "col"),
            P("col", "row"),
            P("col", "row", None),
            P("col", "row", None),
            P("col", None, "row"),
        ),
        check_vma=False,
    )
```

```python
import functools
import math

import jax
import jax.numpy as jnp
from jax import lax
from jax.experimental import pallas as pl
from jax.experimental.pallas import tpu as pltpu
from jax.sharding import PartitionSpec as P

HEAD_DIM = 128
SEQ_LEN = 1024
QBLOCK = 256
TILE = 256
norm_eps = 1e-06
rope_base = 1000000.0
bf16 = jnp.bfloat16
f32 = jnp.float32


def mm(left, right):
    return jnp.dot(left, right, preferred_element_type=f32)


def mm_nt(left, right):
    return lax.dot_general(left, right, (((1,), (1,)), ((), ())), preferred_element_type=f32)


def mm_tn(left, right):
    return lax.dot_general(left, right, (((0,), (0,)), ((), ())), preferred_element_type=f32)


def rope_tables():
    positions = jnp.arange(SEQ_LEN).astype(f32)
    freqs = jnp.power(f32(rope_base), -jnp.arange(0, HEAD_DIM, 2).astype(f32) / HEAD_DIM)
    angles = positions[:, None] * freqs[None, :]
    cosine, sine = jnp.cos(angles), jnp.sin(angles)
    return (
        jnp.concatenate([cosine, cosine], axis=-1),
        jnp.concatenate([-sine, sine], axis=-1),
    )


def block_scores(rows, keys, start, length, scale):
    raw = mm_nt(rows, keys) * scale
    query_pos = start + lax.broadcasted_iota(jnp.int32, raw.shape, 0)
    key_pos = lax.broadcasted_iota(jnp.int32, raw.shape, 1)
    return jnp.where((key_pos <= query_pos) & (key_pos < length), raw, -1e30)


def attend_forward_kernel(length_ref, raw_ref, cos_ref, sin_ref, qkv_ref, context_ref, lse_ref):
    length = length_ref[pl.program_id(0)]
    scale = 1.0 / math.sqrt(HEAD_DIM)
    hd = HEAD_DIM
    for part in range(2):
        raw = raw_ref[:, part * hd : (part + 1) * hd]
        turned = raw * cos_ref[...] + pltpu.roll(raw, hd // 2, 1) * sin_ref[...]
        qkv_ref[:, part * hd : (part + 1) * hd] = turned.astype(bf16)
    qkv_ref[:, 2 * hd :] = raw_ref[:, 2 * hd :].astype(bf16)
    for at in range(0, SEQ_LEN, QBLOCK):
        seen = at + QBLOCK
        scores = block_scores(
            qkv_ref[at:seen, :hd], qkv_ref[:seen, hd : 2 * hd], at, length, scale
        )
        top = jnp.max(scores, axis=-1, keepdims=True)
        expo = jnp.exp(scores - top)
        total = jnp.sum(expo, axis=-1, keepdims=True)
        probs = (expo / total).astype(bf16)
        context_ref[at:seen, :] = mm(probs, qkv_ref[:seen, 2 * hd :]).astype(bf16)
        lse_ref[at:seen, :] = jnp.broadcast_to(top + jnp.log(total), (QBLOCK, hd))


def attend_forward(raw, lengths, cosine, sine):
    tokens, width = raw.shape
    heads = width // (3 * HEAD_DIM)
    slots = tokens // SEQ_LEN
    wide = pl.BlockSpec((SEQ_LEN, 3 * HEAD_DIM), lambda s, h, _: (s, h))
    one = pl.BlockSpec((SEQ_LEN, HEAD_DIM), lambda s, h, _: (s, h))
    table = pl.BlockSpec((SEQ_LEN, HEAD_DIM), lambda s, h, _: (0, 0))
    pairs = slots * heads * SEQ_LEN * SEQ_LEN
    return pl.pallas_call(
        attend_forward_kernel,
        grid_spec=pltpu.PrefetchScalarGridSpec(
            num_scalar_prefetch=1,
            grid=(slots, heads),
            in_specs=[wide, table, table],
            out_specs=[wide, one, one],
        ),
        out_shape=[
            jax.ShapeDtypeStruct((tokens, width), bf16),
            jax.ShapeDtypeStruct((tokens, heads * HEAD_DIM), bf16),
            jax.ShapeDtypeStruct((tokens, heads * HEAD_DIM), f32),
        ],
        cost_estimate=pl.CostEstimate(
            flops=3 * HEAD_DIM * pairs, bytes_accessed=8 * tokens * width, transcendentals=pairs
        ),
        name="attend_forward",
    )(lengths, raw, cosine, sine)


def attend_backward_kernel(
    length_ref, qkv_ref, dcontext_ref, lse_ref, cos_ref, sin_ref, dqkv_ref, inner_ref, dk_ref, dv_ref
):
    length = length_ref[pl.program_id(0)]
    scale = 1.0 / math.sqrt(HEAD_DIM)
    hd = HEAD_DIM
    @pl.when(pl.program_id(1) == 0)
    def _():
        inner_ref[...] = jnp.zeros_like(inner_ref)

    dk_ref[...] = jnp.zeros_like(dk_ref)
    dv_ref[...] = jnp.zeros_like(dv_ref)

    def turn_back(grad, rows):
        back = grad * cos_ref[rows, :] - pltpu.roll(grad, hd // 2, 1) * sin_ref[rows, :]
        return back.astype(bf16)

    for at in range(0, SEQ_LEN, QBLOCK):
        seen = at + QBLOCK
        rows = qkv_ref[at:seen, :hd]
        keys = qkv_ref[:seen, hd : 2 * hd]
        drows = dcontext_ref[at:seen, :]
        scores = block_scores(rows, keys, at, length, scale)
        probs = jnp.exp(scores - lse_ref[at:seen, :1])
        dv_ref[:seen, :] += mm_tn(probs.astype(bf16), drows)
        dprobs = mm_nt(drows, qkv_ref[:seen, 2 * hd :])
        dscore = probs * (dprobs - jnp.sum(dprobs * probs, axis=-1, keepdims=True))
        draw = (dscore * scale).astype(bf16)
        dquery = mm(draw, keys)
        dk_ref[:seen, :] += mm_tn(draw, rows)
        dqkv_ref[at:seen, :hd] = turn_back(dquery, slice(at, seen))
        inner_ref[at:seen, :] += jnp.sum(dquery * rows.astype(f32), axis=-1, keepdims=True)
    dkey, dvalue = dk_ref[...], dv_ref[...]
    dqkv_ref[:, hd : 2 * hd] = turn_back(dkey, slice(None))
    dqkv_ref[:, 2 * hd :] = dvalue.astype(bf16)
    inner_ref[...] += jnp.sum(
        dkey * qkv_ref[:, hd : 2 * hd].astype(f32) + dvalue * qkv_ref[:, 2 * hd :].astype(f32),
        axis=-1,
        keepdims=True,
    )


def attend_backward(qkv, dcontext, lse, lengths, cosine, sine):
    tokens, width = qkv.shape
    heads = width // (3 * HEAD_DIM)
    slots = tokens // SEQ_LEN
    wide = pl.BlockSpec((SEQ_LEN, 3 * HEAD_DIM), lambda s, h, _: (s, h))
    one = pl.BlockSpec((SEQ_LEN, HEAD_DIM), lambda s, h, _: (s, h))
    table = pl.BlockSpec((SEQ_LEN, HEAD_DIM), lambda s, h, _: (0, 0))
    pairs = slots * heads * SEQ_LEN * SEQ_LEN
    return pl.pallas_call(
        attend_backward_kernel,
        grid_spec=pltpu.PrefetchScalarGridSpec(
            num_scalar_prefetch=1,
            grid=(slots, heads),
            in_specs=[wide, one, one, table, table],
            out_specs=[wide, pl.BlockSpec((SEQ_LEN, 1), lambda s, h, _: (s, 0))],
            scratch_shapes=[pltpu.VMEM((SEQ_LEN, HEAD_DIM), f32)] * 2,
        ),
        out_shape=[
            jax.ShapeDtypeStruct((tokens, width), bf16),
            jax.ShapeDtypeStruct((tokens, 1), f32),
        ],
        cost_estimate=pl.CostEstimate(
            flops=8 * HEAD_DIM * pairs, bytes_accessed=8 * tokens * width, transcendentals=pairs
        ),
        name="attend_backward",
    )(lengths, qkv, dcontext, lse, cosine, sine)


PAIRS = [(0, 1), (1, 0), (2, 3), (3, 2)]
MIDDLE = [(1, 2), (2, 1)]
OUTWARD = [(1, 0), (2, 3)]
INWARD = [(0, 1), (3, 2)]


class Gathered:
    def __init__(self, part, *groups):
        self.part = part
        if lax.axis_size("row") != 4:
            self.pieces = (lax.all_gather(part, "row", axis=0, tiled=True),)
            return
        part = after(part, *groups)
        self.partner = lax.ppermute(part, "row", PAIRS)
        self.near_mid = lax.ppermute(part, "row", MIDDLE)
        self.pieces = None

    def second(self, *groups):
        if self.pieces is None:
            self.near_out = lax.ppermute(after(self.near_mid, *groups), "row", OUTWARD)
            self.far_mid = lax.ppermute(after(self.partner, *groups), "row", MIDDLE)
            return (self.partner, self.near_mid)
        return ()

    def third(self, *groups):
        if self.pieces is None:
            self.far_out = lax.ppermute(after(self.far_mid, *groups), "row", OUTWARD)
            self.pieces = (
                self.part, self.partner, self.near_mid, self.far_mid, self.near_out, self.far_out
            )
            return (self.far_mid, self.near_out)
        return ()


def places(z):
    pair = z // 2
    return z, z + 1 - 2 * lax.rem(z, 2), 2 - pair, 3 - 3 * pair


class RowGather:
    def __init__(self, packs, wholes, sems):
        self.packs, self.wholes, (self.send_sems, self.recv_sems) = packs, wholes, sems
        self.z = lax.axis_index("row")
        self.own, self.partner, self.near, self.far = places(self.z)
        self.across = 3 - self.z
        self.in_middle = (self.z == 1) | (self.z == 2)
        self.outside = jnp.logical_not(self.in_middle)

    def copy_of(self, kind, at, source, block, target):
        return pltpu.make_async_remote_copy(
            src_ref=source,
            dst_ref=self.wholes[at].at[block],
            send_sem=self.send_sems.at[kind, at],
            recv_sem=self.recv_sems.at[kind, at],
            device_id={"row": target},
            device_id_type=pl.DeviceIdType.MESH,
        )

    def swap(self, at):
        return self.copy_of(0, at, self.packs[at], self.own, self.partner)

    def swap_middle(self, at):
        return self.copy_of(1, at, self.packs[at], self.own, self.across)

    def second_middle(self, at):
        return self.copy_of(2, at, self.wholes[at].at[self.partner], self.partner, self.across)

    def hand_near(self, at):
        return self.copy_of(3, at, self.wholes[at].at[self.near], self.near, self.partner)

    def hand_far(self, at):
        return self.copy_of(4, at, self.wholes[at].at[self.far], self.far, self.partner)

    def greet(self, barrier):
        signal_to(barrier, {"row": self.partner})

        @pl.when(self.in_middle)
        def _():
            signal_to(barrier, {"row": self.across})
            pl.semaphore_wait(barrier, 2)

        @pl.when(self.outside)
        def _():
            pl.semaphore_wait(barrier, 1)

    def begin(self):
        for at in range(len(self.packs)):
            @pl.when(self.in_middle)
            def _():
                self.swap_middle(at).start()

            self.swap(at).start()

    def hand_on(self, at):
        @pl.when(self.in_middle)
        def _():
            self.swap_middle(at).wait_recv()
            self.hand_near(at).start()
            self.swap(at).wait_recv()
            self.second_middle(at).start()

    def hand_last(self, at):
        @pl.when(self.in_middle)
        def _():
            self.second_middle(at).wait_recv()
            self.hand_far(at).start()

    def finish(self):
        for at in range(len(self.packs)):
            @pl.when(self.in_middle)
            def _():
                for copy in (
                    self.swap,
                    self.swap_middle,
                    self.second_middle,
                    self.hand_near,
                    self.hand_far,
                ):
                    copy(at).wait_send()

            @pl.when(self.outside)
            def _():
                self.swap(at).wait()
                self.hand_near(at).wait_recv()
                self.hand_far(at).wait_recv()


class RowReduce:
    def __init__(self, grads, total, refs):
        self.grads, self.total = grads, total
        self.far_in, self.near_in, self.far_sum, self.near_sum, self.last = refs[:5]
        self.held, self.more, self.send_sems, self.recv_sems, self.local_sems = refs[5:]
        self.z = lax.axis_index("row")
        self.own, self.partner, self.near, self.far = places(self.z)
        self.across = 3 - self.z
        self.in_middle = (self.z == 1) | (self.z == 2)
        self.outside = jnp.logical_not(self.in_middle)

    def copy_of(self, kind, source, target, device):
        return pltpu.make_async_remote_copy(
            src_ref=source,
            dst_ref=target,
            send_sem=self.send_sems.at[kind],
            recv_sem=self.recv_sems.at[kind],
            device_id={"row": device},
            device_id_type=pl.DeviceIdType.MESH,
        )

    def send_far(self):
        return self.copy_of(0, self.grads.at[self.far], self.far_in, self.partner)

    def send_near(self):
        return self.copy_of(1, self.grads.at[self.near], self.near_in, self.partner)

    def cross_far(self):
        return self.copy_of(2, self.far_in, self.far_sum, self.across)

    def cross_near(self):
        return self.copy_of(3, self.near_in, self.near_sum, self.across)

    def swap_middle(self):
        return self.copy_of(4, self.far_sum, self.last, self.partner)

    def swap_outer(self):
        return self.copy_of(4, self.grads.at[self.partner], self.last, self.partner)

    def load(self, kind, block):
        target = self.more if kind % 2 else self.held
        return pltpu.make_async_copy(self.grads.at[block], target, self.local_sems.at[kind])

    def add(self, target, source):
        @pl.loop(0, target.shape[0], step=64)
        def _(at):
            tile = pl.ds(pl.multiple_of(at, 64), 64)
            target[tile, :] = (target[tile, :].astype(f32) + source[tile, :].astype(f32)).astype(bf16)

    def begin(self):
        @pl.when(self.outside)
        def _():
            self.send_far().start()
            self.send_near().start()
            self.swap_outer().start()
            self.load(3, self.own).start()

        @pl.when(self.in_middle)
        def _():
            self.load(0, self.far).start()
            self.load(1, self.near).start()

    def second_far(self):
        @pl.when(self.in_middle)
        def _():
            self.load(0, self.far).wait()
            self.send_far().wait_recv()
            self.add(self.far_in, self.held)
            self.cross_far().start()
            self.load(2, self.partner).start()

    def second_near(self):
        @pl.when(self.in_middle)
        def _():
            self.load(1, self.near).wait()
            self.send_near().wait_recv()
            self.add(self.near_in, self.more)
            self.cross_near().start()
            self.load(3, self.own).start()

    def third(self):
        @pl.when(self.in_middle)
        def _():
            self.load(2, self.partner).wait()
            self.cross_far().wait_recv()
            self.add(self.far_sum, self.held)
            self.swap_middle().start()

    def finish(self):
        self.load(3, self.own).wait()
        self.swap_outer().wait_recv()

        @pl.when(self.in_middle)
        def _():
            self.cross_near().wait_recv()

        @pl.loop(0, self.total.shape[0], step=64)
        def _(at):
            tile = pl.ds(pl.multiple_of(at, 64), 64)
            self.total[tile, :] = self.more[tile, :].astype(f32) + self.last[tile, :].astype(f32)

        @pl.when(self.in_middle)
        def _():
            @pl.loop(0, self.total.shape[0], step=64)
            def _(at):
                tile = pl.ds(pl.multiple_of(at, 64), 64)
                self.total[tile, :] += self.near_sum[tile, :].astype(f32)

            self.cross_far().wait_send()
            self.cross_near().wait_send()
            self.swap_middle().wait_send()

        @pl.when(self.outside)
        def _():
            self.send_far().wait_send()
            self.send_near().wait_send()
            self.swap_outer().wait_send()


def signal_to(barrier, device):
    pl.semaphore_signal(barrier, inc=1, device_id=device, device_id_type=pl.DeviceIdType.MESH)


def gather_kernel(count, *refs):
    rows = RowGather(refs[:count], refs[count : 2 * count], refs[2 * count :])
    rows.greet(pltpu.get_barrier_semaphore())
    rows.begin()
    for at in range(count):
        rows.hand_on(at)
    for at in range(count):
        rows.hand_last(at)
    rows.finish()


PIECES = 4


def plane_kernel(pointwise, given, made, gather, count, reducing, *refs):
    p_ref, inputs = refs[0], refs[1 : 1 + given]
    at = 1 + given
    packs = refs[at : at + count]
    at += count
    grads = refs[at] if reducing else None
    at += reducing
    results = refs[at : at + made]
    at += made
    total_ref = refs[at] if reducing else None
    at += reducing
    whole_refs = refs[at : at + gather + count]
    at += gather + count
    mine, from_core, from_first, summed, from_second, shared, send_sems, recv_sems, local_sems = refs[
        at : at + 9
    ]
    out_ref = whole_refs[0] if gather else None
    me = lax.axis_index("col")
    core, x, y = lax.rem(me, 2), lax.rem(me // 2, 2), me // 4
    core_mate, x_mate, y_mate = me + 1 - 2 * core, me + 2 - 4 * x, me + 4 - 8 * y
    diagonal = x_mate + 4 - 8 * y
    size = mine.shape[3]
    share = mine.shape[4]
    barrier = pltpu.get_barrier_semaphore()
    for mate in (core_mate, x_mate, y_mate):
        signal_to(barrier, {"col": mate})
    rows, reduction = None, None
    if count or reducing:
        if count:
            rows = RowGather(packs, whole_refs[gather:], refs[at + 9 : at + 11])
            at += 2
        if reducing:
            reduction = RowReduce(grads, total_ref, refs[at + 9 : at + 19])
        chain = rows or reduction
        signal_to(barrier, {"row": chain.partner})

        @pl.when(chain.in_middle)
        def _():
            signal_to(barrier, {"row": chain.across})
            pl.semaphore_wait(barrier, 5)

        @pl.when(chain.outside)
        def _():
            pl.semaphore_wait(barrier, 4)

        if count:
            rows.begin()
        if reducing:
            reduction.begin()
    else:
        pl.semaphore_wait(barrier, 3)

    def remote(kind, i, source, target, mate):
        return pltpu.make_async_remote_copy(
            src_ref=source,
            dst_ref=target,
            send_sem=send_sems.at[kind, i],
            recv_sem=recv_sems.at[kind, i],
            device_id={"col": mate},
            device_id_type=pl.DeviceIdType.MESH,
        )

    def x_first(i):
        return i < PIECES // 2

    def span(i):
        return pl.ds(i * size, size)

    def core_copy(i):
        return remote(0, i, p_ref.at[:, :, 1 - core, span(i), :], from_core.at[i], core_mate)

    def load(i):
        return pltpu.make_async_copy(
            p_ref.at[:, :, core, span(i), :], mine.at[i], local_sems.at[0, i]
        )

    def first_copy(i):
        if x_first(i):
            return remote(1, i, mine.at[i, :, 1 - x], from_first.at[i], x_mate)
        return remote(1, i, mine.at[i, 1 - y], from_first.at[i], y_mate)

    def second_copy(i):
        if x_first(i):
            return remote(2, i, summed.at[i, 1 - y], from_second.at[i], y_mate)
        return remote(2, i, summed.at[i, 1 - x], from_second.at[i], x_mate)

    def columns(i, device):
        return out_ref.at[span(i), pl.ds(pl.multiple_of(device * share, share), share)]

    def spread(kind, i, mate):
        return remote(kind, i, shared.at[i], columns(i, me), mate)

    def keep(i):
        return pltpu.make_async_copy(shared.at[i], columns(i, me), local_sems.at[1, i])

    def pass_on(kind, i, device, mate):
        return remote(kind, i, columns(i, device), columns(i, device), mate)

    def forward(i):
        if x_first(i):
            return pass_on(6, i, y_mate, x_mate)
        return pass_on(6, i, x_mate, y_mate)

    order = [0, 2, 1, 3]
    for i in order:
        core_copy(i).start()
        load(i).start()
    for i in order:
        load(i).wait()
        core_copy(i).wait_recv()
        for a in range(2):
            for b in range(2):
                mine[i, a, b] = (mine[i, a, b].astype(f32) + from_core[i, a, b].astype(f32)).astype(bf16)
        first_copy(i).start()
    for i in order:
        first_copy(i).wait_recv()
        for a in range(2):
            kept = mine[i, a, x] if x_first(i) else mine[i, y, a]
            summed[i, a] = (kept.astype(f32) + from_first[i, a].astype(f32)).astype(bf16)
        second_copy(i).start()
    if count:
        for at in range(count):
            rows.hand_on(at)
    if reducing:
        reduction.second_far()
    for i in order:
        second_copy(i).wait_recv()
        total = summed[i, y if x_first(i) else x].astype(f32) + from_second[i].astype(f32)
        span_rows = slice(i * size, (i + 1) * size)
        values = pointwise(
            total, *[ref[span_rows, :] if ref.shape[0] > 8 else ref[...] for ref in inputs]
        )
        if gather:
            shared[i] = values[0].astype(bf16)
            values = values[1:]
        for ref, value in zip(results, values):
            ref[span_rows, :] = value
        if gather:
            spread(4, i, x_mate).start()
            spread(5, i, y_mate).start()
            spread(3, i, core_mate).start()
            keep(i).start()
    if count:
        rows.hand_last(0)
    if reducing and not gather:
        reduction.second_near()
    if gather:
        for i in order:
            spread(5 if x_first(i) else 4, i, y_mate).wait_recv()
            forward(i).start()
            pass_on(7, i, y_mate if x_first(i) else x_mate, core_mate).start()
        for i in order:
            spread(4 if x_first(i) else 5, i, x_mate).wait_recv()
            pass_on(8, i, x_mate if x_first(i) else y_mate, core_mate).start()
    if count:
        for at in range(1, count):
            rows.hand_last(at)
    if reducing and gather:
        reduction.second_near()
    if reducing:
        reduction.third()
    if gather:
        for i in order:
            forward(i).wait_recv()
            pass_on(9, i, diagonal, core_mate).start()
    for i in order:
        core_copy(i).wait_send()
        first_copy(i).wait_send()
        second_copy(i).wait_send()
        if gather:
            keep(i).wait()
            spread(3, i, core_mate).wait()
            spread(4, i, x_mate).wait_send()
            spread(5, i, y_mate).wait_send()
            forward(i).wait_send()
            for kind, device in (
                (7, y_mate if x_first(i) else x_mate),
                (8, x_mate if x_first(i) else y_mate),
                (9, diagonal),
            ):
                pass_on(kind, i, device, core_mate).wait()
    if count:
        rows.finish()
    if reducing:
        reduction.finish()


def plane_step(partial, pointwise, inputs, made, gather, number, packs=(), grads=None):
    tokens, share = partial.shape[3:]
    size = tokens // PIECES
    count = len(packs)
    reducing = 0 if grads is None else 1
    totals, more_scratch, given_grads = [], [], []
    if reducing:
        block, columns = grads.shape[0] // 4, grads.shape[1]
        given_grads = [grads.reshape(4, block, columns)]
        totals = [jax.ShapeDtypeStruct((block, columns), f32)]
        more_scratch = [pltpu.VMEM((block, columns), bf16)] * 7 + [
            pltpu.SemaphoreType.DMA((5,)),
            pltpu.SemaphoreType.DMA((5,)),
            pltpu.SemaphoreType.DMA((4,)),
        ]
    anywhere = pl.BlockSpec(memory_space=pl.ANY)
    vmem = pl.BlockSpec(memory_space=pltpu.VMEM)
    whole_shapes = [jax.ShapeDtypeStruct((tokens, 8 * share), bf16)] * gather + [
        jax.ShapeDtypeStruct((4,) + pack.shape, bf16) for pack in packs
    ]
    outs = pl.pallas_call(
        functools.partial(plane_kernel, pointwise, len(inputs), made, gather, count, reducing),
        in_specs=[anywhere] + [vmem] * len(inputs) + [anywhere] * (count + reducing),
        out_specs=[vmem] * (made + reducing) + [anywhere] * (gather + count),
        out_shape=[jax.ShapeDtypeStruct((tokens, share), f32)] * made + totals + whole_shapes,
        scratch_shapes=[
            pltpu.VMEM((PIECES, 2, 2, size, share), bf16),
            pltpu.VMEM((PIECES, 2, 2, size, share), bf16),
            pltpu.VMEM((PIECES, 2, size, share), bf16),
            pltpu.VMEM((PIECES, 2, size, share), bf16),
            pltpu.VMEM((PIECES, size, share), bf16),
            pltpu.VMEM((PIECES, size, share), bf16),
            pltpu.SemaphoreType.DMA((10, PIECES)),
            pltpu.SemaphoreType.DMA((10, PIECES)),
            pltpu.SemaphoreType.DMA((2, PIECES)),
        ]
        + [pltpu.SemaphoreType.DMA((5, count))] * (2 if count else 0)
        + more_scratch,
        compiler_params=pltpu.CompilerParams(collective_id=number, has_side_effects=True),
        cost_estimate=pl.CostEstimate(
            flops=60 * 10**9, bytes_accessed=32 * tokens * share, transcendentals=0
        ),
        name="plane_step",
    )(partial, *inputs, *packs, *given_grads)
    at = made + reducing
    wholes = [whole.reshape((4 * whole.shape[1],) + whole.shape[2:]) for whole in outs[at + gather :]]
    return outs[:at], outs[at : at + gather], wholes


def gather_now(packs, number):
    if lax.axis_size("row") != 4:
        return [lax.all_gather(pack, "row", axis=0, tiled=True) for pack in packs]
    count = len(packs)
    sent = sum(pack.size for pack in packs) * 2
    anywhere = pl.BlockSpec(memory_space=pl.ANY)
    wholes = pl.pallas_call(
        functools.partial(gather_kernel, count),
        in_specs=[anywhere] * count,
        out_specs=[anywhere] * count,
        out_shape=[jax.ShapeDtypeStruct((4,) + pack.shape, pack.dtype) for pack in packs],
        scratch_shapes=[pltpu.SemaphoreType.DMA((5, count)), pltpu.SemaphoreType.DMA((5, count))],
        compiler_params=pltpu.CompilerParams(collective_id=number, has_side_effects=True),
        cost_estimate=pl.CostEstimate(
            flops=6 * 9000 * sent, bytes_accessed=6 * sent, transcendentals=0
        ),
        name="gather_rows",
    )(*packs)
    return [whole.reshape((4 * whole.shape[1],) + whole.shape[2:]) for whole in wholes]


def put_own(whole, part):
    if lax.axis_size("row") != 4:
        return whole
    return lax.dynamic_update_slice_in_dim(
        whole, part, lax.axis_index("row") * part.shape[0], 0
    )


class Reduced:
    def __init__(self, grads):
        self.chained = lax.axis_size("row") == 4
        if not self.chained:
            self.total = lax.psum_scatter(grads, "row", scatter_dimension=0, tiled=True).astype(f32)
            return
        z = lax.axis_index("row")
        self.own, self.partner, _, _ = places(z)
        self.grads, self.size = grads, grads.shape[0] // 4
        self.pair = self.rows_of(grads, (1 - z // 2) * 2, 2)
        self.first = lax.ppermute(self.pair, "row", INWARD)

    def rows_of(self, value, at, count):
        return lax.dynamic_slice_in_dim(value, at * self.size, count * self.size, 0)

    def two(self, at):
        mine = self.rows_of(self.grads, at, 1).astype(f32)
        return mine + self.rows_of(self.crossed, lax.rem(at, 2), 1).astype(f32)

    def second(self, *groups):
        if not self.chained:
            return ()
        first = after(self.first, *groups)
        value = (self.pair.astype(f32) + first.astype(f32)).astype(bf16)
        self.crossed = lax.ppermute(value, "row", MIDDLE)
        return (value,)

    def third(self, *groups):
        if not self.chained:
            return ()
        self.crossed = after(self.crossed, *groups)
        value = self.two(self.partner).astype(bf16)
        self.swapped = lax.ppermute(value, "row", PAIRS)
        return (value,)

    def result(self):
        if self.chained:
            return self.two(self.own) + self.swapped.astype(f32)
        return self.total


def one_reduction(grads):
    one = Reduced(grads)
    one.second()
    one.third()
    return one.result()


def after(value, *groups):
    others = tuple(item for group in groups for item in group)
    return lax.optimization_barrier((value,) + others)[0] if others else value


def expert_kernel(size, steps, count, ahead, *refs):
    pieces = refs[:count]
    (x_ref, cot_ref, x_cols, cot_cols, coef_ref) = refs[count : count + 5]
    at = count + 5 + ahead
    (dpair_ref, hidden_ref, sums_ref, grads_ref, whole_ref) = refs[at : at + 5]
    weights, dpair, hidden, sems, out_sem = refs[at + 5 + ahead : at + 10 + ahead]
    step = pl.program_id(0)
    final = pl.num_programs(0) - 1
    if ahead:
        rows = RowGather(refs[count + 5 : count + 6], refs[at + 5 : at + 6], refs[at + 10 + ahead :])

        @pl.when(step == 0)
        def _():
            rows.greet(pltpu.get_barrier_semaphore())
            rows.begin()

        @pl.when(step == final - 2)
        def _():
            rows.hand_on(0)

    write = pltpu.make_async_copy(weights, whole_ref, out_sem)

    @pl.when(step == 0)
    def _():
        if count == 1:
            copy = pltpu.make_async_copy(pieces[0], weights, sems.at[0])
            copy.start()
            copy.wait()
        elif count == 2:
            block = pieces[0].shape[0]

            def block_copy(back):
                at = pl.multiple_of(lax.rem(lax.axis_index("row") + back, 4) * block, block)
                source = pieces[1].at[pl.ds(at, block)] if back else pieces[0]
                return pltpu.make_async_copy(source, weights.at[pl.ds(at, block)], sems.at[back])

            for back in range(4):
                block_copy(back).start()
            for back in range(4):
                block_copy(back).wait()
        else:
            z = lax.axis_index("row")
            block = pieces[0].shape[0]

            def copy_of(piece, which):
                at = pl.multiple_of(places(z)[which] * block, block)
                return pltpu.make_async_copy(
                    piece, weights.at[pl.ds(at, block)], sems.at[which]
                )

            copy_of(pieces[0], 0).start()
            copy_of(pieces[1], 1).start()
            in_middle = (z == 1) | (z == 2)

            @pl.when(in_middle)
            def _():
                copy_of(pieces[2], 2).start()
                copy_of(pieces[3], 3).start()

            @pl.when(jnp.logical_not(in_middle))
            def _():
                copy_of(pieces[4], 2).start()
                copy_of(pieces[5], 3).start()

            for which in range(4):
                copy_of(pieces[which], which).wait()
        write.start()

    @pl.when(step < steps)
    def _():
        at = pl.multiple_of(step * TILE, TILE)
        rows, cots = x_ref[...], cot_ref[...]
        scale, weight = coef_ref[:, 0:1], coef_ref[:, 1:2]
        dots = jnp.zeros((TILE, 1), f32)
        inner = jnp.zeros((TILE, 1), f32)
        for a in range(0, size, TILE):
            b = min(a + TILE, size)
            gate = scale * mm(rows, weights[:, a:b])
            up = scale * mm(rows, weights[:, size + a : size + b])
            dhid = mm(cots, weights[:, 2 * size + a : 2 * size + b])
            sigma = jax.nn.sigmoid(gate)
            silu = gate * sigma
            hid = silu * up
            dots += jnp.sum(hid * dhid, axis=1, keepdims=True)
            dhid = weight * dhid
            dgate = dhid * up * sigma * (1.0 + gate * (1.0 - sigma))
            dup = dhid * silu
            inner += jnp.sum(dgate * gate + dup * up, axis=1, keepdims=True)
            for into, at_col, value in (
                ((hidden_ref, hidden), a, weight * hid),
                ((dpair_ref, dpair), a, scale * dgate),
                ((dpair_ref, dpair), size + a, scale * dup),
            ):
                value = value.astype(bf16)
                into[0][:, at_col : at_col + b - a] = value
                into[1][pl.ds(at, TILE), at_col : at_col + b - a] = value
        sums_ref[:, 0:1] = dots
        sums_ref[:, 1:2] = inner

    @pl.when(step >= steps)
    def _():
        for a in range(0, 2 * size, TILE):
            b = min(a + TILE, 2 * size)
            grads_ref[:, a:b] = mm_tn(x_cols[...], dpair[:, a:b]).astype(bf16)
        for a in range(0, size, TILE):
            b = min(a + TILE, size)
            grads_ref[:, 2 * size + a : 2 * size + b] = mm_tn(
                cot_cols[...], hidden[:, a:b]
            ).astype(bf16)

    @pl.when(step == final)
    def _():
        write.wait()
        if ahead:
            rows.hand_last(0)
            rows.finish()


def expert_chunk(pieces, scaled, cots, coef, pack=None, number=None):
    tokens, width = scaled.shape
    size = pieces[0].shape[1] // 3
    steps, more_steps = tokens // TILE, width // TILE
    count = len(pieces)
    rows = lambda i: (jnp.minimum(i, steps - 1), 0)
    cols = lambda i: (0, jnp.maximum(i - steps, 0))
    down = lambda i: (jnp.maximum(i - steps, 0), 0)
    anywhere = pl.BlockSpec(memory_space=pl.ANY)
    ahead, more, more_shapes, more_scratch, params = 0, [], [], [], {}
    if pack is not None:
        ahead, more = 1, [pack]
        more_shapes = [jax.ShapeDtypeStruct((4,) + pack.shape, bf16)]
        more_scratch = [pltpu.SemaphoreType.DMA((5, 1))] * 2
        params = dict(collective_id=number, has_side_effects=True)
    outs = pl.pallas_call(
        functools.partial(expert_kernel, size, steps, count, ahead),
        grid_spec=pl.GridSpec(
            grid=(steps + more_steps,),
            in_specs=[pl.BlockSpec(memory_space=pl.ANY)] * count
            + [
                pl.BlockSpec((TILE, width), rows),
                pl.BlockSpec((TILE, width), rows),
                pl.BlockSpec((tokens, TILE), cols),
                pl.BlockSpec((tokens, TILE), cols),
                pl.BlockSpec((TILE, 2), rows),
            ]
            + [anywhere] * ahead,
            out_specs=[
                pl.BlockSpec((TILE, 2 * size), rows),
                pl.BlockSpec((TILE, size), rows),
                pl.BlockSpec((TILE, 2), rows),
                pl.BlockSpec((TILE, 3 * size), down),
                anywhere,
            ]
            + [anywhere] * ahead,
            scratch_shapes=[
                pltpu.VMEM((width, 3 * size), bf16),
                pltpu.VMEM((tokens, 2 * size), bf16),
                pltpu.VMEM((tokens, size), bf16),
                pltpu.SemaphoreType.DMA((4,)),
                pltpu.SemaphoreType.DMA,
            ]
            + more_scratch,
        ),
        out_shape=[
            jax.ShapeDtypeStruct((tokens, 2 * size), bf16),
            jax.ShapeDtypeStruct((tokens, size), bf16),
            jax.ShapeDtypeStruct((tokens, 2), f32),
            jax.ShapeDtypeStruct((width, 3 * size), bf16),
            jax.ShapeDtypeStruct((width, 3 * size), bf16),
        ]
        + more_shapes,
        compiler_params=pltpu.CompilerParams(**params),
        cost_estimate=pl.CostEstimate(
            flops=12 * tokens * width * size,
            bytes_accessed=8 * tokens * width + 24 * width * size,
            transcendentals=tokens * size,
        ),
        name="expert_chunk",
    )(*pieces, scaled, cots, scaled, cots, coef, *more)
    if ahead:
        return outs[:5], (pack, outs[5].reshape(4 * pack.shape[0], pack.shape[1]))
    return outs, None


def joint_kernel(count, based, planar, *refs):
    out_ref = refs[-1]
    for a in range(0, refs[count].shape[0], TILE):
        total = refs[2 * count][:, a : a + TILE] if based else None
        for left, weights in zip(refs[:count], refs[count : 2 * count]):
            part = mm_nt(left[...], weights[a : a + TILE, :])
            total = part if total is None else total + part
        if planar:
            at = a // TILE
            out_ref[at // 4, at // 2 % 2, at % 2] = total.astype(out_ref.dtype)
        else:
            out_ref[:, a : a + TILE] = total.astype(out_ref.dtype)


def joint_back(lefts, weights, column, kind, *base, planar=False):
    tokens, width = lefts[0].shape[0], weights[0].shape[0]
    row = lambda i: (i, 0)
    fixed = lambda i: (0, column)
    depth = sum(left.shape[1] for left in lefts)
    return pl.pallas_call(
        functools.partial(joint_kernel, len(lefts), len(base) > 0, planar),
        grid=(tokens // TILE,),
        in_specs=[pl.BlockSpec((TILE, left.shape[1]), row) for left in lefts]
        + [
            pl.BlockSpec((width, left.shape[1]), fixed, pipeline_mode=pl.Buffered(1))
            for left in lefts
        ]
        + [pl.BlockSpec((TILE, width), row)] * len(base),
        out_specs=pl.BlockSpec((2, 2, 2, TILE, TILE), lambda i: (0, 0, 0, i, 0))
        if planar
        else pl.BlockSpec((TILE, width), row),
        out_shape=jax.ShapeDtypeStruct((2, 2, 2, tokens, TILE) if planar else (tokens, width), kind),
        cost_estimate=pl.CostEstimate(
            flops=2 * tokens * width * depth,
            bytes_accessed=2 * (tokens + width) * depth + 4 * tokens * width,
            transcendentals=0,
        ),
        name="joint_back",
    )(*lefts, *weights, *base)


def split_three(values):
    high = values.astype(bf16)
    rest = values - high.astype(f32)
    middle = rest.astype(bf16)
    return high, middle, (rest - middle.astype(f32)).astype(bf16)


def cuts_of(width, sizes):
    cuts, at = [], 0
    for size in sizes:
        if at + size < width:
            cuts.append((at, at + size))
            at += size
    return cuts + [(at, width)]


def stream_step(total, rows, gain):
    stream = rows.astype(f32) + total
    return stream * gain, stream


def dstream_step(total, back, cots, stream, damp, gain):
    dscaled = back + total
    dstream = cots.astype(f32) + gain * dscaled - stream * damp
    return dstream, dstream, dscaled


def per_device(
    block_input,
    seq_lengths,
    slot_order,
    routes,
    input_gain,
    query_weight,
    key_weight,
    value_weight,
    output_weight,
    mlp_gain,
    router_weight,
    score_shared,
    gate_shared,
    up_shared,
    down_shared,
    gate_expert,
    up_expert,
    down_expert,
    grad_output,
):
    tokens, share = block_input.shape
    cols = lax.axis_size("col")
    col_id = lax.axis_index("col")
    row_id = lax.axis_index("row")
    width = share * cols
    slots = tokens // SEQ_LEN
    local_experts = gate_expert.shape[0]
    experts = router_weight.shape[1]
    head_width = query_weight.shape[1]
    heads = head_width // HEAD_DIM
    rows_block = query_weight.shape[0]
    lengths = lax.dynamic_slice_in_dim(seq_lengths[slot_order], row_id * slots, slots, 0)
    cosine, sine = rope_tables()

    def by_head(weight):
        return weight.reshape(rows_block, heads, 1, HEAD_DIM)

    qkv_pack = jnp.concatenate(
        [by_head(query_weight), by_head(key_weight), by_head(value_weight)], axis=2
    ).reshape(rows_block, 3 * head_width)
    router_pack = jnp.concatenate([router_weight, score_shared[:, None]], axis=1)
    router_pack = jnp.pad(router_pack, ((0, 0), (0, -router_pack.shape[1] % 128)))
    out_pack = jnp.concatenate([output_weight.T, router_pack], axis=1)
    qkv_whole, out_whole = gather_now([qkv_pack, out_pack], 0)
    qkv_full, out_weights = put_own(qkv_whole, qkv_pack), put_own(out_whole, out_pack)
    out_full = out_weights[:, :head_width]
    router_full = out_weights[:, head_width : head_width + experts + 1]
    shared_cuts = [(None, a, b) for a, b in cuts_of(gate_shared.shape[1], (512,))]
    expert_cuts = [
        (local, a, b)
        for local in range(local_experts)
        for a, b in cuts_of(gate_expert.shape[2], (512, 512))
    ]
    chunks = shared_cuts[-1:] + expert_cuts[:-1] + shared_cuts[:-1] + expert_cuts[-1:]

    def pack(kind, a, b):
        if kind is None:
            parts = [gate_shared[:, a:b], up_shared[:, a:b], down_shared[a:b].T]
        else:
            parts = [gate_expert[kind, :, a:b], up_expert[kind, :, a:b], down_expert[kind, a:b].T]
        fill = -(b - a) % 128
        return jnp.concatenate([jnp.pad(part, ((0, 0), (0, fill))) for part in parts], axis=1)

    packs = [pack(*chunk) for chunk in chunks]
    chained = lax.axis_size("row") == 4
    planar = chained and cols == 8 and share == TILE
    gathered = {}
    gathered[0] = Gathered(packs[0])

    rows_in = lax.all_gather(block_input, "col", axis=1, tiled=True)
    gains = lax.all_gather(jnp.stack([input_gain, mlp_gain]), "col", axis=1, tiled=True).astype(f32)
    cot_rows = lax.all_gather(grad_output, "col", axis=1, tiled=True)
    rows_f = rows_in.astype(f32)
    scale_a = lax.rsqrt(jnp.mean(rows_f * rows_f, axis=-1, keepdims=True) + norm_eps)
    normed_a = (rows_f * scale_a * gains[0]).astype(bf16)
    raw = mm(normed_a, qkv_full)
    raw = after(raw, gathered[0].second())
    qkv, context, lse = attend_forward(raw, lengths, cosine, sine)
    context = after(context, gathered[0].third())
    x_share = block_input.astype(f32)
    gain_b = mlp_gain.astype(f32)
    if planar:
        attn_part = joint_back([context], [out_weights], 0, bf16, planar=True)
        attn_part = after(attn_part, (cot_rows,))
        (stream,), (scaled,), wholes_now = plane_step(
            attn_part, stream_step, [block_input, gain_b[None]], 1, 1, 1, packs[1:2]
        )
        gathered[1] = (packs[1], wholes_now[0])
    else:
        attn_part = mm_nt(context, out_full).astype(bf16)
        attn_sum = lax.psum_scatter(attn_part, "col", scatter_dimension=1, tiled=True)
        scaled_share, stream = stream_step(attn_sum.astype(f32), block_input, gain_b[None])
        scaled = lax.all_gather(scaled_share.astype(bf16), "col", axis=1, tiled=True)
    for at in range(1, 1 if planar else len(chunks)):
        if at not in gathered:
            gathered[at] = Gathered(packs[at], (scaled,))

    def pieces_of(at):
        return gathered[at] if isinstance(gathered[at], tuple) else gathered[at].pieces

    stream_f = scaled.astype(f32) / gains[1]
    scale_b = lax.rsqrt(jnp.mean(stream_f * stream_f, axis=1, keepdims=True) + norm_eps)

    both_logits = scale_b * mm(scaled, router_full)
    logits, slogit = both_logits[:, :experts], both_logits[:, experts]
    top = jnp.max(logits, axis=-1, keepdims=True)
    expo = jnp.exp(logits - top)
    router_probs = expo / jnp.sum(expo, axis=-1, keepdims=True)
    shared_gate = jax.nn.sigmoid(slogit)

    inner = jnp.zeros((tokens,), f32)
    dots = {}
    members, shares = {None: None}, {None: shared_gate}
    for local in range(local_experts):
        expert = col_id * local_experts + local
        members[local] = jnp.any(routes == expert, axis=1)
        column = lax.dynamic_index_in_dim(router_probs, expert, 1, False)
        shares[local] = jnp.where(members[local], column, 0.0)
    dpairs, hiddens, wholes, reduced = [], [], [], []
    last = len(chunks) - 1
    waits = ()
    if not planar:
        for at in range(1, len(chunks)):
            gathered[at].second()
            gathered[at].third()

    def joints(*base):
        return (
            joint_back(dpairs[-2:], wholes[-2:], 0, f32, *base[:1]),
            joint_back(hiddens[-2:], wholes[-2:], 2, f32, *base[1:]),
        )

    for at, (kind, a, b) in enumerate(chunks):
        coef = jnp.concatenate([scale_b, shares[kind][:, None]], axis=1)
        coef = after(coef, waits)
        later = at + 2 if planar and at + 2 <= last else None
        (dpair, hidden, sums, grads, whole), found = expert_chunk(
            pieces_of(at),
            scaled,
            cot_rows,
            coef,
            None if later is None else packs[later],
            4 + at,
        )
        if later is not None:
            gathered[later] = found
        dots[kind] = dots.get(kind, 0.0) + sums[:, 0]
        inner = inner + sums[:, 1]
        dpairs.append(dpair)
        hiddens.append(hidden)
        wholes.append(whole)
        now = (sums,)
        waits = ()
        if at == 1:
            early, joined = joints(), 2
            waits += early
        elif at == 3 and at < last:
            early, joined = joints(*early), 4
            waits += early
        if at == 3:
            now = early
        if not planar:
            reduced.append(Reduced(grads))
        elif at < last:
            if at >= 1:
                waits += reduced[at - 1].second(now)
            if at >= 2:
                waits += reduced[at - 2].third((sums,))
            reduced.append(Reduced(grads))
            waits += (reduced[at].pair,)
    now = (sums,)
    if planar:
        waits = reduced[3].second(now)
        waits += reduced[2].third(now)
    else:
        waits = ()
        for one in reduced:
            one.second()
            one.third()
    late_pairs, late_wholes, late_hiddens = dpairs[joined:], wholes[joined:], hiddens[joined:]
    late_pairs[-1] = after(late_pairs[-1], waits)
    dscaled_part = joint_back(late_pairs, late_wholes, 0, bf16, early[0], planar=planar)

    named = [jnp.where(members[local], dots[local], 0.0) for local in range(local_experts)]
    table = lax.all_gather(jnp.stack(named + [dots[None], inner]), "col", axis=0)
    dprob = table[:, :local_experts].reshape(experts, tokens).T
    dshared_gate, inner = jnp.sum(table[:, local_experts], axis=0), jnp.sum(table[:, local_experts + 1], axis=0)
    dlogits = router_probs * (dprob - jnp.sum(dprob * router_probs, axis=1, keepdims=True))
    dslogit = dshared_gate * shared_gate * (1.0 - shared_gate)
    dboth = jnp.concatenate([dlogits, dslogit[:, None]], axis=1)
    inner = inner + jnp.sum(dboth * both_logits, axis=1)
    dboth = scale_b * dboth
    parts = split_three(dboth)
    router_rows = lax.dynamic_slice_in_dim(router_full, col_id * share, share, 0)
    back_term = mm_nt(jnp.concatenate(parts, axis=1), jnp.concatenate([router_rows] * 3, axis=1))
    damp = scale_b * scale_b * inner[:, None] / width
    step_inputs = [back_term, grad_output, stream, damp, gain_b[None]]
    if planar:
        (dstream, dscaled, last_grad), (dattn,), _ = plane_step(
            dscaled_part, dstream_step, step_inputs, 2, 1, 2, (), grads
        )
    else:
        dscaled_sum = lax.psum_scatter(dscaled_part, "col", scatter_dimension=1, tiled=True)
        dstream_low, dstream, dscaled = dstream_step(dscaled_sum.astype(f32), *step_inputs)
        dattn = lax.all_gather(dstream_low.astype(bf16), "col", axis=1, tiled=True)
    gain_b_grad = jnp.sum(dscaled * stream, axis=0)

    late_hiddens[-1] = after(late_hiddens[-1], (dattn,))
    moe_part = joint_back(late_hiddens, late_wholes, 2, bf16, early[1])
    moe_share = lax.psum_scatter(moe_part, "col", scatter_dimension=1, tiled=True).astype(f32)
    block_output = (stream + moe_share).astype(bf16)
    out_part = mm_tn(dattn, context).astype(bf16)
    dcontext = mm(dattn, out_full).astype(bf16)
    if planar:
        dcontext = after(dcontext, reduced[3].third((dattn,)))
    router_left = after(jnp.concatenate(parts, axis=1), (dattn,))
    grad_router_part = mm_tn(router_left, scaled).reshape(3, experts + 1, width).sum(axis=0)
    grad_router_both = lax.psum_scatter(grad_router_part, "row", scatter_dimension=1, tiled=True)
    dqkv, inner_a = attend_backward(qkv, dcontext, lse, lengths, cosine, sine)
    inner_a = lax.psum(inner_a[:, 0], "col")[:, None]
    attn_grads = jnp.concatenate([mm_tn(normed_a, dqkv).astype(bf16), out_part], axis=1)
    if planar:
        dnormed_part = joint_back([dqkv], [qkv_full], 0, bf16, planar=True)
        dnormed_part = after(dnormed_part, (inner_a,))
        (dnormed_a, attn_grad), _, _ = plane_step(
            dnormed_part, lambda total: (total,), [], 1, 0, 3, (), attn_grads
        )
    else:
        dnormed_a = lax.psum_scatter(
            mm_nt(dqkv, qkv_full).astype(bf16), "col", scatter_dimension=1, tiled=True
        ).astype(f32)
        attn_grad = one_reduction(attn_grads)
    qkv_grad, out_grad = attn_grad[:, : 3 * head_width], attn_grad[:, 3 * head_width :]
    unit_grads = [one.result() for one in reduced]
    if planar:
        unit_grads.append(last_grad)
    gain_a_share = input_gain.astype(f32)
    dinput = dstream + scale_a * gain_a_share * dnormed_a
    dinput = dinput - x_share * (scale_a * scale_a * inner_a / width)
    gain_a_grad = jnp.sum(dnormed_a * x_share * scale_a, axis=0)
    grad_gain_a, grad_gain_b = lax.psum((gain_a_grad, gain_b_grad), "row")

    qkv_grad = qkv_grad.reshape(rows_block, heads, 3, HEAD_DIM)
    grad_query, grad_key, grad_value = (
        qkv_grad[:, :, part].reshape(rows_block, head_width) for part in range(3)
    )
    def unpack(kind, which):
        found = []
        for (of, a, b), grad in zip(chunks, unit_grads):
            if of == kind:
                size = grad.shape[1] // 3
                part = grad[:, which * size : which * size + b - a]
                found.append((a, part.T if which == 2 else part))
        found = [part for _, part in sorted(found, key=lambda item: item[0])]
        return jnp.concatenate(found, axis=0 if which == 2 else 1)

    locals_ = range(local_experts)
    return (
        block_output,
        dinput.astype(bf16),
        grad_gain_a,
        grad_query,
        grad_key,
        grad_value,
        out_grad.T,
        grad_gain_b,
        grad_router_both[:experts].T,
        grad_router_both[experts],
        unpack(None, 0),
        unpack(None, 1),
        unpack(None, 2),
        jnp.stack([unpack(local, 0) for local in locals_]),
        jnp.stack([unpack(local, 1) for local in locals_]),
        jnp.stack([unpack(local, 2) for local in locals_]),
    )


def solution(mesh):
    return jax.shard_map(
        per_device,
        mesh=mesh,
        in_specs=(
            P("row", "col"),
            P(),
            P(),
            P("row", None),
            P("col"),
            P("row", "col"),
            P("row", "col"),
            P("row", "col"),
            P("col", "row"),
            P("col"),
            P("row", None),
            P("row"),
            P("row", "col"),
            P("row", "col"),
            P("col", "row"),
            P("col", "row", None),
            P("col", "row", None),
            P("col", None, "row"),
            P("row", "col"),
        ),
        out_specs=(
            P("row", "col"),
            P("row", "col"),
            P("col"),
            P("row", "col"),
            P("row", "col"),
            P("row", "col"),
            P("col", "row"),
            P("col"),
            P("row", None),
            P("row"),
            P("row", "col"),
            P("row", "col"),
            P("col", "row"),
            P("col", "row", None),
            P("col", "row", None),
            P("col", None, "row"),
        ),
        check_vma=False,
    )
```

```python
import functools
import math

import jax
import jax.numpy as jnp
from jax import lax
from jax.experimental import pallas as pl
from jax.experimental.pallas import tpu as pltpu
from jax.sharding import PartitionSpec as P

HEAD_DIM = 128
SEQ_LEN = 1024
QBLOCK = 256
TILE = 256
norm_eps = 1e-06
rope_base = 1000000.0
bf16 = jnp.bfloat16
f32 = jnp.float32


def mm(left, right):
    return jnp.dot(left, right, preferred_element_type=f32)


def mm_nt(left, right):
    return lax.dot_general(left, right, (((1,), (1,)), ((), ())), preferred_element_type=f32)


def mm_tn(left, right):
    return lax.dot_general(left, right, (((0,), (0,)), ((), ())), preferred_element_type=f32)


def rope_tables():
    positions = jnp.arange(SEQ_LEN).astype(f32)
    freqs = jnp.power(f32(rope_base), -jnp.arange(0, HEAD_DIM, 2).astype(f32) / HEAD_DIM)
    angles = positions[:, None] * freqs[None, :]
    cosine, sine = jnp.cos(angles), jnp.sin(angles)
    return (
        jnp.concatenate([cosine, cosine], axis=-1),
        jnp.concatenate([-sine, sine], axis=-1),
    )


def block_scores(rows, keys, start, length, scale):
    raw = mm_nt(rows, keys) * scale
    query_pos = start + lax.broadcasted_iota(jnp.int32, raw.shape, 0)
    key_pos = lax.broadcasted_iota(jnp.int32, raw.shape, 1)
    return jnp.where((key_pos <= query_pos) & (key_pos < length), raw, -1e30)


def attend_forward_kernel(length_ref, raw_ref, cos_ref, sin_ref, qkv_ref, context_ref, lse_ref):
    length = length_ref[pl.program_id(0)]
    scale = 1.0 / math.sqrt(HEAD_DIM)
    hd = HEAD_DIM
    for part in range(2):
        raw = raw_ref[:, part * hd : (part + 1) * hd]
        turned = raw * cos_ref[...] + pltpu.roll(raw, hd // 2, 1) * sin_ref[...]
        qkv_ref[:, part * hd : (part + 1) * hd] = turned.astype(bf16)
    qkv_ref[:, 2 * hd :] = raw_ref[:, 2 * hd :].astype(bf16)
    for at in range(0, SEQ_LEN, QBLOCK):
        seen = at + QBLOCK
        scores = block_scores(
            qkv_ref[at:seen, :hd], qkv_ref[:seen, hd : 2 * hd], at, length, scale
        )
        top = jnp.max(scores, axis=-1, keepdims=True)
        expo = jnp.exp(scores - top)
        total = jnp.sum(expo, axis=-1, keepdims=True)
        probs = (expo / total).astype(bf16)
        context_ref[at:seen, :] = mm(probs, qkv_ref[:seen, 2 * hd :]).astype(bf16)
        lse_ref[at:seen, :] = jnp.broadcast_to(top + jnp.log(total), (QBLOCK, hd))


def attend_forward(raw, lengths, cosine, sine):
    tokens, width = raw.shape
    heads = width // (3 * HEAD_DIM)
    slots = tokens // SEQ_LEN
    wide = pl.BlockSpec((SEQ_LEN, 3 * HEAD_DIM), lambda s, h, _: (s, h))
    one = pl.BlockSpec((SEQ_LEN, HEAD_DIM), lambda s, h, _: (s, h))
    table = pl.BlockSpec((SEQ_LEN, HEAD_DIM), lambda s, h, _: (0, 0))
    pairs = slots * heads * SEQ_LEN * SEQ_LEN
    return pl.pallas_call(
        attend_forward_kernel,
        grid_spec=pltpu.PrefetchScalarGridSpec(
            num_scalar_prefetch=1,
            grid=(slots, heads),
            in_specs=[wide, table, table],
            out_specs=[wide, one, one],
        ),
        out_shape=[
            jax.ShapeDtypeStruct((tokens, width), bf16),
            jax.ShapeDtypeStruct((tokens, heads * HEAD_DIM), bf16),
            jax.ShapeDtypeStruct((tokens, heads * HEAD_DIM), f32),
        ],
        cost_estimate=pl.CostEstimate(
            flops=3 * HEAD_DIM * pairs, bytes_accessed=8 * tokens * width, transcendentals=pairs
        ),
        name="attend_forward",
    )(lengths, raw, cosine, sine)


def attend_backward_kernel(
    length_ref, qkv_ref, dcontext_ref, lse_ref, cos_ref, sin_ref, dqkv_ref, inner_ref, dk_ref, dv_ref
):
    length = length_ref[pl.program_id(0)]
    scale = 1.0 / math.sqrt(HEAD_DIM)
    hd = HEAD_DIM
    @pl.when(pl.program_id(1) == 0)
    def _():
        inner_ref[...] = jnp.zeros_like(inner_ref)

    dk_ref[...] = jnp.zeros_like(dk_ref)
    dv_ref[...] = jnp.zeros_like(dv_ref)

    def turn_back(grad, rows):
        back = grad * cos_ref[rows, :] - pltpu.roll(grad, hd // 2, 1) * sin_ref[rows, :]
        return back.astype(bf16)

    for at in range(0, SEQ_LEN, QBLOCK):
        seen = at + QBLOCK
        rows = qkv_ref[at:seen, :hd]
        keys = qkv_ref[:seen, hd : 2 * hd]
        drows = dcontext_ref[at:seen, :]
        scores = block_scores(rows, keys, at, length, scale)
        probs = jnp.exp(scores - lse_ref[at:seen, :1])
        dv_ref[:seen, :] += mm_tn(probs.astype(bf16), drows)
        dprobs = mm_nt(drows, qkv_ref[:seen, 2 * hd :])
        dscore = probs * (dprobs - jnp.sum(dprobs * probs, axis=-1, keepdims=True))
        draw = (dscore * scale).astype(bf16)
        dquery = mm(draw, keys)
        dk_ref[:seen, :] += mm_tn(draw, rows)
        dqkv_ref[at:seen, :hd] = turn_back(dquery, slice(at, seen))
        inner_ref[at:seen, :] += jnp.sum(dquery * rows.astype(f32), axis=-1, keepdims=True)
    dkey, dvalue = dk_ref[...], dv_ref[...]
    dqkv_ref[:, hd : 2 * hd] = turn_back(dkey, slice(None))
    dqkv_ref[:, 2 * hd :] = dvalue.astype(bf16)
    inner_ref[...] += jnp.sum(
        dkey * qkv_ref[:, hd : 2 * hd].astype(f32) + dvalue * qkv_ref[:, 2 * hd :].astype(f32),
        axis=-1,
        keepdims=True,
    )


def attend_backward(qkv, dcontext, lse, lengths, cosine, sine):
    tokens, width = qkv.shape
    heads = width // (3 * HEAD_DIM)
    slots = tokens // SEQ_LEN
    wide = pl.BlockSpec((SEQ_LEN, 3 * HEAD_DIM), lambda s, h, _: (s, h))
    one = pl.BlockSpec((SEQ_LEN, HEAD_DIM), lambda s, h, _: (s, h))
    table = pl.BlockSpec((SEQ_LEN, HEAD_DIM), lambda s, h, _: (0, 0))
    pairs = slots * heads * SEQ_LEN * SEQ_LEN
    return pl.pallas_call(
        attend_backward_kernel,
        grid_spec=pltpu.PrefetchScalarGridSpec(
            num_scalar_prefetch=1,
            grid=(slots, heads),
            in_specs=[wide, one, one, table, table],
            out_specs=[wide, pl.BlockSpec((SEQ_LEN, 1), lambda s, h, _: (s, 0))],
            scratch_shapes=[pltpu.VMEM((SEQ_LEN, HEAD_DIM), f32)] * 2,
        ),
        out_shape=[
            jax.ShapeDtypeStruct((tokens, width), bf16),
            jax.ShapeDtypeStruct((tokens, 1), f32),
        ],
        cost_estimate=pl.CostEstimate(
            flops=8 * HEAD_DIM * pairs, bytes_accessed=8 * tokens * width, transcendentals=pairs
        ),
        name="attend_backward",
    )(lengths, qkv, dcontext, lse, cosine, sine)


PAIRS = [(0, 1), (1, 0), (2, 3), (3, 2)]
MIDDLE = [(1, 2), (2, 1)]
OUTWARD = [(1, 0), (2, 3)]
INWARD = [(0, 1), (3, 2)]


class Gathered:
    def __init__(self, part, *groups):
        self.part = part
        if lax.axis_size("row") != 4:
            self.pieces = (lax.all_gather(part, "row", axis=0, tiled=True),)
            return
        part = after(part, *groups)
        self.partner = lax.ppermute(part, "row", PAIRS)
        self.near_mid = lax.ppermute(part, "row", MIDDLE)
        self.pieces = None

    def second(self, *groups):
        if self.pieces is None:
            self.near_out = lax.ppermute(after(self.near_mid, *groups), "row", OUTWARD)
            self.far_mid = lax.ppermute(after(self.partner, *groups), "row", MIDDLE)
            return (self.partner, self.near_mid)
        return ()

    def third(self, *groups):
        if self.pieces is None:
            self.far_out = lax.ppermute(after(self.far_mid, *groups), "row", OUTWARD)
            self.pieces = (
                self.part, self.partner, self.near_mid, self.far_mid, self.near_out, self.far_out
            )
            return (self.far_mid, self.near_out)
        return ()


def places(z):
    pair = z // 2
    return z, z + 1 - 2 * lax.rem(z, 2), 2 - pair, 3 - 3 * pair


class RowGather:
    def __init__(self, packs, wholes, sems):
        self.packs, self.wholes, (self.send_sems, self.recv_sems) = packs, wholes, sems
        self.z = lax.axis_index("row")
        self.own, self.partner, self.near, self.far = places(self.z)
        self.across = 3 - self.z
        self.in_middle = (self.z == 1) | (self.z == 2)
        self.outside = jnp.logical_not(self.in_middle)

    def copy_of(self, kind, at, source, block, target):
        return pltpu.make_async_remote_copy(
            src_ref=source,
            dst_ref=self.wholes[at].at[block],
            send_sem=self.send_sems.at[kind, at],
            recv_sem=self.recv_sems.at[kind, at],
            device_id={"row": target},
            device_id_type=pl.DeviceIdType.MESH,
        )

    def swap(self, at):
        return self.copy_of(0, at, self.packs[at], self.own, self.partner)

    def swap_middle(self, at):
        return self.copy_of(1, at, self.packs[at], self.own, self.across)

    def second_middle(self, at):
        return self.copy_of(2, at, self.wholes[at].at[self.partner], self.partner, self.across)

    def hand_near(self, at):
        return self.copy_of(3, at, self.wholes[at].at[self.near], self.near, self.partner)

    def hand_far(self, at):
        return self.copy_of(4, at, self.wholes[at].at[self.far], self.far, self.partner)

    def greet(self, barrier):
        signal_to(barrier, {"row": self.partner})

        @pl.when(self.in_middle)
        def _():
            signal_to(barrier, {"row": self.across})
            pl.semaphore_wait(barrier, 2)

        @pl.when(self.outside)
        def _():
            pl.semaphore_wait(barrier, 1)

    def begin(self):
        for at in range(len(self.packs)):
            @pl.when(self.in_middle)
            def _():
                self.swap_middle(at).start()

            self.swap(at).start()

    def hand_on(self, at):
        @pl.when(self.in_middle)
        def _():
            self.swap_middle(at).wait_recv()
            self.hand_near(at).start()
            self.swap(at).wait_recv()
            self.second_middle(at).start()

    def hand_last(self, at):
        @pl.when(self.in_middle)
        def _():
            self.second_middle(at).wait_recv()
            self.hand_far(at).start()

    def finish(self):
        for at in range(len(self.packs)):
            @pl.when(self.in_middle)
            def _():
                for copy in (
                    self.swap,
                    self.swap_middle,
                    self.second_middle,
                    self.hand_near,
                    self.hand_far,
                ):
                    copy(at).wait_send()

            @pl.when(self.outside)
            def _():
                self.swap(at).wait()
                self.hand_near(at).wait_recv()
                self.hand_far(at).wait_recv()


class RowReduce:
    def __init__(self, grads, total, refs):
        self.grads, self.total = grads, total
        self.far_in, self.near_in, self.far_sum, self.near_sum, self.last = refs[:5]
        self.held, self.more, self.send_sems, self.recv_sems, self.local_sems = refs[5:]
        self.z = lax.axis_index("row")
        self.own, self.partner, self.near, self.far = places(self.z)
        self.across = 3 - self.z
        self.in_middle = (self.z == 1) | (self.z == 2)
        self.outside = jnp.logical_not(self.in_middle)

    def copy_of(self, kind, source, target, device):
        return pltpu.make_async_remote_copy(
            src_ref=source,
            dst_ref=target,
            send_sem=self.send_sems.at[kind],
            recv_sem=self.recv_sems.at[kind],
            device_id={"row": device},
            device_id_type=pl.DeviceIdType.MESH,
        )

    def send_far(self):
        return self.copy_of(0, self.grads.at[self.far], self.far_in, self.partner)

    def send_near(self):
        return self.copy_of(1, self.grads.at[self.near], self.near_in, self.partner)

    def cross_far(self):
        return self.copy_of(2, self.far_in, self.far_sum, self.across)

    def cross_near(self):
        return self.copy_of(3, self.near_in, self.near_sum, self.across)

    def swap_middle(self):
        return self.copy_of(4, self.far_sum, self.last, self.partner)

    def swap_outer(self):
        return self.copy_of(4, self.grads.at[self.partner], self.last, self.partner)

    def load(self, kind, block):
        target = self.more if kind % 2 else self.held
        return pltpu.make_async_copy(self.grads.at[block], target, self.local_sems.at[kind])

    def add(self, target, source):
        @pl.loop(0, target.shape[0], step=64)
        def _(at):
            tile = pl.ds(pl.multiple_of(at, 64), 64)
            target[tile, :] = (target[tile, :].astype(f32) + source[tile, :].astype(f32)).astype(bf16)

    def begin(self):
        @pl.when(self.outside)
        def _():
            self.send_far().start()
            self.send_near().start()
            self.swap_outer().start()
            self.load(3, self.own).start()

        @pl.when(self.in_middle)
        def _():
            self.load(0, self.far).start()
            self.load(1, self.near).start()

    def second_far(self):
        @pl.when(self.in_middle)
        def _():
            self.load(0, self.far).wait()
            self.send_far().wait_recv()
            self.add(self.far_in, self.held)
            self.cross_far().start()
            self.load(2, self.partner).start()

    def second_near(self):
        @pl.when(self.in_middle)
        def _():
            self.load(1, self.near).wait()
            self.send_near().wait_recv()
            self.add(self.near_in, self.more)
            self.cross_near().start()
            self.load(3, self.own).start()

    def third(self):
        @pl.when(self.in_middle)
        def _():
            self.load(2, self.partner).wait()
            self.cross_far().wait_recv()
            self.add(self.far_sum, self.held)
            self.swap_middle().start()

    def finish(self):
        self.load(3, self.own).wait()
        self.swap_outer().wait_recv()

        @pl.when(self.in_middle)
        def _():
            self.cross_near().wait_recv()

        @pl.loop(0, self.total.shape[0], step=64)
        def _(at):
            tile = pl.ds(pl.multiple_of(at, 64), 64)
            self.total[tile, :] = self.more[tile, :].astype(f32) + self.last[tile, :].astype(f32)

        @pl.when(self.in_middle)
        def _():
            @pl.loop(0, self.total.shape[0], step=64)
            def _(at):
                tile = pl.ds(pl.multiple_of(at, 64), 64)
                self.total[tile, :] += self.near_sum[tile, :].astype(f32)

            self.cross_far().wait_send()
            self.cross_near().wait_send()
            self.swap_middle().wait_send()

        @pl.when(self.outside)
        def _():
            self.send_far().wait_send()
            self.send_near().wait_send()
            self.swap_outer().wait_send()


class RowHop:
    def __init__(self, kind, given, found, sems):
        self.kind, self.given, self.found, (self.send_sems, self.recv_sems) = kind, given, found, sems
        self.z = lax.axis_index("row")
        self.partner, self.across = places(self.z)[1], 3 - self.z
        self.in_middle = (self.z == 1) | (self.z == 2)
        self.outside = jnp.logical_not(self.in_middle)

    def copy_of(self, at, source, target, device):
        return pltpu.make_async_remote_copy(
            src_ref=source,
            dst_ref=target,
            send_sem=self.send_sems.at[at],
            recv_sem=self.recv_sems.at[at],
            device_id={"row": device},
            device_id_type=pl.DeviceIdType.MESH,
        )

    def across_copy(self):
        if self.kind == 1:
            return self.copy_of(0, self.given[0], self.found[1], self.across)
        return self.copy_of(0, self.given[0], self.found[0], self.across)

    def outward_copy(self):
        if self.kind == 1:
            return self.copy_of(1, self.given[0], self.found[0], self.partner)
        if self.kind == 3:
            return self.copy_of(1, self.given[0], self.found[0], self.partner)
        return self.copy_of(1, self.given[1], self.found[1], self.partner)

    def last_copy(self):
        return self.copy_of(2, self.found[0], self.found[2], self.partner)

    def begin(self):
        barrier = pltpu.get_barrier_semaphore()
        signal_to(barrier, {"row": self.partner})

        @pl.when(self.in_middle)
        def _():
            signal_to(barrier, {"row": self.across})
            pl.semaphore_wait(barrier, 2)
            if self.kind != 3:
                self.across_copy().start()
            self.outward_copy().start()

        @pl.when(self.outside)
        def _():
            pl.semaphore_wait(barrier, 1)
            if self.kind == 1:
                self.outward_copy().start()

    def finish(self):
        @pl.when(self.in_middle)
        def _():
            if self.kind != 3:
                self.across_copy().wait()
            if self.kind == 23:
                self.last_copy().start()
            if self.kind == 1:
                self.outward_copy().wait()
            else:
                self.outward_copy().wait_send()
            if self.kind == 23:
                self.last_copy().wait_send()

        @pl.when(self.outside)
        def _():
            if self.kind == 1:
                self.outward_copy().wait()
            else:
                self.outward_copy().wait_recv()
            if self.kind == 23:
                self.last_copy().wait_recv()


HOP_COUNTS = {1: (1, 2), 2: (2, 2), 3: (1, 1), 23: (2, 3), None: (0, 0)}


def hop_parts(hop, number):
    if hop is None:
        return [], [], [], pltpu.CompilerParams()
    kind, given = hop
    shape = jax.ShapeDtypeStruct(given[0].shape, bf16)
    scratch = [pltpu.SemaphoreType.DMA((3,)), pltpu.SemaphoreType.DMA((3,))]
    params = pltpu.CompilerParams(collective_id=number, has_side_effects=True)
    return list(given), [shape] * HOP_COUNTS[kind][1], scratch, params


def hop_kernel(kind, *refs):
    given, found = HOP_COUNTS[kind]
    hop = RowHop(kind, refs[:given], refs[given : given + found], refs[given + found :])
    hop.begin()
    hop.finish()


def hop_now(hop, number):
    given, shapes, scratch, params = hop_parts(hop, number)
    anywhere = pl.BlockSpec(memory_space=pl.ANY)
    return pl.pallas_call(
        functools.partial(hop_kernel, hop[0]),
        in_specs=[anywhere] * len(given),
        out_specs=[anywhere] * len(shapes),
        out_shape=shapes,
        scratch_shapes=scratch,
        compiler_params=params,
        name="gather_hops",
    )(*given)


def signal_to(barrier, device):
    pl.semaphore_signal(barrier, inc=1, device_id=device, device_id_type=pl.DeviceIdType.MESH)


def gather_kernel(count, *refs):
    rows = RowGather(refs[:count], refs[count : 2 * count], refs[2 * count :])
    rows.greet(pltpu.get_barrier_semaphore())
    rows.begin()
    for at in range(count):
        rows.hand_on(at)
    for at in range(count):
        rows.hand_last(at)
    rows.finish()


PIECES = 4


def plane_kernel(pointwise, given, made, gather, count, reducing, *refs):
    p_ref, inputs = refs[0], refs[1 : 1 + given]
    at = 1 + given
    packs = refs[at : at + count]
    at += count
    grads = refs[at] if reducing else None
    at += reducing
    results = refs[at : at + made]
    at += made
    total_ref = refs[at] if reducing else None
    at += reducing
    whole_refs = refs[at : at + gather + count]
    at += gather + count
    mine, from_core, from_first, summed, from_second, shared, send_sems, recv_sems, local_sems = refs[
        at : at + 9
    ]
    out_ref = whole_refs[0] if gather else None
    me = lax.axis_index("col")
    core, x, y = lax.rem(me, 2), lax.rem(me // 2, 2), me // 4
    core_mate, x_mate, y_mate = me + 1 - 2 * core, me + 2 - 4 * x, me + 4 - 8 * y
    diagonal = x_mate + 4 - 8 * y
    size = mine.shape[3]
    share = mine.shape[4]
    barrier = pltpu.get_barrier_semaphore()
    for mate in (core_mate, x_mate, y_mate):
        signal_to(barrier, {"col": mate})
    rows, reduction = None, None
    if count or reducing:
        if count:
            rows = RowGather(packs, whole_refs[gather:], refs[at + 9 : at + 11])
            at += 2
        if reducing:
            reduction = RowReduce(grads, total_ref, refs[at + 9 : at + 19])
        chain = rows or reduction
        signal_to(barrier, {"row": chain.partner})

        @pl.when(chain.in_middle)
        def _():
            signal_to(barrier, {"row": chain.across})
            pl.semaphore_wait(barrier, 5)

        @pl.when(chain.outside)
        def _():
            pl.semaphore_wait(barrier, 4)

        if count:
            rows.begin()
        if reducing:
            reduction.begin()
    else:
        pl.semaphore_wait(barrier, 3)

    def remote(kind, i, source, target, mate):
        return pltpu.make_async_remote_copy(
            src_ref=source,
            dst_ref=target,
            send_sem=send_sems.at[kind, i],
            recv_sem=recv_sems.at[kind, i],
            device_id={"col": mate},
            device_id_type=pl.DeviceIdType.MESH,
        )

    def x_first(i):
        return i < PIECES // 2

    def span(i):
        return pl.ds(i * size, size)

    def core_copy(i):
        return remote(0, i, p_ref.at[:, :, 1 - core, span(i), :], from_core.at[i], core_mate)

    def load(i):
        return pltpu.make_async_copy(
            p_ref.at[:, :, core, span(i), :], mine.at[i], local_sems.at[0, i]
        )

    def first_copy(i):
        if x_first(i):
            return remote(1, i, mine.at[i, :, 1 - x], from_first.at[i], x_mate)
        return remote(1, i, mine.at[i, 1 - y], from_first.at[i], y_mate)

    def second_copy(i):
        if x_first(i):
            return remote(2, i, summed.at[i, 1 - y], from_second.at[i], y_mate)
        return remote(2, i, summed.at[i, 1 - x], from_second.at[i], x_mate)

    def columns(i, device):
        return out_ref.at[span(i), pl.ds(pl.multiple_of(device * share, share), share)]

    def spread(kind, i, mate):
        return remote(kind, i, shared.at[i], columns(i, me), mate)

    def keep(i):
        return pltpu.make_async_copy(shared.at[i], columns(i, me), local_sems.at[1, i])

    def pass_on(kind, i, device, mate):
        return remote(kind, i, columns(i, device), columns(i, device), mate)

    def forward(i):
        if x_first(i):
            return pass_on(6, i, y_mate, x_mate)
        return pass_on(6, i, x_mate, y_mate)

    order = [0, 2, 1, 3]
    for i in order:
        core_copy(i).start()
        load(i).start()
    for i in order:
        load(i).wait()
        core_copy(i).wait_recv()
        for a in range(2):
            for b in range(2):
                mine[i, a, b] = (mine[i, a, b].astype(f32) + from_core[i, a, b].astype(f32)).astype(bf16)
        first_copy(i).start()
    for i in order:
        first_copy(i).wait_recv()
        for a in range(2):
            kept = mine[i, a, x] if x_first(i) else mine[i, y, a]
            summed[i, a] = (kept.astype(f32) + from_first[i, a].astype(f32)).astype(bf16)
        second_copy(i).start()
    if count:
        for at in range(count):
            rows.hand_on(at)
    if reducing:
        reduction.second_far()
    for i in order:
        second_copy(i).wait_recv()
        total = summed[i, y if x_first(i) else x].astype(f32) + from_second[i].astype(f32)
        span_rows = slice(i * size, (i + 1) * size)
        values = pointwise(
            total, *[ref[span_rows, :] if ref.shape[0] > 8 else ref[...] for ref in inputs]
        )
        if gather:
            shared[i] = values[0].astype(bf16)
            values = values[1:]
        for ref, value in zip(results, values):
            ref[span_rows, :] = value
        if gather:
            spread(4, i, x_mate).start()
            spread(5, i, y_mate).start()
            spread(3, i, core_mate).start()
            keep(i).start()
    if count:
        rows.hand_last(0)
    if reducing and not gather:
        reduction.second_near()
    if gather:
        for i in order:
            spread(5 if x_first(i) else 4, i, y_mate).wait_recv()
            forward(i).start()
            pass_on(7, i, y_mate if x_first(i) else x_mate, core_mate).start()
        for i in order:
            spread(4 if x_first(i) else 5, i, x_mate).wait_recv()
            pass_on(8, i, x_mate if x_first(i) else y_mate, core_mate).start()
    if count:
        for at in range(1, count):
            rows.hand_last(at)
    if reducing and gather:
        reduction.second_near()
    if reducing:
        reduction.third()
    if gather:
        for i in order:
            forward(i).wait_recv()
            pass_on(9, i, diagonal, core_mate).start()
    for i in order:
        core_copy(i).wait_send()
        first_copy(i).wait_send()
        second_copy(i).wait_send()
        if gather:
            keep(i).wait()
            spread(3, i, core_mate).wait()
            spread(4, i, x_mate).wait_send()
            spread(5, i, y_mate).wait_send()
            forward(i).wait_send()
            for kind, device in (
                (7, y_mate if x_first(i) else x_mate),
                (8, x_mate if x_first(i) else y_mate),
                (9, diagonal),
            ):
                pass_on(kind, i, device, core_mate).wait()
    if count:
        rows.finish()
    if reducing:
        reduction.finish()


def plane_step(partial, pointwise, inputs, made, gather, number, packs=(), grads=None):
    tokens, share = partial.shape[3:]
    size = tokens // PIECES
    count = len(packs)
    reducing = 0 if grads is None else 1
    totals, more_scratch, given_grads = [], [], []
    if reducing:
        block, columns = grads.shape[0] // 4, grads.shape[1]
        given_grads = [grads.reshape(4, block, columns)]
        totals = [jax.ShapeDtypeStruct((block, columns), f32)]
        more_scratch = [pltpu.VMEM((block, columns), bf16)] * 7 + [
            pltpu.SemaphoreType.DMA((5,)),
            pltpu.SemaphoreType.DMA((5,)),
            pltpu.SemaphoreType.DMA((4,)),
        ]
    anywhere = pl.BlockSpec(memory_space=pl.ANY)
    vmem = pl.BlockSpec(memory_space=pltpu.VMEM)
    whole_shapes = [jax.ShapeDtypeStruct((tokens, 8 * share), bf16)] * gather + [
        jax.ShapeDtypeStruct((4,) + pack.shape, bf16) for pack in packs
    ]
    outs = pl.pallas_call(
        functools.partial(plane_kernel, pointwise, len(inputs), made, gather, count, reducing),
        in_specs=[anywhere] + [vmem] * len(inputs) + [anywhere] * (count + reducing),
        out_specs=[vmem] * (made + reducing) + [anywhere] * (gather + count),
        out_shape=[jax.ShapeDtypeStruct((tokens, share), f32)] * made + totals + whole_shapes,
        scratch_shapes=[
            pltpu.VMEM((PIECES, 2, 2, size, share), bf16),
            pltpu.VMEM((PIECES, 2, 2, size, share), bf16),
            pltpu.VMEM((PIECES, 2, size, share), bf16),
            pltpu.VMEM((PIECES, 2, size, share), bf16),
            pltpu.VMEM((PIECES, size, share), bf16),
            pltpu.VMEM((PIECES, size, share), bf16),
            pltpu.SemaphoreType.DMA((10, PIECES)),
            pltpu.SemaphoreType.DMA((10, PIECES)),
            pltpu.SemaphoreType.DMA((2, PIECES)),
        ]
        + [pltpu.SemaphoreType.DMA((5, count))] * (2 if count else 0)
        + more_scratch,
        compiler_params=pltpu.CompilerParams(collective_id=number, has_side_effects=True),
        cost_estimate=pl.CostEstimate(
            flops=60 * 10**9, bytes_accessed=32 * tokens * share, transcendentals=0
        ),
        name="plane_step",
    )(partial, *inputs, *packs, *given_grads)
    at = made + reducing
    wholes = [whole.reshape((4 * whole.shape[1],) + whole.shape[2:]) for whole in outs[at + gather :]]
    return outs[:at], outs[at : at + gather], wholes


def gather_now(packs, number):
    if lax.axis_size("row") != 4:
        return [lax.all_gather(pack, "row", axis=0, tiled=True) for pack in packs]
    count = len(packs)
    sent = sum(pack.size for pack in packs) * 2
    anywhere = pl.BlockSpec(memory_space=pl.ANY)
    wholes = pl.pallas_call(
        functools.partial(gather_kernel, count),
        in_specs=[anywhere] * count,
        out_specs=[anywhere] * count,
        out_shape=[jax.ShapeDtypeStruct((4,) + pack.shape, pack.dtype) for pack in packs],
        scratch_shapes=[pltpu.SemaphoreType.DMA((5, count)), pltpu.SemaphoreType.DMA((5, count))],
        compiler_params=pltpu.CompilerParams(collective_id=number, has_side_effects=True),
        cost_estimate=pl.CostEstimate(
            flops=6 * 9000 * sent, bytes_accessed=6 * sent, transcendentals=0
        ),
        name="gather_rows",
    )(*packs)
    return [whole.reshape((4 * whole.shape[1],) + whole.shape[2:]) for whole in wholes]


def put_own(whole, part):
    if lax.axis_size("row") != 4:
        return whole
    return lax.dynamic_update_slice_in_dim(
        whole, part, lax.axis_index("row") * part.shape[0], 0
    )


class Reduced:
    def __init__(self, grads):
        self.chained = lax.axis_size("row") == 4
        if not self.chained:
            self.total = lax.psum_scatter(grads, "row", scatter_dimension=0, tiled=True).astype(f32)
            return
        z = lax.axis_index("row")
        self.own, self.partner, _, _ = places(z)
        self.grads, self.size = grads, grads.shape[0] // 4
        self.pair = self.rows_of(grads, (1 - z // 2) * 2, 2)
        self.first = lax.ppermute(self.pair, "row", INWARD)

    def rows_of(self, value, at, count):
        return lax.dynamic_slice_in_dim(value, at * self.size, count * self.size, 0)

    def two(self, at):
        mine = self.rows_of(self.grads, at, 1).astype(f32)
        return mine + self.rows_of(self.crossed, lax.rem(at, 2), 1).astype(f32)

    def second(self, *groups):
        if not self.chained:
            return ()
        first = after(self.first, *groups)
        value = (self.pair.astype(f32) + first.astype(f32)).astype(bf16)
        self.crossed = lax.ppermute(value, "row", MIDDLE)
        return (value,)

    def third(self, *groups):
        if not self.chained:
            return ()
        self.crossed = after(self.crossed, *groups)
        value = self.two(self.partner).astype(bf16)
        self.swapped = lax.ppermute(value, "row", PAIRS)
        return (value,)

    def result(self):
        if self.chained:
            return self.two(self.own) + self.swapped.astype(f32)
        return self.total


def one_reduction(grads):
    one = Reduced(grads)
    one.second()
    one.third()
    return one.result()


def after(value, *groups):
    others = tuple(item for group in groups for item in group)
    return lax.optimization_barrier((value,) + others)[0] if others else value


def expert_kernel(size, steps, count, kind, *refs):
    pieces = refs[:count]
    (x_ref, cot_ref, x_cols, cot_cols, coef_ref) = refs[count : count + 5]
    taken, found = HOP_COUNTS[kind]
    at = count + 5 + taken
    (dpair_ref, hidden_ref, sums_ref, grads_ref, whole_ref) = refs[at : at + 5]
    weights, dpair, hidden, sems, out_sem = refs[at + 5 + found : at + 10 + found]
    step = pl.program_id(0)
    final = pl.num_programs(0) - 1
    if kind:
        hop = RowHop(
            kind, refs[count + 5 : at], refs[at + 5 : at + 5 + found], refs[at + 10 + found :]
        )

        @pl.when(step == 0)
        def _():
            hop.begin()

    write = pltpu.make_async_copy(weights, whole_ref, out_sem)

    @pl.when(step == 0)
    def _():
        if count == 1:
            copy = pltpu.make_async_copy(pieces[0], weights, sems.at[0])
            copy.start()
            copy.wait()
        elif count == 2:
            block = pieces[0].shape[0]

            def block_copy(back):
                at = pl.multiple_of(lax.rem(lax.axis_index("row") + back, 4) * block, block)
                source = pieces[1].at[pl.ds(at, block)] if back else pieces[0]
                return pltpu.make_async_copy(source, weights.at[pl.ds(at, block)], sems.at[back])

            for back in range(4):
                block_copy(back).start()
            for back in range(4):
                block_copy(back).wait()
        else:
            z = lax.axis_index("row")
            block = pieces[0].shape[0]

            def copy_of(piece, which):
                at = pl.multiple_of(places(z)[which] * block, block)
                return pltpu.make_async_copy(
                    piece, weights.at[pl.ds(at, block)], sems.at[which]
                )

            copy_of(pieces[0], 0).start()
            copy_of(pieces[1], 1).start()
            in_middle = (z == 1) | (z == 2)

            @pl.when(in_middle)
            def _():
                copy_of(pieces[2], 2).start()
                copy_of(pieces[3], 3).start()

            @pl.when(jnp.logical_not(in_middle))
            def _():
                copy_of(pieces[4], 2).start()
                copy_of(pieces[5], 3).start()

            for which in range(4):
                copy_of(pieces[which], which).wait()
        write.start()

    @pl.when(step < steps)
    def _():
        at = pl.multiple_of(step * TILE, TILE)
        rows, cots = x_ref[...], cot_ref[...]
        scale, weight = coef_ref[:, 0:1], coef_ref[:, 1:2]
        dots = jnp.zeros((TILE, 1), f32)
        inner = jnp.zeros((TILE, 1), f32)
        for a in range(0, size, TILE):
            b = min(a + TILE, size)
            gate = scale * mm(rows, weights[:, a:b])
            up = scale * mm(rows, weights[:, size + a : size + b])
            dhid = mm(cots, weights[:, 2 * size + a : 2 * size + b])
            sigma = jax.nn.sigmoid(gate)
            silu = gate * sigma
            hid = silu * up
            dots += jnp.sum(hid * dhid, axis=1, keepdims=True)
            dhid = weight * dhid
            dgate = dhid * up * sigma * (1.0 + gate * (1.0 - sigma))
            dup = dhid * silu
            inner += jnp.sum(dgate * gate + dup * up, axis=1, keepdims=True)
            for into, at_col, value in (
                ((hidden_ref, hidden), a, weight * hid),
                ((dpair_ref, dpair), a, scale * dgate),
                ((dpair_ref, dpair), size + a, scale * dup),
            ):
                value = value.astype(bf16)
                into[0][:, at_col : at_col + b - a] = value
                into[1][pl.ds(at, TILE), at_col : at_col + b - a] = value
        sums_ref[:, 0:1] = dots
        sums_ref[:, 1:2] = inner

    @pl.when(step >= steps)
    def _():
        for a in range(0, 2 * size, TILE):
            b = min(a + TILE, 2 * size)
            grads_ref[:, a:b] = mm_tn(x_cols[...], dpair[:, a:b]).astype(bf16)
        for a in range(0, size, TILE):
            b = min(a + TILE, size)
            grads_ref[:, 2 * size + a : 2 * size + b] = mm_tn(
                cot_cols[...], hidden[:, a:b]
            ).astype(bf16)

    @pl.when(step == final)
    def _():
        write.wait()
        if kind:
            hop.finish()


def expert_chunk(pieces, scaled, cots, coef, hop=None, number=None):
    tokens, width = scaled.shape
    size = pieces[0].shape[1] // 3
    steps, more_steps = tokens // TILE, width // TILE
    count = len(pieces)
    rows = lambda i: (jnp.minimum(i, steps - 1), 0)
    cols = lambda i: (0, jnp.maximum(i - steps, 0))
    down = lambda i: (jnp.maximum(i - steps, 0), 0)
    anywhere = pl.BlockSpec(memory_space=pl.ANY)
    more, more_shapes, more_scratch, params = hop_parts(hop, number)
    outs = pl.pallas_call(
        functools.partial(expert_kernel, size, steps, count, hop and hop[0]),
        grid_spec=pl.GridSpec(
            grid=(steps + more_steps,),
            in_specs=[pl.BlockSpec(memory_space=pl.ANY)] * count
            + [
                pl.BlockSpec((TILE, width), rows),
                pl.BlockSpec((TILE, width), rows),
                pl.BlockSpec((tokens, TILE), cols),
                pl.BlockSpec((tokens, TILE), cols),
                pl.BlockSpec((TILE, 2), rows),
            ]
            + [anywhere] * len(more),
            out_specs=[
                pl.BlockSpec((TILE, 2 * size), rows),
                pl.BlockSpec((TILE, size), rows),
                pl.BlockSpec((TILE, 2), rows),
                pl.BlockSpec((TILE, 3 * size), down),
                anywhere,
            ]
            + [anywhere] * len(more_shapes),
            scratch_shapes=[
                pltpu.VMEM((width, 3 * size), bf16),
                pltpu.VMEM((tokens, 2 * size), bf16),
                pltpu.VMEM((tokens, size), bf16),
                pltpu.SemaphoreType.DMA((4,)),
                pltpu.SemaphoreType.DMA,
            ]
            + more_scratch,
        ),
        out_shape=[
            jax.ShapeDtypeStruct((tokens, 2 * size), bf16),
            jax.ShapeDtypeStruct((tokens, size), bf16),
            jax.ShapeDtypeStruct((tokens, 2), f32),
            jax.ShapeDtypeStruct((width, 3 * size), bf16),
            jax.ShapeDtypeStruct((width, 3 * size), bf16),
        ]
        + more_shapes,
        compiler_params=params,
        cost_estimate=pl.CostEstimate(
            flops=12 * tokens * width * size,
            bytes_accessed=8 * tokens * width + 24 * width * size,
            transcendentals=tokens * size,
        ),
        name="expert_chunk",
    )(*pieces, scaled, cots, scaled, cots, coef, *more)
    return outs[:5], outs[5:]


def joint_kernel(count, based, planar, kind, *refs):
    taken, found = HOP_COUNTS[kind]
    at = 2 * count + based + taken
    out_ref = refs[at]
    if kind:
        hop = RowHop(kind, refs[at - taken : at], refs[at + 1 : at + 1 + found], refs[at + 1 + found :])

        @pl.when(pl.program_id(0) == 0)
        def _():
            hop.begin()

    for a in range(0, refs[count].shape[0], TILE):
        total = refs[2 * count][:, a : a + TILE] if based else None
        for left, weights in zip(refs[:count], refs[count : 2 * count]):
            part = mm_nt(left[...], weights[a : a + TILE, :])
            total = part if total is None else total + part
        if planar:
            at = a // TILE
            out_ref[at // 4, at // 2 % 2, at % 2] = total.astype(out_ref.dtype)
        else:
            out_ref[:, a : a + TILE] = total.astype(out_ref.dtype)
    if kind:
        @pl.when(pl.program_id(0) == pl.num_programs(0) - 1)
        def _():
            hop.finish()


def joint_back(lefts, weights, column, kind, *base, planar=False, hop=None, number=None):
    tokens, width = lefts[0].shape[0], weights[0].shape[0]
    row = lambda i: (i, 0)
    fixed = lambda i: (0, column)
    depth = sum(left.shape[1] for left in lefts)
    more, more_shapes, more_scratch, params = hop_parts(hop, number)
    anywhere = pl.BlockSpec(memory_space=pl.ANY)
    out_spec = pl.BlockSpec((TILE, width), row)
    if planar:
        out_spec = pl.BlockSpec((2, 2, 2, TILE, TILE), lambda i: (0, 0, 0, i, 0))
    outs = pl.pallas_call(
        functools.partial(joint_kernel, len(lefts), len(base), planar, hop and hop[0]),
        grid=(tokens // TILE,),
        in_specs=[pl.BlockSpec((TILE, left.shape[1]), row) for left in lefts]
        + [
            pl.BlockSpec((width, left.shape[1]), fixed, pipeline_mode=pl.Buffered(1))
            for left in lefts
        ]
        + [pl.BlockSpec((TILE, width), row)] * len(base)
        + [anywhere] * len(more),
        out_specs=[out_spec] + [anywhere] * len(more_shapes),
        out_shape=[
            jax.ShapeDtypeStruct((2, 2, 2, tokens, TILE) if planar else (tokens, width), kind)
        ]
        + more_shapes,
        scratch_shapes=more_scratch,
        compiler_params=params,
        cost_estimate=pl.CostEstimate(
            flops=2 * tokens * width * depth,
            bytes_accessed=2 * (tokens + width) * depth + 4 * tokens * width,
            transcendentals=0,
        ),
        name="joint_back",
    )(*lefts, *weights, *base, *more)
    return outs[0] if hop is None else outs


def split_three(values):
    high = values.astype(bf16)
    rest = values - high.astype(f32)
    middle = rest.astype(bf16)
    return high, middle, (rest - middle.astype(f32)).astype(bf16)


def cuts_of(width, sizes):
    cuts, at = [], 0
    for size in sizes:
        if at + size < width:
            cuts.append((at, at + size))
            at += size
    return cuts + [(at, width)]


def stream_step(total, rows, gain):
    stream = rows.astype(f32) + total
    return stream * gain, stream


def dstream_step(total, back, cots, stream, damp, gain):
    dscaled = back + total
    dstream = cots.astype(f32) + gain * dscaled - stream * damp
    return dstream, dstream, dscaled


def per_device(
    block_input,
    seq_lengths,
    slot_order,
    routes,
    input_gain,
    query_weight,
    key_weight,
    value_weight,
    output_weight,
    mlp_gain,
    router_weight,
    score_shared,
    gate_shared,
    up_shared,
    down_shared,
    gate_expert,
    up_expert,
    down_expert,
    grad_output,
):
    tokens, share = block_input.shape
    cols = lax.axis_size("col")
    col_id = lax.axis_index("col")
    row_id = lax.axis_index("row")
    width = share * cols
    slots = tokens // SEQ_LEN
    local_experts = gate_expert.shape[0]
    experts = router_weight.shape[1]
    head_width = query_weight.shape[1]
    heads = head_width // HEAD_DIM
    rows_block = query_weight.shape[0]
    lengths = lax.dynamic_slice_in_dim(seq_lengths[slot_order], row_id * slots, slots, 0)
    cosine, sine = rope_tables()

    def by_head(weight):
        return weight.reshape(rows_block, heads, 1, HEAD_DIM)

    qkv_pack = jnp.concatenate(
        [by_head(query_weight), by_head(key_weight), by_head(value_weight)], axis=2
    ).reshape(rows_block, 3 * head_width)
    router_pack = jnp.concatenate([router_weight, score_shared[:, None]], axis=1)
    router_pack = jnp.pad(router_pack, ((0, 0), (0, -router_pack.shape[1] % 128)))
    out_pack = jnp.concatenate([output_weight.T, router_pack], axis=1)
    qkv_whole, out_whole = gather_now([qkv_pack, out_pack], 0)
    qkv_full, out_weights = put_own(qkv_whole, qkv_pack), put_own(out_whole, out_pack)
    out_full = out_weights[:, :head_width]
    router_full = out_weights[:, head_width : head_width + experts + 1]
    shared_cuts = [(None, a, b) for a, b in cuts_of(gate_shared.shape[1], (512,))]
    expert_cuts = [
        (local, a, b)
        for local in range(local_experts)
        for a, b in cuts_of(gate_expert.shape[2], (512, 512))
    ]
    chunks = shared_cuts[-1:] + expert_cuts[:-1] + shared_cuts[:-1] + expert_cuts[-1:]

    def pack(kind, a, b):
        if kind is None:
            parts = [gate_shared[:, a:b], up_shared[:, a:b], down_shared[a:b].T]
        else:
            parts = [gate_expert[kind, :, a:b], up_expert[kind, :, a:b], down_expert[kind, a:b].T]
        fill = -(b - a) % 128
        return jnp.concatenate([jnp.pad(part, ((0, 0), (0, fill))) for part in parts], axis=1)

    packs = [pack(*chunk) for chunk in chunks]
    chained = lax.axis_size("row") == 4
    planar = chained and cols == 8 and share == TILE
    gathered = {}
    gathered[0] = Gathered(packs[0])

    rows_in = lax.all_gather(block_input, "col", axis=1, tiled=True)
    gains = lax.all_gather(jnp.stack([input_gain, mlp_gain]), "col", axis=1, tiled=True).astype(f32)
    cot_rows = lax.all_gather(grad_output, "col", axis=1, tiled=True)
    rows_f = rows_in.astype(f32)
    scale_a = lax.rsqrt(jnp.mean(rows_f * rows_f, axis=-1, keepdims=True) + norm_eps)
    normed_a = (rows_f * scale_a * gains[0]).astype(bf16)
    raw = mm(normed_a, qkv_full)
    raw = after(raw, gathered[0].second())
    qkv, context, lse = attend_forward(raw, lengths, cosine, sine)
    context = after(context, gathered[0].third())
    x_share = block_input.astype(f32)
    gain_b = mlp_gain.astype(f32)
    if planar:
        attn_part = joint_back([context], [out_weights], 0, bf16, planar=True)
        attn_part = after(attn_part, (cot_rows,))
        (stream,), (scaled,), wholes_now = plane_step(
            attn_part, stream_step, [block_input, gain_b[None]], 1, 1, 1, packs[1:2]
        )
        gathered[1] = (packs[1], wholes_now[0])
    else:
        attn_part = mm_nt(context, out_full).astype(bf16)
        attn_sum = lax.psum_scatter(attn_part, "col", scatter_dimension=1, tiled=True)
        scaled_share, stream = stream_step(attn_sum.astype(f32), block_input, gain_b[None])
        scaled = lax.all_gather(scaled_share.astype(bf16), "col", axis=1, tiled=True)
    for at in range(1, 1 if planar else len(chunks)):
        if at not in gathered:
            gathered[at] = Gathered(packs[at], (scaled,))

    def pieces_of(at):
        return gathered[at] if isinstance(gathered[at], tuple) else gathered[at].pieces

    stream_f = scaled.astype(f32) / gains[1]
    scale_b = lax.rsqrt(jnp.mean(stream_f * stream_f, axis=1, keepdims=True) + norm_eps)

    both_logits = scale_b * mm(scaled, router_full)
    logits, slogit = both_logits[:, :experts], both_logits[:, experts]
    top = jnp.max(logits, axis=-1, keepdims=True)
    expo = jnp.exp(logits - top)
    router_probs = expo / jnp.sum(expo, axis=-1, keepdims=True)
    shared_gate = jax.nn.sigmoid(slogit)

    inner = jnp.zeros((tokens,), f32)
    dots = {}
    members, shares = {None: None}, {None: shared_gate}
    for local in range(local_experts):
        expert = col_id * local_experts + local
        members[local] = jnp.any(routes == expert, axis=1)
        column = lax.dynamic_index_in_dim(router_probs, expert, 1, False)
        shares[local] = jnp.where(members[local], column, 0.0)
    dpairs, hiddens, wholes, reduced = [], [], [], []
    last = len(chunks) - 1
    waits = ()
    if not planar:
        for at in range(1, len(chunks)):
            gathered[at].second()
            gathered[at].third()

    carried = []
    for at, (kind, a, b) in enumerate(chunks):
        coef = jnp.concatenate([scale_b, shares[kind][:, None]], axis=1)
        coef = after(coef, waits)
        hop = None
        if planar:
            hop = {0: (1, packs[2:3]), 1: (2, carried), 2: (1, packs[3:4]), 3: (1, packs[4:5])}.get(at)
        (dpair, hidden, sums, grads, whole), found = expert_chunk(
            pieces_of(at), scaled, cot_rows, coef, hop, 4 + at
        )
        carried = carried + list(found) if at == 1 else list(found)
        dots[kind] = dots.get(kind, 0.0) + sums[:, 0]
        inner = inner + sums[:, 1]
        dpairs.append(dpair)
        hiddens.append(hidden)
        wholes.append(whole)
        now = (sums,)
        waits = ()
        early = ()
        if planar and at == 1:
            dscaled_early, last_piece = joint_back(
                dpairs, wholes, 0, f32, hop=(3, carried[2:3]), number=9
            )
            gathered[2] = (packs[2], *carried[:2], carried[2], carried[3], last_piece)
            early = (dscaled_early,)
        elif planar and at == 2:
            rest = hop_now((23, [after(carried[0], now), carried[1]]), 10)
            gathered[3] = (packs[3], *carried, *rest)
            early = (rest[2],)
        elif planar and at == 3:
            dscaled_early, *next_pieces = joint_back(
                dpairs[2:], wholes[2:], 0, f32, dscaled_early, hop=(2, carried), number=11
            )
            moe_early, last_piece = joint_back(
                hiddens, wholes, 2, f32, hop=(3, next_pieces[:1]), number=12
            )
            gathered[4] = (packs[4], *carried, *next_pieces, last_piece)
            early = (dscaled_early, moe_early)
            now = early
        waits += early
        if not planar:
            reduced.append(Reduced(grads))
        elif at < last:
            if at >= 1:
                waits += reduced[at - 1].second(now)
            if at >= 2:
                waits += reduced[at - 2].third((sums,))
            reduced.append(Reduced(grads))
            waits += (reduced[at].pair,)
    now = (sums,)
    if planar:
        waits = reduced[3].second(now)
        waits += reduced[2].third(now)
    else:
        waits = ()
        for one in reduced:
            one.second()
            one.third()
    joined = 4 if planar else 0
    bases = ((dscaled_early,), (moe_early,)) if planar else ((), ())
    late_pairs, late_wholes, late_hiddens = dpairs[joined:], wholes[joined:], hiddens[joined:]
    late_pairs[-1] = after(late_pairs[-1], waits)
    dscaled_part = joint_back(late_pairs, late_wholes, 0, bf16, *bases[0], planar=planar)

    named = [jnp.where(members[local], dots[local], 0.0) for local in range(local_experts)]
    table = lax.all_gather(jnp.stack(named + [dots[None], inner]), "col", axis=0)
    dprob = table[:, :local_experts].reshape(experts, tokens).T
    dshared_gate, inner = jnp.sum(table[:, local_experts], axis=0), jnp.sum(table[:, local_experts + 1], axis=0)
    dlogits = router_probs * (dprob - jnp.sum(dprob * router_probs, axis=1, keepdims=True))
    dslogit = dshared_gate * shared_gate * (1.0 - shared_gate)
    dboth = jnp.concatenate([dlogits, dslogit[:, None]], axis=1)
    inner = inner + jnp.sum(dboth * both_logits, axis=1)
    dboth = scale_b * dboth
    parts = split_three(dboth)
    router_rows = lax.dynamic_slice_in_dim(router_full, col_id * share, share, 0)
    back_term = mm_nt(jnp.concatenate(parts, axis=1), jnp.concatenate([router_rows] * 3, axis=1))
    damp = scale_b * scale_b * inner[:, None] / width
    step_inputs = [back_term, grad_output, stream, damp, gain_b[None]]
    if planar:
        (dstream, dscaled, last_grad), (dattn,), _ = plane_step(
            dscaled_part, dstream_step, step_inputs, 2, 1, 2, (), grads
        )
    else:
        dscaled_sum = lax.psum_scatter(dscaled_part, "col", scatter_dimension=1, tiled=True)
        dstream_low, dstream, dscaled = dstream_step(dscaled_sum.astype(f32), *step_inputs)
        dattn = lax.all_gather(dstream_low.astype(bf16), "col", axis=1, tiled=True)
    gain_b_grad = jnp.sum(dscaled * stream, axis=0)

    late_hiddens[-1] = after(late_hiddens[-1], (dattn,))
    moe_part = joint_back(late_hiddens, late_wholes, 2, bf16, *bases[1])
    moe_share = lax.psum_scatter(moe_part, "col", scatter_dimension=1, tiled=True).astype(f32)
    block_output = (stream + moe_share).astype(bf16)
    out_part = mm_tn(dattn, context).astype(bf16)
    dcontext = mm(dattn, out_full).astype(bf16)
    if planar:
        dcontext = after(dcontext, reduced[3].third((dattn,)))
    router_left = after(jnp.concatenate(parts, axis=1), (dattn,))
    grad_router_part = mm_tn(router_left, scaled).reshape(3, experts + 1, width).sum(axis=0)
    grad_router_both = lax.psum_scatter(grad_router_part, "row", scatter_dimension=1, tiled=True)
    dqkv, inner_a = attend_backward(qkv, dcontext, lse, lengths, cosine, sine)
    inner_a = lax.psum(inner_a[:, 0], "col")[:, None]
    attn_grads = jnp.concatenate([mm_tn(normed_a, dqkv).astype(bf16), out_part], axis=1)
    if planar:
        dnormed_part = joint_back([dqkv], [qkv_full], 0, bf16, planar=True)
        dnormed_part = after(dnormed_part, (inner_a,))
        (dnormed_a, attn_grad), _, _ = plane_step(
            dnormed_part, lambda total: (total,), [], 1, 0, 3, (), attn_grads
        )
    else:
        dnormed_a = lax.psum_scatter(
            mm_nt(dqkv, qkv_full).astype(bf16), "col", scatter_dimension=1, tiled=True
        ).astype(f32)
        attn_grad = one_reduction(attn_grads)
    qkv_grad, out_grad = attn_grad[:, : 3 * head_width], attn_grad[:, 3 * head_width :]
    unit_grads = [one.result() for one in reduced]
    if planar:
        unit_grads.append(last_grad)
    gain_a_share = input_gain.astype(f32)
    dinput = dstream + scale_a * gain_a_share * dnormed_a
    dinput = dinput - x_share * (scale_a * scale_a * inner_a / width)
    gain_a_grad = jnp.sum(dnormed_a * x_share * scale_a, axis=0)
    grad_gain_a, grad_gain_b = lax.psum((gain_a_grad, gain_b_grad), "row")

    qkv_grad = qkv_grad.reshape(rows_block, heads, 3, HEAD_DIM)
    grad_query, grad_key, grad_value = (
        qkv_grad[:, :, part].reshape(rows_block, head_width) for part in range(3)
    )
    def unpack(kind, which):
        found = []
        for (of, a, b), grad in zip(chunks, unit_grads):
            if of == kind:
                size = grad.shape[1] // 3
                part = grad[:, which * size : which * size + b - a]
                found.append((a, part.T if which == 2 else part))
        found = [part for _, part in sorted(found, key=lambda item: item[0])]
        return jnp.concatenate(found, axis=0 if which == 2 else 1)

    locals_ = range(local_experts)
    return (
        block_output,
        dinput.astype(bf16),
        grad_gain_a,
        grad_query,
        grad_key,
        grad_value,
        out_grad.T,
        grad_gain_b,
        grad_router_both[:experts].T,
        grad_router_both[experts],
        unpack(None, 0),
        unpack(None, 1),
        unpack(None, 2),
        jnp.stack([unpack(local, 0) for local in locals_]),
        jnp.stack([unpack(local, 1) for local in locals_]),
        jnp.stack([unpack(local, 2) for local in locals_]),
    )


def solution(mesh):
    return jax.shard_map(
        per_device,
        mesh=mesh,
        in_specs=(
            P("row", "col"),
            P(),
            P(),
            P("row", None),
            P("col"),
            P("row", "col"),
            P("row", "col"),
            P("row", "col"),
            P("col", "row"),
            P("col"),
            P("row", None),
            P("row"),
            P("row", "col"),
            P("row", "col"),
            P("col", "row"),
            P("col", "row", None),
            P("col", "row", None),
            P("col", None, "row"),
            P("row", "col"),
        ),
        out_specs=(
            P("row", "col"),
            P("row", "col"),
            P("col"),
            P("row", "col"),
            P("row", "col"),
            P("row", "col"),
            P("col", "row"),
            P("col"),
            P("row", None),
            P("row"),
            P("row", "col"),
            P("row", "col"),
            P("col", "row"),
            P("col", "row", None),
            P("col", "row", None),
            P("col", None, "row"),
        ),
        check_vma=False,
    )
```

```python
import functools
import math

import jax
import jax.numpy as jnp
from jax import lax
from jax.experimental import pallas as pl
from jax.experimental.pallas import tpu as pltpu
from jax.sharding import PartitionSpec as P

HEAD_DIM = 128
SEQ_LEN = 1024
QBLOCK = 256
TILE = 256
norm_eps = 1e-06
rope_base = 1000000.0
bf16 = jnp.bfloat16
f32 = jnp.float32


def mm(left, right):
    return jnp.dot(left, right, preferred_element_type=f32)


def mm_nt(left, right):
    return lax.dot_general(left, right, (((1,), (1,)), ((), ())), preferred_element_type=f32)


def mm_tn(left, right):
    return lax.dot_general(left, right, (((0,), (0,)), ((), ())), preferred_element_type=f32)


def rope_tables():
    positions = jnp.arange(SEQ_LEN).astype(f32)
    freqs = jnp.power(f32(rope_base), -jnp.arange(0, HEAD_DIM, 2).astype(f32) / HEAD_DIM)
    angles = positions[:, None] * freqs[None, :]
    cosine, sine = jnp.cos(angles), jnp.sin(angles)
    return (
        jnp.concatenate([cosine, cosine], axis=-1),
        jnp.concatenate([-sine, sine], axis=-1),
    )


def block_scores(rows, keys, start, length, scale):
    raw = mm_nt(rows, keys) * scale
    query_pos = start + lax.broadcasted_iota(jnp.int32, raw.shape, 0)
    key_pos = lax.broadcasted_iota(jnp.int32, raw.shape, 1)
    return jnp.where((key_pos <= query_pos) & (key_pos < length), raw, -1e30)


def attend_forward_kernel(length_ref, raw_ref, cos_ref, sin_ref, qkv_ref, context_ref, lse_ref):
    length = length_ref[pl.program_id(0)]
    scale = 1.0 / math.sqrt(HEAD_DIM)
    hd = HEAD_DIM
    for part in range(2):
        raw = raw_ref[:, part * hd : (part + 1) * hd]
        turned = raw * cos_ref[...] + pltpu.roll(raw, hd // 2, 1) * sin_ref[...]
        qkv_ref[:, part * hd : (part + 1) * hd] = turned.astype(bf16)
    qkv_ref[:, 2 * hd :] = raw_ref[:, 2 * hd :].astype(bf16)
    for at in range(0, SEQ_LEN, QBLOCK):
        seen = at + QBLOCK
        scores = block_scores(
            qkv_ref[at:seen, :hd], qkv_ref[:seen, hd : 2 * hd], at, length, scale
        )
        top = jnp.max(scores, axis=-1, keepdims=True)
        expo = jnp.exp(scores - top)
        total = jnp.sum(expo, axis=-1, keepdims=True)
        probs = (expo / total).astype(bf16)
        context_ref[at:seen, :] = mm(probs, qkv_ref[:seen, 2 * hd :]).astype(bf16)
        lse_ref[at:seen, :] = jnp.broadcast_to(top + jnp.log(total), (QBLOCK, hd))


def attend_forward(raw, lengths, cosine, sine):
    tokens, width = raw.shape
    heads = width // (3 * HEAD_DIM)
    slots = tokens // SEQ_LEN
    wide = pl.BlockSpec((SEQ_LEN, 3 * HEAD_DIM), lambda s, h, _: (s, h))
    one = pl.BlockSpec((SEQ_LEN, HEAD_DIM), lambda s, h, _: (s, h))
    table = pl.BlockSpec((SEQ_LEN, HEAD_DIM), lambda s, h, _: (0, 0))
    pairs = slots * heads * SEQ_LEN * SEQ_LEN
    return pl.pallas_call(
        attend_forward_kernel,
        grid_spec=pltpu.PrefetchScalarGridSpec(
            num_scalar_prefetch=1,
            grid=(slots, heads),
            in_specs=[wide, table, table],
            out_specs=[wide, one, one],
        ),
        out_shape=[
            jax.ShapeDtypeStruct((tokens, width), bf16),
            jax.ShapeDtypeStruct((tokens, heads * HEAD_DIM), bf16),
            jax.ShapeDtypeStruct((tokens, heads * HEAD_DIM), f32),
        ],
        cost_estimate=pl.CostEstimate(
            flops=3 * HEAD_DIM * pairs, bytes_accessed=8 * tokens * width, transcendentals=pairs
        ),
        name="attend_forward",
    )(lengths, raw, cosine, sine)


def attend_backward_kernel(
    length_ref, qkv_ref, dcontext_ref, lse_ref, cos_ref, sin_ref, dqkv_ref, inner_ref, dk_ref, dv_ref
):
    length = length_ref[pl.program_id(0)]
    scale = 1.0 / math.sqrt(HEAD_DIM)
    hd = HEAD_DIM
    @pl.when(pl.program_id(1) == 0)
    def _():
        inner_ref[...] = jnp.zeros_like(inner_ref)

    dk_ref[...] = jnp.zeros_like(dk_ref)
    dv_ref[...] = jnp.zeros_like(dv_ref)

    def turn_back(grad, rows):
        back = grad * cos_ref[rows, :] - pltpu.roll(grad, hd // 2, 1) * sin_ref[rows, :]
        return back.astype(bf16)

    for at in range(0, SEQ_LEN, QBLOCK):
        seen = at + QBLOCK
        rows = qkv_ref[at:seen, :hd]
        keys = qkv_ref[:seen, hd : 2 * hd]
        drows = dcontext_ref[at:seen, :]
        scores = block_scores(rows, keys, at, length, scale)
        probs = jnp.exp(scores - lse_ref[at:seen, :1])
        dv_ref[:seen, :] += mm_tn(probs.astype(bf16), drows)
        dprobs = mm_nt(drows, qkv_ref[:seen, 2 * hd :])
        dscore = probs * (dprobs - jnp.sum(dprobs * probs, axis=-1, keepdims=True))
        draw = (dscore * scale).astype(bf16)
        dquery = mm(draw, keys)
        dk_ref[:seen, :] += mm_tn(draw, rows)
        dqkv_ref[at:seen, :hd] = turn_back(dquery, slice(at, seen))
        inner_ref[at:seen, :] += jnp.sum(dquery * rows.astype(f32), axis=-1, keepdims=True)
    dkey, dvalue = dk_ref[...], dv_ref[...]
    dqkv_ref[:, hd : 2 * hd] = turn_back(dkey, slice(None))
    dqkv_ref[:, 2 * hd :] = dvalue.astype(bf16)
    inner_ref[...] += jnp.sum(
        dkey * qkv_ref[:, hd : 2 * hd].astype(f32) + dvalue * qkv_ref[:, 2 * hd :].astype(f32),
        axis=-1,
        keepdims=True,
    )


def attend_backward(qkv, dcontext, lse, lengths, cosine, sine):
    tokens, width = qkv.shape
    heads = width // (3 * HEAD_DIM)
    slots = tokens // SEQ_LEN
    wide = pl.BlockSpec((SEQ_LEN, 3 * HEAD_DIM), lambda s, h, _: (s, h))
    one = pl.BlockSpec((SEQ_LEN, HEAD_DIM), lambda s, h, _: (s, h))
    table = pl.BlockSpec((SEQ_LEN, HEAD_DIM), lambda s, h, _: (0, 0))
    pairs = slots * heads * SEQ_LEN * SEQ_LEN
    return pl.pallas_call(
        attend_backward_kernel,
        grid_spec=pltpu.PrefetchScalarGridSpec(
            num_scalar_prefetch=1,
            grid=(slots, heads),
            in_specs=[wide, one, one, table, table],
            out_specs=[wide, pl.BlockSpec((SEQ_LEN, 1), lambda s, h, _: (s, 0))],
            scratch_shapes=[pltpu.VMEM((SEQ_LEN, HEAD_DIM), f32)] * 2,
        ),
        out_shape=[
            jax.ShapeDtypeStruct((tokens, width), bf16),
            jax.ShapeDtypeStruct((tokens, 1), f32),
        ],
        cost_estimate=pl.CostEstimate(
            flops=8 * HEAD_DIM * pairs, bytes_accessed=8 * tokens * width, transcendentals=pairs
        ),
        name="attend_backward",
    )(lengths, qkv, dcontext, lse, cosine, sine)


PAIRS = [(0, 1), (1, 0), (2, 3), (3, 2)]
MIDDLE = [(1, 2), (2, 1)]
OUTWARD = [(1, 0), (2, 3)]
INWARD = [(0, 1), (3, 2)]


class Gathered:
    def __init__(self, part, *groups):
        self.part = part
        if lax.axis_size("row") != 4:
            self.pieces = (lax.all_gather(part, "row", axis=0, tiled=True),)
            return
        part = after(part, *groups)
        self.partner = lax.ppermute(part, "row", PAIRS)
        self.near_mid = lax.ppermute(part, "row", MIDDLE)
        self.pieces = None

    def second(self, *groups):
        if self.pieces is None:
            self.near_out = lax.ppermute(after(self.near_mid, *groups), "row", OUTWARD)
            self.far_mid = lax.ppermute(after(self.partner, *groups), "row", MIDDLE)
            return (self.partner, self.near_mid)
        return ()

    def third(self, *groups):
        if self.pieces is None:
            self.far_out = lax.ppermute(after(self.far_mid, *groups), "row", OUTWARD)
            self.pieces = (
                self.part, self.partner, self.near_mid, self.far_mid, self.near_out, self.far_out
            )
            return (self.far_mid, self.near_out)
        return ()


def places(z):
    pair = z // 2
    return z, z + 1 - 2 * lax.rem(z, 2), 2 - pair, 3 - 3 * pair


class RowGather:
    def __init__(self, packs, wholes, sems):
        self.packs, self.wholes, (self.send_sems, self.recv_sems) = packs, wholes, sems
        self.z = lax.axis_index("row")
        self.own, self.partner, self.near, self.far = places(self.z)
        self.across = 3 - self.z
        self.in_middle = (self.z == 1) | (self.z == 2)
        self.outside = jnp.logical_not(self.in_middle)

    def copy_of(self, kind, at, source, block, target):
        return pltpu.make_async_remote_copy(
            src_ref=source,
            dst_ref=self.wholes[at].at[block],
            send_sem=self.send_sems.at[kind, at],
            recv_sem=self.recv_sems.at[kind, at],
            device_id={"row": target},
            device_id_type=pl.DeviceIdType.MESH,
        )

    def swap(self, at):
        return self.copy_of(0, at, self.packs[at], self.own, self.partner)

    def swap_middle(self, at):
        return self.copy_of(1, at, self.packs[at], self.own, self.across)

    def second_middle(self, at):
        return self.copy_of(2, at, self.wholes[at].at[self.partner], self.partner, self.across)

    def hand_near(self, at):
        return self.copy_of(3, at, self.wholes[at].at[self.near], self.near, self.partner)

    def hand_far(self, at):
        return self.copy_of(4, at, self.wholes[at].at[self.far], self.far, self.partner)

    def greet(self, barrier):
        signal_to(barrier, {"row": self.partner})

        @pl.when(self.in_middle)
        def _():
            signal_to(barrier, {"row": self.across})
            pl.semaphore_wait(barrier, 2)

        @pl.when(self.outside)
        def _():
            pl.semaphore_wait(barrier, 1)

    def begin(self):
        for at in range(len(self.packs)):
            @pl.when(self.in_middle)
            def _():
                self.swap_middle(at).start()

            self.swap(at).start()

    def hand_on(self, at):
        @pl.when(self.in_middle)
        def _():
            self.swap_middle(at).wait_recv()
            self.hand_near(at).start()
            self.swap(at).wait_recv()
            self.second_middle(at).start()

    def hand_last(self, at):
        @pl.when(self.in_middle)
        def _():
            self.second_middle(at).wait_recv()
            self.hand_far(at).start()

    def finish(self):
        for at in range(len(self.packs)):
            @pl.when(self.in_middle)
            def _():
                for copy in (
                    self.swap,
                    self.swap_middle,
                    self.second_middle,
                    self.hand_near,
                    self.hand_far,
                ):
                    copy(at).wait_send()

            @pl.when(self.outside)
            def _():
                self.swap(at).wait()
                self.hand_near(at).wait_recv()
                self.hand_far(at).wait_recv()


class RowReduce:
    def __init__(self, grads, total, refs):
        self.grads, self.total = grads, total
        self.far_in, self.near_in, self.far_sum, self.near_sum, self.last = refs[:5]
        self.held, self.more, self.send_sems, self.recv_sems, self.local_sems = refs[5:]
        self.z = lax.axis_index("row")
        self.own, self.partner, self.near, self.far = places(self.z)
        self.across = 3 - self.z
        self.in_middle = (self.z == 1) | (self.z == 2)
        self.outside = jnp.logical_not(self.in_middle)

    def copy_of(self, kind, source, target, device):
        return pltpu.make_async_remote_copy(
            src_ref=source,
            dst_ref=target,
            send_sem=self.send_sems.at[kind],
            recv_sem=self.recv_sems.at[kind],
            device_id={"row": device},
            device_id_type=pl.DeviceIdType.MESH,
        )

    def send_far(self):
        return self.copy_of(0, self.grads.at[self.far], self.far_in, self.partner)

    def send_near(self):
        return self.copy_of(1, self.grads.at[self.near], self.near_in, self.partner)

    def cross_far(self):
        return self.copy_of(2, self.far_in, self.far_sum, self.across)

    def cross_near(self):
        return self.copy_of(3, self.near_in, self.near_sum, self.across)

    def swap_middle(self):
        return self.copy_of(4, self.far_sum, self.last, self.partner)

    def swap_outer(self):
        return self.copy_of(4, self.grads.at[self.partner], self.last, self.partner)

    def load(self, kind, block):
        target = self.more if kind % 2 else self.held
        return pltpu.make_async_copy(self.grads.at[block], target, self.local_sems.at[kind])

    def add(self, target, source):
        @pl.loop(0, target.shape[0], step=64)
        def _(at):
            tile = pl.ds(pl.multiple_of(at, 64), 64)
            target[tile, :] = (target[tile, :].astype(f32) + source[tile, :].astype(f32)).astype(bf16)

    def begin(self):
        @pl.when(self.outside)
        def _():
            self.send_far().start()
            self.send_near().start()
            self.swap_outer().start()
            self.load(3, self.own).start()

        @pl.when(self.in_middle)
        def _():
            self.load(0, self.far).start()
            self.load(1, self.near).start()

    def second_far(self):
        @pl.when(self.in_middle)
        def _():
            self.load(0, self.far).wait()
            self.send_far().wait_recv()
            self.add(self.far_in, self.held)
            self.cross_far().start()
            self.load(2, self.partner).start()

    def second_near(self):
        @pl.when(self.in_middle)
        def _():
            self.load(1, self.near).wait()
            self.send_near().wait_recv()
            self.add(self.near_in, self.more)
            self.cross_near().start()
            self.load(3, self.own).start()

    def third(self):
        @pl.when(self.in_middle)
        def _():
            self.load(2, self.partner).wait()
            self.cross_far().wait_recv()
            self.add(self.far_sum, self.held)
            self.swap_middle().start()

    def finish(self):
        self.load(3, self.own).wait()
        self.swap_outer().wait_recv()

        @pl.when(self.in_middle)
        def _():
            self.cross_near().wait_recv()

        @pl.loop(0, self.total.shape[0], step=64)
        def _(at):
            tile = pl.ds(pl.multiple_of(at, 64), 64)
            self.total[tile, :] = self.more[tile, :].astype(f32) + self.last[tile, :].astype(f32)

        @pl.when(self.in_middle)
        def _():
            @pl.loop(0, self.total.shape[0], step=64)
            def _(at):
                tile = pl.ds(pl.multiple_of(at, 64), 64)
                self.total[tile, :] += self.near_sum[tile, :].astype(f32)

            self.cross_far().wait_send()
            self.cross_near().wait_send()
            self.swap_middle().wait_send()

        @pl.when(self.outside)
        def _():
            self.send_far().wait_send()
            self.send_near().wait_send()
            self.swap_outer().wait_send()


class RowHop:
    def __init__(self, kind, given, found, sems):
        self.kind, self.given, self.found, (self.send_sems, self.recv_sems) = kind, given, found, sems
        self.z = lax.axis_index("row")
        self.partner, self.across = places(self.z)[1], 3 - self.z
        self.in_middle = (self.z == 1) | (self.z == 2)
        self.outside = jnp.logical_not(self.in_middle)

    def copy_of(self, at, source, target, device):
        return pltpu.make_async_remote_copy(
            src_ref=source,
            dst_ref=target,
            send_sem=self.send_sems.at[at],
            recv_sem=self.recv_sems.at[at],
            device_id={"row": device},
            device_id_type=pl.DeviceIdType.MESH,
        )

    def across_copy(self):
        if self.kind == 1:
            return self.copy_of(0, self.given[0], self.found[1], self.across)
        return self.copy_of(0, self.given[0], self.found[0], self.across)

    def outward_copy(self):
        if self.kind == 1:
            return self.copy_of(1, self.given[0], self.found[0], self.partner)
        if self.kind == 3:
            return self.copy_of(1, self.given[0], self.found[0], self.partner)
        return self.copy_of(1, self.given[1], self.found[1], self.partner)

    def last_copy(self):
        return self.copy_of(2, self.found[0], self.found[2], self.partner)

    def begin(self):
        barrier = pltpu.get_barrier_semaphore()
        signal_to(barrier, {"row": self.partner})

        @pl.when(self.in_middle)
        def _():
            signal_to(barrier, {"row": self.across})
            pl.semaphore_wait(barrier, 2)
            if self.kind != 3:
                self.across_copy().start()
            self.outward_copy().start()

        @pl.when(self.outside)
        def _():
            pl.semaphore_wait(barrier, 1)
            if self.kind == 1:
                self.outward_copy().start()

    def finish(self):
        @pl.when(self.in_middle)
        def _():
            if self.kind != 3:
                self.across_copy().wait()
            if self.kind == 23:
                self.last_copy().start()
            if self.kind == 1:
                self.outward_copy().wait()
            else:
                self.outward_copy().wait_send()
            if self.kind == 23:
                self.last_copy().wait_send()

        @pl.when(self.outside)
        def _():
            if self.kind == 1:
                self.outward_copy().wait()
            else:
                self.outward_copy().wait_recv()
            if self.kind == 23:
                self.last_copy().wait_recv()


HOP_COUNTS = {1: (1, 2), 2: (2, 2), 3: (1, 1), 23: (2, 3), None: (0, 0)}


def hop_parts(hop, number):
    if hop is None:
        return [], [], [], pltpu.CompilerParams()
    kind, given = hop
    shape = jax.ShapeDtypeStruct(given[0].shape, bf16)
    scratch = [pltpu.SemaphoreType.DMA((3,)), pltpu.SemaphoreType.DMA((3,))]
    params = pltpu.CompilerParams(collective_id=number, has_side_effects=True)
    return list(given), [shape] * HOP_COUNTS[kind][1], scratch, params


def hop_kernel(kind, *refs):
    given, found = HOP_COUNTS[kind]
    hop = RowHop(kind, refs[:given], refs[given : given + found], refs[given + found :])
    hop.begin()
    hop.finish()


def hop_now(hop, number):
    given, shapes, scratch, params = hop_parts(hop, number)
    anywhere = pl.BlockSpec(memory_space=pl.ANY)
    return pl.pallas_call(
        functools.partial(hop_kernel, hop[0]),
        in_specs=[anywhere] * len(given),
        out_specs=[anywhere] * len(shapes),
        out_shape=shapes,
        scratch_shapes=scratch,
        compiler_params=params,
        name="gather_hops",
    )(*given)


def signal_to(barrier, device):
    pl.semaphore_signal(barrier, inc=1, device_id=device, device_id_type=pl.DeviceIdType.MESH)


def gather_kernel(count, *refs):
    rows = RowGather(refs[:count], refs[count : 2 * count], refs[2 * count :])
    rows.greet(pltpu.get_barrier_semaphore())
    rows.begin()
    for at in range(count):
        rows.hand_on(at)
    for at in range(count):
        rows.hand_last(at)
    rows.finish()


PIECES = 4


def plane_kernel(pointwise, given, made, gather, count, reducing, *refs):
    p_ref, inputs = refs[0], refs[1 : 1 + given]
    at = 1 + given
    packs = refs[at : at + count]
    at += count
    grads = refs[at] if reducing else None
    at += reducing
    results = refs[at : at + made]
    at += made
    total_ref = refs[at] if reducing else None
    at += reducing
    whole_refs = refs[at : at + gather + count]
    at += gather + count
    mine, from_core, from_first, summed, from_second, shared, send_sems, recv_sems, local_sems = refs[
        at : at + 9
    ]
    out_ref = whole_refs[0] if gather else None
    me = lax.axis_index("col")
    core, x, y = lax.rem(me, 2), lax.rem(me // 2, 2), me // 4
    core_mate, x_mate, y_mate = me + 1 - 2 * core, me + 2 - 4 * x, me + 4 - 8 * y
    diagonal = x_mate + 4 - 8 * y
    size = mine.shape[3]
    share = mine.shape[4]
    barrier = pltpu.get_barrier_semaphore()
    for mate in (core_mate, x_mate, y_mate):
        signal_to(barrier, {"col": mate})
    rows, reduction = None, None
    if count or reducing:
        if count:
            rows = RowGather(packs, whole_refs[gather:], refs[at + 9 : at + 11])
            at += 2
        if reducing:
            reduction = RowReduce(grads, total_ref, refs[at + 9 : at + 19])
        chain = rows or reduction
        signal_to(barrier, {"row": chain.partner})

        @pl.when(chain.in_middle)
        def _():
            signal_to(barrier, {"row": chain.across})
            pl.semaphore_wait(barrier, 5)

        @pl.when(chain.outside)
        def _():
            pl.semaphore_wait(barrier, 4)

        if count:
            rows.begin()
        if reducing:
            reduction.begin()
    else:
        pl.semaphore_wait(barrier, 3)

    def remote(kind, i, source, target, mate):
        return pltpu.make_async_remote_copy(
            src_ref=source,
            dst_ref=target,
            send_sem=send_sems.at[kind, i],
            recv_sem=recv_sems.at[kind, i],
            device_id={"col": mate},
            device_id_type=pl.DeviceIdType.MESH,
        )

    def x_first(i):
        return i < PIECES // 2

    def span(i):
        return pl.ds(i * size, size)

    def core_copy(i):
        return remote(0, i, p_ref.at[:, :, 1 - core, span(i), :], from_core.at[i], core_mate)

    def load(i):
        return pltpu.make_async_copy(
            p_ref.at[:, :, core, span(i), :], mine.at[i], local_sems.at[0, i]
        )

    def first_copy(i):
        if x_first(i):
            return remote(1, i, mine.at[i, :, 1 - x], from_first.at[i], x_mate)
        return remote(1, i, mine.at[i, 1 - y], from_first.at[i], y_mate)

    def second_copy(i):
        if x_first(i):
            return remote(2, i, summed.at[i, 1 - y], from_second.at[i], y_mate)
        return remote(2, i, summed.at[i, 1 - x], from_second.at[i], x_mate)

    def columns(i, device):
        return out_ref.at[span(i), pl.ds(pl.multiple_of(device * share, share), share)]

    def spread(kind, i, mate):
        return remote(kind, i, shared.at[i], columns(i, me), mate)

    def keep(i):
        return pltpu.make_async_copy(shared.at[i], columns(i, me), local_sems.at[1, i])

    def pass_on(kind, i, device, mate):
        return remote(kind, i, columns(i, device), columns(i, device), mate)

    def forward(i):
        if x_first(i):
            return pass_on(6, i, y_mate, x_mate)
        return pass_on(6, i, x_mate, y_mate)

    order = [0, 2, 1, 3]
    for i in order:
        core_copy(i).start()
        load(i).start()
    for i in order:
        load(i).wait()
        core_copy(i).wait_recv()
        for a in range(2):
            for b in range(2):
                mine[i, a, b] = (mine[i, a, b].astype(f32) + from_core[i, a, b].astype(f32)).astype(bf16)
        first_copy(i).start()
    for i in order:
        first_copy(i).wait_recv()
        for a in range(2):
            kept = mine[i, a, x] if x_first(i) else mine[i, y, a]
            summed[i, a] = (kept.astype(f32) + from_first[i, a].astype(f32)).astype(bf16)
        second_copy(i).start()
    if count:
        for at in range(count):
            rows.hand_on(at)
    if reducing:
        reduction.second_far()
    for i in order:
        second_copy(i).wait_recv()
        total = summed[i, y if x_first(i) else x].astype(f32) + from_second[i].astype(f32)
        span_rows = slice(i * size, (i + 1) * size)
        values = pointwise(
            total, *[ref[span_rows, :] if ref.shape[0] > 8 else ref[...] for ref in inputs]
        )
        if gather:
            shared[i] = values[0].astype(bf16)
            values = values[1:]
        for ref, value in zip(results, values):
            ref[span_rows, :] = value
        if gather:
            spread(4, i, x_mate).start()
            spread(5, i, y_mate).start()
            spread(3, i, core_mate).start()
            keep(i).start()
    if count:
        rows.hand_last(0)
    if reducing and not gather:
        reduction.second_near()
    if gather:
        for i in order:
            spread(5 if x_first(i) else 4, i, y_mate).wait_recv()
            forward(i).start()
            pass_on(7, i, y_mate if x_first(i) else x_mate, core_mate).start()
        for i in order:
            spread(4 if x_first(i) else 5, i, x_mate).wait_recv()
            pass_on(8, i, x_mate if x_first(i) else y_mate, core_mate).start()
    if count:
        for at in range(1, count):
            rows.hand_last(at)
    if reducing and gather:
        reduction.second_near()
    if reducing:
        reduction.third()
    if gather:
        for i in order:
            forward(i).wait_recv()
            pass_on(9, i, diagonal, core_mate).start()
    for i in order:
        core_copy(i).wait_send()
        first_copy(i).wait_send()
        second_copy(i).wait_send()
        if gather:
            keep(i).wait()
            spread(3, i, core_mate).wait()
            spread(4, i, x_mate).wait_send()
            spread(5, i, y_mate).wait_send()
            forward(i).wait_send()
            for kind, device in (
                (7, y_mate if x_first(i) else x_mate),
                (8, x_mate if x_first(i) else y_mate),
                (9, diagonal),
            ):
                pass_on(kind, i, device, core_mate).wait()
    if count:
        rows.finish()
    if reducing:
        reduction.finish()


def plane_step(partial, pointwise, inputs, made, gather, number, packs=(), grads=None):
    tokens, share = partial.shape[3:]
    size = tokens // PIECES
    count = len(packs)
    reducing = 0 if grads is None else 1
    totals, more_scratch, given_grads = [], [], []
    if reducing:
        block, columns = grads.shape[0] // 4, grads.shape[1]
        given_grads = [grads.reshape(4, block, columns)]
        totals = [jax.ShapeDtypeStruct((block, columns), f32)]
        more_scratch = [pltpu.VMEM((block, columns), bf16)] * 7 + [
            pltpu.SemaphoreType.DMA((5,)),
            pltpu.SemaphoreType.DMA((5,)),
            pltpu.SemaphoreType.DMA((4,)),
        ]
    anywhere = pl.BlockSpec(memory_space=pl.ANY)
    vmem = pl.BlockSpec(memory_space=pltpu.VMEM)
    whole_shapes = [jax.ShapeDtypeStruct((tokens, 8 * share), bf16)] * gather + [
        jax.ShapeDtypeStruct((4,) + pack.shape, bf16) for pack in packs
    ]
    outs = pl.pallas_call(
        functools.partial(plane_kernel, pointwise, len(inputs), made, gather, count, reducing),
        in_specs=[anywhere] + [vmem] * len(inputs) + [anywhere] * (count + reducing),
        out_specs=[vmem] * (made + reducing) + [anywhere] * (gather + count),
        out_shape=[jax.ShapeDtypeStruct((tokens, share), f32)] * made + totals + whole_shapes,
        scratch_shapes=[
            pltpu.VMEM((PIECES, 2, 2, size, share), bf16),
            pltpu.VMEM((PIECES, 2, 2, size, share), bf16),
            pltpu.VMEM((PIECES, 2, size, share), bf16),
            pltpu.VMEM((PIECES, 2, size, share), bf16),
            pltpu.VMEM((PIECES, size, share), bf16),
            pltpu.VMEM((PIECES, size, share), bf16),
            pltpu.SemaphoreType.DMA((10, PIECES)),
            pltpu.SemaphoreType.DMA((10, PIECES)),
            pltpu.SemaphoreType.DMA((2, PIECES)),
        ]
        + [pltpu.SemaphoreType.DMA((5, count))] * (2 if count else 0)
        + more_scratch,
        compiler_params=pltpu.CompilerParams(collective_id=number, has_side_effects=True),
        cost_estimate=pl.CostEstimate(
            flops=60 * 10**9, bytes_accessed=32 * tokens * share, transcendentals=0
        ),
        name="plane_step",
    )(partial, *inputs, *packs, *given_grads)
    at = made + reducing
    wholes = [whole.reshape((4 * whole.shape[1],) + whole.shape[2:]) for whole in outs[at + gather :]]
    return outs[:at], outs[at : at + gather], wholes


def gather_now(packs, number):
    if lax.axis_size("row") != 4:
        return [lax.all_gather(pack, "row", axis=0, tiled=True) for pack in packs]
    count = len(packs)
    sent = sum(pack.size for pack in packs) * 2
    anywhere = pl.BlockSpec(memory_space=pl.ANY)
    wholes = pl.pallas_call(
        functools.partial(gather_kernel, count),
        in_specs=[anywhere] * count,
        out_specs=[anywhere] * count,
        out_shape=[jax.ShapeDtypeStruct((4,) + pack.shape, pack.dtype) for pack in packs],
        scratch_shapes=[pltpu.SemaphoreType.DMA((5, count)), pltpu.SemaphoreType.DMA((5, count))],
        compiler_params=pltpu.CompilerParams(collective_id=number, has_side_effects=True),
        cost_estimate=pl.CostEstimate(
            flops=6 * 9000 * sent, bytes_accessed=6 * sent, transcendentals=0
        ),
        name="gather_rows",
    )(*packs)
    return [whole.reshape((4 * whole.shape[1],) + whole.shape[2:]) for whole in wholes]


def put_own(whole, part):
    if lax.axis_size("row") != 4:
        return whole
    return lax.dynamic_update_slice_in_dim(
        whole, part, lax.axis_index("row") * part.shape[0], 0
    )


class Reduced:
    def __init__(self, grads):
        self.chained = lax.axis_size("row") == 4
        if not self.chained:
            self.total = lax.psum_scatter(grads, "row", scatter_dimension=0, tiled=True).astype(f32)
            return
        z = lax.axis_index("row")
        self.own, self.partner, _, _ = places(z)
        self.grads, self.size = grads, grads.shape[0] // 4
        self.pair = self.rows_of(grads, (1 - z // 2) * 2, 2)
        self.first = lax.ppermute(self.pair, "row", INWARD)

    def rows_of(self, value, at, count):
        return lax.dynamic_slice_in_dim(value, at * self.size, count * self.size, 0)

    def two(self, at):
        mine = self.rows_of(self.grads, at, 1).astype(f32)
        return mine + self.rows_of(self.crossed, lax.rem(at, 2), 1).astype(f32)

    def second(self, *groups):
        if not self.chained:
            return ()
        first = after(self.first, *groups)
        value = (self.pair.astype(f32) + first.astype(f32)).astype(bf16)
        self.crossed = lax.ppermute(value, "row", MIDDLE)
        return (value,)

    def third(self, *groups):
        if not self.chained:
            return ()
        self.crossed = after(self.crossed, *groups)
        value = self.two(self.partner).astype(bf16)
        self.swapped = lax.ppermute(value, "row", PAIRS)
        return (value,)

    def result(self):
        if self.chained:
            return self.two(self.own) + self.swapped.astype(f32)
        return self.total


def one_reduction(grads):
    one = Reduced(grads)
    one.second()
    one.third()
    return one.result()


def after(value, *groups):
    others = tuple(item for group in groups for item in group)
    return lax.optimization_barrier((value,) + others)[0] if others else value


def expert_kernel(size, steps, count, kind, *refs):
    pieces = refs[:count]
    (x_ref, cot_ref, x_cols, cot_cols, coef_ref) = refs[count : count + 5]
    taken, found = HOP_COUNTS[kind]
    at = count + 5 + taken
    (dpair_ref, hidden_ref, sums_ref, grads_ref, whole_ref) = refs[at : at + 5]
    weights, dpair, hidden, sems, out_sem = refs[at + 5 + found : at + 10 + found]
    step = pl.program_id(0)
    final = pl.num_programs(0) - 1
    if kind:
        hop = RowHop(
            kind, refs[count + 5 : at], refs[at + 5 : at + 5 + found], refs[at + 10 + found :]
        )

        @pl.when(step == 0)
        def _():
            hop.begin()

    write = pltpu.make_async_copy(weights, whole_ref, out_sem)

    @pl.when(step == 0)
    def _():
        if count == 1:
            copy = pltpu.make_async_copy(pieces[0], weights, sems.at[0])
            copy.start()
            copy.wait()
        elif count == 2:
            block = pieces[0].shape[0]

            def block_copy(back):
                at = pl.multiple_of(lax.rem(lax.axis_index("row") + back, 4) * block, block)
                source = pieces[1].at[pl.ds(at, block)] if back else pieces[0]
                return pltpu.make_async_copy(source, weights.at[pl.ds(at, block)], sems.at[back])

            for back in range(4):
                block_copy(back).start()
            for back in range(4):
                block_copy(back).wait()
        else:
            z = lax.axis_index("row")
            block = pieces[0].shape[0]

            def copy_of(piece, which):
                at = pl.multiple_of(places(z)[which] * block, block)
                return pltpu.make_async_copy(
                    piece, weights.at[pl.ds(at, block)], sems.at[which]
                )

            copy_of(pieces[0], 0).start()
            copy_of(pieces[1], 1).start()
            in_middle = (z == 1) | (z == 2)

            @pl.when(in_middle)
            def _():
                copy_of(pieces[2], 2).start()
                copy_of(pieces[3], 3).start()

            @pl.when(jnp.logical_not(in_middle))
            def _():
                copy_of(pieces[4], 2).start()
                copy_of(pieces[5], 3).start()

            for which in range(4):
                copy_of(pieces[which], which).wait()
        write.start()

    @pl.when(step < steps)
    def _():
        at = pl.multiple_of(step * TILE, TILE)
        rows, cots = x_ref[...], cot_ref[...]
        scale, weight = coef_ref[:, 0:1], coef_ref[:, 1:2]
        dots = jnp.zeros((TILE, 1), f32)
        inner = jnp.zeros((TILE, 1), f32)
        for a in range(0, size, TILE):
            b = min(a + TILE, size)
            gate = scale * mm(rows, weights[:, a:b])
            up = scale * mm(rows, weights[:, size + a : size + b])
            dhid = mm(cots, weights[:, 2 * size + a : 2 * size + b])
            sigma = jax.nn.sigmoid(gate)
            silu = gate * sigma
            hid = silu * up
            dots += jnp.sum(hid * dhid, axis=1, keepdims=True)
            dhid = weight * dhid
            dgate = dhid * up * sigma * (1.0 + gate * (1.0 - sigma))
            dup = dhid * silu
            inner += jnp.sum(dgate * gate + dup * up, axis=1, keepdims=True)
            for into, at_col, value in (
                ((hidden_ref, hidden), a, weight * hid),
                ((dpair_ref, dpair), a, scale * dgate),
                ((dpair_ref, dpair), size + a, scale * dup),
            ):
                value = value.astype(bf16)
                into[0][:, at_col : at_col + b - a] = value
                into[1][pl.ds(at, TILE), at_col : at_col + b - a] = value
        sums_ref[:, 0:1] = dots
        sums_ref[:, 1:2] = inner

    @pl.when(step >= steps)
    def _():
        for a in range(0, 2 * size, TILE):
            b = min(a + TILE, 2 * size)
            grads_ref[:, a:b] = mm_tn(x_cols[...], dpair[:, a:b]).astype(bf16)
        for a in range(0, size, TILE):
            b = min(a + TILE, size)
            grads_ref[:, 2 * size + a : 2 * size + b] = mm_tn(
                cot_cols[...], hidden[:, a:b]
            ).astype(bf16)

    @pl.when(step == final)
    def _():
        write.wait()
        if kind:
            hop.finish()


def expert_chunk(pieces, scaled, cots, coef, hop=None, number=None):
    tokens, width = scaled.shape
    size = pieces[0].shape[1] // 3
    steps, more_steps = tokens // TILE, width // TILE
    count = len(pieces)
    rows = lambda i: (jnp.minimum(i, steps - 1), 0)
    cols = lambda i: (0, jnp.maximum(i - steps, 0))
    down = lambda i: (jnp.maximum(i - steps, 0), 0)
    anywhere = pl.BlockSpec(memory_space=pl.ANY)
    more, more_shapes, more_scratch, params = hop_parts(hop, number)
    outs = pl.pallas_call(
        functools.partial(expert_kernel, size, steps, count, hop and hop[0]),
        grid_spec=pl.GridSpec(
            grid=(steps + more_steps,),
            in_specs=[pl.BlockSpec(memory_space=pl.ANY)] * count
            + [
                pl.BlockSpec((TILE, width), rows),
                pl.BlockSpec((TILE, width), rows),
                pl.BlockSpec((tokens, TILE), cols),
                pl.BlockSpec((tokens, TILE), cols),
                pl.BlockSpec((TILE, 2), rows),
            ]
            + [anywhere] * len(more),
            out_specs=[
                pl.BlockSpec((TILE, 2 * size), rows),
                pl.BlockSpec((TILE, size), rows),
                pl.BlockSpec((TILE, 2), rows),
                pl.BlockSpec((TILE, 3 * size), down),
                anywhere,
            ]
            + [anywhere] * len(more_shapes),
            scratch_shapes=[
                pltpu.VMEM((width, 3 * size), bf16),
                pltpu.VMEM((tokens, 2 * size), bf16),
                pltpu.VMEM((tokens, size), bf16),
                pltpu.SemaphoreType.DMA((4,)),
                pltpu.SemaphoreType.DMA,
            ]
            + more_scratch,
        ),
        out_shape=[
            jax.ShapeDtypeStruct((tokens, 2 * size), bf16),
            jax.ShapeDtypeStruct((tokens, size), bf16),
            jax.ShapeDtypeStruct((tokens, 2), f32),
            jax.ShapeDtypeStruct((width, 3 * size), bf16),
            jax.ShapeDtypeStruct((width, 3 * size), bf16),
        ]
        + more_shapes,
        compiler_params=params,
        cost_estimate=pl.CostEstimate(
            flops=12 * tokens * width * size,
            bytes_accessed=8 * tokens * width + 24 * width * size,
            transcendentals=tokens * size,
        ),
        name="expert_chunk",
    )(*pieces, scaled, cots, scaled, cots, coef, *more)
    return outs[:5], outs[5:]


def joint_kernel(count, based, planar, kind, *refs):
    taken, found = HOP_COUNTS[kind]
    at = 2 * count + based + taken
    out_ref = refs[at]
    if kind:
        hop = RowHop(kind, refs[at - taken : at], refs[at + 1 : at + 1 + found], refs[at + 1 + found :])

        @pl.when(pl.program_id(0) == 0)
        def _():
            hop.begin()

    for a in range(0, refs[count].shape[0], TILE):
        total = refs[2 * count][:, a : a + TILE] if based else None
        for left, weights in zip(refs[:count], refs[count : 2 * count]):
            part = mm_nt(left[...], weights[a : a + TILE, :])
            total = part if total is None else total + part
        if planar:
            at = a // TILE
            out_ref[at // 4, at // 2 % 2, at % 2] = total.astype(out_ref.dtype)
        else:
            out_ref[:, a : a + TILE] = total.astype(out_ref.dtype)
    if kind:
        @pl.when(pl.program_id(0) == pl.num_programs(0) - 1)
        def _():
            hop.finish()


def joint_back(lefts, weights, column, kind, *base, planar=False, hop=None, number=None):
    tokens, width = lefts[0].shape[0], weights[0].shape[0]
    row = lambda i: (i, 0)
    fixed = lambda i: (0, column)
    depth = sum(left.shape[1] for left in lefts)
    more, more_shapes, more_scratch, params = hop_parts(hop, number)
    anywhere = pl.BlockSpec(memory_space=pl.ANY)
    out_spec = pl.BlockSpec((TILE, width), row)
    if planar:
        out_spec = pl.BlockSpec((2, 2, 2, TILE, TILE), lambda i: (0, 0, 0, i, 0))
    outs = pl.pallas_call(
        functools.partial(joint_kernel, len(lefts), len(base), planar, hop and hop[0]),
        grid=(tokens // TILE,),
        in_specs=[pl.BlockSpec((TILE, left.shape[1]), row) for left in lefts]
        + [
            pl.BlockSpec((width, left.shape[1]), fixed, pipeline_mode=pl.Buffered(1))
            for left in lefts
        ]
        + [pl.BlockSpec((TILE, width), row)] * len(base)
        + [anywhere] * len(more),
        out_specs=[out_spec] + [anywhere] * len(more_shapes),
        out_shape=[
            jax.ShapeDtypeStruct((2, 2, 2, tokens, TILE) if planar else (tokens, width), kind)
        ]
        + more_shapes,
        scratch_shapes=more_scratch,
        compiler_params=params,
        cost_estimate=pl.CostEstimate(
            flops=2 * tokens * width * depth,
            bytes_accessed=2 * (tokens + width) * depth + 4 * tokens * width,
            transcendentals=0,
        ),
        name="joint_back",
    )(*lefts, *weights, *base, *more)
    return outs[0] if hop is None else outs


def split_three(values):
    high = values.astype(bf16)
    rest = values - high.astype(f32)
    middle = rest.astype(bf16)
    return high, middle, (rest - middle.astype(f32)).astype(bf16)


def cuts_of(width, sizes):
    cuts, at = [], 0
    for size in sizes:
        if at + size < width:
            cuts.append((at, at + size))
            at += size
    return cuts + [(at, width)]


def stream_step(total, rows, gain):
    stream = rows.astype(f32) + total
    return stream * gain, stream


def dstream_step(total, back, cots, stream, damp, gain):
    dscaled = back + total
    dstream = cots.astype(f32) + gain * dscaled - stream * damp
    return dstream, dstream, dscaled


def per_device(
    block_input,
    seq_lengths,
    slot_order,
    routes,
    input_gain,
    query_weight,
    key_weight,
    value_weight,
    output_weight,
    mlp_gain,
    router_weight,
    score_shared,
    gate_shared,
    up_shared,
    down_shared,
    gate_expert,
    up_expert,
    down_expert,
    grad_output,
):
    tokens, share = block_input.shape
    cols = lax.axis_size("col")
    col_id = lax.axis_index("col")
    row_id = lax.axis_index("row")
    width = share * cols
    slots = tokens // SEQ_LEN
    local_experts = gate_expert.shape[0]
    experts = router_weight.shape[1]
    head_width = query_weight.shape[1]
    heads = head_width // HEAD_DIM
    rows_block = query_weight.shape[0]
    lengths = lax.dynamic_slice_in_dim(seq_lengths[slot_order], row_id * slots, slots, 0)
    cosine, sine = rope_tables()

    def by_head(weight):
        return weight.reshape(rows_block, heads, 1, HEAD_DIM)

    qkv_pack = jnp.concatenate(
        [by_head(query_weight), by_head(key_weight), by_head(value_weight)], axis=2
    ).reshape(rows_block, 3 * head_width)
    router_pack = jnp.concatenate([router_weight, score_shared[:, None]], axis=1)
    router_pack = jnp.pad(router_pack, ((0, 0), (0, -router_pack.shape[1] % 128)))
    out_pack = jnp.concatenate([output_weight.T, router_pack], axis=1)
    qkv_whole, out_whole = gather_now([qkv_pack, out_pack], 0)
    qkv_full, out_weights = put_own(qkv_whole, qkv_pack), put_own(out_whole, out_pack)
    out_full = out_weights[:, :head_width]
    router_full = out_weights[:, head_width : head_width + experts + 1]
    shared_cuts = [(None, a, b) for a, b in cuts_of(gate_shared.shape[1], (512,))]
    expert_cuts = [
        (local, a, b)
        for local in range(local_experts)
        for a, b in cuts_of(gate_expert.shape[2], (512, 512))
    ]
    chunks = shared_cuts[-1:] + expert_cuts[:-1] + shared_cuts[:-1] + expert_cuts[-1:]

    def pack(kind, a, b):
        if kind is None:
            parts = [gate_shared[:, a:b], up_shared[:, a:b], down_shared[a:b].T]
        else:
            parts = [gate_expert[kind, :, a:b], up_expert[kind, :, a:b], down_expert[kind, a:b].T]
        fill = -(b - a) % 128
        return jnp.concatenate([jnp.pad(part, ((0, 0), (0, fill))) for part in parts], axis=1)

    packs = [pack(*chunk) for chunk in chunks]
    chained = lax.axis_size("row") == 4
    planar = chained and cols == 8 and share == TILE
    gathered = {}
    gathered[0] = Gathered(packs[0])

    rows_in = lax.all_gather(block_input, "col", axis=1, tiled=True)
    gains = lax.all_gather(jnp.stack([input_gain, mlp_gain]), "col", axis=1, tiled=True).astype(f32)
    cot_rows = lax.all_gather(grad_output, "col", axis=1, tiled=True)
    rows_f = rows_in.astype(f32)
    scale_a = lax.rsqrt(jnp.mean(rows_f * rows_f, axis=-1, keepdims=True) + norm_eps)
    normed_a = (rows_f * scale_a * gains[0]).astype(bf16)
    raw = mm(normed_a, qkv_full)
    raw = after(raw, gathered[0].second())
    qkv, context, lse = attend_forward(raw, lengths, cosine, sine)
    context = after(context, gathered[0].third())
    x_share = block_input.astype(f32)
    gain_b = mlp_gain.astype(f32)
    if planar:
        attn_part = joint_back([context], [out_weights], 0, bf16, planar=True)
        attn_part = after(attn_part, (cot_rows,))
        (stream,), (scaled,), wholes_now = plane_step(
            attn_part, stream_step, [block_input, gain_b[None]], 1, 1, 1, packs[1:2]
        )
        gathered[1] = (packs[1], wholes_now[0])
    else:
        attn_part = mm_nt(context, out_full).astype(bf16)
        attn_sum = lax.psum_scatter(attn_part, "col", scatter_dimension=1, tiled=True)
        scaled_share, stream = stream_step(attn_sum.astype(f32), block_input, gain_b[None])
        scaled = lax.all_gather(scaled_share.astype(bf16), "col", axis=1, tiled=True)
    for at in range(1, 1 if planar else len(chunks)):
        if at not in gathered:
            gathered[at] = Gathered(packs[at], (scaled,))

    def pieces_of(at):
        return gathered[at] if isinstance(gathered[at], tuple) else gathered[at].pieces

    stream_f = scaled.astype(f32) / gains[1]
    scale_b = lax.rsqrt(jnp.mean(stream_f * stream_f, axis=1, keepdims=True) + norm_eps)

    both_logits = scale_b * mm(scaled, router_full)
    logits, slogit = both_logits[:, :experts], both_logits[:, experts]
    top = jnp.max(logits, axis=-1, keepdims=True)
    expo = jnp.exp(logits - top)
    router_probs = expo / jnp.sum(expo, axis=-1, keepdims=True)
    shared_gate = jax.nn.sigmoid(slogit)

    inner = jnp.zeros((tokens,), f32)
    dots = {}
    members, shares = {None: None}, {None: shared_gate}
    for local in range(local_experts):
        expert = col_id * local_experts + local
        members[local] = jnp.any(routes == expert, axis=1)
        column = lax.dynamic_index_in_dim(router_probs, expert, 1, False)
        shares[local] = jnp.where(members[local], column, 0.0)
    dpairs, hiddens, wholes, reduced = [], [], [], []
    last = len(chunks) - 1
    waits = ()
    if not planar:
        for at in range(1, len(chunks)):
            gathered[at].second()
            gathered[at].third()

    carried = []
    for at, (kind, a, b) in enumerate(chunks):
        coef = jnp.concatenate([scale_b, shares[kind][:, None]], axis=1)
        coef = after(coef, waits)
        hop = None
        if planar:
            hop = {0: (1, packs[2:3]), 1: (2, carried), 2: (1, packs[3:4]), 3: (1, packs[4:5])}.get(at)
        (dpair, hidden, sums, grads, whole), found = expert_chunk(
            pieces_of(at), scaled, cot_rows, coef, hop, 4 + at
        )
        carried = carried + list(found) if at == 1 else list(found)
        dots[kind] = dots.get(kind, 0.0) + sums[:, 0]
        inner = inner + sums[:, 1]
        dpairs.append(dpair)
        hiddens.append(hidden)
        wholes.append(whole)
        now = (sums,)
        waits = ()
        if at < last or not planar:
            reduced.append(Reduced(grads))
        if planar and at == 0:
            waits = (reduced[0].pair,)
        elif planar and at == 1:
            first_pair = after(dpairs[0], reduced[0].second(now), (reduced[1].pair,))
            dscaled_early, last_piece = joint_back(
                [first_pair, dpair], wholes, 0, f32, hop=(3, carried[2:3]), number=9
            )
            gathered[2] = (packs[2], *carried[:2], carried[2], carried[3], last_piece)
            waits = (dscaled_early,)
        elif planar and at == 2:
            rest = hop_now((23, [after(carried[0], now, (reduced[2].pair,)), carried[1]]), 10)
            gathered[3] = (packs[3], *carried, *rest)
            waits = (rest[2],)
        elif planar and at == 3:
            third_pair = after(dpairs[2], (reduced[3].pair,))
            dscaled_early, *next_pieces = joint_back(
                [third_pair, dpair], wholes[2:], 0, f32, dscaled_early, hop=(2, carried), number=11
            )
            first_hidden = after(hiddens[0], reduced[1].second((dscaled_early,)))
            moe_early, last_piece = joint_back(
                [first_hidden] + hiddens[1:], wholes, 2, f32, hop=(3, next_pieces[:1]), number=12
            )
            gathered[4] = (packs[4], *carried, *next_pieces, last_piece)
            waits = (dscaled_early, moe_early)
    now = (sums,)
    if planar:
        waits = reduced[2].second(now) + reduced[0].third(now) + reduced[1].third(now)
    else:
        waits = ()
        for one in reduced:
            one.second()
            one.third()
    joined = 4 if planar else 0
    bases = ((dscaled_early,), (moe_early,)) if planar else ((), ())
    late_pairs, late_wholes, late_hiddens = dpairs[joined:], wholes[joined:], hiddens[joined:]
    late_pairs[-1] = after(late_pairs[-1], waits)
    dscaled_part = joint_back(late_pairs, late_wholes, 0, bf16, *bases[0], planar=planar)

    named = [jnp.where(members[local], dots[local], 0.0) for local in range(local_experts)]
    table = lax.all_gather(jnp.stack(named + [dots[None], inner]), "col", axis=0)
    dprob = table[:, :local_experts].reshape(experts, tokens).T
    dshared_gate, inner = jnp.sum(table[:, local_experts], axis=0), jnp.sum(table[:, local_experts + 1], axis=0)
    dlogits = router_probs * (dprob - jnp.sum(dprob * router_probs, axis=1, keepdims=True))
    dslogit = dshared_gate * shared_gate * (1.0 - shared_gate)
    dboth = jnp.concatenate([dlogits, dslogit[:, None]], axis=1)
    inner = inner + jnp.sum(dboth * both_logits, axis=1)
    dboth = scale_b * dboth
    parts = split_three(dboth)
    router_rows = lax.dynamic_slice_in_dim(router_full, col_id * share, share, 0)
    back_term = mm_nt(jnp.concatenate(parts, axis=1), jnp.concatenate([router_rows] * 3, axis=1))
    damp = scale_b * scale_b * inner[:, None] / width
    step_inputs = [back_term, grad_output, stream, damp, gain_b[None]]
    if planar:
        (dstream, dscaled, last_grad), (dattn,), _ = plane_step(
            dscaled_part, dstream_step, step_inputs, 2, 1, 2, (), grads
        )
    else:
        dscaled_sum = lax.psum_scatter(dscaled_part, "col", scatter_dimension=1, tiled=True)
        dstream_low, dstream, dscaled = dstream_step(dscaled_sum.astype(f32), *step_inputs)
        dattn = lax.all_gather(dstream_low.astype(bf16), "col", axis=1, tiled=True)
    gain_b_grad = jnp.sum(dscaled * stream, axis=0)

    late_hiddens[-1] = after(late_hiddens[-1], (dattn,))
    moe_part = joint_back(late_hiddens, late_wholes, 2, bf16, *bases[1])
    moe_share = lax.psum_scatter(moe_part, "col", scatter_dimension=1, tiled=True).astype(f32)
    block_output = (stream + moe_share).astype(bf16)
    out_part = mm_tn(dattn, context).astype(bf16)
    dcontext = mm(dattn, out_full).astype(bf16)
    if planar:
        dcontext = after(dcontext, reduced[3].second((dattn,)), reduced[2].third((dattn,)))
    router_left = after(jnp.concatenate(parts, axis=1), (dattn,))
    grad_router_part = mm_tn(router_left, scaled).reshape(3, experts + 1, width).sum(axis=0)
    grad_router_both = lax.psum_scatter(grad_router_part, "row", scatter_dimension=1, tiled=True)
    dqkv, inner_a = attend_backward(qkv, dcontext, lse, lengths, cosine, sine)
    if planar:
        dqkv = after(dqkv, reduced[3].third((inner_a,)))
    inner_a = lax.psum(inner_a[:, 0], "col")[:, None]
    attn_grads = jnp.concatenate([mm_tn(normed_a, dqkv).astype(bf16), out_part], axis=1)
    if planar:
        dnormed_part = joint_back([dqkv], [qkv_full], 0, bf16, planar=True)
        dnormed_part = after(dnormed_part, (inner_a,))
        (dnormed_a, attn_grad), _, _ = plane_step(
            dnormed_part, lambda total: (total,), [], 1, 0, 3, (), attn_grads
        )
    else:
        dnormed_a = lax.psum_scatter(
            mm_nt(dqkv, qkv_full).astype(bf16), "col", scatter_dimension=1, tiled=True
        ).astype(f32)
        attn_grad = one_reduction(attn_grads)
    qkv_grad, out_grad = attn_grad[:, : 3 * head_width], attn_grad[:, 3 * head_width :]
    unit_grads = [one.result() for one in reduced]
    if planar:
        unit_grads.append(last_grad)
    gain_a_share = input_gain.astype(f32)
    dinput = dstream + scale_a * gain_a_share * dnormed_a
    dinput = dinput - x_share * (scale_a * scale_a * inner_a / width)
    gain_a_grad = jnp.sum(dnormed_a * x_share * scale_a, axis=0)
    grad_gain_a, grad_gain_b = lax.psum((gain_a_grad, gain_b_grad), "row")

    qkv_grad = qkv_grad.reshape(rows_block, heads, 3, HEAD_DIM)
    grad_query, grad_key, grad_value = (
        qkv_grad[:, :, part].reshape(rows_block, head_width) for part in range(3)
    )
    def unpack(kind, which):
        found = []
        for (of, a, b), grad in zip(chunks, unit_grads):
            if of == kind:
                size = grad.shape[1] // 3
                part = grad[:, which * size : which * size + b - a]
                found.append((a, part.T if which == 2 else part))
        found = [part for _, part in sorted(found, key=lambda item: item[0])]
        return jnp.concatenate(found, axis=0 if which == 2 else 1)

    locals_ = range(local_experts)
    return (
        block_output,
        dinput.astype(bf16),
        grad_gain_a,
        grad_query,
        grad_key,
        grad_value,
        out_grad.T,
        grad_gain_b,
        grad_router_both[:experts].T,
        grad_router_both[experts],
        unpack(None, 0),
        unpack(None, 1),
        unpack(None, 2),
        jnp.stack([unpack(local, 0) for local in locals_]),
        jnp.stack([unpack(local, 1) for local in locals_]),
        jnp.stack([unpack(local, 2) for local in locals_]),
    )


def solution(mesh):
    return jax.shard_map(
        per_device,
        mesh=mesh,
        in_specs=(
            P("row", "col"),
            P(),
            P(),
            P("row", None),
            P("col"),
            P("row", "col"),
            P("row", "col"),
            P("row", "col"),
            P("col", "row"),
            P("col"),
            P("row", None),
            P("row"),
            P("row", "col"),
            P("row", "col"),
            P("col", "row"),
            P("col", "row", None),
            P("col", "row", None),
            P("col", None, "row"),
            P("row", "col"),
        ),
        out_specs=(
            P("row", "col"),
            P("row", "col"),
            P("col"),
            P("row", "col"),
            P("row", "col"),
            P("row", "col"),
            P("col", "row"),
            P("col"),
            P("row", None),
            P("row"),
            P("row", "col"),
            P("row", "col"),
            P("col", "row"),
            P("col", "row", None),
            P("col", "row", None),
            P("col", None, "row"),
        ),
        check_vma=False,
    )
```

```python
import functools
import math

import jax
import jax.numpy as jnp
from jax import lax
from jax.experimental import pallas as pl
from jax.experimental.pallas import tpu as pltpu
from jax.sharding import PartitionSpec as P

HEAD_DIM = 128
SEQ_LEN = 1024
QBLOCK = 256
TILE = 256
norm_eps = 1e-06
rope_base = 1000000.0
bf16 = jnp.bfloat16
f32 = jnp.float32


def mm(left, right):
    return jnp.dot(left, right, preferred_element_type=f32)


def mm_nt(left, right):
    return lax.dot_general(left, right, (((1,), (1,)), ((), ())), preferred_element_type=f32)


def mm_tn(left, right):
    return lax.dot_general(left, right, (((0,), (0,)), ((), ())), preferred_element_type=f32)


def rope_tables():
    positions = jnp.arange(SEQ_LEN).astype(f32)
    freqs = jnp.power(f32(rope_base), -jnp.arange(0, HEAD_DIM, 2).astype(f32) / HEAD_DIM)
    angles = positions[:, None] * freqs[None, :]
    cosine, sine = jnp.cos(angles), jnp.sin(angles)
    return (
        jnp.concatenate([cosine, cosine], axis=-1),
        jnp.concatenate([-sine, sine], axis=-1),
    )


def block_scores(rows, keys, start, length, scale):
    raw = mm_nt(rows, keys) * scale
    query_pos = start + lax.broadcasted_iota(jnp.int32, raw.shape, 0)
    key_pos = lax.broadcasted_iota(jnp.int32, raw.shape, 1)
    return jnp.where((key_pos <= query_pos) & (key_pos < length), raw, -1e30)


def attend_forward_kernel(length_ref, raw_ref, cos_ref, sin_ref, qkv_ref, context_ref, lse_ref):
    length = length_ref[pl.program_id(0)]
    scale = 1.0 / math.sqrt(HEAD_DIM)
    hd = HEAD_DIM
    for part in range(2):
        raw = raw_ref[:, part * hd : (part + 1) * hd]
        turned = raw * cos_ref[...] + pltpu.roll(raw, hd // 2, 1) * sin_ref[...]
        qkv_ref[:, part * hd : (part + 1) * hd] = turned.astype(bf16)
    qkv_ref[:, 2 * hd :] = raw_ref[:, 2 * hd :].astype(bf16)
    for at in range(0, SEQ_LEN, QBLOCK):
        seen = at + QBLOCK
        scores = block_scores(
            qkv_ref[at:seen, :hd], qkv_ref[:seen, hd : 2 * hd], at, length, scale
        )
        top = jnp.max(scores, axis=-1, keepdims=True)
        expo = jnp.exp(scores - top)
        total = jnp.sum(expo, axis=-1, keepdims=True)
        probs = (expo / total).astype(bf16)
        context_ref[at:seen, :] = mm(probs, qkv_ref[:seen, 2 * hd :]).astype(bf16)
        lse_ref[at:seen, :] = jnp.broadcast_to(top + jnp.log(total), (QBLOCK, hd))


def attend_forward(raw, lengths, cosine, sine):
    tokens, width = raw.shape
    heads = width // (3 * HEAD_DIM)
    slots = tokens // SEQ_LEN
    wide = pl.BlockSpec((SEQ_LEN, 3 * HEAD_DIM), lambda s, h, _: (s, h))
    one = pl.BlockSpec((SEQ_LEN, HEAD_DIM), lambda s, h, _: (s, h))
    table = pl.BlockSpec((SEQ_LEN, HEAD_DIM), lambda s, h, _: (0, 0))
    pairs = slots * heads * SEQ_LEN * SEQ_LEN
    return pl.pallas_call(
        attend_forward_kernel,
        grid_spec=pltpu.PrefetchScalarGridSpec(
            num_scalar_prefetch=1,
            grid=(slots, heads),
            in_specs=[wide, table, table],
            out_specs=[wide, one, one],
        ),
        out_shape=[
            jax.ShapeDtypeStruct((tokens, width), bf16),
            jax.ShapeDtypeStruct((tokens, heads * HEAD_DIM), bf16),
            jax.ShapeDtypeStruct((tokens, heads * HEAD_DIM), f32),
        ],
        cost_estimate=pl.CostEstimate(
            flops=3 * HEAD_DIM * pairs, bytes_accessed=8 * tokens * width, transcendentals=pairs
        ),
        name="attend_forward",
    )(lengths, raw, cosine, sine)


def attend_backward_kernel(
    length_ref, qkv_ref, dcontext_ref, lse_ref, cos_ref, sin_ref, dqkv_ref, inner_ref, dk_ref, dv_ref
):
    length = length_ref[pl.program_id(0)]
    scale = 1.0 / math.sqrt(HEAD_DIM)
    hd = HEAD_DIM
    @pl.when(pl.program_id(1) == 0)
    def _():
        inner_ref[...] = jnp.zeros_like(inner_ref)

    dk_ref[...] = jnp.zeros_like(dk_ref)
    dv_ref[...] = jnp.zeros_like(dv_ref)

    def turn_back(grad, rows):
        back = grad * cos_ref[rows, :] - pltpu.roll(grad, hd // 2, 1) * sin_ref[rows, :]
        return back.astype(bf16)

    for at in range(0, SEQ_LEN, QBLOCK):
        seen = at + QBLOCK
        rows = qkv_ref[at:seen, :hd]
        keys = qkv_ref[:seen, hd : 2 * hd]
        drows = dcontext_ref[at:seen, :]
        scores = block_scores(rows, keys, at, length, scale)
        probs = jnp.exp(scores - lse_ref[at:seen, :1])
        dv_ref[:seen, :] += mm_tn(probs.astype(bf16), drows)
        dprobs = mm_nt(drows, qkv_ref[:seen, 2 * hd :])
        dscore = probs * (dprobs - jnp.sum(dprobs * probs, axis=-1, keepdims=True))
        draw = (dscore * scale).astype(bf16)
        dquery = mm(draw, keys)
        dk_ref[:seen, :] += mm_tn(draw, rows)
        dqkv_ref[at:seen, :hd] = turn_back(dquery, slice(at, seen))
        inner_ref[at:seen, :] += jnp.sum(dquery * rows.astype(f32), axis=-1, keepdims=True)
    dkey, dvalue = dk_ref[...], dv_ref[...]
    dqkv_ref[:, hd : 2 * hd] = turn_back(dkey, slice(None))
    dqkv_ref[:, 2 * hd :] = dvalue.astype(bf16)
    inner_ref[...] += jnp.sum(
        dkey * qkv_ref[:, hd : 2 * hd].astype(f32) + dvalue * qkv_ref[:, 2 * hd :].astype(f32),
        axis=-1,
        keepdims=True,
    )


def attend_backward(qkv, dcontext, lse, lengths, cosine, sine):
    tokens, width = qkv.shape
    heads = width // (3 * HEAD_DIM)
    slots = tokens // SEQ_LEN
    wide = pl.BlockSpec((SEQ_LEN, 3 * HEAD_DIM), lambda s, h, _: (s, h))
    one = pl.BlockSpec((SEQ_LEN, HEAD_DIM), lambda s, h, _: (s, h))
    table = pl.BlockSpec((SEQ_LEN, HEAD_DIM), lambda s, h, _: (0, 0))
    pairs = slots * heads * SEQ_LEN * SEQ_LEN
    return pl.pallas_call(
        attend_backward_kernel,
        grid_spec=pltpu.PrefetchScalarGridSpec(
            num_scalar_prefetch=1,
            grid=(slots, heads),
            in_specs=[wide, one, one, table, table],
            out_specs=[wide, pl.BlockSpec((SEQ_LEN, 1), lambda s, h, _: (s, 0))],
            scratch_shapes=[pltpu.VMEM((SEQ_LEN, HEAD_DIM), f32)] * 2,
        ),
        out_shape=[
            jax.ShapeDtypeStruct((tokens, width), bf16),
            jax.ShapeDtypeStruct((tokens, 1), f32),
        ],
        cost_estimate=pl.CostEstimate(
            flops=8 * HEAD_DIM * pairs, bytes_accessed=8 * tokens * width, transcendentals=pairs
        ),
        name="attend_backward",
    )(lengths, qkv, dcontext, lse, cosine, sine)


PAIRS = [(0, 1), (1, 0), (2, 3), (3, 2)]
MIDDLE = [(1, 2), (2, 1)]
OUTWARD = [(1, 0), (2, 3)]
INWARD = [(0, 1), (3, 2)]


class Gathered:
    def __init__(self, part, *groups):
        self.part = part
        if lax.axis_size("row") != 4:
            self.pieces = (lax.all_gather(part, "row", axis=0, tiled=True),)
            return
        part = after(part, *groups)
        self.partner = lax.ppermute(part, "row", PAIRS)
        self.near_mid = lax.ppermute(part, "row", MIDDLE)
        self.pieces = None

    def second(self, *groups):
        if self.pieces is None:
            self.near_out = lax.ppermute(after(self.near_mid, *groups), "row", OUTWARD)
            self.far_mid = lax.ppermute(after(self.partner, *groups), "row", MIDDLE)
            return (self.partner, self.near_mid)
        return ()

    def third(self, *groups):
        if self.pieces is None:
            self.far_out = lax.ppermute(after(self.far_mid, *groups), "row", OUTWARD)
            self.pieces = (
                self.part, self.partner, self.near_mid, self.far_mid, self.near_out, self.far_out
            )
            return (self.far_mid, self.near_out)
        return ()


def places(z):
    pair = z // 2
    return z, z + 1 - 2 * lax.rem(z, 2), 2 - pair, 3 - 3 * pair


class RowGather:
    def __init__(self, packs, wholes, sems):
        self.packs, self.wholes, (self.send_sems, self.recv_sems) = packs, wholes, sems
        self.z = lax.axis_index("row")
        self.own, self.partner, self.near, self.far = places(self.z)
        self.across = 3 - self.z
        self.in_middle = (self.z == 1) | (self.z == 2)
        self.outside = jnp.logical_not(self.in_middle)

    def copy_of(self, kind, at, source, block, target):
        return pltpu.make_async_remote_copy(
            src_ref=source,
            dst_ref=self.wholes[at].at[block],
            send_sem=self.send_sems.at[kind, at],
            recv_sem=self.recv_sems.at[kind, at],
            device_id={"row": target},
            device_id_type=pl.DeviceIdType.MESH,
        )

    def swap(self, at):
        return self.copy_of(0, at, self.packs[at], self.own, self.partner)

    def swap_middle(self, at):
        return self.copy_of(1, at, self.packs[at], self.own, self.across)

    def second_middle(self, at):
        return self.copy_of(2, at, self.wholes[at].at[self.partner], self.partner, self.across)

    def hand_near(self, at):
        return self.copy_of(3, at, self.wholes[at].at[self.near], self.near, self.partner)

    def hand_far(self, at):
        return self.copy_of(4, at, self.wholes[at].at[self.far], self.far, self.partner)

    def greet(self, barrier):
        signal_to(barrier, {"row": self.partner})

        @pl.when(self.in_middle)
        def _():
            signal_to(barrier, {"row": self.across})
            pl.semaphore_wait(barrier, 2)

        @pl.when(self.outside)
        def _():
            pl.semaphore_wait(barrier, 1)

    def begin(self):
        for at in range(len(self.packs)):
            @pl.when(self.in_middle)
            def _():
                self.swap_middle(at).start()

            self.swap(at).start()

    def hand_on(self, at):
        @pl.when(self.in_middle)
        def _():
            self.swap_middle(at).wait_recv()
            self.hand_near(at).start()
            self.swap(at).wait_recv()
            self.second_middle(at).start()

    def hand_last(self, at):
        @pl.when(self.in_middle)
        def _():
            self.second_middle(at).wait_recv()
            self.hand_far(at).start()

    def finish(self):
        for at in range(len(self.packs)):
            @pl.when(self.in_middle)
            def _():
                for copy in (
                    self.swap,
                    self.swap_middle,
                    self.second_middle,
                    self.hand_near,
                    self.hand_far,
                ):
                    copy(at).wait_send()

            @pl.when(self.outside)
            def _():
                self.swap(at).wait()
                self.hand_near(at).wait_recv()
                self.hand_far(at).wait_recv()


class RowReduce:
    def __init__(self, grads, total, refs):
        self.grads, self.total = grads, total
        self.far_in, self.near_in, self.far_sum, self.near_sum, self.last = refs[:5]
        self.held, self.more, self.send_sems, self.recv_sems, self.local_sems = refs[5:]
        self.z = lax.axis_index("row")
        self.own, self.partner, self.near, self.far = places(self.z)
        self.across = 3 - self.z
        self.in_middle = (self.z == 1) | (self.z == 2)
        self.outside = jnp.logical_not(self.in_middle)

    def copy_of(self, kind, source, target, device):
        return pltpu.make_async_remote_copy(
            src_ref=source,
            dst_ref=target,
            send_sem=self.send_sems.at[kind],
            recv_sem=self.recv_sems.at[kind],
            device_id={"row": device},
            device_id_type=pl.DeviceIdType.MESH,
        )

    def send_far(self):
        return self.copy_of(0, self.grads.at[self.far], self.far_in, self.partner)

    def send_near(self):
        return self.copy_of(1, self.grads.at[self.near], self.near_in, self.partner)

    def cross_far(self):
        return self.copy_of(2, self.far_in, self.far_sum, self.across)

    def cross_near(self):
        return self.copy_of(3, self.near_in, self.near_sum, self.across)

    def swap_middle(self):
        return self.copy_of(4, self.far_sum, self.last, self.partner)

    def swap_outer(self):
        return self.copy_of(4, self.grads.at[self.partner], self.last, self.partner)

    def load(self, kind, block):
        target = self.more if kind % 2 else self.held
        return pltpu.make_async_copy(self.grads.at[block], target, self.local_sems.at[kind])

    def add(self, target, source):
        @pl.loop(0, target.shape[0], step=64)
        def _(at):
            tile = pl.ds(pl.multiple_of(at, 64), 64)
            target[tile, :] = (target[tile, :].astype(f32) + source[tile, :].astype(f32)).astype(bf16)

    def begin(self):
        @pl.when(self.outside)
        def _():
            self.send_far().start()
            self.send_near().start()
            self.swap_outer().start()
            self.load(3, self.own).start()

        @pl.when(self.in_middle)
        def _():
            self.load(0, self.far).start()
            self.load(1, self.near).start()

    def second_far(self):
        @pl.when(self.in_middle)
        def _():
            self.load(0, self.far).wait()
            self.send_far().wait_recv()
            self.add(self.far_in, self.held)
            self.cross_far().start()
            self.load(2, self.partner).start()

    def second_near(self):
        @pl.when(self.in_middle)
        def _():
            self.load(1, self.near).wait()
            self.send_near().wait_recv()
            self.add(self.near_in, self.more)
            self.cross_near().start()
            self.load(3, self.own).start()

    def third(self):
        @pl.when(self.in_middle)
        def _():
            self.load(2, self.partner).wait()
            self.cross_far().wait_recv()
            self.add(self.far_sum, self.held)
            self.swap_middle().start()

    def finish(self):
        self.load(3, self.own).wait()
        self.swap_outer().wait_recv()

        @pl.when(self.in_middle)
        def _():
            self.cross_near().wait_recv()

        @pl.loop(0, self.total.shape[0], step=64)
        def _(at):
            tile = pl.ds(pl.multiple_of(at, 64), 64)
            self.total[tile, :] = self.more[tile, :].astype(f32) + self.last[tile, :].astype(f32)

        @pl.when(self.in_middle)
        def _():
            @pl.loop(0, self.total.shape[0], step=64)
            def _(at):
                tile = pl.ds(pl.multiple_of(at, 64), 64)
                self.total[tile, :] += self.near_sum[tile, :].astype(f32)

            self.cross_far().wait_send()
            self.cross_near().wait_send()
            self.swap_middle().wait_send()

        @pl.when(self.outside)
        def _():
            self.send_far().wait_send()
            self.send_near().wait_send()
            self.swap_outer().wait_send()


class RowHop:
    def __init__(self, kind, given, found, sems):
        self.kind, self.given, self.found, (self.send_sems, self.recv_sems) = kind, given, found, sems
        self.z = lax.axis_index("row")
        self.partner, self.across = places(self.z)[1], 3 - self.z
        self.in_middle = (self.z == 1) | (self.z == 2)
        self.outside = jnp.logical_not(self.in_middle)

    def copy_of(self, at, source, target, device):
        return pltpu.make_async_remote_copy(
            src_ref=source,
            dst_ref=target,
            send_sem=self.send_sems.at[at],
            recv_sem=self.recv_sems.at[at],
            device_id={"row": device},
            device_id_type=pl.DeviceIdType.MESH,
        )

    def across_copy(self):
        if self.kind == 1:
            return self.copy_of(0, self.given[0], self.found[1], self.across)
        return self.copy_of(0, self.given[0], self.found[0], self.across)

    def outward_copy(self):
        if self.kind == 1:
            return self.copy_of(1, self.given[0], self.found[0], self.partner)
        if self.kind == 3:
            return self.copy_of(1, self.given[0], self.found[0], self.partner)
        return self.copy_of(1, self.given[1], self.found[1], self.partner)

    def last_copy(self):
        return self.copy_of(2, self.found[0], self.found[2], self.partner)

    def begin(self):
        barrier = pltpu.get_barrier_semaphore()
        signal_to(barrier, {"row": self.partner})

        @pl.when(self.in_middle)
        def _():
            signal_to(barrier, {"row": self.across})
            pl.semaphore_wait(barrier, 2)
            if self.kind != 3:
                self.across_copy().start()
            self.outward_copy().start()

        @pl.when(self.outside)
        def _():
            pl.semaphore_wait(barrier, 1)
            if self.kind == 1:
                self.outward_copy().start()

    def finish(self):
        @pl.when(self.in_middle)
        def _():
            if self.kind != 3:
                self.across_copy().wait()
            if self.kind == 23:
                self.last_copy().start()
            if self.kind == 1:
                self.outward_copy().wait()
            else:
                self.outward_copy().wait_send()
            if self.kind == 23:
                self.last_copy().wait_send()

        @pl.when(self.outside)
        def _():
            if self.kind == 1:
                self.outward_copy().wait()
            else:
                self.outward_copy().wait_recv()
            if self.kind == 23:
                self.last_copy().wait_recv()


HOP_COUNTS = {1: (1, 2), 2: (2, 2), 3: (1, 1), 23: (2, 3), None: (0, 0)}


def hop_parts(hop, number):
    if hop is None:
        return [], [], [], pltpu.CompilerParams()
    kind, given = hop
    shape = jax.ShapeDtypeStruct(given[0].shape, bf16)
    scratch = [pltpu.SemaphoreType.DMA((3,)), pltpu.SemaphoreType.DMA((3,))]
    params = pltpu.CompilerParams(collective_id=number, has_side_effects=True)
    return list(given), [shape] * HOP_COUNTS[kind][1], scratch, params


def hop_kernel(kind, *refs):
    given, found = HOP_COUNTS[kind]
    hop = RowHop(kind, refs[:given], refs[given : given + found], refs[given + found :])
    hop.begin()
    hop.finish()


def hop_now(hop, number):
    given, shapes, scratch, params = hop_parts(hop, number)
    anywhere = pl.BlockSpec(memory_space=pl.ANY)
    return pl.pallas_call(
        functools.partial(hop_kernel, hop[0]),
        in_specs=[anywhere] * len(given),
        out_specs=[anywhere] * len(shapes),
        out_shape=shapes,
        scratch_shapes=scratch,
        compiler_params=params,
        name="gather_hops",
    )(*given)


def signal_to(barrier, device):
    pl.semaphore_signal(barrier, inc=1, device_id=device, device_id_type=pl.DeviceIdType.MESH)


def gather_kernel(count, *refs):
    rows = RowGather(refs[:count], refs[count : 2 * count], refs[2 * count :])
    rows.greet(pltpu.get_barrier_semaphore())
    rows.begin()
    for at in range(count):
        rows.hand_on(at)
    for at in range(count):
        rows.hand_last(at)
    rows.finish()


PIECES = 4


def plane_kernel(pointwise, given, made, gather, count, reducing, *refs):
    p_ref, inputs = refs[0], refs[1 : 1 + given]
    at = 1 + given
    packs = refs[at : at + count]
    at += count
    grads = refs[at] if reducing else None
    at += reducing
    results = refs[at : at + made]
    at += made
    total_ref = refs[at] if reducing else None
    at += reducing
    whole_refs = refs[at : at + gather + count]
    at += gather + count
    mine, from_core, from_first, summed, from_second, shared, send_sems, recv_sems, local_sems = refs[
        at : at + 9
    ]
    out_ref = whole_refs[0] if gather else None
    me = lax.axis_index("col")
    core, x, y = lax.rem(me, 2), lax.rem(me // 2, 2), me // 4
    core_mate, x_mate, y_mate = me + 1 - 2 * core, me + 2 - 4 * x, me + 4 - 8 * y
    diagonal = x_mate + 4 - 8 * y
    size = mine.shape[3]
    share = mine.shape[4]
    barrier = pltpu.get_barrier_semaphore()
    for mate in (core_mate, x_mate, y_mate):
        signal_to(barrier, {"col": mate})
    rows, reduction = None, None
    if count or reducing:
        if count:
            rows = RowGather(packs, whole_refs[gather:], refs[at + 9 : at + 11])
            at += 2
        if reducing:
            reduction = RowReduce(grads, total_ref, refs[at + 9 : at + 19])
        chain = rows or reduction
        signal_to(barrier, {"row": chain.partner})

        @pl.when(chain.in_middle)
        def _():
            signal_to(barrier, {"row": chain.across})
            pl.semaphore_wait(barrier, 5)

        @pl.when(chain.outside)
        def _():
            pl.semaphore_wait(barrier, 4)

        if count:
            rows.begin()
        if reducing:
            reduction.begin()
    else:
        pl.semaphore_wait(barrier, 3)

    def remote(kind, i, source, target, mate):
        return pltpu.make_async_remote_copy(
            src_ref=source,
            dst_ref=target,
            send_sem=send_sems.at[kind, i],
            recv_sem=recv_sems.at[kind, i],
            device_id={"col": mate},
            device_id_type=pl.DeviceIdType.MESH,
        )

    def x_first(i):
        return i < PIECES // 2

    def span(i):
        return pl.ds(i * size, size)

    def core_copy(i):
        return remote(0, i, p_ref.at[:, :, 1 - core, span(i), :], from_core.at[i], core_mate)

    def load(i):
        return pltpu.make_async_copy(
            p_ref.at[:, :, core, span(i), :], mine.at[i], local_sems.at[0, i]
        )

    def first_copy(i):
        if x_first(i):
            return remote(1, i, mine.at[i, :, 1 - x], from_first.at[i], x_mate)
        return remote(1, i, mine.at[i, 1 - y], from_first.at[i], y_mate)

    def second_copy(i):
        if x_first(i):
            return remote(2, i, summed.at[i, 1 - y], from_second.at[i], y_mate)
        return remote(2, i, summed.at[i, 1 - x], from_second.at[i], x_mate)

    def columns(i, device):
        return out_ref.at[span(i), pl.ds(pl.multiple_of(device * share, share), share)]

    def spread(kind, i, mate):
        return remote(kind, i, shared.at[i], columns(i, me), mate)

    def keep(i):
        return pltpu.make_async_copy(shared.at[i], columns(i, me), local_sems.at[1, i])

    def pass_on(kind, i, device, mate):
        return remote(kind, i, columns(i, device), columns(i, device), mate)

    def forward(i):
        if x_first(i):
            return pass_on(6, i, y_mate, x_mate)
        return pass_on(6, i, x_mate, y_mate)

    order = [0, 2, 1, 3]
    for i in order:
        core_copy(i).start()
        load(i).start()
    for i in order:
        load(i).wait()
        core_copy(i).wait_recv()
        for a in range(2):
            for b in range(2):
                mine[i, a, b] = (mine[i, a, b].astype(f32) + from_core[i, a, b].astype(f32)).astype(bf16)
        first_copy(i).start()
    for i in order:
        first_copy(i).wait_recv()
        for a in range(2):
            kept = mine[i, a, x] if x_first(i) else mine[i, y, a]
            summed[i, a] = (kept.astype(f32) + from_first[i, a].astype(f32)).astype(bf16)
        second_copy(i).start()
    if count:
        for at in range(count):
            rows.hand_on(at)
    if reducing:
        reduction.second_far()
    for i in order:
        second_copy(i).wait_recv()
        total = summed[i, y if x_first(i) else x].astype(f32) + from_second[i].astype(f32)
        span_rows = slice(i * size, (i + 1) * size)
        values = pointwise(
            total, *[ref[span_rows, :] if ref.shape[0] > 8 else ref[...] for ref in inputs]
        )
        if gather:
            shared[i] = values[0].astype(bf16)
            values = values[1:]
        for ref, value in zip(results, values):
            ref[span_rows, :] = value
        if gather:
            spread(4, i, x_mate).start()
            spread(5, i, y_mate).start()
            spread(3, i, core_mate).start()
            keep(i).start()
    if count:
        rows.hand_last(0)
    if reducing and not gather:
        reduction.second_near()
    if gather:
        for i in order:
            spread(5 if x_first(i) else 4, i, y_mate).wait_recv()
            forward(i).start()
            pass_on(7, i, y_mate if x_first(i) else x_mate, core_mate).start()
        for i in order:
            spread(4 if x_first(i) else 5, i, x_mate).wait_recv()
            pass_on(8, i, x_mate if x_first(i) else y_mate, core_mate).start()
    if count:
        for at in range(1, count):
            rows.hand_last(at)
    if reducing and gather:
        reduction.second_near()
    if reducing:
        reduction.third()
    if gather:
        for i in order:
            forward(i).wait_recv()
            pass_on(9, i, diagonal, core_mate).start()
    for i in order:
        core_copy(i).wait_send()
        first_copy(i).wait_send()
        second_copy(i).wait_send()
        if gather:
            keep(i).wait()
            spread(3, i, core_mate).wait()
            spread(4, i, x_mate).wait_send()
            spread(5, i, y_mate).wait_send()
            forward(i).wait_send()
            for kind, device in (
                (7, y_mate if x_first(i) else x_mate),
                (8, x_mate if x_first(i) else y_mate),
                (9, diagonal),
            ):
                pass_on(kind, i, device, core_mate).wait()
    if count:
        rows.finish()
    if reducing:
        reduction.finish()


def plane_step(partial, pointwise, inputs, made, gather, number, packs=(), grads=None):
    tokens, share = partial.shape[3:]
    size = tokens // PIECES
    count = len(packs)
    reducing = 0 if grads is None else 1
    totals, more_scratch, given_grads = [], [], []
    if reducing:
        block, columns = grads.shape[0] // 4, grads.shape[1]
        given_grads = [grads.reshape(4, block, columns)]
        totals = [jax.ShapeDtypeStruct((block, columns), f32)]
        more_scratch = [pltpu.VMEM((block, columns), bf16)] * 7 + [
            pltpu.SemaphoreType.DMA((5,)),
            pltpu.SemaphoreType.DMA((5,)),
            pltpu.SemaphoreType.DMA((4,)),
        ]
    anywhere = pl.BlockSpec(memory_space=pl.ANY)
    vmem = pl.BlockSpec(memory_space=pltpu.VMEM)
    whole_shapes = [jax.ShapeDtypeStruct((tokens, 8 * share), bf16)] * gather + [
        jax.ShapeDtypeStruct((4,) + pack.shape, bf16) for pack in packs
    ]
    outs = pl.pallas_call(
        functools.partial(plane_kernel, pointwise, len(inputs), made, gather, count, reducing),
        in_specs=[anywhere] + [vmem] * len(inputs) + [anywhere] * (count + reducing),
        out_specs=[vmem] * (made + reducing) + [anywhere] * (gather + count),
        out_shape=[jax.ShapeDtypeStruct((tokens, share), f32)] * made + totals + whole_shapes,
        scratch_shapes=[
            pltpu.VMEM((PIECES, 2, 2, size, share), bf16),
            pltpu.VMEM((PIECES, 2, 2, size, share), bf16),
            pltpu.VMEM((PIECES, 2, size, share), bf16),
            pltpu.VMEM((PIECES, 2, size, share), bf16),
            pltpu.VMEM((PIECES, size, share), bf16),
            pltpu.VMEM((PIECES, size, share), bf16),
            pltpu.SemaphoreType.DMA((10, PIECES)),
            pltpu.SemaphoreType.DMA((10, PIECES)),
            pltpu.SemaphoreType.DMA((2, PIECES)),
        ]
        + [pltpu.SemaphoreType.DMA((5, count))] * (2 if count else 0)
        + more_scratch,
        compiler_params=pltpu.CompilerParams(collective_id=number, has_side_effects=True),
        cost_estimate=pl.CostEstimate(
            flops=60 * 10**9, bytes_accessed=32 * tokens * share, transcendentals=0
        ),
        name="plane_step",
    )(partial, *inputs, *packs, *given_grads)
    at = made + reducing
    wholes = [whole.reshape((4 * whole.shape[1],) + whole.shape[2:]) for whole in outs[at + gather :]]
    return outs[:at], outs[at : at + gather], wholes


def gather_now(packs, number):
    if lax.axis_size("row") != 4:
        return [lax.all_gather(pack, "row", axis=0, tiled=True) for pack in packs]
    count = len(packs)
    sent = sum(pack.size for pack in packs) * 2
    anywhere = pl.BlockSpec(memory_space=pl.ANY)
    wholes = pl.pallas_call(
        functools.partial(gather_kernel, count),
        in_specs=[anywhere] * count,
        out_specs=[anywhere] * count,
        out_shape=[jax.ShapeDtypeStruct((4,) + pack.shape, pack.dtype) for pack in packs],
        scratch_shapes=[pltpu.SemaphoreType.DMA((5, count)), pltpu.SemaphoreType.DMA((5, count))],
        compiler_params=pltpu.CompilerParams(collective_id=number, has_side_effects=True),
        cost_estimate=pl.CostEstimate(
            flops=6 * 9000 * sent, bytes_accessed=6 * sent, transcendentals=0
        ),
        name="gather_rows",
    )(*packs)
    return [whole.reshape((4 * whole.shape[1],) + whole.shape[2:]) for whole in wholes]


def put_own(whole, part):
    if lax.axis_size("row") != 4:
        return whole
    return lax.dynamic_update_slice_in_dim(
        whole, part, lax.axis_index("row") * part.shape[0], 0
    )


class Reduced:
    def __init__(self, grads):
        self.chained = lax.axis_size("row") == 4
        if not self.chained:
            self.total = lax.psum_scatter(grads, "row", scatter_dimension=0, tiled=True).astype(f32)
            return
        z = lax.axis_index("row")
        self.own, self.partner, _, _ = places(z)
        self.grads, self.size = grads, grads.shape[0] // 4
        self.pair = self.rows_of(grads, (1 - z // 2) * 2, 2)
        self.first = lax.ppermute(self.pair, "row", INWARD)

    def rows_of(self, value, at, count):
        return lax.dynamic_slice_in_dim(value, at * self.size, count * self.size, 0)

    def two(self, at):
        mine = self.rows_of(self.grads, at, 1).astype(f32)
        return mine + self.rows_of(self.crossed, lax.rem(at, 2), 1).astype(f32)

    def second(self, *groups):
        if not self.chained:
            return ()
        first = after(self.first, *groups)
        value = (self.pair.astype(f32) + first.astype(f32)).astype(bf16)
        self.crossed = lax.ppermute(value, "row", MIDDLE)
        return (value,)

    def third(self, *groups):
        if not self.chained:
            return ()
        self.crossed = after(self.crossed, *groups)
        value = self.two(self.partner).astype(bf16)
        self.swapped = lax.ppermute(value, "row", PAIRS)
        return (value,)

    def result(self, *groups):
        if self.chained:
            return self.two(self.own) + after(self.swapped, *groups).astype(f32)
        return self.total


def one_reduction(grads):
    one = Reduced(grads)
    one.second()
    one.third()
    return one.result()


def after(value, *groups):
    others = tuple(item for group in groups for item in group)
    return lax.optimization_barrier((value,) + others)[0] if others else value


def expert_kernel(size, steps, count, kind, *refs):
    pieces = refs[:count]
    (x_ref, cot_ref, x_cols, cot_cols, coef_ref) = refs[count : count + 5]
    taken, found = HOP_COUNTS[kind]
    at = count + 5 + taken
    (dpair_ref, hidden_ref, sums_ref, grads_ref, whole_ref) = refs[at : at + 5]
    weights, dpair, hidden, sems, out_sem = refs[at + 5 + found : at + 10 + found]
    step = pl.program_id(0)
    final = pl.num_programs(0) - 1
    if kind:
        hop = RowHop(
            kind, refs[count + 5 : at], refs[at + 5 : at + 5 + found], refs[at + 10 + found :]
        )

        @pl.when(step == 0)
        def _():
            hop.begin()

    write = pltpu.make_async_copy(weights, whole_ref, out_sem)

    @pl.when(step == 0)
    def _():
        if count == 1:
            copy = pltpu.make_async_copy(pieces[0], weights, sems.at[0])
            copy.start()
            copy.wait()
        elif count == 2:
            block = pieces[0].shape[0]

            def block_copy(back):
                at = pl.multiple_of(lax.rem(lax.axis_index("row") + back, 4) * block, block)
                source = pieces[1].at[pl.ds(at, block)] if back else pieces[0]
                return pltpu.make_async_copy(source, weights.at[pl.ds(at, block)], sems.at[back])

            for back in range(4):
                block_copy(back).start()
            for back in range(4):
                block_copy(back).wait()
        else:
            z = lax.axis_index("row")
            block = pieces[0].shape[0]

            def copy_of(piece, which):
                at = pl.multiple_of(places(z)[which] * block, block)
                return pltpu.make_async_copy(
                    piece, weights.at[pl.ds(at, block)], sems.at[which]
                )

            copy_of(pieces[0], 0).start()
            copy_of(pieces[1], 1).start()
            in_middle = (z == 1) | (z == 2)

            @pl.when(in_middle)
            def _():
                copy_of(pieces[2], 2).start()
                copy_of(pieces[3], 3).start()

            @pl.when(jnp.logical_not(in_middle))
            def _():
                copy_of(pieces[4], 2).start()
                copy_of(pieces[5], 3).start()

            for which in range(4):
                copy_of(pieces[which], which).wait()
        write.start()

    @pl.when(step < steps)
    def _():
        at = pl.multiple_of(step * TILE, TILE)
        rows, cots = x_ref[...], cot_ref[...]
        scale, weight = coef_ref[:, 0:1], coef_ref[:, 1:2]
        dots = jnp.zeros((TILE, 1), f32)
        inner = jnp.zeros((TILE, 1), f32)
        for a in range(0, size, TILE):
            b = min(a + TILE, size)
            gate = scale * mm(rows, weights[:, a:b])
            up = scale * mm(rows, weights[:, size + a : size + b])
            dhid = mm(cots, weights[:, 2 * size + a : 2 * size + b])
            sigma = jax.nn.sigmoid(gate)
            silu = gate * sigma
            hid = silu * up
            dots += jnp.sum(hid * dhid, axis=1, keepdims=True)
            dhid = weight * dhid
            dgate = dhid * up * sigma * (1.0 + gate * (1.0 - sigma))
            dup = dhid * silu
            inner += jnp.sum(dgate * gate + dup * up, axis=1, keepdims=True)
            for into, at_col, value in (
                ((hidden_ref, hidden), a, weight * hid),
                ((dpair_ref, dpair), a, scale * dgate),
                ((dpair_ref, dpair), size + a, scale * dup),
            ):
                value = value.astype(bf16)
                into[0][:, at_col : at_col + b - a] = value
                into[1][pl.ds(at, TILE), at_col : at_col + b - a] = value
        sums_ref[:, 0:1] = dots
        sums_ref[:, 1:2] = inner

    @pl.when(step >= steps)
    def _():
        for a in range(0, 2 * size, TILE):
            b = min(a + TILE, 2 * size)
            grads_ref[:, a:b] = mm_tn(x_cols[...], dpair[:, a:b]).astype(bf16)
        for a in range(0, size, TILE):
            b = min(a + TILE, size)
            grads_ref[:, 2 * size + a : 2 * size + b] = mm_tn(
                cot_cols[...], hidden[:, a:b]
            ).astype(bf16)

    @pl.when(step == final)
    def _():
        write.wait()
        if kind:
            hop.finish()


def expert_chunk(pieces, scaled, cots, coef, hop=None, number=None):
    tokens, width = scaled.shape
    size = pieces[0].shape[1] // 3
    steps, more_steps = tokens // TILE, width // TILE
    count = len(pieces)
    rows = lambda i: (jnp.minimum(i, steps - 1), 0)
    cols = lambda i: (0, jnp.maximum(i - steps, 0))
    down = lambda i: (jnp.maximum(i - steps, 0), 0)
    anywhere = pl.BlockSpec(memory_space=pl.ANY)
    more, more_shapes, more_scratch, params = hop_parts(hop, number)
    outs = pl.pallas_call(
        functools.partial(expert_kernel, size, steps, count, hop and hop[0]),
        grid_spec=pl.GridSpec(
            grid=(steps + more_steps,),
            in_specs=[pl.BlockSpec(memory_space=pl.ANY)] * count
            + [
                pl.BlockSpec((TILE, width), rows),
                pl.BlockSpec((TILE, width), rows),
                pl.BlockSpec((tokens, TILE), cols),
                pl.BlockSpec((tokens, TILE), cols),
                pl.BlockSpec((TILE, 2), rows),
            ]
            + [anywhere] * len(more),
            out_specs=[
                pl.BlockSpec((TILE, 2 * size), rows),
                pl.BlockSpec((TILE, size), rows),
                pl.BlockSpec((TILE, 2), rows),
                pl.BlockSpec((TILE, 3 * size), down),
                anywhere,
            ]
            + [anywhere] * len(more_shapes),
            scratch_shapes=[
                pltpu.VMEM((width, 3 * size), bf16),
                pltpu.VMEM((tokens, 2 * size), bf16),
                pltpu.VMEM((tokens, size), bf16),
                pltpu.SemaphoreType.DMA((4,)),
                pltpu.SemaphoreType.DMA,
            ]
            + more_scratch,
        ),
        out_shape=[
            jax.ShapeDtypeStruct((tokens, 2 * size), bf16),
            jax.ShapeDtypeStruct((tokens, size), bf16),
            jax.ShapeDtypeStruct((tokens, 2), f32),
            jax.ShapeDtypeStruct((width, 3 * size), bf16),
            jax.ShapeDtypeStruct((width, 3 * size), bf16),
        ]
        + more_shapes,
        compiler_params=params,
        cost_estimate=pl.CostEstimate(
            flops=12 * tokens * width * size,
            bytes_accessed=8 * tokens * width + 24 * width * size,
            transcendentals=tokens * size,
        ),
        name="expert_chunk",
    )(*pieces, scaled, cots, scaled, cots, coef, *more)
    return outs[:5], outs[5:]


def joint_kernel(count, based, planar, kind, *refs):
    taken, found = HOP_COUNTS[kind]
    at = 2 * count + based + taken
    out_ref = refs[at]
    if kind:
        hop = RowHop(kind, refs[at - taken : at], refs[at + 1 : at + 1 + found], refs[at + 1 + found :])

        @pl.when(pl.program_id(0) == 0)
        def _():
            hop.begin()

    for a in range(0, refs[count].shape[0], TILE):
        total = refs[2 * count][:, a : a + TILE] if based else None
        for left, weights in zip(refs[:count], refs[count : 2 * count]):
            part = mm_nt(left[...], weights[a : a + TILE, :])
            total = part if total is None else total + part
        if planar:
            at = a // TILE
            out_ref[at // 4, at // 2 % 2, at % 2] = total.astype(out_ref.dtype)
        else:
            out_ref[:, a : a + TILE] = total.astype(out_ref.dtype)
    if kind:
        @pl.when(pl.program_id(0) == pl.num_programs(0) - 1)
        def _():
            hop.finish()


def joint_back(lefts, weights, column, kind, *base, planar=False, hop=None, number=None):
    tokens, width = lefts[0].shape[0], weights[0].shape[0]
    row = lambda i: (i, 0)
    fixed = lambda i: (0, column)
    depth = sum(left.shape[1] for left in lefts)
    more, more_shapes, more_scratch, params = hop_parts(hop, number)
    anywhere = pl.BlockSpec(memory_space=pl.ANY)
    out_spec = pl.BlockSpec((TILE, width), row)
    if planar:
        out_spec = pl.BlockSpec((2, 2, 2, TILE, TILE), lambda i: (0, 0, 0, i, 0))
    outs = pl.pallas_call(
        functools.partial(joint_kernel, len(lefts), len(base), planar, hop and hop[0]),
        grid=(tokens // TILE,),
        in_specs=[pl.BlockSpec((TILE, left.shape[1]), row) for left in lefts]
        + [
            pl.BlockSpec((width, left.shape[1]), fixed, pipeline_mode=pl.Buffered(1))
            for left in lefts
        ]
        + [pl.BlockSpec((TILE, width), row)] * len(base)
        + [anywhere] * len(more),
        out_specs=[out_spec] + [anywhere] * len(more_shapes),
        out_shape=[
            jax.ShapeDtypeStruct((2, 2, 2, tokens, TILE) if planar else (tokens, width), kind)
        ]
        + more_shapes,
        scratch_shapes=more_scratch,
        compiler_params=params,
        cost_estimate=pl.CostEstimate(
            flops=2 * tokens * width * depth,
            bytes_accessed=2 * (tokens + width) * depth + 4 * tokens * width,
            transcendentals=0,
        ),
        name="joint_back",
    )(*lefts, *weights, *base, *more)
    return outs[0] if hop is None else outs


def split_three(values):
    high = values.astype(bf16)
    rest = values - high.astype(f32)
    middle = rest.astype(bf16)
    return high, middle, (rest - middle.astype(f32)).astype(bf16)


def cuts_of(width, sizes):
    cuts, at = [], 0
    for size in sizes:
        if at + size < width:
            cuts.append((at, at + size))
            at += size
    return cuts + [(at, width)]


def stream_step(total, rows, gain):
    stream = rows.astype(f32) + total
    return stream * gain, stream


def dstream_step(total, back, cots, stream, damp, gain):
    dscaled = back + total
    dstream = cots.astype(f32) + gain * dscaled - stream * damp
    return dstream, dstream, dscaled


def per_device(
    block_input,
    seq_lengths,
    slot_order,
    routes,
    input_gain,
    query_weight,
    key_weight,
    value_weight,
    output_weight,
    mlp_gain,
    router_weight,
    score_shared,
    gate_shared,
    up_shared,
    down_shared,
    gate_expert,
    up_expert,
    down_expert,
    grad_output,
):
    tokens, share = block_input.shape
    cols = lax.axis_size("col")
    col_id = lax.axis_index("col")
    row_id = lax.axis_index("row")
    width = share * cols
    slots = tokens // SEQ_LEN
    local_experts = gate_expert.shape[0]
    experts = router_weight.shape[1]
    head_width = query_weight.shape[1]
    heads = head_width // HEAD_DIM
    rows_block = query_weight.shape[0]
    lengths = lax.dynamic_slice_in_dim(seq_lengths[slot_order], row_id * slots, slots, 0)
    cosine, sine = rope_tables()

    def by_head(weight):
        return weight.reshape(rows_block, heads, 1, HEAD_DIM)

    qkv_pack = jnp.concatenate(
        [by_head(query_weight), by_head(key_weight), by_head(value_weight)], axis=2
    ).reshape(rows_block, 3 * head_width)
    router_pack = jnp.concatenate([router_weight, score_shared[:, None]], axis=1)
    router_pack = jnp.pad(router_pack, ((0, 0), (0, -router_pack.shape[1] % 128)))
    out_pack = jnp.concatenate([output_weight.T, router_pack], axis=1)
    qkv_whole, out_whole = gather_now([qkv_pack, out_pack], 0)
    qkv_full, out_weights = put_own(qkv_whole, qkv_pack), put_own(out_whole, out_pack)
    out_full = out_weights[:, :head_width]
    router_full = out_weights[:, head_width : head_width + experts + 1]
    shared_cuts = [(None, a, b) for a, b in cuts_of(gate_shared.shape[1], (512,))]
    expert_cuts = [
        (local, a, b)
        for local in range(local_experts)
        for a, b in cuts_of(gate_expert.shape[2], (512, 512))
    ]
    chunks = shared_cuts[-1:] + expert_cuts[:-1] + shared_cuts[:-1] + expert_cuts[-1:]

    def pack(kind, a, b):
        if kind is None:
            parts = [gate_shared[:, a:b], up_shared[:, a:b], down_shared[a:b].T]
        else:
            parts = [gate_expert[kind, :, a:b], up_expert[kind, :, a:b], down_expert[kind, a:b].T]
        fill = -(b - a) % 128
        return jnp.concatenate([jnp.pad(part, ((0, 0), (0, fill))) for part in parts], axis=1)

    packs = [pack(*chunk) for chunk in chunks]
    chained = lax.axis_size("row") == 4
    planar = chained and cols == 8 and share == TILE
    gathered = {}
    gathered[0] = Gathered(packs[0], (qkv_whole,))

    gain_rows = jnp.pad(jnp.stack([input_gain, mlp_gain]), ((0, 14), (0, 0)))
    both_in = lax.all_gather(
        jnp.concatenate([block_input, gain_rows], axis=0), "col", axis=1, tiled=True
    )
    rows_in, gains = both_in[:tokens], both_in[tokens : tokens + 2].astype(f32)
    cot_rows = lax.all_gather(grad_output, "col", axis=1, tiled=True)
    rows_f = rows_in.astype(f32)
    scale_a = lax.rsqrt(jnp.mean(rows_f * rows_f, axis=-1, keepdims=True) + norm_eps)
    normed_a = (rows_f * scale_a * gains[0]).astype(bf16)
    raw = mm(normed_a, qkv_full)
    raw = after(raw, gathered[0].second())
    qkv, context, lse = attend_forward(raw, lengths, cosine, sine)
    context = after(context, gathered[0].third())
    x_share = block_input.astype(f32)
    gain_b = mlp_gain.astype(f32)
    if planar:
        attn_part = joint_back([context], [out_weights], 0, bf16, planar=True)
        attn_part = after(attn_part, (cot_rows,))
        (stream,), (scaled,), wholes_now = plane_step(
            attn_part, stream_step, [block_input, gain_b[None]], 1, 1, 1, packs[1:2]
        )
        gathered[1] = (packs[1], wholes_now[0])
    else:
        attn_part = mm_nt(context, out_full).astype(bf16)
        attn_sum = lax.psum_scatter(attn_part, "col", scatter_dimension=1, tiled=True)
        scaled_share, stream = stream_step(attn_sum.astype(f32), block_input, gain_b[None])
        scaled = lax.all_gather(scaled_share.astype(bf16), "col", axis=1, tiled=True)
    for at in range(1, 1 if planar else len(chunks)):
        if at not in gathered:
            gathered[at] = Gathered(packs[at], (scaled,))

    def pieces_of(at):
        return gathered[at] if isinstance(gathered[at], tuple) else gathered[at].pieces

    stream_f = scaled.astype(f32) / gains[1]
    scale_b = lax.rsqrt(jnp.mean(stream_f * stream_f, axis=1, keepdims=True) + norm_eps)

    both_logits = scale_b * mm(scaled, router_full)
    logits, slogit = both_logits[:, :experts], both_logits[:, experts]
    top = jnp.max(logits, axis=-1, keepdims=True)
    expo = jnp.exp(logits - top)
    router_probs = expo / jnp.sum(expo, axis=-1, keepdims=True)
    shared_gate = jax.nn.sigmoid(slogit)

    inner = jnp.zeros((tokens,), f32)
    dots = {}
    members, shares = {None: None}, {None: shared_gate}
    for local in range(local_experts):
        expert = col_id * local_experts + local
        members[local] = jnp.any(routes == expert, axis=1)
        column = lax.dynamic_index_in_dim(router_probs, expert, 1, False)
        shares[local] = jnp.where(members[local], column, 0.0)
    dpairs, hiddens, wholes, reduced = [], [], [], []
    last = len(chunks) - 1
    waits = ()
    if not planar:
        for at in range(1, len(chunks)):
            gathered[at].second()
            gathered[at].third()

    carried = []
    for at, (kind, a, b) in enumerate(chunks):
        coef = jnp.concatenate([scale_b, shares[kind][:, None]], axis=1)
        coef = after(coef, waits)
        hop = None
        if planar:
            hop = {0: (1, packs[2:3]), 1: (2, carried), 2: (1, packs[3:4]), 3: (1, packs[4:5])}.get(at)
        (dpair, hidden, sums, grads, whole), found = expert_chunk(
            pieces_of(at), scaled, cot_rows, coef, hop, 4 + at
        )
        carried = carried + list(found) if at == 1 else list(found)
        dots[kind] = dots.get(kind, 0.0) + sums[:, 0]
        inner = inner + sums[:, 1]
        dpairs.append(dpair)
        hiddens.append(hidden)
        wholes.append(whole)
        now = (sums,)
        waits = ()
        if at < last or not planar:
            reduced.append(Reduced(grads))
        if planar and at == 0:
            waits = (reduced[0].pair,)
        elif planar and at == 1:
            first_pair = after(dpairs[0], reduced[0].second(now), (reduced[1].pair,))
            dscaled_early, last_piece = joint_back(
                [first_pair, dpair], wholes, 0, f32, hop=(3, carried[2:3]), number=9
            )
            gathered[2] = (packs[2], *carried[:2], carried[2], carried[3], last_piece)
            waits = (dscaled_early,)
        elif planar and at == 2:
            rest = hop_now((23, [after(carried[0], now, (reduced[2].pair,)), carried[1]]), 10)
            gathered[3] = (packs[3], *carried, *rest)
            waits = (rest[2],)
        elif planar and at == 3:
            third_pair = after(dpairs[2], (reduced[3].pair,))
            dscaled_early, *next_pieces = joint_back(
                [third_pair, dpair], wholes[2:], 0, f32, dscaled_early, hop=(2, carried), number=11
            )
            first_hidden = after(hiddens[0], reduced[1].second((dscaled_early,)))
            moe_early, last_piece = joint_back(
                [first_hidden] + hiddens[1:], wholes, 2, f32, hop=(3, next_pieces[:1]), number=12
            )
            gathered[4] = (packs[4], *carried, *next_pieces, last_piece)
            waits = (dscaled_early, moe_early)
    now = (sums,)
    if planar:
        waits = reduced[2].second(now) + reduced[0].third(now) + reduced[1].third(now)
    else:
        waits = ()
        for one in reduced:
            one.second()
            one.third()
    joined = 4 if planar else 0
    bases = ((dscaled_early,), (moe_early,)) if planar else ((), ())
    late_pairs, late_wholes, late_hiddens = dpairs[joined:], wholes[joined:], hiddens[joined:]
    late_pairs[-1] = after(late_pairs[-1], waits)
    dscaled_part = joint_back(late_pairs, late_wholes, 0, bf16, *bases[0], planar=planar)

    named = [jnp.where(members[local], dots[local], 0.0) for local in range(local_experts)]
    table = lax.all_gather(jnp.stack(named + [dots[None], inner]), "col", axis=0)
    dprob = table[:, :local_experts].reshape(experts, tokens).T
    dshared_gate, inner = jnp.sum(table[:, local_experts], axis=0), jnp.sum(table[:, local_experts + 1], axis=0)
    dlogits = router_probs * (dprob - jnp.sum(dprob * router_probs, axis=1, keepdims=True))
    dslogit = dshared_gate * shared_gate * (1.0 - shared_gate)
    dboth = jnp.concatenate([dlogits, dslogit[:, None]], axis=1)
    inner = inner + jnp.sum(dboth * both_logits, axis=1)
    dboth = scale_b * dboth
    parts = split_three(dboth)
    router_rows = lax.dynamic_slice_in_dim(router_full, col_id * share, share, 0)
    back_term = mm_nt(jnp.concatenate(parts, axis=1), jnp.concatenate([router_rows] * 3, axis=1))
    damp = scale_b * scale_b * inner[:, None] / width
    step_inputs = [back_term, grad_output, stream, damp, gain_b[None]]
    if planar:
        (dstream, dscaled, last_grad), (dattn,), _ = plane_step(
            dscaled_part, dstream_step, step_inputs, 2, 1, 2, (), grads
        )
    else:
        dscaled_sum = lax.psum_scatter(dscaled_part, "col", scatter_dimension=1, tiled=True)
        dstream_low, dstream, dscaled = dstream_step(dscaled_sum.astype(f32), *step_inputs)
        dattn = lax.all_gather(dstream_low.astype(bf16), "col", axis=1, tiled=True)
    gain_b_grad = jnp.sum(dscaled * stream, axis=0)

    late_hiddens[-1] = after(late_hiddens[-1], (dattn,))
    moe_part = joint_back(late_hiddens, late_wholes, 2, bf16, *bases[1])
    moe_share = lax.psum_scatter(moe_part, "col", scatter_dimension=1, tiled=True).astype(f32)
    block_output = (stream + moe_share).astype(bf16)
    out_part = mm_tn(dattn, context).astype(bf16)
    dcontext = mm(dattn, out_full).astype(bf16)
    if planar:
        out_reduced = Reduced(out_part)
        dcontext = after(
            dcontext, reduced[3].second((dattn,)), reduced[2].third((dattn,)), (out_reduced.pair,)
        )
    router_left = after(jnp.concatenate(parts, axis=1), (dattn,))
    grad_router_part = mm_tn(router_left, scaled).reshape(3, experts + 1, width).sum(axis=0)
    grad_router_both = lax.psum_scatter(grad_router_part, "row", scatter_dimension=1, tiled=True)
    dqkv, inner_a = attend_backward(qkv, dcontext, lse, lengths, cosine, sine)
    if planar:
        dqkv = after(dqkv, reduced[3].third((inner_a,)), out_reduced.second((inner_a,)))
    inner_a = lax.psum(inner_a[:, 0], "col")[:, None]
    qkv_part = mm_tn(normed_a, dqkv).astype(bf16)
    if planar:
        dqkv = after(dqkv, out_reduced.third((qkv_part,)))
        dnormed_part = joint_back([dqkv], [qkv_full], 0, bf16, planar=True)
        dnormed_part = after(dnormed_part, (inner_a,))
        (dnormed_a, qkv_grad), _, _ = plane_step(
            dnormed_part, lambda total: (total,), [], 1, 0, 3, (), qkv_part
        )
        out_grad = out_reduced.result((dnormed_a,))
    else:
        dnormed_a = lax.psum_scatter(
            mm_nt(dqkv, qkv_full).astype(bf16), "col", scatter_dimension=1, tiled=True
        ).astype(f32)
        qkv_grad, out_grad = one_reduction(qkv_part), one_reduction(out_part)
    unit_grads = [one.result((dnormed_a,)) for one in reduced]
    if planar:
        unit_grads.append(last_grad)
    gain_a_share = input_gain.astype(f32)
    dinput = dstream + scale_a * gain_a_share * dnormed_a
    dinput = dinput - x_share * (scale_a * scale_a * inner_a / width)
    gain_a_grad = jnp.sum(dnormed_a * x_share * scale_a, axis=0)
    grad_gain_a, grad_gain_b = lax.psum((gain_a_grad, gain_b_grad), "row")

    qkv_grad = qkv_grad.reshape(rows_block, heads, 3, HEAD_DIM)
    grad_query, grad_key, grad_value = (
        qkv_grad[:, :, part].reshape(rows_block, head_width) for part in range(3)
    )
    def unpack(kind, which):
        found = []
        for (of, a, b), grad in zip(chunks, unit_grads):
            if of == kind:
                size = grad.shape[1] // 3
                part = grad[:, which * size : which * size + b - a]
                found.append((a, part.T if which == 2 else part))
        found = [part for _, part in sorted(found, key=lambda item: item[0])]
        return jnp.concatenate(found, axis=0 if which == 2 else 1)

    locals_ = range(local_experts)
    return (
        block_output,
        dinput.astype(bf16),
        grad_gain_a,
        grad_query,
        grad_key,
        grad_value,
        out_grad.T,
        grad_gain_b,
        grad_router_both[:experts].T,
        grad_router_both[experts],
        unpack(None, 0),
        unpack(None, 1),
        unpack(None, 2),
        jnp.stack([unpack(local, 0) for local in locals_]),
        jnp.stack([unpack(local, 1) for local in locals_]),
        jnp.stack([unpack(local, 2) for local in locals_]),
    )


def solution(mesh):
    return jax.shard_map(
        per_device,
        mesh=mesh,
        in_specs=(
            P("row", "col"),
            P(),
            P(),
            P("row", None),
            P("col"),
            P("row", "col"),
            P("row", "col"),
            P("row", "col"),
            P("col", "row"),
            P("col"),
            P("row", None),
            P("row"),
            P("row", "col"),
            P("row", "col"),
            P("col", "row"),
            P("col", "row", None),
            P("col", "row", None),
            P("col", None, "row"),
            P("row", "col"),
        ),
        out_specs=(
            P("row", "col"),
            P("row", "col"),
            P("col"),
            P("row", "col"),
            P("row", "col"),
            P("row", "col"),
            P("col", "row"),
            P("col"),
            P("row", None),
            P("row"),
            P("row", "col"),
            P("row", "col"),
            P("col", "row"),
            P("col", "row", None),
            P("col", "row", None),
            P("col", None, "row"),
        ),
        check_vma=False,
    )
```

```python
import functools
import math

import jax
import jax.numpy as jnp
from jax import lax
from jax.experimental import pallas as pl
from jax.experimental.pallas import tpu as pltpu
from jax.sharding import PartitionSpec as P

HEAD_DIM = 128
SEQ_LEN = 1024
QBLOCK = 256
TILE = 256
norm_eps = 1e-06
rope_base = 1000000.0
bf16 = jnp.bfloat16
f32 = jnp.float32


def mm(left, right):
    return jnp.dot(left, right, preferred_element_type=f32)


def mm_nt(left, right):
    return lax.dot_general(left, right, (((1,), (1,)), ((), ())), preferred_element_type=f32)


def mm_tn(left, right):
    return lax.dot_general(left, right, (((0,), (0,)), ((), ())), preferred_element_type=f32)


def rope_tables():
    positions = jnp.arange(SEQ_LEN).astype(f32)
    freqs = jnp.power(f32(rope_base), -jnp.arange(0, HEAD_DIM, 2).astype(f32) / HEAD_DIM)
    angles = positions[:, None] * freqs[None, :]
    cosine, sine = jnp.cos(angles), jnp.sin(angles)
    return (
        jnp.concatenate([cosine, cosine], axis=-1),
        jnp.concatenate([-sine, sine], axis=-1),
    )


def block_scores(rows, keys, start, length, scale):
    raw = mm_nt(rows, keys) * scale
    query_pos = start + lax.broadcasted_iota(jnp.int32, raw.shape, 0)
    key_pos = lax.broadcasted_iota(jnp.int32, raw.shape, 1)
    return jnp.where((key_pos <= query_pos) & (key_pos < length), raw, -1e30)


def attend_forward_kernel(length_ref, raw_ref, cos_ref, sin_ref, qkv_ref, context_ref, lse_ref):
    length = length_ref[pl.program_id(0)]
    scale = 1.0 / math.sqrt(HEAD_DIM)
    hd = HEAD_DIM
    for part in range(2):
        raw = raw_ref[:, part * hd : (part + 1) * hd]
        turned = raw * cos_ref[...] + pltpu.roll(raw, hd // 2, 1) * sin_ref[...]
        qkv_ref[:, part * hd : (part + 1) * hd] = turned.astype(bf16)
    qkv_ref[:, 2 * hd :] = raw_ref[:, 2 * hd :].astype(bf16)
    for at in range(0, SEQ_LEN, QBLOCK):
        seen = at + QBLOCK
        scores = block_scores(
            qkv_ref[at:seen, :hd], qkv_ref[:seen, hd : 2 * hd], at, length, scale
        )
        top = jnp.max(scores, axis=-1, keepdims=True)
        expo = jnp.exp(scores - top)
        total = jnp.sum(expo, axis=-1, keepdims=True)
        probs = (expo / total).astype(bf16)
        context_ref[at:seen, :] = mm(probs, qkv_ref[:seen, 2 * hd :]).astype(bf16)
        lse_ref[at:seen, :] = jnp.broadcast_to(top + jnp.log(total), (QBLOCK, hd))


def attend_forward(raw, lengths, cosine, sine):
    tokens, width = raw.shape
    heads = width // (3 * HEAD_DIM)
    slots = tokens // SEQ_LEN
    wide = pl.BlockSpec((SEQ_LEN, 3 * HEAD_DIM), lambda s, h, _: (s, h))
    one = pl.BlockSpec((SEQ_LEN, HEAD_DIM), lambda s, h, _: (s, h))
    table = pl.BlockSpec((SEQ_LEN, HEAD_DIM), lambda s, h, _: (0, 0))
    pairs = slots * heads * SEQ_LEN * SEQ_LEN
    return pl.pallas_call(
        attend_forward_kernel,
        grid_spec=pltpu.PrefetchScalarGridSpec(
            num_scalar_prefetch=1,
            grid=(slots, heads),
            in_specs=[wide, table, table],
            out_specs=[wide, one, one],
        ),
        out_shape=[
            jax.ShapeDtypeStruct((tokens, width), bf16),
            jax.ShapeDtypeStruct((tokens, heads * HEAD_DIM), bf16),
            jax.ShapeDtypeStruct((tokens, heads * HEAD_DIM), f32),
        ],
        cost_estimate=pl.CostEstimate(
            flops=3 * HEAD_DIM * pairs, bytes_accessed=8 * tokens * width, transcendentals=pairs
        ),
        name="attend_forward",
    )(lengths, raw, cosine, sine)


def attend_backward_kernel(
    length_ref, qkv_ref, dcontext_ref, lse_ref, cos_ref, sin_ref, dqkv_ref, inner_ref, dk_ref, dv_ref
):
    length = length_ref[pl.program_id(0)]
    scale = 1.0 / math.sqrt(HEAD_DIM)
    hd = HEAD_DIM
    @pl.when(pl.program_id(1) == 0)
    def _():
        inner_ref[...] = jnp.zeros_like(inner_ref)

    dk_ref[...] = jnp.zeros_like(dk_ref)
    dv_ref[...] = jnp.zeros_like(dv_ref)

    def turn_back(grad, rows):
        back = grad * cos_ref[rows, :] - pltpu.roll(grad, hd // 2, 1) * sin_ref[rows, :]
        return back.astype(bf16)

    for at in range(0, SEQ_LEN, QBLOCK):
        seen = at + QBLOCK
        rows = qkv_ref[at:seen, :hd]
        keys = qkv_ref[:seen, hd : 2 * hd]
        drows = dcontext_ref[at:seen, :]
        scores = block_scores(rows, keys, at, length, scale)
        probs = jnp.exp(scores - lse_ref[at:seen, :1])
        dv_ref[:seen, :] += mm_tn(probs.astype(bf16), drows)
        dprobs = mm_nt(drows, qkv_ref[:seen, 2 * hd :])
        dscore = probs * (dprobs - jnp.sum(dprobs * probs, axis=-1, keepdims=True))
        draw = (dscore * scale).astype(bf16)
        dquery = mm(draw, keys)
        dk_ref[:seen, :] += mm_tn(draw, rows)
        dqkv_ref[at:seen, :hd] = turn_back(dquery, slice(at, seen))
        inner_ref[at:seen, :] += jnp.sum(dquery * rows.astype(f32), axis=-1, keepdims=True)
    dkey, dvalue = dk_ref[...], dv_ref[...]
    dqkv_ref[:, hd : 2 * hd] = turn_back(dkey, slice(None))
    dqkv_ref[:, 2 * hd :] = dvalue.astype(bf16)
    inner_ref[...] += jnp.sum(
        dkey * qkv_ref[:, hd : 2 * hd].astype(f32) + dvalue * qkv_ref[:, 2 * hd :].astype(f32),
        axis=-1,
        keepdims=True,
    )


def attend_backward(qkv, dcontext, lse, lengths, cosine, sine):
    tokens, width = qkv.shape
    heads = width // (3 * HEAD_DIM)
    slots = tokens // SEQ_LEN
    wide = pl.BlockSpec((SEQ_LEN, 3 * HEAD_DIM), lambda s, h, _: (s, h))
    one = pl.BlockSpec((SEQ_LEN, HEAD_DIM), lambda s, h, _: (s, h))
    table = pl.BlockSpec((SEQ_LEN, HEAD_DIM), lambda s, h, _: (0, 0))
    pairs = slots * heads * SEQ_LEN * SEQ_LEN
    return pl.pallas_call(
        attend_backward_kernel,
        grid_spec=pltpu.PrefetchScalarGridSpec(
            num_scalar_prefetch=1,
            grid=(slots, heads),
            in_specs=[wide, one, one, table, table],
            out_specs=[wide, pl.BlockSpec((SEQ_LEN, 1), lambda s, h, _: (s, 0))],
            scratch_shapes=[pltpu.VMEM((SEQ_LEN, HEAD_DIM), f32)] * 2,
        ),
        out_shape=[
            jax.ShapeDtypeStruct((tokens, width), bf16),
            jax.ShapeDtypeStruct((tokens, 1), f32),
        ],
        cost_estimate=pl.CostEstimate(
            flops=8 * HEAD_DIM * pairs, bytes_accessed=8 * tokens * width, transcendentals=pairs
        ),
        name="attend_backward",
    )(lengths, qkv, dcontext, lse, cosine, sine)


PAIRS = [(0, 1), (1, 0), (2, 3), (3, 2)]
MIDDLE = [(1, 2), (2, 1)]
OUTWARD = [(1, 0), (2, 3)]
INWARD = [(0, 1), (3, 2)]


class Gathered:
    def __init__(self, part, *groups):
        self.part = part
        if lax.axis_size("row") != 4:
            self.pieces = (lax.all_gather(part, "row", axis=0, tiled=True),)
            return
        part = after(part, *groups)
        self.partner = lax.ppermute(part, "row", PAIRS)
        self.near_mid = lax.ppermute(part, "row", MIDDLE)
        self.pieces = None

    def second(self, *groups):
        if self.pieces is None:
            self.near_out = lax.ppermute(after(self.near_mid, *groups), "row", OUTWARD)
            self.far_mid = lax.ppermute(after(self.partner, *groups), "row", MIDDLE)
            return (self.partner, self.near_mid)
        return ()

    def third(self, *groups):
        if self.pieces is None:
            self.far_out = lax.ppermute(after(self.far_mid, *groups), "row", OUTWARD)
            self.pieces = (
                self.part, self.partner, self.near_mid, self.far_mid, self.near_out, self.far_out
            )
            return (self.far_mid, self.near_out)
        return ()


def places(z):
    pair = z // 2
    return z, z + 1 - 2 * lax.rem(z, 2), 2 - pair, 3 - 3 * pair


class RowGather:
    def __init__(self, packs, wholes, sems):
        self.packs, self.wholes, (self.send_sems, self.recv_sems) = packs, wholes, sems
        self.z = lax.axis_index("row")
        self.own, self.partner, self.near, self.far = places(self.z)
        self.across = 3 - self.z
        self.in_middle = (self.z == 1) | (self.z == 2)
        self.outside = jnp.logical_not(self.in_middle)

    def copy_of(self, kind, at, source, block, target):
        return pltpu.make_async_remote_copy(
            src_ref=source,
            dst_ref=self.wholes[at].at[block],
            send_sem=self.send_sems.at[kind, at],
            recv_sem=self.recv_sems.at[kind, at],
            device_id={"row": target},
            device_id_type=pl.DeviceIdType.MESH,
        )

    def swap(self, at):
        return self.copy_of(0, at, self.packs[at], self.own, self.partner)

    def swap_middle(self, at):
        return self.copy_of(1, at, self.packs[at], self.own, self.across)

    def second_middle(self, at):
        return self.copy_of(2, at, self.wholes[at].at[self.partner], self.partner, self.across)

    def hand_near(self, at):
        return self.copy_of(3, at, self.wholes[at].at[self.near], self.near, self.partner)

    def hand_far(self, at):
        return self.copy_of(4, at, self.wholes[at].at[self.far], self.far, self.partner)

    def greet(self, barrier):
        signal_to(barrier, {"row": self.partner})

        @pl.when(self.in_middle)
        def _():
            signal_to(barrier, {"row": self.across})
            pl.semaphore_wait(barrier, 2)

        @pl.when(self.outside)
        def _():
            pl.semaphore_wait(barrier, 1)

    def begin(self):
        for at in range(len(self.packs)):
            @pl.when(self.in_middle)
            def _():
                self.swap_middle(at).start()

            self.swap(at).start()

    def hand_on(self, at):
        @pl.when(self.in_middle)
        def _():
            self.swap_middle(at).wait_recv()
            self.hand_near(at).start()
            self.swap(at).wait_recv()
            self.second_middle(at).start()

    def hand_last(self, at):
        @pl.when(self.in_middle)
        def _():
            self.second_middle(at).wait_recv()
            self.hand_far(at).start()

    def finish(self):
        for at in range(len(self.packs)):
            @pl.when(self.in_middle)
            def _():
                for copy in (
                    self.swap,
                    self.swap_middle,
                    self.second_middle,
                    self.hand_near,
                    self.hand_far,
                ):
                    copy(at).wait_send()

            @pl.when(self.outside)
            def _():
                self.swap(at).wait()
                self.hand_near(at).wait_recv()
                self.hand_far(at).wait_recv()


class RowReduce:
    def __init__(self, grads, total, refs):
        self.grads, self.total = grads, total
        self.far_in, self.near_in, self.far_sum, self.near_sum, self.last = refs[:5]
        self.held, self.more, self.send_sems, self.recv_sems, self.local_sems = refs[5:]
        self.z = lax.axis_index("row")
        self.own, self.partner, self.near, self.far = places(self.z)
        self.across = 3 - self.z
        self.in_middle = (self.z == 1) | (self.z == 2)
        self.outside = jnp.logical_not(self.in_middle)

    def copy_of(self, kind, source, target, device):
        return pltpu.make_async_remote_copy(
            src_ref=source,
            dst_ref=target,
            send_sem=self.send_sems.at[kind],
            recv_sem=self.recv_sems.at[kind],
            device_id={"row": device},
            device_id_type=pl.DeviceIdType.MESH,
        )

    def send_far(self):
        return self.copy_of(0, self.grads.at[self.far], self.far_in, self.partner)

    def send_near(self):
        return self.copy_of(1, self.grads.at[self.near], self.near_in, self.partner)

    def cross_far(self):
        return self.copy_of(2, self.far_in, self.far_sum, self.across)

    def cross_near(self):
        return self.copy_of(3, self.near_in, self.near_sum, self.across)

    def swap_middle(self):
        return self.copy_of(4, self.far_sum, self.last, self.partner)

    def swap_outer(self):
        return self.copy_of(4, self.grads.at[self.partner], self.last, self.partner)

    def load(self, kind, block):
        target = self.more if kind % 2 else self.held
        return pltpu.make_async_copy(self.grads.at[block], target, self.local_sems.at[kind])

    def add(self, target, source):
        @pl.loop(0, target.shape[0], step=64)
        def _(at):
            tile = pl.ds(pl.multiple_of(at, 64), 64)
            target[tile, :] = (target[tile, :].astype(f32) + source[tile, :].astype(f32)).astype(bf16)

    def begin(self):
        @pl.when(self.outside)
        def _():
            self.send_far().start()
            self.send_near().start()
            self.swap_outer().start()
            self.load(3, self.own).start()

        @pl.when(self.in_middle)
        def _():
            self.load(0, self.far).start()
            self.load(1, self.near).start()

    def second_far(self):
        @pl.when(self.in_middle)
        def _():
            self.load(0, self.far).wait()
            self.send_far().wait_recv()
            self.add(self.far_in, self.held)
            self.cross_far().start()
            self.load(2, self.partner).start()

    def second_near(self):
        @pl.when(self.in_middle)
        def _():
            self.load(1, self.near).wait()
            self.send_near().wait_recv()
            self.add(self.near_in, self.more)
            self.cross_near().start()
            self.load(3, self.own).start()

    def third(self):
        @pl.when(self.in_middle)
        def _():
            self.load(2, self.partner).wait()
            self.cross_far().wait_recv()
            self.add(self.far_sum, self.held)
            self.swap_middle().start()

    def finish(self):
        self.load(3, self.own).wait()
        self.swap_outer().wait_recv()

        @pl.when(self.in_middle)
        def _():
            self.cross_near().wait_recv()

        @pl.loop(0, self.total.shape[0], step=64)
        def _(at):
            tile = pl.ds(pl.multiple_of(at, 64), 64)
            self.total[tile, :] = self.more[tile, :].astype(f32) + self.last[tile, :].astype(f32)

        @pl.when(self.in_middle)
        def _():
            @pl.loop(0, self.total.shape[0], step=64)
            def _(at):
                tile = pl.ds(pl.multiple_of(at, 64), 64)
                self.total[tile, :] += self.near_sum[tile, :].astype(f32)

            self.cross_far().wait_send()
            self.cross_near().wait_send()
            self.swap_middle().wait_send()

        @pl.when(self.outside)
        def _():
            self.send_far().wait_send()
            self.send_near().wait_send()
            self.swap_outer().wait_send()


class RowHop:
    def __init__(self, kind, given, found, sems):
        self.kind, self.given, self.found, (self.send_sems, self.recv_sems) = kind, given, found, sems
        self.z = lax.axis_index("row")
        self.partner, self.across = places(self.z)[1], 3 - self.z
        self.in_middle = (self.z == 1) | (self.z == 2)
        self.outside = jnp.logical_not(self.in_middle)

    def copy_of(self, at, source, target, device):
        return pltpu.make_async_remote_copy(
            src_ref=source,
            dst_ref=target,
            send_sem=self.send_sems.at[at],
            recv_sem=self.recv_sems.at[at],
            device_id={"row": device},
            device_id_type=pl.DeviceIdType.MESH,
        )

    def across_copy(self):
        if self.kind == 1:
            return self.copy_of(0, self.given[0], self.found[1], self.across)
        return self.copy_of(0, self.given[0], self.found[0], self.across)

    def outward_copy(self):
        if self.kind == 1:
            return self.copy_of(1, self.given[0], self.found[0], self.partner)
        if self.kind == 3:
            return self.copy_of(1, self.given[0], self.found[0], self.partner)
        return self.copy_of(1, self.given[1], self.found[1], self.partner)

    def last_copy(self):
        return self.copy_of(2, self.found[0], self.found[2], self.partner)

    def begin(self):
        barrier = pltpu.get_barrier_semaphore()
        signal_to(barrier, {"row": self.partner})

        @pl.when(self.in_middle)
        def _():
            signal_to(barrier, {"row": self.across})
            pl.semaphore_wait(barrier, 2)
            if self.kind != 3:
                self.across_copy().start()
            self.outward_copy().start()

        @pl.when(self.outside)
        def _():
            pl.semaphore_wait(barrier, 1)
            if self.kind == 1:
                self.outward_copy().start()

    def finish(self):
        @pl.when(self.in_middle)
        def _():
            if self.kind != 3:
                self.across_copy().wait()
            if self.kind == 23:
                self.last_copy().start()
            if self.kind == 1:
                self.outward_copy().wait()
            else:
                self.outward_copy().wait_send()
            if self.kind == 23:
                self.last_copy().wait_send()

        @pl.when(self.outside)
        def _():
            if self.kind == 1:
                self.outward_copy().wait()
            else:
                self.outward_copy().wait_recv()
            if self.kind == 23:
                self.last_copy().wait_recv()


HOP_COUNTS = {1: (1, 2), 2: (2, 2), 3: (1, 1), 23: (2, 3), None: (0, 0)}


def hop_parts(hop, number):
    if hop is None:
        return [], [], [], pltpu.CompilerParams()
    kind, given = hop
    shape = jax.ShapeDtypeStruct(given[0].shape, bf16)
    scratch = [pltpu.SemaphoreType.DMA((3,)), pltpu.SemaphoreType.DMA((3,))]
    params = pltpu.CompilerParams(collective_id=number, has_side_effects=True)
    return list(given), [shape] * HOP_COUNTS[kind][1], scratch, params


def hop_kernel(kind, *refs):
    given, found = HOP_COUNTS[kind]
    hop = RowHop(kind, refs[:given], refs[given : given + found], refs[given + found :])
    hop.begin()
    hop.finish()


def hop_now(hop, number):
    given, shapes, scratch, params = hop_parts(hop, number)
    anywhere = pl.BlockSpec(memory_space=pl.ANY)
    return pl.pallas_call(
        functools.partial(hop_kernel, hop[0]),
        in_specs=[anywhere] * len(given),
        out_specs=[anywhere] * len(shapes),
        out_shape=shapes,
        scratch_shapes=scratch,
        compiler_params=params,
        name="gather_hops",
    )(*given)


def signal_to(barrier, device):
    pl.semaphore_signal(barrier, inc=1, device_id=device, device_id_type=pl.DeviceIdType.MESH)


def gather_kernel(count, *refs):
    rows = RowGather(refs[:count], refs[count : 2 * count], refs[2 * count :])
    rows.greet(pltpu.get_barrier_semaphore())
    rows.begin()
    for at in range(count):
        rows.hand_on(at)
    for at in range(count):
        rows.hand_last(at)
    rows.finish()


PIECES = 4


def plane_kernel(pointwise, given, made, gather, count, reducing, *refs):
    p_ref, inputs = refs[0], refs[1 : 1 + given]
    at = 1 + given
    packs = refs[at : at + count]
    at += count
    grads = refs[at] if reducing else None
    at += reducing
    results = refs[at : at + made]
    at += made
    total_ref = refs[at] if reducing else None
    at += reducing
    whole_refs = refs[at : at + gather + count]
    at += gather + count
    mine, from_core, from_first, summed, from_second, shared, send_sems, recv_sems, local_sems = refs[
        at : at + 9
    ]
    out_ref = whole_refs[0] if gather else None
    me = lax.axis_index("col")
    core, x, y = lax.rem(me, 2), lax.rem(me // 2, 2), me // 4
    core_mate, x_mate, y_mate = me + 1 - 2 * core, me + 2 - 4 * x, me + 4 - 8 * y
    diagonal = x_mate + 4 - 8 * y
    size = mine.shape[3]
    share = mine.shape[4]
    barrier = pltpu.get_barrier_semaphore()
    for mate in (core_mate, x_mate, y_mate):
        signal_to(barrier, {"col": mate})
    rows, reduction = None, None
    if count or reducing:
        if count:
            rows = RowGather(packs, whole_refs[gather:], refs[at + 9 : at + 11])
            at += 2
        if reducing:
            reduction = RowReduce(grads, total_ref, refs[at + 9 : at + 19])
        chain = rows or reduction
        signal_to(barrier, {"row": chain.partner})

        @pl.when(chain.in_middle)
        def _():
            signal_to(barrier, {"row": chain.across})
            pl.semaphore_wait(barrier, 5)

        @pl.when(chain.outside)
        def _():
            pl.semaphore_wait(barrier, 4)

        if count:
            rows.begin()
        if reducing:
            reduction.begin()
    else:
        pl.semaphore_wait(barrier, 3)

    def remote(kind, i, source, target, mate):
        return pltpu.make_async_remote_copy(
            src_ref=source,
            dst_ref=target,
            send_sem=send_sems.at[kind, i],
            recv_sem=recv_sems.at[kind, i],
            device_id={"col": mate},
            device_id_type=pl.DeviceIdType.MESH,
        )

    def x_first(i):
        return i < PIECES // 2

    def span(i):
        return pl.ds(i * size, size)

    def core_copy(i):
        return remote(0, i, p_ref.at[:, :, 1 - core, span(i), :], from_core.at[i], core_mate)

    def load(i):
        return pltpu.make_async_copy(
            p_ref.at[:, :, core, span(i), :], mine.at[i], local_sems.at[0, i]
        )

    def first_copy(i):
        if x_first(i):
            return remote(1, i, mine.at[i, :, 1 - x], from_first.at[i], x_mate)
        return remote(1, i, mine.at[i, 1 - y], from_first.at[i], y_mate)

    def second_copy(i):
        if x_first(i):
            return remote(2, i, summed.at[i, 1 - y], from_second.at[i], y_mate)
        return remote(2, i, summed.at[i, 1 - x], from_second.at[i], x_mate)

    def columns(i, device):
        return out_ref.at[span(i), pl.ds(pl.multiple_of(device * share, share), share)]

    def spread(kind, i, mate):
        return remote(kind, i, shared.at[i], columns(i, me), mate)

    def keep(i):
        return pltpu.make_async_copy(shared.at[i], columns(i, me), local_sems.at[1, i])

    def pass_on(kind, i, device, mate):
        return remote(kind, i, columns(i, device), columns(i, device), mate)

    def forward(i):
        if x_first(i):
            return pass_on(6, i, y_mate, x_mate)
        return pass_on(6, i, x_mate, y_mate)

    order = [0, 2, 1, 3]
    for i in order:
        core_copy(i).start()
        load(i).start()
    for i in order:
        load(i).wait()
        core_copy(i).wait_recv()
        for a in range(2):
            for b in range(2):
                mine[i, a, b] = (mine[i, a, b].astype(f32) + from_core[i, a, b].astype(f32)).astype(bf16)
        first_copy(i).start()
    for i in order:
        first_copy(i).wait_recv()
        for a in range(2):
            kept = mine[i, a, x] if x_first(i) else mine[i, y, a]
            summed[i, a] = (kept.astype(f32) + from_first[i, a].astype(f32)).astype(bf16)
        second_copy(i).start()
    if count:
        for at in range(count):
            rows.hand_on(at)
    if reducing:
        reduction.second_far()
    for i in order:
        second_copy(i).wait_recv()
        total = summed[i, y if x_first(i) else x].astype(f32) + from_second[i].astype(f32)
        span_rows = slice(i * size, (i + 1) * size)
        values = pointwise(
            total, *[ref[span_rows, :] if ref.shape[0] > 8 else ref[...] for ref in inputs]
        )
        if gather:
            shared[i] = values[0].astype(bf16)
            values = values[1:]
        for ref, value in zip(results, values):
            ref[span_rows, :] = value
        if gather:
            spread(4, i, x_mate).start()
            spread(5, i, y_mate).start()
            spread(3, i, core_mate).start()
            keep(i).start()
    if count:
        rows.hand_last(0)
    if reducing and not gather:
        reduction.second_near()
    if gather:
        for i in order:
            spread(5 if x_first(i) else 4, i, y_mate).wait_recv()
            forward(i).start()
            pass_on(7, i, y_mate if x_first(i) else x_mate, core_mate).start()
        for i in order:
            spread(4 if x_first(i) else 5, i, x_mate).wait_recv()
            pass_on(8, i, x_mate if x_first(i) else y_mate, core_mate).start()
    if count:
        for at in range(1, count):
            rows.hand_last(at)
    if reducing and gather:
        reduction.second_near()
    if reducing:
        reduction.third()
    if gather:
        for i in order:
            forward(i).wait_recv()
            pass_on(9, i, diagonal, core_mate).start()
    for i in order:
        core_copy(i).wait_send()
        first_copy(i).wait_send()
        second_copy(i).wait_send()
        if gather:
            keep(i).wait()
            spread(3, i, core_mate).wait()
            spread(4, i, x_mate).wait_send()
            spread(5, i, y_mate).wait_send()
            forward(i).wait_send()
            for kind, device in (
                (7, y_mate if x_first(i) else x_mate),
                (8, x_mate if x_first(i) else y_mate),
                (9, diagonal),
            ):
                pass_on(kind, i, device, core_mate).wait()
    if count:
        rows.finish()
    if reducing:
        reduction.finish()


def plane_step(partial, pointwise, inputs, made, gather, number, packs=(), grads=None):
    tokens, share = partial.shape[3:]
    size = tokens // PIECES
    count = len(packs)
    reducing = 0 if grads is None else 1
    totals, more_scratch, given_grads = [], [], []
    if reducing:
        block, columns = grads.shape[0] // 4, grads.shape[1]
        given_grads = [grads.reshape(4, block, columns)]
        totals = [jax.ShapeDtypeStruct((block, columns), f32)]
        more_scratch = [pltpu.VMEM((block, columns), bf16)] * 7 + [
            pltpu.SemaphoreType.DMA((5,)),
            pltpu.SemaphoreType.DMA((5,)),
            pltpu.SemaphoreType.DMA((4,)),
        ]
    anywhere = pl.BlockSpec(memory_space=pl.ANY)
    vmem = pl.BlockSpec(memory_space=pltpu.VMEM)
    whole_shapes = [jax.ShapeDtypeStruct((tokens, 8 * share), bf16)] * gather + [
        jax.ShapeDtypeStruct((4,) + pack.shape, bf16) for pack in packs
    ]
    outs = pl.pallas_call(
        functools.partial(plane_kernel, pointwise, len(inputs), made, gather, count, reducing),
        in_specs=[anywhere] + [vmem] * len(inputs) + [anywhere] * (count + reducing),
        out_specs=[vmem] * (made + reducing) + [anywhere] * (gather + count),
        out_shape=[jax.ShapeDtypeStruct((tokens, share), f32)] * made + totals + whole_shapes,
        scratch_shapes=[
            pltpu.VMEM((PIECES, 2, 2, size, share), bf16),
            pltpu.VMEM((PIECES, 2, 2, size, share), bf16),
            pltpu.VMEM((PIECES, 2, size, share), bf16),
            pltpu.VMEM((PIECES, 2, size, share), bf16),
            pltpu.VMEM((PIECES, size, share), bf16),
            pltpu.VMEM((PIECES, size, share), bf16),
            pltpu.SemaphoreType.DMA((10, PIECES)),
            pltpu.SemaphoreType.DMA((10, PIECES)),
            pltpu.SemaphoreType.DMA((2, PIECES)),
        ]
        + [pltpu.SemaphoreType.DMA((5, count))] * (2 if count else 0)
        + more_scratch,
        compiler_params=pltpu.CompilerParams(collective_id=number, has_side_effects=True),
        cost_estimate=pl.CostEstimate(
            flops=60 * 10**9, bytes_accessed=32 * tokens * share, transcendentals=0
        ),
        name="plane_step",
    )(partial, *inputs, *packs, *given_grads)
    at = made + reducing
    wholes = [whole.reshape((4 * whole.shape[1],) + whole.shape[2:]) for whole in outs[at + gather :]]
    return outs[:at], outs[at : at + gather], wholes


def gather_now(packs, number):
    if lax.axis_size("row") != 4:
        return [lax.all_gather(pack, "row", axis=0, tiled=True) for pack in packs]
    count = len(packs)
    sent = sum(pack.size for pack in packs) * 2
    anywhere = pl.BlockSpec(memory_space=pl.ANY)
    wholes = pl.pallas_call(
        functools.partial(gather_kernel, count),
        in_specs=[anywhere] * count,
        out_specs=[anywhere] * count,
        out_shape=[jax.ShapeDtypeStruct((4,) + pack.shape, pack.dtype) for pack in packs],
        scratch_shapes=[pltpu.SemaphoreType.DMA((5, count)), pltpu.SemaphoreType.DMA((5, count))],
        compiler_params=pltpu.CompilerParams(collective_id=number, has_side_effects=True),
        cost_estimate=pl.CostEstimate(
            flops=6 * 9000 * sent, bytes_accessed=6 * sent, transcendentals=0
        ),
        name="gather_rows",
    )(*packs)
    return [whole.reshape((4 * whole.shape[1],) + whole.shape[2:]) for whole in wholes]


def join_rows(pieces):
    if len(pieces) == 1:
        return pieces[0]
    part = pieces[0]
    whole = jnp.zeros((4,) + part.shape, part.dtype)
    blocks = (part, pieces[1], pieces[2] + pieces[4], pieces[3] + pieces[5])
    for at, piece in zip(places(lax.axis_index("row")), blocks):
        whole = lax.dynamic_update_slice_in_dim(whole, piece[None], at, 0)
    return whole.reshape((4 * part.shape[0],) + part.shape[1:])


def put_own(whole, part):
    if lax.axis_size("row") != 4:
        return whole
    return lax.dynamic_update_slice_in_dim(
        whole, part, lax.axis_index("row") * part.shape[0], 0
    )


class Reduced:
    def __init__(self, grads):
        self.chained = lax.axis_size("row") == 4
        if not self.chained:
            self.total = lax.psum_scatter(grads, "row", scatter_dimension=0, tiled=True).astype(f32)
            return
        z = lax.axis_index("row")
        self.own, self.partner, _, _ = places(z)
        self.grads, self.size = grads, grads.shape[0] // 4
        self.pair = self.rows_of(grads, (1 - z // 2) * 2, 2)
        self.first = lax.ppermute(self.pair, "row", INWARD)

    def rows_of(self, value, at, count):
        return lax.dynamic_slice_in_dim(value, at * self.size, count * self.size, 0)

    def two(self, at, cut=slice(None)):
        mine = self.rows_of(self.grads, at, 1)[:, cut].astype(f32)
        return mine + self.rows_of(self.crossed, lax.rem(at, 2), 1)[:, cut].astype(f32)

    def second(self, *groups):
        if not self.chained:
            return ()
        first = after(self.first, *groups)
        value = (self.pair.astype(f32) + first.astype(f32)).astype(bf16)
        self.crossed = lax.ppermute(value, "row", MIDDLE)
        return (value,)

    def third(self, *groups):
        if not self.chained:
            return ()
        self.crossed = after(self.crossed, *groups)
        value = self.two(self.partner).astype(bf16)
        self.swapped = lax.ppermute(value, "row", PAIRS)
        return (value,)

    def result(self, *groups):
        if not self.chained:
            return lambda cut: self.total[:, cut]
        swapped = after(self.swapped, *groups)
        return lambda cut: self.two(self.own, cut) + swapped[:, cut].astype(f32)


def one_reduction(grads):
    one = Reduced(grads)
    one.second()
    one.third()
    return one.result()(slice(None))


def after(value, *groups):
    others = tuple(item for group in groups for item in group)
    return lax.optimization_barrier((value,) + others)[0] if others else value


def expert_kernel(size, steps, count, kind, *refs):
    pieces = refs[:count]
    (x_ref, cot_ref, x_cols, cot_cols, coef_ref) = refs[count : count + 5]
    taken, found = HOP_COUNTS[kind]
    at = count + 5 + taken
    (dpair_ref, hidden_ref, sums_ref, grads_ref, whole_ref) = refs[at : at + 5]
    weights, dpair, hidden, sems, out_sem = refs[at + 5 + found : at + 10 + found]
    step = pl.program_id(0)
    final = pl.num_programs(0) - 1
    if kind:
        hop = RowHop(
            kind, refs[count + 5 : at], refs[at + 5 : at + 5 + found], refs[at + 10 + found :]
        )

        @pl.when(step == 0)
        def _():
            hop.begin()

    write = pltpu.make_async_copy(weights, whole_ref, out_sem)

    @pl.when(step == 0)
    def _():
        if count == 1:
            copy = pltpu.make_async_copy(pieces[0], weights, sems.at[0])
            copy.start()
            copy.wait()
        elif count == 2:
            block = pieces[0].shape[0]

            def block_copy(back):
                at = pl.multiple_of(lax.rem(lax.axis_index("row") + back, 4) * block, block)
                source = pieces[1].at[pl.ds(at, block)] if back else pieces[0]
                return pltpu.make_async_copy(source, weights.at[pl.ds(at, block)], sems.at[back])

            for back in range(4):
                block_copy(back).start()
            for back in range(4):
                block_copy(back).wait()
        else:
            z = lax.axis_index("row")
            block = pieces[0].shape[0]

            def copy_of(piece, which):
                at = pl.multiple_of(places(z)[which] * block, block)
                return pltpu.make_async_copy(
                    piece, weights.at[pl.ds(at, block)], sems.at[which]
                )

            copy_of(pieces[0], 0).start()
            copy_of(pieces[1], 1).start()
            in_middle = (z == 1) | (z == 2)

            @pl.when(in_middle)
            def _():
                copy_of(pieces[2], 2).start()
                copy_of(pieces[3], 3).start()

            @pl.when(jnp.logical_not(in_middle))
            def _():
                copy_of(pieces[4], 2).start()
                copy_of(pieces[5], 3).start()

            for which in range(4):
                copy_of(pieces[which], which).wait()
        write.start()

    @pl.when(step < steps)
    def _():
        at = pl.multiple_of(step * TILE, TILE)
        rows, cots = x_ref[...], cot_ref[...]
        scale, weight = coef_ref[:, 0:1], coef_ref[:, 1:2]
        dots = jnp.zeros((TILE, 1), f32)
        inner = jnp.zeros((TILE, 1), f32)
        for a in range(0, size, TILE):
            b = min(a + TILE, size)
            gate = scale * mm(rows, weights[:, a:b])
            up = scale * mm(rows, weights[:, size + a : size + b])
            dhid = mm(cots, weights[:, 2 * size + a : 2 * size + b])
            sigma = jax.nn.sigmoid(gate)
            silu = gate * sigma
            hid = silu * up
            dots += jnp.sum(hid * dhid, axis=1, keepdims=True)
            dhid = weight * dhid
            dgate = dhid * up * sigma * (1.0 + gate * (1.0 - sigma))
            dup = dhid * silu
            inner += jnp.sum(dgate * gate + dup * up, axis=1, keepdims=True)
            for into, at_col, value in (
                ((hidden_ref, hidden), a, weight * hid),
                ((dpair_ref, dpair), a, scale * dgate),
                ((dpair_ref, dpair), size + a, scale * dup),
            ):
                value = value.astype(bf16)
                into[0][:, at_col : at_col + b - a] = value
                into[1][pl.ds(at, TILE), at_col : at_col + b - a] = value
        sums_ref[:, 0:1] = dots
        sums_ref[:, 1:2] = inner

    @pl.when(step >= steps)
    def _():
        for a in range(0, 2 * size, TILE):
            b = min(a + TILE, 2 * size)
            grads_ref[:, a:b] = mm_tn(x_cols[...], dpair[:, a:b]).astype(bf16)
        for a in range(0, size, TILE):
            b = min(a + TILE, size)
            grads_ref[:, 2 * size + a : 2 * size + b] = mm_tn(
                cot_cols[...], hidden[:, a:b]
            ).astype(bf16)

    @pl.when(step == final)
    def _():
        write.wait()
        if kind:
            hop.finish()


def expert_chunk(pieces, scaled, cots, coef, hop=None, number=None):
    tokens, width = scaled.shape
    size = pieces[0].shape[1] // 3
    steps, more_steps = tokens // TILE, width // TILE
    count = len(pieces)
    rows = lambda i: (jnp.minimum(i, steps - 1), 0)
    cols = lambda i: (0, jnp.maximum(i - steps, 0))
    down = lambda i: (jnp.maximum(i - steps, 0), 0)
    anywhere = pl.BlockSpec(memory_space=pl.ANY)
    more, more_shapes, more_scratch, params = hop_parts(hop, number)
    outs = pl.pallas_call(
        functools.partial(expert_kernel, size, steps, count, hop and hop[0]),
        grid_spec=pl.GridSpec(
            grid=(steps + more_steps,),
            in_specs=[pl.BlockSpec(memory_space=pl.ANY)] * count
            + [
                pl.BlockSpec((TILE, width), rows),
                pl.BlockSpec((TILE, width), rows),
                pl.BlockSpec((tokens, TILE), cols),
                pl.BlockSpec((tokens, TILE), cols),
                pl.BlockSpec((TILE, 2), rows),
            ]
            + [anywhere] * len(more),
            out_specs=[
                pl.BlockSpec((TILE, 2 * size), rows),
                pl.BlockSpec((TILE, size), rows),
                pl.BlockSpec((TILE, 2), rows),
                pl.BlockSpec((TILE, 3 * size), down),
                anywhere,
            ]
            + [anywhere] * len(more_shapes),
            scratch_shapes=[
                pltpu.VMEM((width, 3 * size), bf16),
                pltpu.VMEM((tokens, 2 * size), bf16),
                pltpu.VMEM((tokens, size), bf16),
                pltpu.SemaphoreType.DMA((4,)),
                pltpu.SemaphoreType.DMA,
            ]
            + more_scratch,
        ),
        out_shape=[
            jax.ShapeDtypeStruct((tokens, 2 * size), bf16),
            jax.ShapeDtypeStruct((tokens, size), bf16),
            jax.ShapeDtypeStruct((tokens, 2), f32),
            jax.ShapeDtypeStruct((width, 3 * size), bf16),
            jax.ShapeDtypeStruct((width, 3 * size), bf16),
        ]
        + more_shapes,
        compiler_params=params,
        cost_estimate=pl.CostEstimate(
            flops=12 * tokens * width * size,
            bytes_accessed=8 * tokens * width + 24 * width * size,
            transcendentals=tokens * size,
        ),
        name="expert_chunk",
    )(*pieces, scaled, cots, scaled, cots, coef, *more)
    return outs[:5], outs[5:]


def joint_kernel(count, based, planar, kind, *refs):
    taken, found = HOP_COUNTS[kind]
    at = 2 * count + based + taken
    out_ref = refs[at]
    if kind:
        hop = RowHop(kind, refs[at - taken : at], refs[at + 1 : at + 1 + found], refs[at + 1 + found :])

        @pl.when(pl.program_id(0) == 0)
        def _():
            hop.begin()

    for a in range(0, refs[count].shape[0], TILE):
        total = refs[2 * count][:, a : a + TILE] if based else None
        for left, weights in zip(refs[:count], refs[count : 2 * count]):
            part = mm_nt(left[...], weights[a : a + TILE, :])
            total = part if total is None else total + part
        if planar:
            at = a // TILE
            out_ref[at // 4, at // 2 % 2, at % 2] = total.astype(out_ref.dtype)
        else:
            out_ref[:, a : a + TILE] = total.astype(out_ref.dtype)
    if kind:
        @pl.when(pl.program_id(0) == pl.num_programs(0) - 1)
        def _():
            hop.finish()


def joint_back(lefts, weights, column, kind, *base, planar=False, hop=None, number=None):
    tokens, width = lefts[0].shape[0], weights[0].shape[0]
    row = lambda i: (i, 0)
    fixed = lambda i: (0, column)
    depth = sum(left.shape[1] for left in lefts)
    more, more_shapes, more_scratch, params = hop_parts(hop, number)
    anywhere = pl.BlockSpec(memory_space=pl.ANY)
    out_spec = pl.BlockSpec((TILE, width), row)
    if planar:
        out_spec = pl.BlockSpec((2, 2, 2, TILE, TILE), lambda i: (0, 0, 0, i, 0))
    outs = pl.pallas_call(
        functools.partial(joint_kernel, len(lefts), len(base), planar, hop and hop[0]),
        grid=(tokens // TILE,),
        in_specs=[pl.BlockSpec((TILE, left.shape[1]), row) for left in lefts]
        + [
            pl.BlockSpec((width, left.shape[1]), fixed, pipeline_mode=pl.Buffered(1))
            for left in lefts
        ]
        + [pl.BlockSpec((TILE, width), row)] * len(base)
        + [anywhere] * len(more),
        out_specs=[out_spec] + [anywhere] * len(more_shapes),
        out_shape=[
            jax.ShapeDtypeStruct((2, 2, 2, tokens, TILE) if planar else (tokens, width), kind)
        ]
        + more_shapes,
        scratch_shapes=more_scratch,
        compiler_params=params,
        cost_estimate=pl.CostEstimate(
            flops=2 * tokens * width * depth,
            bytes_accessed=2 * (tokens + width) * depth + 4 * tokens * width,
            transcendentals=0,
        ),
        name="joint_back",
    )(*lefts, *weights, *base, *more)
    return outs[0] if hop is None else outs


def split_three(values):
    high = values.astype(bf16)
    rest = values - high.astype(f32)
    middle = rest.astype(bf16)
    return high, middle, (rest - middle.astype(f32)).astype(bf16)


def cuts_of(width, sizes):
    cuts, at = [], 0
    for size in sizes:
        if at + size < width:
            cuts.append((at, at + size))
            at += size
    return cuts + [(at, width)]


def stream_step(total, rows, gain):
    stream = rows.astype(f32) + total
    return stream * gain, stream


def dstream_step(total, back, cots, stream, damp, gain):
    dscaled = back + total
    dstream = cots.astype(f32) + gain * dscaled - stream * damp
    return dstream, dstream, dscaled


def per_device(
    block_input,
    seq_lengths,
    slot_order,
    routes,
    input_gain,
    query_weight,
    key_weight,
    value_weight,
    output_weight,
    mlp_gain,
    router_weight,
    score_shared,
    gate_shared,
    up_shared,
    down_shared,
    gate_expert,
    up_expert,
    down_expert,
    grad_output,
):
    tokens, share = block_input.shape
    cols = lax.axis_size("col")
    col_id = lax.axis_index("col")
    row_id = lax.axis_index("row")
    width = share * cols
    slots = tokens // SEQ_LEN
    local_experts = gate_expert.shape[0]
    experts = router_weight.shape[1]
    head_width = query_weight.shape[1]
    heads = head_width // HEAD_DIM
    rows_block = query_weight.shape[0]
    lengths = lax.dynamic_slice_in_dim(seq_lengths[slot_order], row_id * slots, slots, 0)
    cosine, sine = rope_tables()

    def by_head(weight):
        return weight.reshape(rows_block, heads, 1, HEAD_DIM)

    qkv_pack = jnp.concatenate(
        [by_head(query_weight), by_head(key_weight), by_head(value_weight)], axis=2
    ).reshape(rows_block, 3 * head_width)
    router_pack = jnp.concatenate([router_weight, score_shared[:, None]], axis=1)
    router_pack = jnp.pad(router_pack, ((0, 0), (0, -router_pack.shape[1] % 128)))
    out_pack = jnp.concatenate([output_weight.T, router_pack], axis=1)
    (qkv_whole,) = gather_now([qkv_pack], 0)
    qkv_full = put_own(qkv_whole, qkv_pack)
    out_gathered = Gathered(out_pack, (qkv_whole,))
    out_gathered.second()
    out_gathered.third()
    out_weights = join_rows(out_gathered.pieces)
    out_full = out_weights[:, :head_width]
    router_full = out_weights[:, head_width : head_width + experts + 1]
    shared_cuts = [(None, a, b) for a, b in cuts_of(gate_shared.shape[1], (512,))]
    expert_cuts = [
        (local, a, b)
        for local in range(local_experts)
        for a, b in cuts_of(gate_expert.shape[2], (512, 512))
    ]
    chunks = shared_cuts[-1:] + expert_cuts[:-1] + shared_cuts[:-1] + expert_cuts[-1:]

    def pack(kind, a, b):
        if kind is None:
            parts = [gate_shared[:, a:b], up_shared[:, a:b], down_shared[a:b].T]
        else:
            parts = [gate_expert[kind, :, a:b], up_expert[kind, :, a:b], down_expert[kind, a:b].T]
        fill = -(b - a) % 128
        return jnp.concatenate([jnp.pad(part, ((0, 0), (0, fill))) for part in parts], axis=1)

    packs = [pack(*chunk) for chunk in chunks]
    chained = lax.axis_size("row") == 4
    planar = chained and cols == 8 and share == TILE
    gathered = {}
    gathered[0] = Gathered(packs[0], (qkv_whole,))

    gain_rows = jnp.pad(jnp.stack([input_gain, mlp_gain]), ((0, 14), (0, 0)))
    both_in = lax.all_gather(
        jnp.concatenate([block_input, gain_rows], axis=0), "col", axis=1, tiled=True
    )
    rows_in, gains = both_in[:tokens], both_in[tokens : tokens + 2].astype(f32)
    cot_rows = lax.all_gather(grad_output, "col", axis=1, tiled=True)
    rows_f = rows_in.astype(f32)
    scale_a = lax.rsqrt(jnp.mean(rows_f * rows_f, axis=-1, keepdims=True) + norm_eps)
    normed_a = (rows_f * scale_a * gains[0]).astype(bf16)
    raw = mm(normed_a, qkv_full)
    raw = after(raw, gathered[0].second())
    qkv, context, lse = attend_forward(raw, lengths, cosine, sine)
    context = after(context, gathered[0].third())
    x_share = block_input.astype(f32)
    gain_b = mlp_gain.astype(f32)
    if planar:
        attn_part = joint_back([context], [out_weights], 0, bf16, planar=True)
        attn_part = after(attn_part, (cot_rows,))
        (stream,), (scaled,), wholes_now = plane_step(
            attn_part, stream_step, [block_input, gain_b[None]], 1, 1, 1, packs[1:2]
        )
        gathered[1] = (packs[1], wholes_now[0])
    else:
        attn_part = mm_nt(context, out_full).astype(bf16)
        attn_sum = lax.psum_scatter(attn_part, "col", scatter_dimension=1, tiled=True)
        scaled_share, stream = stream_step(attn_sum.astype(f32), block_input, gain_b[None])
        scaled = lax.all_gather(scaled_share.astype(bf16), "col", axis=1, tiled=True)
    for at in range(1, 1 if planar else len(chunks)):
        if at not in gathered:
            gathered[at] = Gathered(packs[at], (scaled,))

    def pieces_of(at):
        return gathered[at] if isinstance(gathered[at], tuple) else gathered[at].pieces

    stream_f = scaled.astype(f32) / gains[1]
    scale_b = lax.rsqrt(jnp.mean(stream_f * stream_f, axis=1, keepdims=True) + norm_eps)

    both_logits = scale_b * mm(scaled, router_full)
    logits, slogit = both_logits[:, :experts], both_logits[:, experts]
    top = jnp.max(logits, axis=-1, keepdims=True)
    expo = jnp.exp(logits - top)
    router_probs = expo / jnp.sum(expo, axis=-1, keepdims=True)
    shared_gate = jax.nn.sigmoid(slogit)

    inner = jnp.zeros((tokens,), f32)
    dots = {}
    members, shares = {None: None}, {None: shared_gate}
    for local in range(local_experts):
        expert = col_id * local_experts + local
        members[local] = jnp.any(routes == expert, axis=1)
        column = lax.dynamic_index_in_dim(router_probs, expert, 1, False)
        shares[local] = jnp.where(members[local], column, 0.0)
    dpairs, hiddens, wholes, reduced = [], [], [], []
    last = len(chunks) - 1
    waits = ()
    if not planar:
        for at in range(1, len(chunks)):
            gathered[at].second()
            gathered[at].third()

    carried = []
    for at, (kind, a, b) in enumerate(chunks):
        coef = jnp.concatenate([scale_b, shares[kind][:, None]], axis=1)
        coef = after(coef, waits)
        hop = None
        if planar:
            hop = {0: (1, packs[2:3]), 1: (2, carried), 2: (1, packs[3:4]), 3: (1, packs[4:5])}.get(at)
        (dpair, hidden, sums, grads, whole), found = expert_chunk(
            pieces_of(at), scaled, cot_rows, coef, hop, 4 + at
        )
        carried = carried + list(found) if at == 1 else list(found)
        dots[kind] = dots.get(kind, 0.0) + sums[:, 0]
        inner = inner + sums[:, 1]
        dpairs.append(dpair)
        hiddens.append(hidden)
        wholes.append(whole)
        now = (sums,)
        waits = ()
        if at < last or not planar:
            reduced.append(Reduced(grads))
        if planar and at == 0:
            waits = (reduced[0].pair,)
        elif planar and at == 1:
            first_pair = after(dpairs[0], reduced[0].second(now), (reduced[1].pair,))
            dscaled_early, last_piece = joint_back(
                [first_pair, dpair], wholes, 0, f32, hop=(3, carried[2:3]), number=9
            )
            gathered[2] = (packs[2], *carried[:2], carried[2], carried[3], last_piece)
            waits = (dscaled_early,)
        elif planar and at == 2:
            rest = hop_now((23, [after(carried[0], now, (reduced[2].pair,)), carried[1]]), 10)
            gathered[3] = (packs[3], *carried, *rest)
            waits = (rest[2],)
        elif planar and at == 3:
            third_pair = after(dpairs[2], (reduced[3].pair,))
            dscaled_early, *next_pieces = joint_back(
                [third_pair, dpair], wholes[2:], 0, f32, dscaled_early, hop=(2, carried), number=11
            )
            first_hidden = after(
                hiddens[0], reduced[1].second((dscaled_early,)), reduced[2].second((dscaled_early,))
            )
            moe_early, last_piece = joint_back(
                [first_hidden] + hiddens[1:], wholes, 2, f32, hop=(3, next_pieces[:1]), number=12
            )
            gathered[4] = (packs[4], *carried, *next_pieces, last_piece)
            waits = (dscaled_early, moe_early)
    now = (sums,)
    if planar:
        waits = reduced[0].third(now)
    else:
        waits = ()
        for one in reduced:
            one.second()
            one.third()
    joined = 4 if planar else 0
    bases = ((dscaled_early,), (moe_early,)) if planar else ((), ())
    late_pairs, late_wholes, late_hiddens = dpairs[joined:], wholes[joined:], hiddens[joined:]
    late_pairs[-1] = after(late_pairs[-1], waits)
    dscaled_part = joint_back(late_pairs, late_wholes, 0, bf16, *bases[0], planar=planar)

    named = [jnp.where(members[local], dots[local], 0.0) for local in range(local_experts)]
    table = lax.all_gather(jnp.stack(named + [dots[None], inner]), "col", axis=0)
    dprob = table[:, :local_experts].reshape(experts, tokens).T
    dshared_gate, inner = jnp.sum(table[:, local_experts], axis=0), jnp.sum(table[:, local_experts + 1], axis=0)
    dlogits = router_probs * (dprob - jnp.sum(dprob * router_probs, axis=1, keepdims=True))
    dslogit = dshared_gate * shared_gate * (1.0 - shared_gate)
    dboth = jnp.concatenate([dlogits, dslogit[:, None]], axis=1)
    inner = inner + jnp.sum(dboth * both_logits, axis=1)
    dboth = scale_b * dboth
    parts = split_three(dboth)
    router_rows = lax.dynamic_slice_in_dim(router_full, col_id * share, share, 0)
    back_term = mm_nt(jnp.concatenate(parts, axis=1), jnp.concatenate([router_rows] * 3, axis=1))
    damp = scale_b * scale_b * inner[:, None] / width
    step_inputs = [back_term, grad_output, stream, damp, gain_b[None]]
    if planar:
        (dstream, dscaled, last_grad), (dattn,), _ = plane_step(
            dscaled_part, dstream_step, step_inputs, 2, 1, 2, (), grads
        )
    else:
        dscaled_sum = lax.psum_scatter(dscaled_part, "col", scatter_dimension=1, tiled=True)
        dstream_low, dstream, dscaled = dstream_step(dscaled_sum.astype(f32), *step_inputs)
        dattn = lax.all_gather(dstream_low.astype(bf16), "col", axis=1, tiled=True)
    gain_b_grad = jnp.sum(dscaled * stream, axis=0)

    late_hiddens[-1] = after(late_hiddens[-1], (dattn,))
    moe_part = joint_back(late_hiddens, late_wholes, 2, bf16, *bases[1])
    moe_share = lax.psum_scatter(moe_part, "col", scatter_dimension=1, tiled=True).astype(f32)
    block_output = (stream + moe_share).astype(bf16)
    out_part = mm_tn(dattn, context).astype(bf16)
    dcontext = mm(dattn, out_full).astype(bf16)
    if planar:
        out_reduced = Reduced(out_part)
        dcontext = after(
            dcontext,
            reduced[3].second((dattn,)),
            reduced[1].third((dattn,)),
            reduced[2].third((dattn,)),
            (out_reduced.pair,),
        )
    router_left = after(jnp.concatenate(parts, axis=1), (dattn,))
    grad_router_part = mm_tn(router_left, scaled).reshape(3, experts + 1, width).sum(axis=0)
    grad_router_both = lax.psum_scatter(grad_router_part, "row", scatter_dimension=1, tiled=True)
    dqkv, inner_a = attend_backward(qkv, dcontext, lse, lengths, cosine, sine)
    if planar:
        dqkv = after(dqkv, reduced[3].third((inner_a,)), out_reduced.second((inner_a,)))
    inner_a = lax.psum(inner_a[:, 0], "col")[:, None]
    qkv_part = mm_tn(normed_a, dqkv).astype(bf16)
    if planar:
        dqkv = after(dqkv, out_reduced.third((qkv_part,)))
        dnormed_part = joint_back([dqkv], [qkv_full], 0, bf16, planar=True)
        dnormed_part = after(dnormed_part, (inner_a,))
        (dnormed_a, qkv_grad), _, _ = plane_step(
            dnormed_part, lambda total: (total,), [], 1, 0, 3, (), qkv_part
        )
        out_grad = out_reduced.result((dnormed_a,))(slice(None))
    else:
        dnormed_a = lax.psum_scatter(
            mm_nt(dqkv, qkv_full).astype(bf16), "col", scatter_dimension=1, tiled=True
        ).astype(f32)
        qkv_grad, out_grad = one_reduction(qkv_part), one_reduction(out_part)
    unit_grads = [one.result((dnormed_a,)) for one in reduced]
    if planar:
        unit_grads.append(lambda cut: last_grad[:, cut])
    gain_a_share = input_gain.astype(f32)
    dinput = dstream + scale_a * gain_a_share * dnormed_a
    dinput = dinput - x_share * (scale_a * scale_a * inner_a / width)
    gain_a_grad = jnp.sum(dnormed_a * x_share * scale_a, axis=0)
    grad_gain_a, grad_gain_b = lax.psum((gain_a_grad, gain_b_grad), "row")

    qkv_grad = qkv_grad.reshape(rows_block, heads, 3, HEAD_DIM)
    grad_query, grad_key, grad_value = (
        qkv_grad[:, :, part].reshape(rows_block, head_width) for part in range(3)
    )
    def unpack(kind, which):
        found = []
        for (of, a, b), grad in zip(chunks, unit_grads):
            if of == kind:
                size = b - a + -(b - a) % 128
                part = grad(slice(which * size, which * size + b - a))
                found.append((a, part.T if which == 2 else part))
        found = [part for _, part in sorted(found, key=lambda item: item[0])]
        return jnp.concatenate(found, axis=0 if which == 2 else 1)

    locals_ = range(local_experts)
    return (
        block_output,
        dinput.astype(bf16),
        grad_gain_a,
        grad_query,
        grad_key,
        grad_value,
        out_grad.T,
        grad_gain_b,
        grad_router_both[:experts].T,
        grad_router_both[experts],
        unpack(None, 0),
        unpack(None, 1),
        unpack(None, 2),
        jnp.stack([unpack(local, 0) for local in locals_]),
        jnp.stack([unpack(local, 1) for local in locals_]),
        jnp.stack([unpack(local, 2) for local in locals_]),
    )


def solution(mesh):
    return jax.shard_map(
        per_device,
        mesh=mesh,
        in_specs=(
            P("row", "col"),
            P(),
            P(),
            P("row", None),
            P("col"),
            P("row", "col"),
            P("row", "col"),
            P("row", "col"),
            P("col", "row"),
            P("col"),
            P("row", None),
            P("row"),
            P("row", "col"),
            P("row", "col"),
            P("col", "row"),
            P("col", "row", None),
            P("col", "row", None),
            P("col", None, "row"),
            P("row", "col"),
        ),
        out_specs=(
            P("row", "col"),
            P("row", "col"),
            P("col"),
            P("row", "col"),
            P("row", "col"),
            P("row", "col"),
            P("col", "row"),
            P("col"),
            P("row", None),
            P("row"),
            P("row", "col"),
            P("row", "col"),
            P("col", "row"),
            P("col", "row", None),
            P("col", "row", None),
            P("col", None, "row"),
        ),
        check_vma=False,
    )
```

```python
import functools
import math

import jax
import jax.numpy as jnp
from jax import lax
from jax.experimental import pallas as pl
from jax.experimental.pallas import tpu as pltpu
from jax.sharding import PartitionSpec as P

HEAD_DIM = 128
SEQ_LEN = 1024
QBLOCK = 256
TILE = 256
norm_eps = 1e-06
rope_base = 1000000.0
bf16 = jnp.bfloat16
f32 = jnp.float32


def mm(left, right):
    return jnp.dot(left, right, preferred_element_type=f32)


def mm_nt(left, right):
    return lax.dot_general(left, right, (((1,), (1,)), ((), ())), preferred_element_type=f32)


def mm_tn(left, right):
    return lax.dot_general(left, right, (((0,), (0,)), ((), ())), preferred_element_type=f32)


def rope_tables():
    positions = jnp.arange(SEQ_LEN).astype(f32)
    freqs = jnp.power(f32(rope_base), -jnp.arange(0, HEAD_DIM, 2).astype(f32) / HEAD_DIM)
    angles = positions[:, None] * freqs[None, :]
    cosine, sine = jnp.cos(angles), jnp.sin(angles)
    return (
        jnp.concatenate([cosine, cosine], axis=-1),
        jnp.concatenate([-sine, sine], axis=-1),
    )


def block_scores(rows, keys, start, length, scale):
    raw = mm_nt(rows, keys) * scale
    query_pos = start + lax.broadcasted_iota(jnp.int32, raw.shape, 0)
    key_pos = lax.broadcasted_iota(jnp.int32, raw.shape, 1)
    return jnp.where((key_pos <= query_pos) & (key_pos < length), raw, -1e30)


def attend_forward_kernel(length_ref, raw_ref, cos_ref, sin_ref, qkv_ref, context_ref, lse_ref):
    length = length_ref[pl.program_id(0)]
    scale = 1.0 / math.sqrt(HEAD_DIM)
    hd = HEAD_DIM
    for part in range(2):
        raw = raw_ref[:, part * hd : (part + 1) * hd]
        turned = raw * cos_ref[...] + pltpu.roll(raw, hd // 2, 1) * sin_ref[...]
        qkv_ref[:, part * hd : (part + 1) * hd] = turned.astype(bf16)
    qkv_ref[:, 2 * hd :] = raw_ref[:, 2 * hd :].astype(bf16)
    for at in range(0, SEQ_LEN, QBLOCK):
        seen = at + QBLOCK
        scores = block_scores(
            qkv_ref[at:seen, :hd], qkv_ref[:seen, hd : 2 * hd], at, length, scale
        )
        top = jnp.max(scores, axis=-1, keepdims=True)
        expo = jnp.exp(scores - top)
        total = jnp.sum(expo, axis=-1, keepdims=True)
        probs = (expo / total).astype(bf16)
        context_ref[at:seen, :] = mm(probs, qkv_ref[:seen, 2 * hd :]).astype(bf16)
        lse_ref[at:seen, :] = jnp.broadcast_to(top + jnp.log(total), (QBLOCK, hd))


def attend_forward(raw, lengths, cosine, sine):
    tokens, width = raw.shape
    heads = width // (3 * HEAD_DIM)
    slots = tokens // SEQ_LEN
    wide = pl.BlockSpec((SEQ_LEN, 3 * HEAD_DIM), lambda s, h, _: (s, h))
    one = pl.BlockSpec((SEQ_LEN, HEAD_DIM), lambda s, h, _: (s, h))
    table = pl.BlockSpec((SEQ_LEN, HEAD_DIM), lambda s, h, _: (0, 0))
    pairs = slots * heads * SEQ_LEN * SEQ_LEN
    return pl.pallas_call(
        attend_forward_kernel,
        grid_spec=pltpu.PrefetchScalarGridSpec(
            num_scalar_prefetch=1,
            grid=(slots, heads),
            in_specs=[wide, table, table],
            out_specs=[wide, one, one],
        ),
        out_shape=[
            jax.ShapeDtypeStruct((tokens, width), bf16),
            jax.ShapeDtypeStruct((tokens, heads * HEAD_DIM), bf16),
            jax.ShapeDtypeStruct((tokens, heads * HEAD_DIM), f32),
        ],
        cost_estimate=pl.CostEstimate(
            flops=3 * HEAD_DIM * pairs, bytes_accessed=8 * tokens * width, transcendentals=pairs
        ),
        name="attend_forward",
    )(lengths, raw, cosine, sine)


def attend_backward_kernel(
    length_ref, qkv_ref, dcontext_ref, lse_ref, cos_ref, sin_ref, dqkv_ref, inner_ref, dk_ref, dv_ref
):
    length = length_ref[pl.program_id(0)]
    scale = 1.0 / math.sqrt(HEAD_DIM)
    hd = HEAD_DIM
    @pl.when(pl.program_id(1) == 0)
    def _():
        inner_ref[...] = jnp.zeros_like(inner_ref)

    dk_ref[...] = jnp.zeros_like(dk_ref)
    dv_ref[...] = jnp.zeros_like(dv_ref)

    def turn_back(grad, rows):
        back = grad * cos_ref[rows, :] - pltpu.roll(grad, hd // 2, 1) * sin_ref[rows, :]
        return back.astype(bf16)

    for at in range(0, SEQ_LEN, QBLOCK):
        seen = at + QBLOCK
        rows = qkv_ref[at:seen, :hd]
        keys = qkv_ref[:seen, hd : 2 * hd]
        drows = dcontext_ref[at:seen, :]
        scores = block_scores(rows, keys, at, length, scale)
        probs = jnp.exp(scores - lse_ref[at:seen, :1])
        dv_ref[:seen, :] += mm_tn(probs.astype(bf16), drows)
        dprobs = mm_nt(drows, qkv_ref[:seen, 2 * hd :])
        dscore = probs * (dprobs - jnp.sum(dprobs * probs, axis=-1, keepdims=True))
        draw = (dscore * scale).astype(bf16)
        dquery = mm(draw, keys)
        dk_ref[:seen, :] += mm_tn(draw, rows)
        dqkv_ref[at:seen, :hd] = turn_back(dquery, slice(at, seen))
        inner_ref[at:seen, :] += jnp.sum(dquery * rows.astype(f32), axis=-1, keepdims=True)
    dkey, dvalue = dk_ref[...], dv_ref[...]
    dqkv_ref[:, hd : 2 * hd] = turn_back(dkey, slice(None))
    dqkv_ref[:, 2 * hd :] = dvalue.astype(bf16)
    inner_ref[...] += jnp.sum(
        dkey * qkv_ref[:, hd : 2 * hd].astype(f32) + dvalue * qkv_ref[:, 2 * hd :].astype(f32),
        axis=-1,
        keepdims=True,
    )


def attend_backward(qkv, dcontext, lse, lengths, cosine, sine):
    tokens, width = qkv.shape
    heads = width // (3 * HEAD_DIM)
    slots = tokens // SEQ_LEN
    wide = pl.BlockSpec((SEQ_LEN, 3 * HEAD_DIM), lambda s, h, _: (s, h))
    one = pl.BlockSpec((SEQ_LEN, HEAD_DIM), lambda s, h, _: (s, h))
    table = pl.BlockSpec((SEQ_LEN, HEAD_DIM), lambda s, h, _: (0, 0))
    pairs = slots * heads * SEQ_LEN * SEQ_LEN
    return pl.pallas_call(
        attend_backward_kernel,
        grid_spec=pltpu.PrefetchScalarGridSpec(
            num_scalar_prefetch=1,
            grid=(slots, heads),
            in_specs=[wide, one, one, table, table],
            out_specs=[wide, pl.BlockSpec((SEQ_LEN, 1), lambda s, h, _: (s, 0))],
            scratch_shapes=[pltpu.VMEM((SEQ_LEN, HEAD_DIM), f32)] * 2,
        ),
        out_shape=[
            jax.ShapeDtypeStruct((tokens, width), bf16),
            jax.ShapeDtypeStruct((tokens, 1), f32),
        ],
        cost_estimate=pl.CostEstimate(
            flops=8 * HEAD_DIM * pairs, bytes_accessed=8 * tokens * width, transcendentals=pairs
        ),
        name="attend_backward",
    )(lengths, qkv, dcontext, lse, cosine, sine)


PAIRS = [(0, 1), (1, 0), (2, 3), (3, 2)]
MIDDLE = [(1, 2), (2, 1)]
OUTWARD = [(1, 0), (2, 3)]
INWARD = [(0, 1), (3, 2)]


class Gathered:
    def __init__(self, part, *groups):
        self.part = part
        if lax.axis_size("row") != 4:
            self.pieces = (lax.all_gather(part, "row", axis=0, tiled=True),)
            return
        part = after(part, *groups)
        self.partner = lax.ppermute(part, "row", PAIRS)
        self.near_mid = lax.ppermute(part, "row", MIDDLE)
        self.pieces = None

    def second(self, *groups):
        if self.pieces is None:
            self.near_out = lax.ppermute(after(self.near_mid, *groups), "row", OUTWARD)
            self.far_mid = lax.ppermute(after(self.partner, *groups), "row", MIDDLE)
            return (self.partner, self.near_mid)
        return ()

    def third(self, *groups):
        if self.pieces is None:
            self.far_out = lax.ppermute(after(self.far_mid, *groups), "row", OUTWARD)
            self.pieces = (
                self.part, self.partner, self.near_mid, self.far_mid, self.near_out, self.far_out
            )
            return (self.far_mid, self.near_out)
        return ()


def places(z):
    pair = z // 2
    return z, z + 1 - 2 * lax.rem(z, 2), 2 - pair, 3 - 3 * pair


class RowGather:
    def __init__(self, packs, wholes, sems):
        self.packs, self.wholes, (self.send_sems, self.recv_sems) = packs, wholes, sems
        self.z = lax.axis_index("row")
        self.own, self.partner, self.near, self.far = places(self.z)
        self.across = 3 - self.z
        self.in_middle = (self.z == 1) | (self.z == 2)
        self.outside = jnp.logical_not(self.in_middle)

    def copy_of(self, kind, at, source, block, target):
        return pltpu.make_async_remote_copy(
            src_ref=source,
            dst_ref=self.wholes[at].at[block],
            send_sem=self.send_sems.at[kind, at],
            recv_sem=self.recv_sems.at[kind, at],
            device_id={"row": target},
            device_id_type=pl.DeviceIdType.MESH,
        )

    def swap(self, at):
        return self.copy_of(0, at, self.packs[at], self.own, self.partner)

    def swap_middle(self, at):
        return self.copy_of(1, at, self.packs[at], self.own, self.across)

    def second_middle(self, at):
        return self.copy_of(2, at, self.wholes[at].at[self.partner], self.partner, self.across)

    def hand_near(self, at):
        return self.copy_of(3, at, self.wholes[at].at[self.near], self.near, self.partner)

    def hand_far(self, at):
        return self.copy_of(4, at, self.wholes[at].at[self.far], self.far, self.partner)

    def greet(self, barrier):
        signal_to(barrier, {"row": self.partner})

        @pl.when(self.in_middle)
        def _():
            signal_to(barrier, {"row": self.across})
            pl.semaphore_wait(barrier, 2)

        @pl.when(self.outside)
        def _():
            pl.semaphore_wait(barrier, 1)

    def begin(self):
        for at in range(len(self.packs)):
            @pl.when(self.in_middle)
            def _():
                self.swap_middle(at).start()

            self.swap(at).start()

    def hand_on(self, at):
        @pl.when(self.in_middle)
        def _():
            self.swap_middle(at).wait_recv()
            self.hand_near(at).start()
            self.swap(at).wait_recv()
            self.second_middle(at).start()

    def hand_last(self, at):
        @pl.when(self.in_middle)
        def _():
            self.second_middle(at).wait_recv()
            self.hand_far(at).start()

    def finish(self):
        for at in range(len(self.packs)):
            @pl.when(self.in_middle)
            def _():
                for copy in (
                    self.swap,
                    self.swap_middle,
                    self.second_middle,
                    self.hand_near,
                    self.hand_far,
                ):
                    copy(at).wait_send()

            @pl.when(self.outside)
            def _():
                self.swap(at).wait()
                self.hand_near(at).wait_recv()
                self.hand_far(at).wait_recv()


class RowReduce:
    def __init__(self, grads, total, refs):
        self.grads, self.total = grads, total
        self.far_in, self.near_in, self.far_sum, self.near_sum, self.last = refs[:5]
        self.held, self.more, self.send_sems, self.recv_sems, self.local_sems = refs[5:]
        self.z = lax.axis_index("row")
        self.own, self.partner, self.near, self.far = places(self.z)
        self.across = 3 - self.z
        self.in_middle = (self.z == 1) | (self.z == 2)
        self.outside = jnp.logical_not(self.in_middle)

    def copy_of(self, kind, source, target, device):
        return pltpu.make_async_remote_copy(
            src_ref=source,
            dst_ref=target,
            send_sem=self.send_sems.at[kind],
            recv_sem=self.recv_sems.at[kind],
            device_id={"row": device},
            device_id_type=pl.DeviceIdType.MESH,
        )

    def send_far(self):
        return self.copy_of(0, self.grads.at[self.far], self.far_in, self.partner)

    def send_near(self):
        return self.copy_of(1, self.grads.at[self.near], self.near_in, self.partner)

    def cross_far(self):
        return self.copy_of(2, self.far_in, self.far_sum, self.across)

    def cross_near(self):
        return self.copy_of(3, self.near_in, self.near_sum, self.across)

    def swap_middle(self):
        return self.copy_of(4, self.far_sum, self.last, self.partner)

    def swap_outer(self):
        return self.copy_of(4, self.grads.at[self.partner], self.last, self.partner)

    def load(self, kind, block):
        target = self.more if kind % 2 else self.held
        return pltpu.make_async_copy(self.grads.at[block], target, self.local_sems.at[kind])

    def add(self, target, source):
        @pl.loop(0, target.shape[0], step=64)
        def _(at):
            tile = pl.ds(pl.multiple_of(at, 64), 64)
            target[tile, :] = (target[tile, :].astype(f32) + source[tile, :].astype(f32)).astype(bf16)

    def begin(self):
        @pl.when(self.outside)
        def _():
            self.send_far().start()
            self.send_near().start()
            self.swap_outer().start()
            self.load(3, self.own).start()

        @pl.when(self.in_middle)
        def _():
            self.load(0, self.far).start()
            self.load(1, self.near).start()

    def second_far(self):
        @pl.when(self.in_middle)
        def _():
            self.load(0, self.far).wait()
            self.send_far().wait_recv()
            self.add(self.far_in, self.held)
            self.cross_far().start()
            self.load(2, self.partner).start()

    def second_near(self):
        @pl.when(self.in_middle)
        def _():
            self.load(1, self.near).wait()
            self.send_near().wait_recv()
            self.add(self.near_in, self.more)
            self.cross_near().start()
            self.load(3, self.own).start()

    def third(self):
        @pl.when(self.in_middle)
        def _():
            self.load(2, self.partner).wait()
            self.cross_far().wait_recv()
            self.add(self.far_sum, self.held)
            self.swap_middle().start()

    def finish(self):
        self.load(3, self.own).wait()
        self.swap_outer().wait_recv()

        @pl.when(self.in_middle)
        def _():
            self.cross_near().wait_recv()

        @pl.loop(0, self.total.shape[0], step=64)
        def _(at):
            tile = pl.ds(pl.multiple_of(at, 64), 64)
            self.total[tile, :] = self.more[tile, :].astype(f32) + self.last[tile, :].astype(f32)

        @pl.when(self.in_middle)
        def _():
            @pl.loop(0, self.total.shape[0], step=64)
            def _(at):
                tile = pl.ds(pl.multiple_of(at, 64), 64)
                self.total[tile, :] += self.near_sum[tile, :].astype(f32)

            self.cross_far().wait_send()
            self.cross_near().wait_send()
            self.swap_middle().wait_send()

        @pl.when(self.outside)
        def _():
            self.send_far().wait_send()
            self.send_near().wait_send()
            self.swap_outer().wait_send()


class RowHop:
    def __init__(self, kind, given, found, sems):
        self.kind, self.given, self.found, (self.send_sems, self.recv_sems) = kind, given, found, sems
        self.z = lax.axis_index("row")
        self.partner, self.across = places(self.z)[1], 3 - self.z
        self.in_middle = (self.z == 1) | (self.z == 2)
        self.outside = jnp.logical_not(self.in_middle)

    def copy_of(self, at, source, target, device):
        return pltpu.make_async_remote_copy(
            src_ref=source,
            dst_ref=target,
            send_sem=self.send_sems.at[at],
            recv_sem=self.recv_sems.at[at],
            device_id={"row": device},
            device_id_type=pl.DeviceIdType.MESH,
        )

    def across_copy(self):
        if self.kind == 1:
            return self.copy_of(0, self.given[0], self.found[1], self.across)
        return self.copy_of(0, self.given[0], self.found[0], self.across)

    def outward_copy(self):
        if self.kind == 1:
            return self.copy_of(1, self.given[0], self.found[0], self.partner)
        if self.kind == 3:
            return self.copy_of(1, self.given[0], self.found[0], self.partner)
        return self.copy_of(1, self.given[1], self.found[1], self.partner)

    def last_copy(self):
        return self.copy_of(2, self.found[0], self.found[2], self.partner)

    def begin(self):
        barrier = pltpu.get_barrier_semaphore()
        signal_to(barrier, {"row": self.partner})

        @pl.when(self.in_middle)
        def _():
            signal_to(barrier, {"row": self.across})
            pl.semaphore_wait(barrier, 2)
            if self.kind != 3:
                self.across_copy().start()
            self.outward_copy().start()

        @pl.when(self.outside)
        def _():
            pl.semaphore_wait(barrier, 1)
            if self.kind == 1:
                self.outward_copy().start()

    def finish(self):
        @pl.when(self.in_middle)
        def _():
            if self.kind != 3:
                self.across_copy().wait()
            if self.kind == 23:
                self.last_copy().start()
            if self.kind == 1:
                self.outward_copy().wait()
            else:
                self.outward_copy().wait_send()
            if self.kind == 23:
                self.last_copy().wait_send()

        @pl.when(self.outside)
        def _():
            if self.kind == 1:
                self.outward_copy().wait()
            else:
                self.outward_copy().wait_recv()
            if self.kind == 23:
                self.last_copy().wait_recv()


HOP_COUNTS = {1: (1, 2), 2: (2, 2), 3: (1, 1), 23: (2, 3), None: (0, 0)}


def hop_parts(hop, number):
    if hop is None:
        return [], [], [], pltpu.CompilerParams()
    kind, given = hop
    shape = jax.ShapeDtypeStruct(given[0].shape, bf16)
    scratch = [pltpu.SemaphoreType.DMA((3,)), pltpu.SemaphoreType.DMA((3,))]
    params = pltpu.CompilerParams(collective_id=number, has_side_effects=True)
    return list(given), [shape] * HOP_COUNTS[kind][1], scratch, params


def hop_kernel(kind, *refs):
    given, found = HOP_COUNTS[kind]
    hop = RowHop(kind, refs[:given], refs[given : given + found], refs[given + found :])
    hop.begin()
    hop.finish()


def hop_now(hop, number):
    given, shapes, scratch, params = hop_parts(hop, number)
    anywhere = pl.BlockSpec(memory_space=pl.ANY)
    return pl.pallas_call(
        functools.partial(hop_kernel, hop[0]),
        in_specs=[anywhere] * len(given),
        out_specs=[anywhere] * len(shapes),
        out_shape=shapes,
        scratch_shapes=scratch,
        compiler_params=params,
        name="gather_hops",
    )(*given)


def signal_to(barrier, device):
    pl.semaphore_signal(barrier, inc=1, device_id=device, device_id_type=pl.DeviceIdType.MESH)


def gather_kernel(count, *refs):
    rows = RowGather(refs[:count], refs[count : 2 * count], refs[2 * count :])
    rows.greet(pltpu.get_barrier_semaphore())
    rows.begin()
    for at in range(count):
        rows.hand_on(at)
    for at in range(count):
        rows.hand_last(at)
    rows.finish()


PIECES = 4


def plane_kernel(pointwise, given, made, gather, count, reducing, *refs):
    p_ref, inputs = refs[0], refs[1 : 1 + given]
    at = 1 + given
    packs = refs[at : at + count]
    at += count
    grads = refs[at] if reducing else None
    at += reducing
    results = refs[at : at + made]
    at += made
    total_ref = refs[at] if reducing else None
    at += reducing
    whole_refs = refs[at : at + gather + count]
    at += gather + count
    mine, from_core, from_first, summed, from_second, shared, send_sems, recv_sems, local_sems = refs[
        at : at + 9
    ]
    out_ref = whole_refs[0] if gather else None
    me = lax.axis_index("col")
    core, x, y = lax.rem(me, 2), lax.rem(me // 2, 2), me // 4
    core_mate, x_mate, y_mate = me + 1 - 2 * core, me + 2 - 4 * x, me + 4 - 8 * y
    diagonal = x_mate + 4 - 8 * y
    size = mine.shape[3]
    share = mine.shape[4]
    barrier = pltpu.get_barrier_semaphore()
    for mate in (core_mate, x_mate, y_mate):
        signal_to(barrier, {"col": mate})
    rows, reduction = None, None
    if count or reducing:
        if count:
            rows = RowGather(packs, whole_refs[gather:], refs[at + 9 : at + 11])
            at += 2
        if reducing:
            reduction = RowReduce(grads, total_ref, refs[at + 9 : at + 19])
        chain = rows or reduction
        signal_to(barrier, {"row": chain.partner})

        @pl.when(chain.in_middle)
        def _():
            signal_to(barrier, {"row": chain.across})
            pl.semaphore_wait(barrier, 5)

        @pl.when(chain.outside)
        def _():
            pl.semaphore_wait(barrier, 4)

        if count:
            rows.begin()
        if reducing:
            reduction.begin()
    else:
        pl.semaphore_wait(barrier, 3)

    def remote(kind, i, source, target, mate):
        return pltpu.make_async_remote_copy(
            src_ref=source,
            dst_ref=target,
            send_sem=send_sems.at[kind, i],
            recv_sem=recv_sems.at[kind, i],
            device_id={"col": mate},
            device_id_type=pl.DeviceIdType.MESH,
        )

    def x_first(i):
        return i < PIECES // 2

    def span(i):
        return pl.ds(i * size, size)

    def core_copy(i):
        return remote(0, i, p_ref.at[:, :, 1 - core, span(i), :], from_core.at[i], core_mate)

    def load(i):
        return pltpu.make_async_copy(
            p_ref.at[:, :, core, span(i), :], mine.at[i], local_sems.at[0, i]
        )

    def first_copy(i):
        if x_first(i):
            return remote(1, i, mine.at[i, :, 1 - x], from_first.at[i], x_mate)
        return remote(1, i, mine.at[i, 1 - y], from_first.at[i], y_mate)

    def second_copy(i):
        if x_first(i):
            return remote(2, i, summed.at[i, 1 - y], from_second.at[i], y_mate)
        return remote(2, i, summed.at[i, 1 - x], from_second.at[i], x_mate)

    def columns(i, device):
        return out_ref.at[span(i), pl.ds(pl.multiple_of(device * share, share), share)]

    def spread(kind, i, mate):
        return remote(kind, i, shared.at[i], columns(i, me), mate)

    def keep(i):
        return pltpu.make_async_copy(shared.at[i], columns(i, me), local_sems.at[1, i])

    def pass_on(kind, i, device, mate):
        return remote(kind, i, columns(i, device), columns(i, device), mate)

    def forward(i):
        if x_first(i):
            return pass_on(6, i, y_mate, x_mate)
        return pass_on(6, i, x_mate, y_mate)

    order = [0, 2, 1, 3]
    for i in order:
        core_copy(i).start()
        load(i).start()
    for i in order:
        load(i).wait()
        core_copy(i).wait_recv()
        for a in range(2):
            for b in range(2):
                mine[i, a, b] = (mine[i, a, b].astype(f32) + from_core[i, a, b].astype(f32)).astype(bf16)
        first_copy(i).start()
    for i in order:
        first_copy(i).wait_recv()
        for a in range(2):
            kept = mine[i, a, x] if x_first(i) else mine[i, y, a]
            summed[i, a] = (kept.astype(f32) + from_first[i, a].astype(f32)).astype(bf16)
        second_copy(i).start()
    if count:
        for at in range(count):
            rows.hand_on(at)
    if reducing:
        reduction.second_far()
    for i in order:
        second_copy(i).wait_recv()
        total = summed[i, y if x_first(i) else x].astype(f32) + from_second[i].astype(f32)
        span_rows = slice(i * size, (i + 1) * size)
        values = pointwise(
            total, *[ref[span_rows, :] if ref.shape[0] > 8 else ref[...] for ref in inputs]
        )
        if gather:
            shared[i] = values[0].astype(bf16)
            values = values[1:]
        for ref, value in zip(results, values):
            ref[span_rows, :] = value
        if gather:
            spread(4, i, x_mate).start()
            spread(5, i, y_mate).start()
            spread(3, i, core_mate).start()
            keep(i).start()
    if count:
        rows.hand_last(0)
    if reducing and not gather:
        reduction.second_near()
    if gather:
        for i in order:
            spread(5 if x_first(i) else 4, i, y_mate).wait_recv()
            forward(i).start()
            pass_on(7, i, y_mate if x_first(i) else x_mate, core_mate).start()
        for i in order:
            spread(4 if x_first(i) else 5, i, x_mate).wait_recv()
            pass_on(8, i, x_mate if x_first(i) else y_mate, core_mate).start()
    if count:
        for at in range(1, count):
            rows.hand_last(at)
    if reducing and gather:
        reduction.second_near()
    if reducing:
        reduction.third()
    if gather:
        for i in order:
            forward(i).wait_recv()
            pass_on(9, i, diagonal, core_mate).start()
    for i in order:
        core_copy(i).wait_send()
        first_copy(i).wait_send()
        second_copy(i).wait_send()
        if gather:
            keep(i).wait()
            spread(3, i, core_mate).wait()
            spread(4, i, x_mate).wait_send()
            spread(5, i, y_mate).wait_send()
            forward(i).wait_send()
            for kind, device in (
                (7, y_mate if x_first(i) else x_mate),
                (8, x_mate if x_first(i) else y_mate),
                (9, diagonal),
            ):
                pass_on(kind, i, device, core_mate).wait()
    if count:
        rows.finish()
    if reducing:
        reduction.finish()


def plane_step(partial, pointwise, inputs, made, gather, number, packs=(), grads=None):
    tokens, share = partial.shape[3:]
    size = tokens // PIECES
    count = len(packs)
    reducing = 0 if grads is None else 1
    totals, more_scratch, given_grads = [], [], []
    if reducing:
        block, columns = grads.shape[0] // 4, grads.shape[1]
        given_grads = [grads.reshape(4, block, columns)]
        totals = [jax.ShapeDtypeStruct((block, columns), f32)]
        more_scratch = [pltpu.VMEM((block, columns), bf16)] * 7 + [
            pltpu.SemaphoreType.DMA((5,)),
            pltpu.SemaphoreType.DMA((5,)),
            pltpu.SemaphoreType.DMA((4,)),
        ]
    anywhere = pl.BlockSpec(memory_space=pl.ANY)
    vmem = pl.BlockSpec(memory_space=pltpu.VMEM)
    whole_shapes = [jax.ShapeDtypeStruct((tokens, 8 * share), bf16)] * gather + [
        jax.ShapeDtypeStruct((4,) + pack.shape, bf16) for pack in packs
    ]
    outs = pl.pallas_call(
        functools.partial(plane_kernel, pointwise, len(inputs), made, gather, count, reducing),
        in_specs=[anywhere] + [vmem] * len(inputs) + [anywhere] * (count + reducing),
        out_specs=[vmem] * (made + reducing) + [anywhere] * (gather + count),
        out_shape=[jax.ShapeDtypeStruct((tokens, share), f32)] * made + totals + whole_shapes,
        scratch_shapes=[
            pltpu.VMEM((PIECES, 2, 2, size, share), bf16),
            pltpu.VMEM((PIECES, 2, 2, size, share), bf16),
            pltpu.VMEM((PIECES, 2, size, share), bf16),
            pltpu.VMEM((PIECES, 2, size, share), bf16),
            pltpu.VMEM((PIECES, size, share), bf16),
            pltpu.VMEM((PIECES, size, share), bf16),
            pltpu.SemaphoreType.DMA((10, PIECES)),
            pltpu.SemaphoreType.DMA((10, PIECES)),
            pltpu.SemaphoreType.DMA((2, PIECES)),
        ]
        + [pltpu.SemaphoreType.DMA((5, count))] * (2 if count else 0)
        + more_scratch,
        compiler_params=pltpu.CompilerParams(collective_id=number, has_side_effects=True),
        cost_estimate=pl.CostEstimate(
            flops=60 * 10**9, bytes_accessed=32 * tokens * share, transcendentals=0
        ),
        name="plane_step",
    )(partial, *inputs, *packs, *given_grads)
    at = made + reducing
    wholes = [whole.reshape((4 * whole.shape[1],) + whole.shape[2:]) for whole in outs[at + gather :]]
    return outs[:at], outs[at : at + gather], wholes


def gather_now(packs, number):
    if lax.axis_size("row") != 4:
        return [lax.all_gather(pack, "row", axis=0, tiled=True) for pack in packs]
    count = len(packs)
    sent = sum(pack.size for pack in packs) * 2
    anywhere = pl.BlockSpec(memory_space=pl.ANY)
    wholes = pl.pallas_call(
        functools.partial(gather_kernel, count),
        in_specs=[anywhere] * count,
        out_specs=[anywhere] * count,
        out_shape=[jax.ShapeDtypeStruct((4,) + pack.shape, pack.dtype) for pack in packs],
        scratch_shapes=[pltpu.SemaphoreType.DMA((5, count)), pltpu.SemaphoreType.DMA((5, count))],
        compiler_params=pltpu.CompilerParams(collective_id=number, has_side_effects=True),
        cost_estimate=pl.CostEstimate(
            flops=6 * 9000 * sent, bytes_accessed=6 * sent, transcendentals=0
        ),
        name="gather_rows",
    )(*packs)
    return [whole.reshape((4 * whole.shape[1],) + whole.shape[2:]) for whole in wholes]


def join_rows(pieces):
    if len(pieces) == 1:
        return pieces[0]
    part = pieces[0]
    whole = jnp.zeros((4,) + part.shape, part.dtype)
    blocks = (part, pieces[1], pieces[2] + pieces[4], pieces[3] + pieces[5])
    for at, piece in zip(places(lax.axis_index("row")), blocks):
        whole = lax.dynamic_update_slice_in_dim(whole, piece[None], at, 0)
    return whole.reshape((4 * part.shape[0],) + part.shape[1:])


def put_own(whole, part):
    if lax.axis_size("row") != 4:
        return whole
    return lax.dynamic_update_slice_in_dim(
        whole, part, lax.axis_index("row") * part.shape[0], 0
    )


class Reduced:
    def __init__(self, grads, halves=False):
        self.chained = lax.axis_size("row") == 4
        if not self.chained:
            self.total = lax.psum_scatter(grads, "row", scatter_dimension=0, tiled=True).astype(f32)
            return
        z = lax.axis_index("row")
        self.own, self.partner, _, _ = places(z)
        self.grads, self.size = grads, grads.shape[0] // 4
        self.pair = self.rows_of(grads, (1 - z // 2) * 2, 2)
        if halves:
            self.first = lax.ppermute(self.pair[: self.size], "row", INWARD)
        else:
            self.first = lax.ppermute(self.pair, "row", INWARD)

    def first_rest(self, *groups):
        rest = after(self.pair[self.size :], *groups)
        self.first = jnp.concatenate([self.first, lax.ppermute(rest, "row", INWARD)], axis=0)
        return (rest,)

    def rows_of(self, value, at, count):
        return lax.dynamic_slice_in_dim(value, at * self.size, count * self.size, 0)

    def two(self, at, cut=slice(None)):
        mine = self.rows_of(self.grads, at, 1)[:, cut].astype(f32)
        return mine + self.rows_of(self.crossed, lax.rem(at, 2), 1)[:, cut].astype(f32)

    def second(self, *groups):
        if not self.chained:
            return ()
        first = after(self.first, *groups)
        value = (self.pair.astype(f32) + first.astype(f32)).astype(bf16)
        self.crossed = lax.ppermute(value, "row", MIDDLE)
        return (value,)

    def third(self, *groups):
        if not self.chained:
            return ()
        self.crossed = after(self.crossed, *groups)
        value = self.two(self.partner).astype(bf16)
        self.swapped = lax.ppermute(value, "row", PAIRS)
        return (value,)

    def result(self, *groups):
        if not self.chained:
            return lambda cut: self.total[:, cut]
        swapped = after(self.swapped, *groups)
        return lambda cut: self.two(self.own, cut) + swapped[:, cut].astype(f32)


def one_reduction(grads):
    one = Reduced(grads)
    one.second()
    one.third()
    return one.result()(slice(None))


def after(value, *groups):
    others = tuple(item for group in groups for item in group)
    return lax.optimization_barrier((value,) + others)[0] if others else value


def expert_kernel(size, steps, count, kind, *refs):
    pieces = refs[:count]
    (x_ref, cot_ref, x_cols, cot_cols, coef_ref) = refs[count : count + 5]
    taken, found = HOP_COUNTS[kind]
    at = count + 5 + taken
    (dpair_ref, hidden_ref, sums_ref, grads_ref, whole_ref) = refs[at : at + 5]
    weights, dpair, hidden, sems, out_sem = refs[at + 5 + found : at + 10 + found]
    step = pl.program_id(0)
    final = pl.num_programs(0) - 1
    if kind:
        hop = RowHop(
            kind, refs[count + 5 : at], refs[at + 5 : at + 5 + found], refs[at + 10 + found :]
        )

        @pl.when(step == 0)
        def _():
            hop.begin()

    write = pltpu.make_async_copy(weights, whole_ref, out_sem)

    @pl.when(step == 0)
    def _():
        if count == 1:
            copy = pltpu.make_async_copy(pieces[0], weights, sems.at[0])
            copy.start()
            copy.wait()
        elif count == 2:
            block = pieces[0].shape[0]

            def block_copy(back):
                at = pl.multiple_of(lax.rem(lax.axis_index("row") + back, 4) * block, block)
                source = pieces[1].at[pl.ds(at, block)] if back else pieces[0]
                return pltpu.make_async_copy(source, weights.at[pl.ds(at, block)], sems.at[back])

            for back in range(4):
                block_copy(back).start()
            for back in range(4):
                block_copy(back).wait()
        else:
            z = lax.axis_index("row")
            block = pieces[0].shape[0]

            def copy_of(piece, which):
                at = pl.multiple_of(places(z)[which] * block, block)
                return pltpu.make_async_copy(
                    piece, weights.at[pl.ds(at, block)], sems.at[which]
                )

            copy_of(pieces[0], 0).start()
            copy_of(pieces[1], 1).start()
            in_middle = (z == 1) | (z == 2)

            @pl.when(in_middle)
            def _():
                copy_of(pieces[2], 2).start()
                copy_of(pieces[3], 3).start()

            @pl.when(jnp.logical_not(in_middle))
            def _():
                copy_of(pieces[4], 2).start()
                copy_of(pieces[5], 3).start()

            for which in range(4):
                copy_of(pieces[which], which).wait()
        write.start()

    @pl.when(step < steps)
    def _():
        at = pl.multiple_of(step * TILE, TILE)
        rows, cots = x_ref[...], cot_ref[...]
        scale, weight = coef_ref[:, 0:1], coef_ref[:, 1:2]
        dots = jnp.zeros((TILE, 1), f32)
        inner = jnp.zeros((TILE, 1), f32)
        for a in range(0, size, TILE):
            b = min(a + TILE, size)
            gate = scale * mm(rows, weights[:, a:b])
            up = scale * mm(rows, weights[:, size + a : size + b])
            dhid = mm(cots, weights[:, 2 * size + a : 2 * size + b])
            sigma = jax.nn.sigmoid(gate)
            silu = gate * sigma
            hid = silu * up
            dots += jnp.sum(hid * dhid, axis=1, keepdims=True)
            dhid = weight * dhid
            dgate = dhid * up * sigma * (1.0 + gate * (1.0 - sigma))
            dup = dhid * silu
            inner += jnp.sum(dgate * gate + dup * up, axis=1, keepdims=True)
            for into, at_col, value in (
                ((hidden_ref, hidden), a, weight * hid),
                ((dpair_ref, dpair), a, scale * dgate),
                ((dpair_ref, dpair), size + a, scale * dup),
            ):
                value = value.astype(bf16)
                into[0][:, at_col : at_col + b - a] = value
                into[1][pl.ds(at, TILE), at_col : at_col + b - a] = value
        sums_ref[:, 0:1] = dots
        sums_ref[:, 1:2] = inner

    @pl.when(step >= steps)
    def _():
        for a in range(0, 2 * size, TILE):
            b = min(a + TILE, 2 * size)
            grads_ref[:, a:b] = mm_tn(x_cols[...], dpair[:, a:b]).astype(bf16)
        for a in range(0, size, TILE):
            b = min(a + TILE, size)
            grads_ref[:, 2 * size + a : 2 * size + b] = mm_tn(
                cot_cols[...], hidden[:, a:b]
            ).astype(bf16)

    @pl.when(step == final)
    def _():
        write.wait()
        if kind:
            hop.finish()


def expert_chunk(pieces, scaled, cots, coef, hop=None, number=None):
    tokens, width = scaled.shape
    size = pieces[0].shape[1] // 3
    steps, more_steps = tokens // TILE, width // TILE
    count = len(pieces)
    rows = lambda i: (jnp.minimum(i, steps - 1), 0)
    cols = lambda i: (0, jnp.maximum(i - steps, 0))
    down = lambda i: (jnp.maximum(i - steps, 0), 0)
    anywhere = pl.BlockSpec(memory_space=pl.ANY)
    more, more_shapes, more_scratch, params = hop_parts(hop, number)
    outs = pl.pallas_call(
        functools.partial(expert_kernel, size, steps, count, hop and hop[0]),
        grid_spec=pl.GridSpec(
            grid=(steps + more_steps,),
            in_specs=[pl.BlockSpec(memory_space=pl.ANY)] * count
            + [
                pl.BlockSpec((TILE, width), rows),
                pl.BlockSpec((TILE, width), rows),
                pl.BlockSpec((tokens, TILE), cols),
                pl.BlockSpec((tokens, TILE), cols),
                pl.BlockSpec((TILE, 2), rows),
            ]
            + [anywhere] * len(more),
            out_specs=[
                pl.BlockSpec((TILE, 2 * size), rows),
                pl.BlockSpec((TILE, size), rows),
                pl.BlockSpec((TILE, 2), rows),
                pl.BlockSpec((TILE, 3 * size), down),
                anywhere,
            ]
            + [anywhere] * len(more_shapes),
            scratch_shapes=[
                pltpu.VMEM((width, 3 * size), bf16),
                pltpu.VMEM((tokens, 2 * size), bf16),
                pltpu.VMEM((tokens, size), bf16),
                pltpu.SemaphoreType.DMA((4,)),
                pltpu.SemaphoreType.DMA,
            ]
            + more_scratch,
        ),
        out_shape=[
            jax.ShapeDtypeStruct((tokens, 2 * size), bf16),
            jax.ShapeDtypeStruct((tokens, size), bf16),
            jax.ShapeDtypeStruct((tokens, 2), f32),
            jax.ShapeDtypeStruct((width, 3 * size), bf16),
            jax.ShapeDtypeStruct((width, 3 * size), bf16),
        ]
        + more_shapes,
        compiler_params=params,
        cost_estimate=pl.CostEstimate(
            flops=12 * tokens * width * size,
            bytes_accessed=8 * tokens * width + 24 * width * size,
            transcendentals=tokens * size,
        ),
        name="expert_chunk",
    )(*pieces, scaled, cots, scaled, cots, coef, *more)
    return outs[:5], outs[5:]


def joint_kernel(count, based, planar, kind, *refs):
    taken, found = HOP_COUNTS[kind]
    at = 2 * count + based + taken
    out_ref = refs[at]
    if kind:
        hop = RowHop(kind, refs[at - taken : at], refs[at + 1 : at + 1 + found], refs[at + 1 + found :])

        @pl.when(pl.program_id(0) == 0)
        def _():
            hop.begin()

    for a in range(0, refs[count].shape[0], TILE):
        total = refs[2 * count][:, a : a + TILE].astype(f32) if based else None
        for left, weights in zip(refs[:count], refs[count : 2 * count]):
            part = mm_nt(left[...], weights[a : a + TILE, :])
            total = part if total is None else total + part
        if planar:
            at = a // TILE
            out_ref[at // 4, at // 2 % 2, at % 2] = total.astype(out_ref.dtype)
        else:
            out_ref[:, a : a + TILE] = total.astype(out_ref.dtype)
    if kind:
        @pl.when(pl.program_id(0) == pl.num_programs(0) - 1)
        def _():
            hop.finish()


def joint_back(lefts, weights, column, kind, *base, planar=False, hop=None, number=None):
    tokens, width = lefts[0].shape[0], weights[0].shape[0]
    row = lambda i: (i, 0)
    fixed = lambda i: (0, column)
    depth = sum(left.shape[1] for left in lefts)
    more, more_shapes, more_scratch, params = hop_parts(hop, number)
    anywhere = pl.BlockSpec(memory_space=pl.ANY)
    out_spec = pl.BlockSpec((TILE, width), row)
    if planar:
        out_spec = pl.BlockSpec((2, 2, 2, TILE, TILE), lambda i: (0, 0, 0, i, 0))
    outs = pl.pallas_call(
        functools.partial(joint_kernel, len(lefts), len(base), planar, hop and hop[0]),
        grid=(tokens // TILE,),
        in_specs=[pl.BlockSpec((TILE, left.shape[1]), row) for left in lefts]
        + [
            pl.BlockSpec((width, left.shape[1]), fixed, pipeline_mode=pl.Buffered(1))
            for left in lefts
        ]
        + [pl.BlockSpec((TILE, width), row)] * len(base)
        + [anywhere] * len(more),
        out_specs=[out_spec] + [anywhere] * len(more_shapes),
        out_shape=[
            jax.ShapeDtypeStruct((2, 2, 2, tokens, TILE) if planar else (tokens, width), kind)
        ]
        + more_shapes,
        scratch_shapes=more_scratch,
        compiler_params=params,
        cost_estimate=pl.CostEstimate(
            flops=2 * tokens * width * depth,
            bytes_accessed=2 * (tokens + width) * depth + 4 * tokens * width,
            transcendentals=0,
        ),
        name="joint_back",
    )(*lefts, *weights, *base, *more)
    return outs[0] if hop is None else outs


def split_three(values):
    high = values.astype(bf16)
    rest = values - high.astype(f32)
    middle = rest.astype(bf16)
    return high, middle, (rest - middle.astype(f32)).astype(bf16)


def cuts_of(width, sizes):
    cuts, at = [], 0
    for size in sizes:
        if at + size < width:
            cuts.append((at, at + size))
            at += size
    return cuts + [(at, width)]


def stream_step(total, rows, gain):
    stream = rows.astype(f32) + total
    return stream * gain, stream


def dstream_step(total, back, cots, stream, damp, gain):
    dscaled = back + total
    dstream = cots.astype(f32) + gain * dscaled - stream * damp
    return dstream, dstream, dscaled


def per_device(
    block_input,
    seq_lengths,
    slot_order,
    routes,
    input_gain,
    query_weight,
    key_weight,
    value_weight,
    output_weight,
    mlp_gain,
    router_weight,
    score_shared,
    gate_shared,
    up_shared,
    down_shared,
    gate_expert,
    up_expert,
    down_expert,
    grad_output,
):
    tokens, share = block_input.shape
    cols = lax.axis_size("col")
    col_id = lax.axis_index("col")
    row_id = lax.axis_index("row")
    width = share * cols
    slots = tokens // SEQ_LEN
    local_experts = gate_expert.shape[0]
    experts = router_weight.shape[1]
    head_width = query_weight.shape[1]
    heads = head_width // HEAD_DIM
    rows_block = query_weight.shape[0]
    lengths = lax.dynamic_slice_in_dim(seq_lengths[slot_order], row_id * slots, slots, 0)
    cosine, sine = rope_tables()

    def by_head(weight):
        return weight.reshape(rows_block, heads, 1, HEAD_DIM)

    qkv_pack = jnp.concatenate(
        [by_head(query_weight), by_head(key_weight), by_head(value_weight)], axis=2
    ).reshape(rows_block, 3 * head_width)
    router_pack = jnp.concatenate([router_weight, score_shared[:, None]], axis=1)
    router_pack = jnp.pad(router_pack, ((0, 0), (0, -router_pack.shape[1] % 128)))
    out_pack = jnp.concatenate([output_weight.T, router_pack], axis=1)
    (qkv_whole,) = gather_now([qkv_pack], 0)
    qkv_full = put_own(qkv_whole, qkv_pack)
    out_gathered = Gathered(out_pack, (qkv_whole,))
    out_gathered.second()
    out_gathered.third()
    out_weights = join_rows(out_gathered.pieces)
    out_full = out_weights[:, :head_width]
    router_full = out_weights[:, head_width : head_width + experts + 1]
    shared_cuts = [(None, a, b) for a, b in cuts_of(gate_shared.shape[1], (512,))]
    expert_cuts = [
        (local, a, b)
        for local in range(local_experts)
        for a, b in cuts_of(gate_expert.shape[2], (512, 512))
    ]
    chunks = shared_cuts[-1:] + expert_cuts[:-1] + shared_cuts[:-1] + expert_cuts[-1:]

    def pack(kind, a, b):
        if kind is None:
            parts = [gate_shared[:, a:b], up_shared[:, a:b], down_shared[a:b].T]
        else:
            parts = [gate_expert[kind, :, a:b], up_expert[kind, :, a:b], down_expert[kind, a:b].T]
        fill = -(b - a) % 128
        return jnp.concatenate([jnp.pad(part, ((0, 0), (0, fill))) for part in parts], axis=1)

    packs = [pack(*chunk) for chunk in chunks]
    chained = lax.axis_size("row") == 4
    planar = chained and cols == 8 and share == TILE
    gathered = {}
    gathered[0] = Gathered(packs[0], (qkv_whole,))

    gain_rows = jnp.pad(jnp.stack([input_gain, mlp_gain]), ((0, 14), (0, 0)))
    both_in = lax.all_gather(
        jnp.concatenate([block_input, gain_rows], axis=0), "col", axis=1, tiled=True
    )
    rows_in, gains = both_in[:tokens], both_in[tokens : tokens + 2].astype(f32)
    cot_rows = lax.all_gather(grad_output, "col", axis=1, tiled=True)
    rows_f = rows_in.astype(f32)
    scale_a = lax.rsqrt(jnp.mean(rows_f * rows_f, axis=-1, keepdims=True) + norm_eps)
    normed_a = (rows_f * scale_a * gains[0]).astype(bf16)
    raw = mm(normed_a, qkv_full)
    raw = after(raw, gathered[0].second())
    qkv, context, lse = attend_forward(raw, lengths, cosine, sine)
    context = after(context, gathered[0].third())
    x_share = block_input.astype(f32)
    gain_b = mlp_gain.astype(f32)
    if planar:
        attn_part = joint_back([context], [out_weights], 0, bf16, planar=True)
        attn_part = after(attn_part, (cot_rows,))
        (stream,), (scaled,), wholes_now = plane_step(
            attn_part, stream_step, [block_input, gain_b[None]], 1, 1, 1, packs[1:2]
        )
        gathered[1] = (packs[1], wholes_now[0])
    else:
        attn_part = mm_nt(context, out_full).astype(bf16)
        attn_sum = lax.psum_scatter(attn_part, "col", scatter_dimension=1, tiled=True)
        scaled_share, stream = stream_step(attn_sum.astype(f32), block_input, gain_b[None])
        scaled = lax.all_gather(scaled_share.astype(bf16), "col", axis=1, tiled=True)
    for at in range(1, 1 if planar else len(chunks)):
        if at not in gathered:
            gathered[at] = Gathered(packs[at], (scaled,))

    def pieces_of(at):
        return gathered[at] if isinstance(gathered[at], tuple) else gathered[at].pieces

    stream_f = scaled.astype(f32) / gains[1]
    scale_b = lax.rsqrt(jnp.mean(stream_f * stream_f, axis=1, keepdims=True) + norm_eps)

    both_logits = scale_b * mm(scaled, router_full)
    logits, slogit = both_logits[:, :experts], both_logits[:, experts]
    top = jnp.max(logits, axis=-1, keepdims=True)
    expo = jnp.exp(logits - top)
    router_probs = expo / jnp.sum(expo, axis=-1, keepdims=True)
    shared_gate = jax.nn.sigmoid(slogit)

    inner = jnp.zeros((tokens,), f32)
    dots = {}
    members, shares = {None: None}, {None: shared_gate}
    for local in range(local_experts):
        expert = col_id * local_experts + local
        members[local] = jnp.any(routes == expert, axis=1)
        column = lax.dynamic_index_in_dim(router_probs, expert, 1, False)
        shares[local] = jnp.where(members[local], column, 0.0)
    dpairs, hiddens, wholes, reduced = [], [], [], []
    last = len(chunks) - 1
    waits = ()
    if not planar:
        for at in range(1, len(chunks)):
            gathered[at].second()
            gathered[at].third()

    carried = []
    for at, (kind, a, b) in enumerate(chunks):
        coef = jnp.concatenate([scale_b, shares[kind][:, None]], axis=1)
        coef = after(coef, waits)
        hop = None
        if planar:
            hop = {0: (1, packs[2:3]), 1: (2, carried), 2: (1, packs[3:4]), 3: (1, packs[4:5])}.get(at)
        (dpair, hidden, sums, grads, whole), found = expert_chunk(
            pieces_of(at), scaled, cot_rows, coef, hop, 4 + at
        )
        carried = carried + list(found) if at == 1 else list(found)
        dots[kind] = dots.get(kind, 0.0) + sums[:, 0]
        inner = inner + sums[:, 1]
        dpairs.append(dpair)
        hiddens.append(hidden)
        wholes.append(whole)
        now = (sums,)
        waits = ()
        if at < last or not planar:
            reduced.append(Reduced(grads, planar and at == 1))
        if planar and at == 0:
            waits = (reduced[0].pair,)
        elif planar and at == 1:
            first_pair = after(dpairs[0], reduced[0].second(now), (reduced[1].pair,))
            dscaled_early, last_piece = joint_back(
                [first_pair, dpair], wholes, 0, f32, hop=(3, carried[2:3]), number=9
            )
            gathered[2] = (packs[2], *carried[:2], carried[2], carried[3], last_piece)
            waits = (dscaled_early,)
        elif planar and at == 2:
            rest = hop_now((23, [after(carried[0], now, (reduced[2].pair,)), carried[1]]), 10)
            gathered[3] = (packs[3], *carried, *rest)
            waits = (rest[2],)
        elif planar and at == 3:
            third_pair = after(dpairs[2], reduced[1].first_rest(now), (reduced[3].pair,))
            dscaled_early, *next_pieces = joint_back(
                [third_pair, dpair], wholes[2:], 0, bf16, dscaled_early, hop=(2, carried), number=11
            )
            first_hidden = after(
                hiddens[0], reduced[1].second((dscaled_early,)), reduced[2].second((dscaled_early,))
            )
            moe_early, last_piece = joint_back(
                [first_hidden] + hiddens[1:], wholes, 2, bf16, hop=(3, next_pieces[:1]), number=12
            )
            gathered[4] = (packs[4], *carried, *next_pieces, last_piece)
            waits = (dscaled_early, moe_early)
    now = (sums,)
    if planar:
        waits = reduced[0].third(now)
    else:
        waits = ()
        for one in reduced:
            one.second()
            one.third()
    joined = 4 if planar else 0
    bases = ((dscaled_early,), (moe_early,)) if planar else ((), ())
    late_pairs, late_wholes, late_hiddens = dpairs[joined:], wholes[joined:], hiddens[joined:]
    late_pairs[-1] = after(late_pairs[-1], waits)
    dscaled_part = joint_back(late_pairs, late_wholes, 0, bf16, *bases[0], planar=planar)

    named = [jnp.where(members[local], dots[local], 0.0) for local in range(local_experts)]
    table = lax.all_gather(jnp.stack(named + [dots[None], inner]), "col", axis=0)
    dprob = table[:, :local_experts].reshape(experts, tokens).T
    dshared_gate, inner = jnp.sum(table[:, local_experts], axis=0), jnp.sum(table[:, local_experts + 1], axis=0)
    dlogits = router_probs * (dprob - jnp.sum(dprob * router_probs, axis=1, keepdims=True))
    dslogit = dshared_gate * shared_gate * (1.0 - shared_gate)
    dboth = jnp.concatenate([dlogits, dslogit[:, None]], axis=1)
    inner = inner + jnp.sum(dboth * both_logits, axis=1)
    dboth = scale_b * dboth
    parts = split_three(dboth)
    router_rows = lax.dynamic_slice_in_dim(router_full, col_id * share, share, 0)
    back_term = mm_nt(jnp.concatenate(parts, axis=1), jnp.concatenate([router_rows] * 3, axis=1))
    damp = scale_b * scale_b * inner[:, None] / width
    step_inputs = [back_term, grad_output, stream, damp, gain_b[None]]
    if planar:
        (dstream, dscaled, last_grad), (dattn,), _ = plane_step(
            dscaled_part, dstream_step, step_inputs, 2, 1, 2, (), grads
        )
    else:
        dscaled_sum = lax.psum_scatter(dscaled_part, "col", scatter_dimension=1, tiled=True)
        dstream_low, dstream, dscaled = dstream_step(dscaled_sum.astype(f32), *step_inputs)
        dattn = lax.all_gather(dstream_low.astype(bf16), "col", axis=1, tiled=True)
    gain_b_grad = jnp.sum(dscaled * stream, axis=0)

    late_hiddens[-1] = after(late_hiddens[-1], (dattn,))
    moe_part = joint_back(late_hiddens, late_wholes, 2, bf16, *bases[1])
    moe_share = lax.psum_scatter(moe_part, "col", scatter_dimension=1, tiled=True).astype(f32)
    block_output = (stream + moe_share).astype(bf16)
    out_part = mm_tn(dattn, context).astype(bf16)
    dcontext = mm(dattn, out_full).astype(bf16)
    if planar:
        out_reduced = Reduced(out_part)
        dcontext = after(
            dcontext,
            reduced[3].second((dattn,)),
            reduced[1].third((dattn,)),
            reduced[2].third((dattn,)),
            (out_reduced.pair,),
        )
    router_left = after(jnp.concatenate(parts, axis=1), (dattn,))
    grad_router_part = mm_tn(router_left, scaled).reshape(3, experts + 1, width).sum(axis=0)
    grad_router_both = lax.psum_scatter(grad_router_part, "row", scatter_dimension=1, tiled=True)
    dqkv, inner_a = attend_backward(qkv, dcontext, lse, lengths, cosine, sine)
    if planar:
        dqkv = after(dqkv, reduced[3].third((inner_a,)), out_reduced.second((inner_a,)))
    inner_a = lax.psum(inner_a[:, 0], "col")[:, None]
    qkv_part = mm_tn(normed_a, dqkv).astype(bf16)
    if planar:
        dqkv = after(dqkv, out_reduced.third((qkv_part,)))
        dnormed_part = joint_back([dqkv], [qkv_full], 0, bf16, planar=True)
        dnormed_part = after(dnormed_part, (inner_a,))
        (dnormed_a, qkv_grad), _, _ = plane_step(
            dnormed_part, lambda total: (total,), [], 1, 0, 3, (), qkv_part
        )
        out_grad = out_reduced.result((dnormed_a,))(slice(None))
    else:
        dnormed_a = lax.psum_scatter(
            mm_nt(dqkv, qkv_full).astype(bf16), "col", scatter_dimension=1, tiled=True
        ).astype(f32)
        qkv_grad, out_grad = one_reduction(qkv_part), one_reduction(out_part)
    unit_grads = [one.result((dnormed_a,)) for one in reduced]
    if planar:
        unit_grads.append(lambda cut: last_grad[:, cut])
    gain_a_share = input_gain.astype(f32)
    dinput = dstream + scale_a * gain_a_share * dnormed_a
    dinput = dinput - x_share * (scale_a * scale_a * inner_a / width)
    gain_a_grad = jnp.sum(dnormed_a * x_share * scale_a, axis=0)
    grad_gain_a, grad_gain_b = lax.psum((gain_a_grad, gain_b_grad), "row")

    qkv_grad = qkv_grad.reshape(rows_block, heads, 3, HEAD_DIM)
    grad_query, grad_key, grad_value = (
        qkv_grad[:, :, part].reshape(rows_block, head_width) for part in range(3)
    )
    def unpack(kind, which):
        found = []
        for (of, a, b), grad in zip(chunks, unit_grads):
            if of == kind:
                size = b - a + -(b - a) % 128
                part = grad(slice(which * size, which * size + b - a))
                found.append((a, part.T if which == 2 else part))
        found = [part for _, part in sorted(found, key=lambda item: item[0])]
        return jnp.concatenate(found, axis=0 if which == 2 else 1)

    locals_ = range(local_experts)
    return (
        block_output,
        dinput.astype(bf16),
        grad_gain_a,
        grad_query,
        grad_key,
        grad_value,
        out_grad.T,
        grad_gain_b,
        grad_router_both[:experts].T,
        grad_router_both[experts],
        unpack(None, 0),
        unpack(None, 1),
        unpack(None, 2),
        jnp.stack([unpack(local, 0) for local in locals_]),
        jnp.stack([unpack(local, 1) for local in locals_]),
        jnp.stack([unpack(local, 2) for local in locals_]),
    )


def solution(mesh):
    return jax.shard_map(
        per_device,
        mesh=mesh,
        in_specs=(
            P("row", "col"),
            P(),
            P(),
            P("row", None),
            P("col"),
            P("row", "col"),
            P("row", "col"),
            P("row", "col"),
            P("col", "row"),
            P("col"),
            P("row", None),
            P("row"),
            P("row", "col"),
            P("row", "col"),
            P("col", "row"),
            P("col", "row", None),
            P("col", "row", None),
            P("col", None, "row"),
            P("row", "col"),
        ),
        out_specs=(
            P("row", "col"),
            P("row", "col"),
            P("col"),
            P("row", "col"),
            P("row", "col"),
            P("row", "col"),
            P("col", "row"),
            P("col"),
            P("row", None),
            P("row"),
            P("row", "col"),
            P("row", "col"),
            P("col", "row"),
            P("col", "row", None),
            P("col", "row", None),
            P("col", None, "row"),
        ),
        check_vma=False,
    )
```

```python
import functools
import math

import jax
import jax.numpy as jnp
from jax import lax
from jax.experimental import pallas as pl
from jax.experimental.pallas import tpu as pltpu
from jax.sharding import PartitionSpec as P

HEAD_DIM = 128
SEQ_LEN = 1024
QBLOCK = 256
TILE = 256
norm_eps = 1e-06
rope_base = 1000000.0
bf16 = jnp.bfloat16
f32 = jnp.float32


def mm(left, right):
    return jnp.dot(left, right, preferred_element_type=f32)


def mm_nt(left, right):
    return lax.dot_general(left, right, (((1,), (1,)), ((), ())), preferred_element_type=f32)


def mm_tn(left, right):
    return lax.dot_general(left, right, (((0,), (0,)), ((), ())), preferred_element_type=f32)


def rope_tables():
    positions = jnp.arange(SEQ_LEN).astype(f32)
    freqs = jnp.power(f32(rope_base), -jnp.arange(0, HEAD_DIM, 2).astype(f32) / HEAD_DIM)
    angles = positions[:, None] * freqs[None, :]
    cosine, sine = jnp.cos(angles), jnp.sin(angles)
    return (
        jnp.concatenate([cosine, cosine], axis=-1),
        jnp.concatenate([-sine, sine], axis=-1),
    )


def block_scores(rows, keys, start, length, scale):
    raw = mm_nt(rows, keys) * scale
    query_pos = start + lax.broadcasted_iota(jnp.int32, raw.shape, 0)
    key_pos = lax.broadcasted_iota(jnp.int32, raw.shape, 1)
    return jnp.where((key_pos <= query_pos) & (key_pos < length), raw, -1e30)


def attend_forward_kernel(length_ref, raw_ref, cos_ref, sin_ref, qkv_ref, context_ref, lse_ref):
    length = length_ref[pl.program_id(0)]
    scale = 1.0 / math.sqrt(HEAD_DIM)
    hd = HEAD_DIM
    for part in range(2):
        raw = raw_ref[:, part * hd : (part + 1) * hd]
        turned = raw * cos_ref[...] + pltpu.roll(raw, hd // 2, 1) * sin_ref[...]
        qkv_ref[:, part * hd : (part + 1) * hd] = turned.astype(bf16)
    qkv_ref[:, 2 * hd :] = raw_ref[:, 2 * hd :].astype(bf16)
    for at in range(0, SEQ_LEN, QBLOCK):
        seen = at + QBLOCK
        scores = block_scores(
            qkv_ref[at:seen, :hd], qkv_ref[:seen, hd : 2 * hd], at, length, scale
        )
        top = jnp.max(scores, axis=-1, keepdims=True)
        expo = jnp.exp(scores - top)
        total = jnp.sum(expo, axis=-1, keepdims=True)
        probs = (expo / total).astype(bf16)
        context_ref[at:seen, :] = mm(probs, qkv_ref[:seen, 2 * hd :]).astype(bf16)
        lse_ref[at:seen, :] = jnp.broadcast_to(top + jnp.log(total), (QBLOCK, hd))


def attend_forward(raw, lengths, cosine, sine):
    tokens, width = raw.shape
    heads = width // (3 * HEAD_DIM)
    slots = tokens // SEQ_LEN
    wide = pl.BlockSpec((SEQ_LEN, 3 * HEAD_DIM), lambda s, h, _: (s, h))
    one = pl.BlockSpec((SEQ_LEN, HEAD_DIM), lambda s, h, _: (s, h))
    table = pl.BlockSpec((SEQ_LEN, HEAD_DIM), lambda s, h, _: (0, 0))
    pairs = slots * heads * SEQ_LEN * SEQ_LEN
    return pl.pallas_call(
        attend_forward_kernel,
        grid_spec=pltpu.PrefetchScalarGridSpec(
            num_scalar_prefetch=1,
            grid=(slots, heads),
            in_specs=[wide, table, table],
            out_specs=[wide, one, one],
        ),
        out_shape=[
            jax.ShapeDtypeStruct((tokens, width), bf16),
            jax.ShapeDtypeStruct((tokens, heads * HEAD_DIM), bf16),
            jax.ShapeDtypeStruct((tokens, heads * HEAD_DIM), f32),
        ],
        cost_estimate=pl.CostEstimate(
            flops=3 * HEAD_DIM * pairs, bytes_accessed=8 * tokens * width, transcendentals=pairs
        ),
        name="attend_forward",
    )(lengths, raw, cosine, sine)


def attend_backward_kernel(
    length_ref, qkv_ref, dcontext_ref, lse_ref, cos_ref, sin_ref, dqkv_ref, inner_ref, dk_ref, dv_ref
):
    length = length_ref[pl.program_id(0)]
    scale = 1.0 / math.sqrt(HEAD_DIM)
    hd = HEAD_DIM
    @pl.when(pl.program_id(1) == 0)
    def _():
        inner_ref[...] = jnp.zeros_like(inner_ref)

    dk_ref[...] = jnp.zeros_like(dk_ref)
    dv_ref[...] = jnp.zeros_like(dv_ref)

    def turn_back(grad, rows):
        back = grad * cos_ref[rows, :] - pltpu.roll(grad, hd // 2, 1) * sin_ref[rows, :]
        return back.astype(bf16)

    for at in range(0, SEQ_LEN, QBLOCK):
        seen = at + QBLOCK
        rows = qkv_ref[at:seen, :hd]
        keys = qkv_ref[:seen, hd : 2 * hd]
        drows = dcontext_ref[at:seen, :]
        scores = block_scores(rows, keys, at, length, scale)
        probs = jnp.exp(scores - lse_ref[at:seen, :1])
        dv_ref[:seen, :] += mm_tn(probs.astype(bf16), drows)
        dprobs = mm_nt(drows, qkv_ref[:seen, 2 * hd :])
        dscore = probs * (dprobs - jnp.sum(dprobs * probs, axis=-1, keepdims=True))
        draw = (dscore * scale).astype(bf16)
        dquery = mm(draw, keys)
        dk_ref[:seen, :] += mm_tn(draw, rows)
        dqkv_ref[at:seen, :hd] = turn_back(dquery, slice(at, seen))
        inner_ref[at:seen, :] += jnp.sum(dquery * rows.astype(f32), axis=-1, keepdims=True)
    dkey, dvalue = dk_ref[...], dv_ref[...]
    dqkv_ref[:, hd : 2 * hd] = turn_back(dkey, slice(None))
    dqkv_ref[:, 2 * hd :] = dvalue.astype(bf16)
    inner_ref[...] += jnp.sum(
        dkey * qkv_ref[:, hd : 2 * hd].astype(f32) + dvalue * qkv_ref[:, 2 * hd :].astype(f32),
        axis=-1,
        keepdims=True,
    )


def attend_backward(qkv, dcontext, lse, lengths, cosine, sine):
    tokens, width = qkv.shape
    heads = width // (3 * HEAD_DIM)
    slots = tokens // SEQ_LEN
    wide = pl.BlockSpec((SEQ_LEN, 3 * HEAD_DIM), lambda s, h, _: (s, h))
    one = pl.BlockSpec((SEQ_LEN, HEAD_DIM), lambda s, h, _: (s, h))
    table = pl.BlockSpec((SEQ_LEN, HEAD_DIM), lambda s, h, _: (0, 0))
    pairs = slots * heads * SEQ_LEN * SEQ_LEN
    return pl.pallas_call(
        attend_backward_kernel,
        grid_spec=pltpu.PrefetchScalarGridSpec(
            num_scalar_prefetch=1,
            grid=(slots, heads),
            in_specs=[wide, one, one, table, table],
            out_specs=[wide, pl.BlockSpec((SEQ_LEN, 1), lambda s, h, _: (s, 0))],
            scratch_shapes=[pltpu.VMEM((SEQ_LEN, HEAD_DIM), f32)] * 2,
        ),
        out_shape=[
            jax.ShapeDtypeStruct((tokens, width), bf16),
            jax.ShapeDtypeStruct((tokens, 1), f32),
        ],
        cost_estimate=pl.CostEstimate(
            flops=8 * HEAD_DIM * pairs, bytes_accessed=8 * tokens * width, transcendentals=pairs
        ),
        name="attend_backward",
    )(lengths, qkv, dcontext, lse, cosine, sine)


PAIRS = [(0, 1), (1, 0), (2, 3), (3, 2)]
MIDDLE = [(1, 2), (2, 1)]
OUTWARD = [(1, 0), (2, 3)]
INWARD = [(0, 1), (3, 2)]


class Gathered:
    def __init__(self, part, *groups):
        self.part = part
        if lax.axis_size("row") != 4:
            self.pieces = (lax.all_gather(part, "row", axis=0, tiled=True),)
            return
        part = after(part, *groups)
        self.partner = lax.ppermute(part, "row", PAIRS)
        self.near_mid = lax.ppermute(part, "row", MIDDLE)
        self.pieces = None

    def second(self, *groups):
        if self.pieces is None:
            self.near_out = lax.ppermute(after(self.near_mid, *groups), "row", OUTWARD)
            self.far_mid = lax.ppermute(after(self.partner, *groups), "row", MIDDLE)
            return (self.partner, self.near_mid)
        return ()

    def third(self, *groups):
        if self.pieces is None:
            self.far_out = lax.ppermute(after(self.far_mid, *groups), "row", OUTWARD)
            self.pieces = (
                self.part, self.partner, self.near_mid, self.far_mid, self.near_out, self.far_out
            )
            return (self.far_mid, self.near_out)
        return ()


def places(z):
    pair = z // 2
    return z, z + 1 - 2 * lax.rem(z, 2), 2 - pair, 3 - 3 * pair


class RowGather:
    def __init__(self, packs, wholes, sems):
        self.packs, self.wholes, (self.send_sems, self.recv_sems) = packs, wholes, sems
        self.z = lax.axis_index("row")
        self.own, self.partner, self.near, self.far = places(self.z)
        self.across = 3 - self.z
        self.in_middle = (self.z == 1) | (self.z == 2)
        self.outside = jnp.logical_not(self.in_middle)

    def copy_of(self, kind, at, source, block, target):
        return pltpu.make_async_remote_copy(
            src_ref=source,
            dst_ref=self.wholes[at].at[block],
            send_sem=self.send_sems.at[kind, at],
            recv_sem=self.recv_sems.at[kind, at],
            device_id={"row": target},
            device_id_type=pl.DeviceIdType.MESH,
        )

    def swap(self, at):
        return self.copy_of(0, at, self.packs[at], self.own, self.partner)

    def swap_middle(self, at):
        return self.copy_of(1, at, self.packs[at], self.own, self.across)

    def second_middle(self, at):
        return self.copy_of(2, at, self.wholes[at].at[self.partner], self.partner, self.across)

    def hand_near(self, at):
        return self.copy_of(3, at, self.wholes[at].at[self.near], self.near, self.partner)

    def hand_far(self, at):
        return self.copy_of(4, at, self.wholes[at].at[self.far], self.far, self.partner)

    def greet(self, barrier):
        signal_to(barrier, {"row": self.partner})

        @pl.when(self.in_middle)
        def _():
            signal_to(barrier, {"row": self.across})
            pl.semaphore_wait(barrier, 2)

        @pl.when(self.outside)
        def _():
            pl.semaphore_wait(barrier, 1)

    def begin(self):
        for at in range(len(self.packs)):
            @pl.when(self.in_middle)
            def _():
                self.swap_middle(at).start()

            self.swap(at).start()

    def hand_on(self, at):
        @pl.when(self.in_middle)
        def _():
            self.swap_middle(at).wait_recv()
            self.hand_near(at).start()
            self.swap(at).wait_recv()
            self.second_middle(at).start()

    def hand_last(self, at):
        @pl.when(self.in_middle)
        def _():
            self.second_middle(at).wait_recv()
            self.hand_far(at).start()

    def finish(self):
        for at in range(len(self.packs)):
            @pl.when(self.in_middle)
            def _():
                for copy in (
                    self.swap,
                    self.swap_middle,
                    self.second_middle,
                    self.hand_near,
                    self.hand_far,
                ):
                    copy(at).wait_send()

            @pl.when(self.outside)
            def _():
                self.swap(at).wait()
                self.hand_near(at).wait_recv()
                self.hand_far(at).wait_recv()


class RowReduce:
    def __init__(self, grads, total, refs):
        self.grads, self.total = grads, total
        self.far_in, self.near_in, self.far_sum, self.near_sum, self.last = refs[:5]
        self.held, self.more, self.send_sems, self.recv_sems, self.local_sems = refs[5:]
        self.z = lax.axis_index("row")
        self.own, self.partner, self.near, self.far = places(self.z)
        self.across = 3 - self.z
        self.in_middle = (self.z == 1) | (self.z == 2)
        self.outside = jnp.logical_not(self.in_middle)

    def copy_of(self, kind, source, target, device):
        return pltpu.make_async_remote_copy(
            src_ref=source,
            dst_ref=target,
            send_sem=self.send_sems.at[kind],
            recv_sem=self.recv_sems.at[kind],
            device_id={"row": device},
            device_id_type=pl.DeviceIdType.MESH,
        )

    def send_far(self):
        return self.copy_of(0, self.grads.at[self.far], self.far_in, self.partner)

    def send_near(self):
        return self.copy_of(1, self.grads.at[self.near], self.near_in, self.partner)

    def cross_far(self):
        return self.copy_of(2, self.far_in, self.far_sum, self.across)

    def cross_near(self):
        return self.copy_of(3, self.near_in, self.near_sum, self.across)

    def swap_middle(self):
        return self.copy_of(4, self.far_sum, self.last, self.partner)

    def swap_outer(self):
        return self.copy_of(4, self.grads.at[self.partner], self.last, self.partner)

    def load(self, kind, block):
        target = self.more if kind % 2 else self.held
        return pltpu.make_async_copy(self.grads.at[block], target, self.local_sems.at[kind])

    def add(self, target, source):
        @pl.loop(0, target.shape[0], step=64)
        def _(at):
            tile = pl.ds(pl.multiple_of(at, 64), 64)
            target[tile, :] = (target[tile, :].astype(f32) + source[tile, :].astype(f32)).astype(bf16)

    def begin(self):
        @pl.when(self.outside)
        def _():
            self.send_far().start()
            self.send_near().start()
            self.swap_outer().start()
            self.load(3, self.own).start()

        @pl.when(self.in_middle)
        def _():
            self.load(0, self.far).start()
            self.load(1, self.near).start()

    def second_far(self):
        @pl.when(self.in_middle)
        def _():
            self.load(0, self.far).wait()
            self.send_far().wait_recv()
            self.add(self.far_in, self.held)
            self.cross_far().start()
            self.load(2, self.partner).start()

    def second_near(self):
        @pl.when(self.in_middle)
        def _():
            self.load(1, self.near).wait()
            self.send_near().wait_recv()
            self.add(self.near_in, self.more)
            self.cross_near().start()
            self.load(3, self.own).start()

    def third(self):
        @pl.when(self.in_middle)
        def _():
            self.load(2, self.partner).wait()
            self.cross_far().wait_recv()
            self.add(self.far_sum, self.held)
            self.swap_middle().start()

    def finish(self):
        self.load(3, self.own).wait()
        self.swap_outer().wait_recv()

        @pl.when(self.in_middle)
        def _():
            self.cross_near().wait_recv()

        @pl.loop(0, self.total.shape[0], step=64)
        def _(at):
            tile = pl.ds(pl.multiple_of(at, 64), 64)
            self.total[tile, :] = self.more[tile, :].astype(f32) + self.last[tile, :].astype(f32)

        @pl.when(self.in_middle)
        def _():
            @pl.loop(0, self.total.shape[0], step=64)
            def _(at):
                tile = pl.ds(pl.multiple_of(at, 64), 64)
                self.total[tile, :] += self.near_sum[tile, :].astype(f32)

            self.cross_far().wait_send()
            self.cross_near().wait_send()
            self.swap_middle().wait_send()

        @pl.when(self.outside)
        def _():
            self.send_far().wait_send()
            self.send_near().wait_send()
            self.swap_outer().wait_send()


class RowHop:
    def __init__(self, kind, given, found, sems):
        self.kind, self.given, self.found, (self.send_sems, self.recv_sems) = kind, given, found, sems
        self.z = lax.axis_index("row")
        self.partner, self.across = places(self.z)[1], 3 - self.z
        self.in_middle = (self.z == 1) | (self.z == 2)
        self.outside = jnp.logical_not(self.in_middle)

    def copy_of(self, at, source, target, device):
        return pltpu.make_async_remote_copy(
            src_ref=source,
            dst_ref=target,
            send_sem=self.send_sems.at[at],
            recv_sem=self.recv_sems.at[at],
            device_id={"row": device},
            device_id_type=pl.DeviceIdType.MESH,
        )

    def across_copy(self):
        if self.kind == 1:
            return self.copy_of(0, self.given[0], self.found[1], self.across)
        return self.copy_of(0, self.given[0], self.found[0], self.across)

    def outward_copy(self):
        if self.kind == 1:
            return self.copy_of(1, self.given[0], self.found[0], self.partner)
        if self.kind == 3:
            return self.copy_of(1, self.given[0], self.found[0], self.partner)
        return self.copy_of(1, self.given[1], self.found[1], self.partner)

    def last_copy(self):
        return self.copy_of(2, self.found[0], self.found[2], self.partner)

    def begin(self):
        barrier = pltpu.get_barrier_semaphore()
        signal_to(barrier, {"row": self.partner})

        @pl.when(self.in_middle)
        def _():
            signal_to(barrier, {"row": self.across})
            pl.semaphore_wait(barrier, 2)
            if self.kind != 3:
                self.across_copy().start()
            self.outward_copy().start()

        @pl.when(self.outside)
        def _():
            pl.semaphore_wait(barrier, 1)
            if self.kind == 1:
                self.outward_copy().start()

    def finish(self):
        @pl.when(self.in_middle)
        def _():
            if self.kind != 3:
                self.across_copy().wait()
            if self.kind == 23:
                self.last_copy().start()
            if self.kind == 1:
                self.outward_copy().wait()
            else:
                self.outward_copy().wait_send()
            if self.kind == 23:
                self.last_copy().wait_send()

        @pl.when(self.outside)
        def _():
            if self.kind == 1:
                self.outward_copy().wait()
            else:
                self.outward_copy().wait_recv()
            if self.kind == 23:
                self.last_copy().wait_recv()


HOP_COUNTS = {1: (1, 2), 2: (2, 2), 3: (1, 1), 23: (2, 3), None: (0, 0)}


def hop_parts(hop, number):
    if hop is None:
        return [], [], [], pltpu.CompilerParams()
    kind, given = hop
    shape = jax.ShapeDtypeStruct(given[0].shape, bf16)
    scratch = [pltpu.SemaphoreType.DMA((3,)), pltpu.SemaphoreType.DMA((3,))]
    params = pltpu.CompilerParams(collective_id=number, has_side_effects=True)
    return list(given), [shape] * HOP_COUNTS[kind][1], scratch, params


def hop_kernel(kind, *refs):
    given, found = HOP_COUNTS[kind]
    hop = RowHop(kind, refs[:given], refs[given : given + found], refs[given + found :])
    hop.begin()
    hop.finish()


def hop_now(hop, number):
    given, shapes, scratch, params = hop_parts(hop, number)
    anywhere = pl.BlockSpec(memory_space=pl.ANY)
    return pl.pallas_call(
        functools.partial(hop_kernel, hop[0]),
        in_specs=[anywhere] * len(given),
        out_specs=[anywhere] * len(shapes),
        out_shape=shapes,
        scratch_shapes=scratch,
        compiler_params=params,
        name="gather_hops",
    )(*given)


def signal_to(barrier, device):
    pl.semaphore_signal(barrier, inc=1, device_id=device, device_id_type=pl.DeviceIdType.MESH)


def gather_kernel(count, *refs):
    rows = RowGather(refs[:count], refs[count : 2 * count], refs[2 * count :])
    rows.greet(pltpu.get_barrier_semaphore())
    rows.begin()
    for at in range(count):
        rows.hand_on(at)
    for at in range(count):
        rows.hand_last(at)
    rows.finish()


PIECES = 4


def plane_kernel(pointwise, given, made, gather, count, reducing, *refs):
    p_ref, inputs = refs[0], refs[1 : 1 + given]
    at = 1 + given
    packs = refs[at : at + count]
    at += count
    grads = refs[at] if reducing else None
    at += reducing
    results = refs[at : at + made]
    at += made
    total_ref = refs[at] if reducing else None
    at += reducing
    whole_refs = refs[at : at + gather + count]
    at += gather + count
    mine, from_core, from_first, summed, from_second, shared, send_sems, recv_sems, local_sems = refs[
        at : at + 9
    ]
    out_ref = whole_refs[0] if gather else None
    me = lax.axis_index("col")
    core, x, y = lax.rem(me, 2), lax.rem(me // 2, 2), me // 4
    core_mate, x_mate, y_mate = me + 1 - 2 * core, me + 2 - 4 * x, me + 4 - 8 * y
    diagonal = x_mate + 4 - 8 * y
    size = mine.shape[3]
    share = mine.shape[4]
    barrier = pltpu.get_barrier_semaphore()
    for mate in (core_mate, x_mate, y_mate):
        signal_to(barrier, {"col": mate})
    rows, reduction = None, None
    if count or reducing:
        if count:
            rows = RowGather(packs, whole_refs[gather:], refs[at + 9 : at + 11])
            at += 2
        if reducing:
            reduction = RowReduce(grads, total_ref, refs[at + 9 : at + 19])
        chain = rows or reduction
        signal_to(barrier, {"row": chain.partner})

        @pl.when(chain.in_middle)
        def _():
            signal_to(barrier, {"row": chain.across})
            pl.semaphore_wait(barrier, 5)

        @pl.when(chain.outside)
        def _():
            pl.semaphore_wait(barrier, 4)

        if count:
            rows.begin()
        if reducing:
            reduction.begin()
    else:
        pl.semaphore_wait(barrier, 3)

    def remote(kind, i, source, target, mate):
        return pltpu.make_async_remote_copy(
            src_ref=source,
            dst_ref=target,
            send_sem=send_sems.at[kind, i],
            recv_sem=recv_sems.at[kind, i],
            device_id={"col": mate},
            device_id_type=pl.DeviceIdType.MESH,
        )

    def x_first(i):
        return i < PIECES // 2

    def span(i):
        return pl.ds(i * size, size)

    def core_copy(i):
        return remote(0, i, p_ref.at[:, :, 1 - core, span(i), :], from_core.at[i], core_mate)

    def load(i):
        return pltpu.make_async_copy(
            p_ref.at[:, :, core, span(i), :], mine.at[i], local_sems.at[0, i]
        )

    def first_copy(i):
        if x_first(i):
            return remote(1, i, mine.at[i, :, 1 - x], from_first.at[i], x_mate)
        return remote(1, i, mine.at[i, 1 - y], from_first.at[i], y_mate)

    def second_copy(i):
        if x_first(i):
            return remote(2, i, summed.at[i, 1 - y], from_second.at[i], y_mate)
        return remote(2, i, summed.at[i, 1 - x], from_second.at[i], x_mate)

    def columns(i, device):
        return out_ref.at[span(i), pl.ds(pl.multiple_of(device * share, share), share)]

    def spread(kind, i, mate):
        return remote(kind, i, shared.at[i], columns(i, me), mate)

    def keep(i):
        return pltpu.make_async_copy(shared.at[i], columns(i, me), local_sems.at[1, i])

    def pass_on(kind, i, device, mate):
        return remote(kind, i, columns(i, device), columns(i, device), mate)

    def forward(i):
        if x_first(i):
            return pass_on(6, i, y_mate, x_mate)
        return pass_on(6, i, x_mate, y_mate)

    order = [0, 2, 1, 3]
    for i in order:
        core_copy(i).start()
        load(i).start()
    for i in order:
        load(i).wait()
        core_copy(i).wait_recv()
        for a in range(2):
            for b in range(2):
                mine[i, a, b] = (mine[i, a, b].astype(f32) + from_core[i, a, b].astype(f32)).astype(bf16)
        first_copy(i).start()
    for i in order:
        first_copy(i).wait_recv()
        for a in range(2):
            kept = mine[i, a, x] if x_first(i) else mine[i, y, a]
            summed[i, a] = (kept.astype(f32) + from_first[i, a].astype(f32)).astype(bf16)
        second_copy(i).start()
    if count:
        for at in range(count):
            rows.hand_on(at)
    if reducing:
        reduction.second_far()
    for i in order:
        second_copy(i).wait_recv()
        total = summed[i, y if x_first(i) else x].astype(f32) + from_second[i].astype(f32)
        span_rows = slice(i * size, (i + 1) * size)
        values = pointwise(
            total, *[ref[span_rows, :] if ref.shape[0] > 8 else ref[...] for ref in inputs]
        )
        if gather:
            shared[i] = values[0].astype(bf16)
            values = values[1:]
        for ref, value in zip(results, values):
            ref[span_rows, :] = value
        if gather:
            spread(4, i, x_mate).start()
            spread(5, i, y_mate).start()
            spread(3, i, core_mate).start()
            keep(i).start()
    if count:
        rows.hand_last(0)
    if reducing and not gather:
        reduction.second_near()
    if gather:
        for i in order:
            spread(5 if x_first(i) else 4, i, y_mate).wait_recv()
            forward(i).start()
            pass_on(7, i, y_mate if x_first(i) else x_mate, core_mate).start()
        for i in order:
            spread(4 if x_first(i) else 5, i, x_mate).wait_recv()
            pass_on(8, i, x_mate if x_first(i) else y_mate, core_mate).start()
    if count:
        for at in range(1, count):
            rows.hand_last(at)
    if reducing and gather:
        reduction.second_near()
    if reducing:
        reduction.third()
    if gather:
        for i in order:
            forward(i).wait_recv()
            pass_on(9, i, diagonal, core_mate).start()
    for i in order:
        core_copy(i).wait_send()
        first_copy(i).wait_send()
        second_copy(i).wait_send()
        if gather:
            keep(i).wait()
            spread(3, i, core_mate).wait()
            spread(4, i, x_mate).wait_send()
            spread(5, i, y_mate).wait_send()
            forward(i).wait_send()
            for kind, device in (
                (7, y_mate if x_first(i) else x_mate),
                (8, x_mate if x_first(i) else y_mate),
                (9, diagonal),
            ):
                pass_on(kind, i, device, core_mate).wait()
    if count:
        rows.finish()
    if reducing:
        reduction.finish()


def plane_step(partial, pointwise, inputs, made, gather, number, packs=(), grads=None):
    tokens, share = partial.shape[3:]
    size = tokens // PIECES
    count = len(packs)
    reducing = 0 if grads is None else 1
    totals, more_scratch, given_grads = [], [], []
    if reducing:
        block, columns = grads.shape[0] // 4, grads.shape[1]
        given_grads = [grads.reshape(4, block, columns)]
        totals = [jax.ShapeDtypeStruct((block, columns), f32)]
        more_scratch = [pltpu.VMEM((block, columns), bf16)] * 7 + [
            pltpu.SemaphoreType.DMA((5,)),
            pltpu.SemaphoreType.DMA((5,)),
            pltpu.SemaphoreType.DMA((4,)),
        ]
    anywhere = pl.BlockSpec(memory_space=pl.ANY)
    vmem = pl.BlockSpec(memory_space=pltpu.VMEM)
    whole_shapes = [jax.ShapeDtypeStruct((tokens, 8 * share), bf16)] * gather + [
        jax.ShapeDtypeStruct((4,) + pack.shape, bf16) for pack in packs
    ]
    outs = pl.pallas_call(
        functools.partial(plane_kernel, pointwise, len(inputs), made, gather, count, reducing),
        in_specs=[anywhere] + [vmem] * len(inputs) + [anywhere] * (count + reducing),
        out_specs=[vmem] * (made + reducing) + [anywhere] * (gather + count),
        out_shape=[jax.ShapeDtypeStruct((tokens, share), f32)] * made + totals + whole_shapes,
        scratch_shapes=[
            pltpu.VMEM((PIECES, 2, 2, size, share), bf16),
            pltpu.VMEM((PIECES, 2, 2, size, share), bf16),
            pltpu.VMEM((PIECES, 2, size, share), bf16),
            pltpu.VMEM((PIECES, 2, size, share), bf16),
            pltpu.VMEM((PIECES, size, share), bf16),
            pltpu.VMEM((PIECES, size, share), bf16),
            pltpu.SemaphoreType.DMA((10, PIECES)),
            pltpu.SemaphoreType.DMA((10, PIECES)),
            pltpu.SemaphoreType.DMA((2, PIECES)),
        ]
        + [pltpu.SemaphoreType.DMA((5, count))] * (2 if count else 0)
        + more_scratch,
        compiler_params=pltpu.CompilerParams(collective_id=number, has_side_effects=True),
        cost_estimate=pl.CostEstimate(
            flops=60 * 10**9, bytes_accessed=32 * tokens * share, transcendentals=0
        ),
        name="plane_step",
    )(partial, *inputs, *packs, *given_grads)
    at = made + reducing
    wholes = [whole.reshape((4 * whole.shape[1],) + whole.shape[2:]) for whole in outs[at + gather :]]
    return outs[:at], outs[at : at + gather], wholes


def gather_now(packs, number):
    if lax.axis_size("row") != 4:
        return [lax.all_gather(pack, "row", axis=0, tiled=True) for pack in packs]
    count = len(packs)
    sent = sum(pack.size for pack in packs) * 2
    anywhere = pl.BlockSpec(memory_space=pl.ANY)
    wholes = pl.pallas_call(
        functools.partial(gather_kernel, count),
        in_specs=[anywhere] * count,
        out_specs=[anywhere] * count,
        out_shape=[jax.ShapeDtypeStruct((4,) + pack.shape, pack.dtype) for pack in packs],
        scratch_shapes=[pltpu.SemaphoreType.DMA((5, count)), pltpu.SemaphoreType.DMA((5, count))],
        compiler_params=pltpu.CompilerParams(collective_id=number, has_side_effects=True),
        cost_estimate=pl.CostEstimate(
            flops=6 * 9000 * sent, bytes_accessed=6 * sent, transcendentals=0
        ),
        name="gather_rows",
    )(*packs)
    return [whole.reshape((4 * whole.shape[1],) + whole.shape[2:]) for whole in wholes]


def join_rows(pieces):
    if len(pieces) == 1:
        return pieces[0]
    part = pieces[0]
    whole = jnp.zeros((4,) + part.shape, part.dtype)
    blocks = (part, pieces[1], pieces[2] + pieces[4], pieces[3] + pieces[5])
    for at, piece in zip(places(lax.axis_index("row")), blocks):
        whole = lax.dynamic_update_slice_in_dim(whole, piece[None], at, 0)
    return whole.reshape((4 * part.shape[0],) + part.shape[1:])


def put_own(whole, part):
    if lax.axis_size("row") != 4:
        return whole
    return lax.dynamic_update_slice_in_dim(
        whole, part, lax.axis_index("row") * part.shape[0], 0
    )


class Reduced:
    def __init__(self, grads, halves=False):
        self.chained = lax.axis_size("row") == 4
        if not self.chained:
            self.total = lax.psum_scatter(grads, "row", scatter_dimension=0, tiled=True).astype(f32)
            return
        z = lax.axis_index("row")
        self.own, self.partner, _, _ = places(z)
        self.grads, self.size = grads, grads.shape[0] // 4
        self.pair = self.rows_of(grads, (1 - z // 2) * 2, 2)
        if halves:
            self.first = lax.ppermute(self.pair[: self.size], "row", INWARD)
        else:
            self.first = lax.ppermute(self.pair, "row", INWARD)

    def first_rest(self, *groups):
        rest = after(self.pair[self.size :], *groups)
        self.first = jnp.concatenate([self.first, lax.ppermute(rest, "row", INWARD)], axis=0)
        return (rest,)

    def rows_of(self, value, at, count):
        return lax.dynamic_slice_in_dim(value, at * self.size, count * self.size, 0)

    def two(self, at, cut=slice(None)):
        mine = self.rows_of(self.grads, at, 1)[:, cut].astype(f32)
        return mine + self.rows_of(self.crossed, lax.rem(at, 2), 1)[:, cut].astype(f32)

    def second(self, *groups):
        if not self.chained:
            return ()
        first = after(self.first, *groups)
        value = (self.pair.astype(f32) + first.astype(f32)).astype(bf16)
        self.crossed = lax.ppermute(value, "row", MIDDLE)
        return (value,)

    def third(self, *groups):
        if not self.chained:
            return ()
        self.crossed = after(self.crossed, *groups)
        value = self.two(self.partner).astype(bf16)
        self.swapped = lax.ppermute(value, "row", PAIRS)
        return (value,)

    def result(self, *groups):
        if not self.chained:
            return lambda cut: self.total[:, cut]
        swapped = after(self.swapped, *groups)
        return lambda cut: self.two(self.own, cut) + swapped[:, cut].astype(f32)


def one_reduction(grads):
    one = Reduced(grads)
    one.second()
    one.third()
    return one.result()(slice(None))


def after(value, *groups):
    others = tuple(item for group in groups for item in group)
    return lax.optimization_barrier((value,) + others)[0] if others else value


def expert_kernel(size, steps, count, kind, *refs):
    pieces = refs[:count]
    (x_ref, cot_ref, x_cols, cot_cols, coef_ref) = refs[count : count + 5]
    taken, found = HOP_COUNTS[kind]
    at = count + 5 + taken
    (dpair_ref, hidden_ref, sums_ref, grads_ref, whole_ref) = refs[at : at + 5]
    weights, dpair, hidden, sems, out_sem = refs[at + 5 + found : at + 10 + found]
    step = pl.program_id(0)
    final = pl.num_programs(0) - 1
    if kind:
        hop = RowHop(
            kind, refs[count + 5 : at], refs[at + 5 : at + 5 + found], refs[at + 10 + found :]
        )

        @pl.when(step == 0)
        def _():
            hop.begin()

    write = pltpu.make_async_copy(weights, whole_ref, out_sem)

    @pl.when(step == 0)
    def _():
        if count == 1:
            copy = pltpu.make_async_copy(pieces[0], weights, sems.at[0])
            copy.start()
            copy.wait()
        elif count == 2:
            block = pieces[0].shape[0]

            def block_copy(back):
                at = pl.multiple_of(lax.rem(lax.axis_index("row") + back, 4) * block, block)
                source = pieces[1].at[pl.ds(at, block)] if back else pieces[0]
                return pltpu.make_async_copy(source, weights.at[pl.ds(at, block)], sems.at[back])

            for back in range(4):
                block_copy(back).start()
            for back in range(4):
                block_copy(back).wait()
        else:
            z = lax.axis_index("row")
            block = pieces[0].shape[0]

            def copy_of(piece, which):
                at = pl.multiple_of(places(z)[which] * block, block)
                return pltpu.make_async_copy(
                    piece, weights.at[pl.ds(at, block)], sems.at[which]
                )

            copy_of(pieces[0], 0).start()
            copy_of(pieces[1], 1).start()
            in_middle = (z == 1) | (z == 2)

            @pl.when(in_middle)
            def _():
                copy_of(pieces[2], 2).start()
                copy_of(pieces[3], 3).start()

            @pl.when(jnp.logical_not(in_middle))
            def _():
                copy_of(pieces[4], 2).start()
                copy_of(pieces[5], 3).start()

            for which in range(4):
                copy_of(pieces[which], which).wait()
        write.start()

    @pl.when(step < steps)
    def _():
        at = pl.multiple_of(step * TILE, TILE)
        rows, cots = x_ref[...], cot_ref[...]
        scale, weight = coef_ref[:, 0:1], coef_ref[:, 1:2]
        dots = jnp.zeros((TILE, 1), f32)
        inner = jnp.zeros((TILE, 1), f32)
        for a in range(0, size, TILE):
            b = min(a + TILE, size)
            gate = scale * mm(rows, weights[:, a:b])
            up = scale * mm(rows, weights[:, size + a : size + b])
            dhid = mm(cots, weights[:, 2 * size + a : 2 * size + b])
            sigma = jax.nn.sigmoid(gate)
            silu = gate * sigma
            hid = silu * up
            dots += jnp.sum(hid * dhid, axis=1, keepdims=True)
            dhid = weight * dhid
            dgate = dhid * up * sigma * (1.0 + gate * (1.0 - sigma))
            dup = dhid * silu
            inner += jnp.sum(dgate * gate + dup * up, axis=1, keepdims=True)
            for into, at_col, value in (
                ((hidden_ref, hidden), a, weight * hid),
                ((dpair_ref, dpair), a, scale * dgate),
                ((dpair_ref, dpair), size + a, scale * dup),
            ):
                value = value.astype(bf16)
                into[0][:, at_col : at_col + b - a] = value
                into[1][pl.ds(at, TILE), at_col : at_col + b - a] = value
        sums_ref[:, 0:1] = dots
        sums_ref[:, 1:2] = inner

    @pl.when(step >= steps)
    def _():
        for a in range(0, 2 * size, TILE):
            b = min(a + TILE, 2 * size)
            grads_ref[:, a:b] = mm_tn(x_cols[...], dpair[:, a:b]).astype(bf16)
        for a in range(0, size, TILE):
            b = min(a + TILE, size)
            grads_ref[:, 2 * size + a : 2 * size + b] = mm_tn(
                cot_cols[...], hidden[:, a:b]
            ).astype(bf16)

    @pl.when(step == final)
    def _():
        write.wait()
        if kind:
            hop.finish()


def expert_chunk(pieces, scaled, cots, coef, hop=None, number=None):
    tokens, width = scaled.shape
    size = pieces[0].shape[1] // 3
    steps, more_steps = tokens // TILE, width // TILE
    count = len(pieces)
    rows = lambda i: (jnp.minimum(i, steps - 1), 0)
    cols = lambda i: (0, jnp.maximum(i - steps, 0))
    down = lambda i: (jnp.maximum(i - steps, 0), 0)
    anywhere = pl.BlockSpec(memory_space=pl.ANY)
    more, more_shapes, more_scratch, params = hop_parts(hop, number)
    outs = pl.pallas_call(
        functools.partial(expert_kernel, size, steps, count, hop and hop[0]),
        grid_spec=pl.GridSpec(
            grid=(steps + more_steps,),
            in_specs=[pl.BlockSpec(memory_space=pl.ANY)] * count
            + [
                pl.BlockSpec((TILE, width), rows),
                pl.BlockSpec((TILE, width), rows),
                pl.BlockSpec((tokens, TILE), cols),
                pl.BlockSpec((tokens, TILE), cols),
                pl.BlockSpec((TILE, 2), rows),
            ]
            + [anywhere] * len(more),
            out_specs=[
                pl.BlockSpec((TILE, 2 * size), rows),
                pl.BlockSpec((TILE, size), rows),
                pl.BlockSpec((TILE, 2), rows),
                pl.BlockSpec((TILE, 3 * size), down),
                anywhere,
            ]
            + [anywhere] * len(more_shapes),
            scratch_shapes=[
                pltpu.VMEM((width, 3 * size), bf16),
                pltpu.VMEM((tokens, 2 * size), bf16),
                pltpu.VMEM((tokens, size), bf16),
                pltpu.SemaphoreType.DMA((4,)),
                pltpu.SemaphoreType.DMA,
            ]
            + more_scratch,
        ),
        out_shape=[
            jax.ShapeDtypeStruct((tokens, 2 * size), bf16),
            jax.ShapeDtypeStruct((tokens, size), bf16),
            jax.ShapeDtypeStruct((tokens, 2), f32),
            jax.ShapeDtypeStruct((width, 3 * size), bf16),
            jax.ShapeDtypeStruct((width, 3 * size), bf16),
        ]
        + more_shapes,
        compiler_params=params,
        cost_estimate=pl.CostEstimate(
            flops=12 * tokens * width * size,
            bytes_accessed=8 * tokens * width + 24 * width * size,
            transcendentals=tokens * size,
        ),
        name="expert_chunk",
    )(*pieces, scaled, cots, scaled, cots, coef, *more)
    return outs[:5], outs[5:]


def joint_kernel(count, based, planar, kind, *refs):
    taken, found = HOP_COUNTS[kind]
    at = 2 * count + based + taken
    out_ref = refs[at]
    if kind:
        hop = RowHop(kind, refs[at - taken : at], refs[at + 1 : at + 1 + found], refs[at + 1 + found :])

        @pl.when(pl.program_id(0) == 0)
        def _():
            hop.begin()

    for a in range(0, refs[count].shape[0], TILE):
        total = refs[2 * count][:, a : a + TILE].astype(f32) if based else None
        for left, weights in zip(refs[:count], refs[count : 2 * count]):
            part = mm_nt(left[...], weights[a : a + TILE, :])
            total = part if total is None else total + part
        if planar:
            at = a // TILE
            out_ref[at // 4, at // 2 % 2, at % 2] = total.astype(out_ref.dtype)
        else:
            out_ref[:, a : a + TILE] = total.astype(out_ref.dtype)
    if kind:
        @pl.when(pl.program_id(0) == pl.num_programs(0) - 1)
        def _():
            hop.finish()


def joint_back(lefts, weights, column, kind, *base, planar=False, hop=None, number=None):
    tokens, width = lefts[0].shape[0], weights[0].shape[0]
    row = lambda i: (i, 0)
    fixed = lambda i: (0, column)
    depth = sum(left.shape[1] for left in lefts)
    more, more_shapes, more_scratch, params = hop_parts(hop, number)
    anywhere = pl.BlockSpec(memory_space=pl.ANY)
    out_spec = pl.BlockSpec((TILE, width), row)
    if planar:
        out_spec = pl.BlockSpec((2, 2, 2, TILE, TILE), lambda i: (0, 0, 0, i, 0))
    outs = pl.pallas_call(
        functools.partial(joint_kernel, len(lefts), len(base), planar, hop and hop[0]),
        grid=(tokens // TILE,),
        in_specs=[pl.BlockSpec((TILE, left.shape[1]), row) for left in lefts]
        + [
            pl.BlockSpec((width, left.shape[1]), fixed, pipeline_mode=pl.Buffered(1))
            for left in lefts
        ]
        + [pl.BlockSpec((TILE, width), row)] * len(base)
        + [anywhere] * len(more),
        out_specs=[out_spec] + [anywhere] * len(more_shapes),
        out_shape=[
            jax.ShapeDtypeStruct((2, 2, 2, tokens, TILE) if planar else (tokens, width), kind)
        ]
        + more_shapes,
        scratch_shapes=more_scratch,
        compiler_params=params,
        cost_estimate=pl.CostEstimate(
            flops=2 * tokens * width * depth,
            bytes_accessed=2 * (tokens + width) * depth + 4 * tokens * width,
            transcendentals=0,
        ),
        name="joint_back",
    )(*lefts, *weights, *base, *more)
    return outs[0] if hop is None else outs


def split_three(values):
    high = values.astype(bf16)
    rest = values - high.astype(f32)
    middle = rest.astype(bf16)
    return high, middle, (rest - middle.astype(f32)).astype(bf16)


def cuts_of(width, sizes):
    cuts, at = [], 0
    for size in sizes:
        if at + size < width:
            cuts.append((at, at + size))
            at += size
    return cuts + [(at, width)]


def stream_step(total, rows, gain):
    stream = rows.astype(f32) + total
    return stream * gain, stream


def dstream_step(total, back, cots, stream, damp, gain):
    dscaled = back + total
    dstream = cots.astype(f32) + gain * dscaled - stream * damp
    return dstream, dstream, dscaled


def per_device(
    block_input,
    seq_lengths,
    slot_order,
    routes,
    input_gain,
    query_weight,
    key_weight,
    value_weight,
    output_weight,
    mlp_gain,
    router_weight,
    score_shared,
    gate_shared,
    up_shared,
    down_shared,
    gate_expert,
    up_expert,
    down_expert,
    grad_output,
):
    tokens, share = block_input.shape
    cols = lax.axis_size("col")
    col_id = lax.axis_index("col")
    row_id = lax.axis_index("row")
    width = share * cols
    slots = tokens // SEQ_LEN
    local_experts = gate_expert.shape[0]
    experts = router_weight.shape[1]
    head_width = query_weight.shape[1]
    heads = head_width // HEAD_DIM
    rows_block = query_weight.shape[0]
    lengths = lax.dynamic_slice_in_dim(seq_lengths[slot_order], row_id * slots, slots, 0)
    cosine, sine = rope_tables()

    def by_head(weight):
        return weight.reshape(rows_block, heads, 1, HEAD_DIM)

    qkv_pack = jnp.concatenate(
        [by_head(query_weight), by_head(key_weight), by_head(value_weight)], axis=2
    ).reshape(rows_block, 3 * head_width)
    router_pack = jnp.concatenate([router_weight, score_shared[:, None]], axis=1)
    router_pack = jnp.pad(router_pack, ((0, 0), (0, -router_pack.shape[1] % 128)))
    out_pack = jnp.concatenate([output_weight.T, router_pack], axis=1)
    (qkv_whole,) = gather_now([qkv_pack], 0)
    qkv_full = put_own(qkv_whole, qkv_pack)
    out_gathered = Gathered(out_pack, (qkv_whole,))
    out_gathered.second()
    out_gathered.third()
    out_weights = join_rows(out_gathered.pieces)
    out_full = out_weights[:, :head_width]
    router_full = out_weights[:, head_width : head_width + experts + 1]
    shared_cuts = [(None, a, b) for a, b in cuts_of(gate_shared.shape[1], (512,))]
    expert_cuts = [
        (local, a, b)
        for local in range(local_experts)
        for a, b in cuts_of(gate_expert.shape[2], (512, 512))
    ]
    chunks = shared_cuts[-1:] + expert_cuts[:-1] + shared_cuts[:-1] + expert_cuts[-1:]

    def pack(kind, a, b):
        if kind is None:
            parts = [gate_shared[:, a:b], up_shared[:, a:b], down_shared[a:b].T]
        else:
            parts = [gate_expert[kind, :, a:b], up_expert[kind, :, a:b], down_expert[kind, a:b].T]
        fill = -(b - a) % 128
        return jnp.concatenate([jnp.pad(part, ((0, 0), (0, fill))) for part in parts], axis=1)

    packs = [pack(*chunk) for chunk in chunks]
    chained = lax.axis_size("row") == 4
    planar = chained and cols == 8 and share == TILE
    gathered = {}
    gathered[0] = Gathered(packs[0], (qkv_whole,))

    gain_rows = jnp.pad(jnp.stack([input_gain, mlp_gain]), ((0, 14), (0, 0)))
    both_in = lax.all_gather(
        jnp.concatenate([block_input, gain_rows], axis=0), "col", axis=1, tiled=True
    )
    rows_in, gains = both_in[:tokens], both_in[tokens : tokens + 2].astype(f32)
    cot_rows = lax.all_gather(grad_output, "col", axis=1, tiled=True)
    rows_f = rows_in.astype(f32)
    scale_a = lax.rsqrt(jnp.mean(rows_f * rows_f, axis=-1, keepdims=True) + norm_eps)
    normed_a = (rows_f * scale_a * gains[0]).astype(bf16)
    raw = mm(normed_a, qkv_full)
    raw = after(raw, gathered[0].second())
    qkv, context, lse = attend_forward(raw, lengths, cosine, sine)
    context = after(context, gathered[0].third())
    x_share = block_input.astype(f32)
    gain_b = mlp_gain.astype(f32)
    if planar:
        attn_part = joint_back([context], [out_weights], 0, bf16, planar=True)
        attn_part = after(attn_part, (cot_rows,))
        (stream,), (scaled,), wholes_now = plane_step(
            attn_part, stream_step, [block_input, gain_b[None]], 1, 1, 1, packs[1:2]
        )
        gathered[1] = (packs[1], wholes_now[0])
    else:
        attn_part = mm_nt(context, out_full).astype(bf16)
        attn_sum = lax.psum_scatter(attn_part, "col", scatter_dimension=1, tiled=True)
        scaled_share, stream = stream_step(attn_sum.astype(f32), block_input, gain_b[None])
        scaled = lax.all_gather(scaled_share.astype(bf16), "col", axis=1, tiled=True)
    for at in range(1, 1 if planar else len(chunks)):
        if at not in gathered:
            gathered[at] = Gathered(packs[at], (scaled,))

    def pieces_of(at):
        return gathered[at] if isinstance(gathered[at], tuple) else gathered[at].pieces

    stream_f = scaled.astype(f32) / gains[1]
    scale_b = lax.rsqrt(jnp.mean(stream_f * stream_f, axis=1, keepdims=True) + norm_eps)

    both_logits = scale_b * mm(scaled, router_full)
    logits, slogit = both_logits[:, :experts], both_logits[:, experts]
    top = jnp.max(logits, axis=-1, keepdims=True)
    expo = jnp.exp(logits - top)
    router_probs = expo / jnp.sum(expo, axis=-1, keepdims=True)
    shared_gate = jax.nn.sigmoid(slogit)

    inner = jnp.zeros((tokens,), f32)
    dots = {}
    members, shares = {None: None}, {None: shared_gate}
    for local in range(local_experts):
        expert = col_id * local_experts + local
        members[local] = jnp.any(routes == expert, axis=1)
        column = lax.dynamic_index_in_dim(router_probs, expert, 1, False)
        shares[local] = jnp.where(members[local], column, 0.0)
    dpairs, hiddens, wholes, reduced = [], [], [], []
    last = len(chunks) - 1
    waits = ()
    if not planar:
        for at in range(1, len(chunks)):
            gathered[at].second()
            gathered[at].third()

    carried = []
    for at, (kind, a, b) in enumerate(chunks):
        coef = jnp.concatenate([scale_b, shares[kind][:, None]], axis=1)
        coef = after(coef, waits)
        hop = None
        if planar:
            hop = {0: (1, packs[2:3]), 1: (2, carried), 2: (1, packs[3:4]), 3: (1, packs[4:5])}.get(at)
        (dpair, hidden, sums, grads, whole), found = expert_chunk(
            pieces_of(at), scaled, cot_rows, coef, hop, 4 + at
        )
        carried = carried + list(found) if at == 1 else list(found)
        dots[kind] = dots.get(kind, 0.0) + sums[:, 0]
        inner = inner + sums[:, 1]
        dpairs.append(dpair)
        hiddens.append(hidden)
        wholes.append(whole)
        now = (sums,)
        waits = ()
        if at < last or not planar:
            reduced.append(Reduced(grads, planar and at == 1))
        if planar and at == 0:
            waits = (reduced[0].pair,)
        elif planar and at == 1:
            first_pair = after(dpairs[0], reduced[0].second(now), (reduced[1].pair,))
            dscaled_early, last_piece = joint_back(
                [first_pair, dpair], wholes, 0, f32, hop=(3, carried[2:3]), number=9
            )
            gathered[2] = (packs[2], *carried[:2], carried[2], carried[3], last_piece)
            waits = (dscaled_early,)
        elif planar and at == 2:
            rest = hop_now((23, [after(carried[0], now, (reduced[2].pair,)), carried[1]]), 10)
            gathered[3] = (packs[3], *carried, *rest)
            waits = (rest[2],)
        elif planar and at == 3:
            third_pair = after(dpairs[2], reduced[1].first_rest(now), (reduced[3].pair,))
            dscaled_early, *next_pieces = joint_back(
                [third_pair, dpair], wholes[2:], 0, bf16, dscaled_early, hop=(2, carried), number=11
            )
            first_hidden = after(
                hiddens[0], reduced[1].second((dscaled_early,)), reduced[2].second((dscaled_early,))
            )
            moe_early, last_piece = joint_back(
                [first_hidden] + hiddens[1:], wholes, 2, bf16, hop=(3, next_pieces[:1]), number=12
            )
            gathered[4] = (packs[4], *carried, *next_pieces, last_piece)
            waits = (dscaled_early, moe_early) + reduced[0].third((moe_early,))
    now = (sums,)
    if planar:
        waits = reduced[1].third(now)
    else:
        waits = ()
        for one in reduced:
            one.second()
            one.third()
    joined = 4 if planar else 0
    bases = ((dscaled_early,), (moe_early,)) if planar else ((), ())
    late_pairs, late_wholes, late_hiddens = dpairs[joined:], wholes[joined:], hiddens[joined:]
    late_pairs[-1] = after(late_pairs[-1], waits)
    dscaled_part = joint_back(late_pairs, late_wholes, 0, bf16, *bases[0], planar=planar)

    named = [jnp.where(members[local], dots[local], 0.0) for local in range(local_experts)]
    table = lax.all_gather(jnp.stack(named + [dots[None], inner]), "col", axis=0)
    dprob = table[:, :local_experts].reshape(experts, tokens).T
    dshared_gate, inner = jnp.sum(table[:, local_experts], axis=0), jnp.sum(table[:, local_experts + 1], axis=0)
    dlogits = router_probs * (dprob - jnp.sum(dprob * router_probs, axis=1, keepdims=True))
    dslogit = dshared_gate * shared_gate * (1.0 - shared_gate)
    dboth = jnp.concatenate([dlogits, dslogit[:, None]], axis=1)
    inner = inner + jnp.sum(dboth * both_logits, axis=1)
    dboth = scale_b * dboth
    parts = split_three(dboth)
    router_rows = lax.dynamic_slice_in_dim(router_full, col_id * share, share, 0)
    back_term = mm_nt(jnp.concatenate(parts, axis=1), jnp.concatenate([router_rows] * 3, axis=1))
    damp = scale_b * scale_b * inner[:, None] / width
    step_inputs = [back_term, grad_output, stream, damp, gain_b[None]]
    if planar:
        (dstream, dscaled, last_grad), (dattn,), _ = plane_step(
            dscaled_part, dstream_step, step_inputs, 2, 1, 2, (), grads
        )
    else:
        dscaled_sum = lax.psum_scatter(dscaled_part, "col", scatter_dimension=1, tiled=True)
        dstream_low, dstream, dscaled = dstream_step(dscaled_sum.astype(f32), *step_inputs)
        dattn = lax.all_gather(dstream_low.astype(bf16), "col", axis=1, tiled=True)
    gain_b_grad = jnp.sum(dscaled * stream, axis=0)

    late_hiddens[-1] = after(late_hiddens[-1], (dattn,))
    moe_part = joint_back(late_hiddens, late_wholes, 2, bf16, *bases[1])
    moe_share = lax.psum_scatter(moe_part, "col", scatter_dimension=1, tiled=True).astype(f32)
    block_output = (stream + moe_share).astype(bf16)
    out_part = mm_tn(dattn, context).astype(bf16)
    dcontext = mm(dattn, out_full).astype(bf16)
    if planar:
        out_reduced = Reduced(out_part)
        dcontext = after(
            dcontext,
            reduced[3].second((dattn,)),
            reduced[2].third((dattn,)),
            (out_reduced.pair,),
        )
    router_left = after(jnp.concatenate(parts, axis=1), (dattn,))
    grad_router_part = mm_tn(router_left, scaled).reshape(3, experts + 1, width).sum(axis=0)
    grad_router_both = lax.psum_scatter(grad_router_part, "row", scatter_dimension=1, tiled=True)
    dqkv, inner_a = attend_backward(qkv, dcontext, lse, lengths, cosine, sine)
    if planar:
        dqkv = after(dqkv, reduced[3].third((inner_a,)), out_reduced.second((inner_a,)))
    inner_a = lax.psum(inner_a[:, 0], "col")[:, None]
    qkv_part = mm_tn(normed_a, dqkv).astype(bf16)
    if planar:
        dqkv = after(dqkv, out_reduced.third((qkv_part,)))
        dnormed_part = joint_back([dqkv], [qkv_full], 0, bf16, planar=True)
        dnormed_part = after(dnormed_part, (inner_a,))
        (dnormed_a, qkv_grad), _, _ = plane_step(
            dnormed_part, lambda total: (total,), [], 1, 0, 3, (), qkv_part
        )
        out_grad = out_reduced.result((dnormed_a,))(slice(None))
    else:
        dnormed_a = lax.psum_scatter(
            mm_nt(dqkv, qkv_full).astype(bf16), "col", scatter_dimension=1, tiled=True
        ).astype(f32)
        qkv_grad, out_grad = one_reduction(qkv_part), one_reduction(out_part)
    unit_grads = [one.result((dnormed_a,)) for one in reduced]
    if planar:
        unit_grads.append(lambda cut: last_grad[:, cut])
    gain_a_share = input_gain.astype(f32)
    dinput = dstream + scale_a * gain_a_share * dnormed_a
    dinput = dinput - x_share * (scale_a * scale_a * inner_a / width)
    gain_a_grad = jnp.sum(dnormed_a * x_share * scale_a, axis=0)
    grad_gain_a, grad_gain_b = lax.psum((gain_a_grad, gain_b_grad), "row")

    qkv_grad = qkv_grad.reshape(rows_block, heads, 3, HEAD_DIM)
    grad_query, grad_key, grad_value = (
        qkv_grad[:, :, part].reshape(rows_block, head_width) for part in range(3)
    )
    def unpack(kind, which):
        found = []
        for (of, a, b), grad in zip(chunks, unit_grads):
            if of == kind:
                size = b - a + -(b - a) % 128
                part = grad(slice(which * size, which * size + b - a))
                found.append((a, part.T if which == 2 else part))
        found = [part for _, part in sorted(found, key=lambda item: item[0])]
        return jnp.concatenate(found, axis=0 if which == 2 else 1)

    locals_ = range(local_experts)
    return (
        block_output,
        dinput.astype(bf16),
        grad_gain_a,
        grad_query,
        grad_key,
        grad_value,
        out_grad.T,
        grad_gain_b,
        grad_router_both[:experts].T,
        grad_router_both[experts],
        unpack(None, 0),
        unpack(None, 1),
        unpack(None, 2),
        jnp.stack([unpack(local, 0) for local in locals_]),
        jnp.stack([unpack(local, 1) for local in locals_]),
        jnp.stack([unpack(local, 2) for local in locals_]),
    )


def solution(mesh):
    return jax.shard_map(
        per_device,
        mesh=mesh,
        in_specs=(
            P("row", "col"),
            P(),
            P(),
            P("row", None),
            P("col"),
            P("row", "col"),
            P("row", "col"),
            P("row", "col"),
            P("col", "row"),
            P("col"),
            P("row", None),
            P("row"),
            P("row", "col"),
            P("row", "col"),
            P("col", "row"),
            P("col", "row", None),
            P("col", "row", None),
            P("col", None, "row"),
            P("row", "col"),
        ),
        out_specs=(
            P("row", "col"),
            P("row", "col"),
            P("col"),
            P("row", "col"),
            P("row", "col"),
            P("row", "col"),
            P("col", "row"),
            P("col"),
            P("row", None),
            P("row"),
            P("row", "col"),
            P("row", "col"),
            P("col", "row"),
            P("col", "row", None),
            P("col", "row", None),
            P("col", None, "row"),
        ),
        check_vma=False,
    )
```
